32 devices in a mesh: seq: 4 (over y, x), fsdp: 8 (over z, core).
Axes of the slice: x: 2, y: 2, z: 4, core: 2. Of those that a mesh axis runs over, the one named last changes fastest.
Arguments:
- tokens: bfloat16 [8, 1536, 1024], P('fsdp', 'seq'), may hold values from -6 to 6
- segment_ids: int32 [8, 1536], P('fsdp', 'seq'), may hold values from 0 to 5, never falling along the last dimension, each value on 1 to 768 neighbouring positions
- random_blocks: int32 [16, 22, 3], P('seq'), may hold values from 1 to 22, as said below
- ln1_gain: bfloat16 [1024], P('fsdp'), may hold values from 0.099609375 to 1.8984375
- ln1_bias: bfloat16 [1024], P('fsdp'), may hold values from -4 to 4
- w_qkv: bfloat16 [1024, 3072], P('fsdp'), may hold values from -0.25 to 0.25
- w_out: bfloat16 [1024, 1024], P('fsdp'), may hold values from -0.5 to 0.5
- ln2_gain: bfloat16 [1024], P('fsdp'), may hold values from 0.099609375 to 1.8984375
- ln2_bias: bfloat16 [1024], P('fsdp'), may hold values from -4 to 4
- w_in: bfloat16 [1024, 4096], P('fsdp'), may hold values from -0.1875 to 0.1875
- b_in: bfloat16 [4096], P('fsdp'), may hold values from -4 to 4
- w_down: bfloat16 [4096, 1024], P('fsdp'), may hold values from -0.09375 to 0.09375
- b_down: bfloat16 [1024], P('fsdp'), may hold values from -4 to 4
- cotangent: bfloat16 [8, 1536, 1024], P('fsdp', 'seq'), may hold values from -6 to 6
Outputs:
- output: bfloat16 [8, 1536, 1024], P('fsdp', 'seq')
- grad_tokens: bfloat16 [8, 1536, 1024], P('fsdp', 'seq')
- grad_ln1_gain: float32 [1024], P('fsdp')
- grad_ln1_bias: float32 [1024], P('fsdp')
- grad_qkv: float32 [1024, 3072], P('fsdp')
- grad_out_proj: float32 [1024, 1024], P('fsdp')
- grad_ln2_gain: float32 [1024], P('fsdp')
- grad_ln2_bias: float32 [1024], P('fsdp')
- grad_in: float32 [1024, 4096], P('fsdp')
- grad_in_bias: float32 [4096], P('fsdp')
- grad_down: float32 [4096, 1024], P('fsdp')
- grad_down_bias: float32 [1024], P('fsdp')
The draws below stay inside these ranges and needn't reach their ends.
Inputs may be any that keep to these rules, and one draw needn't show every extreme that they name: For head h and query block b + 1, the 3 entries random_blocks[h, b, :] are different key blocks, none of them 0, 23, b, b + 1 or b + 2. `segment_ids`: in each sequence the segment numbers start at 0, never fall and take every value up to 5; a document has at most 768 tokens, and some document has exactly that many.
All inputs are finite; a program needn't handle non-finite values.
Results may differ from the reference program's by a relative error of at most 0.014.
Values may be sent and summed in bfloat16 or wider, within the bound.
A program may use at most 256 MiB of HBM per device.

```python
import math
import jax
import jax.numpy as jnp
import numpy as np
from jax import lax

D = 1024
H = 16
DH = 64
FF = 4096
BLK = 64
RAND = 3
SEQ_LEN = 1536
SEQS = 8
NB = 24
DOCS = 6


def draw_random_blocks(key, part):
    middle_ids = jnp.arange(1, NB - 1, dtype=jnp.int32)[None, :, None]
    candidate = jnp.arange(NB, dtype=jnp.int32)[None, None, :]
    ranking = jax.random.randint(key, (H, NB - 2, NB), 0, 65536, dtype=jnp.int32) * NB + candidate
    banned = (candidate == 0) | (candidate == NB - 1) | (jnp.abs(candidate - middle_ids) <= 1)
    ranking = jnp.where(banned, -1, ranking)
    picked = lax.top_k(ranking, RAND)[1]
    return picked.astype(jnp.int32)


def strengthened(array, stream_key, source, target, blocks, factor):
    owner, partner = [(jnp.arange(array.shape[dim]) // (array.shape[dim] // blocks)).reshape([-1 if axis == dim else 1 for axis in range(array.ndim)]) for dim in (source, target)]
    chosen = jax.random.permutation(stream_key, blocks)[partner]
    strong = (owner == chosen) | (owner == (partner + blocks // 2) % blocks)
    return jnp.where(strong, factor * array, array)


def level_of(own_key, dims, shards, smallest, largest):
    factor_of = 1.0
    for position, shards_of in shards:
        draws = jax.random.uniform(jax.random.fold_in(jax.random.fold_in(own_key, 6), position), (shards_of,), jnp.float32, smallest / len(shards), largest / len(shards))
        factor_of = factor_of * jnp.repeat(jnp.exp(draws), dims[position] // shards_of).reshape((-1,) + (1,) * (len(dims) - 1 - position))
    return factor_of


def split_up(number_of, total, most, lean):
    weights = [(1 << 20) // math.isqrt(grade ** lean) + 1 for grade in range(2, number_of + 1)]
    surplus, given = total - most - (number_of - 1), [1] * (number_of - 1)
    while surplus > 0:
        free = [i for i in range(number_of - 1) if given[i] < most]
        mass, budget = sum([weights[i] for i in free]), surplus
        for i in free:
            more = min(most - given[i], max(1, budget * weights[i] // mass), surplus)
            given[i] = given[i] + more
            surplus = surplus - more
    return np.array([most] + given)


def uneven(rng, count, total, limit, slope):
    if count == 2:
        one = jax.random.randint(rng, (), max(1, total - limit), min(limit, total - 1) + 1)
        return jnp.stack([one, total - one])
    lengths = jnp.asarray(split_up(count, total, limit, slope), jnp.int32)
    pairs = (count - 1) // 2
    giver, sink = lengths[1:1 + 2 * pairs:2], lengths[2:2 + 2 * pairs:2]
    slack = jnp.minimum(giver - 1, limit - sink)
    moved = jax.random.randint(jax.random.fold_in(rng, 1), (pairs,), 0, 1 << 20) % (slack + 1)
    lengths = lengths.at[1:1 + 2 * pairs:2].set(giver - moved).at[2:2 + 2 * pairs:2].set(sink + moved)
    return lengths[jax.random.permutation(jax.random.fold_in(rng, 2), count)]


def scatter_about(own_key, extent, deviation, reach, shards=(), held_as=jnp.bfloat16):
    factor_of = level_of(own_key, extent, shards, -0.22, 0.18) if shards else 1.0
    array = jax.random.normal(own_key, extent, jnp.float32) * deviation * factor_of
    return jnp.minimum(jnp.maximum(array, -reach), reach).astype(held_as)


def noise_with(own_key, shape, scale, limit, pieces, heavy, held_as=jnp.bfloat16):
    entries = scale * jax.random.normal(own_key, shape, jnp.float32)
    if pieces:
        entries = entries * level_of(own_key, shape, pieces, -0.22, 0.18)
    return jnp.clip(strengthened(entries, jax.random.fold_in(own_key, 3), *heavy), -limit, limit).astype(held_as)


def setup_inputs(seed: int = 0) -> dict:
    key_of = jax.random.split(jax.random.key(seed), 15)
    return {
        "tokens": scatter_about(key_of[0], (SEQS, SEQ_LEN, D), 1.0, 6.0, ((0, 8), (1, 4))),
        "segment_ids": jax.vmap(lambda own: jnp.searchsorted(jnp.cumsum(uneven(own, DOCS, SEQ_LEN, SEQ_LEN // 2, 2)), jnp.arange(SEQ_LEN), side="right"))(jax.random.split(key_of[1], SEQS)).reshape((SEQS, SEQ_LEN)).astype(jnp.int32),
        "random_blocks": draw_random_blocks(jax.random.fold_in(key_of[14], 71), 0),
        "ln1_gain": jnp.clip(1.0 + 0.18 * jax.random.normal(key_of[3], (D,), jnp.float32), 0.099609375, 1.8984375).astype(jnp.bfloat16),
        "ln1_bias": scatter_about(key_of[4], (D,), 0.3, 4.0, ((0, 8),)),
        "w_qkv": scatter_about(key_of[5], (D, 3 * D), (D // 2) ** -0.5, 0.25, ((0, 8),)),
        "w_out": scatter_about(key_of[6], (D, D), (D // 8) ** -0.5, 0.5, ((0, 8),)),
        "ln2_gain": jnp.clip(1.0 + 0.18 * jax.random.normal(key_of[7], (D,), jnp.float32), 0.099609375, 1.8984375).astype(jnp.bfloat16),
        "ln2_bias": scatter_about(key_of[8], (D,), 0.3, 4.0, ((0, 8),)),
        "w_in": scatter_about(key_of[9], (D, FF), D ** -0.5, 0.1875, ((0, 8),)),
        "b_in": scatter_about(key_of[10], (FF,), 0.5, 4.0, ((0, 8),)),
        "w_down": scatter_about(key_of[11], (FF, D), FF ** -0.5, 0.09375, ((0, 8),)),
        "b_down": scatter_about(key_of[12], (D,), 0.3, 4.0, ((0, 8),)),
        "cotangent": noise_with(key_of[13], (SEQS, SEQ_LEN, D), 1.0, 6.0, ((0, 8), (1, 4)), (0, 2, 8, 2.0)),
    }


@jax.custom_vjp
def lower_precision(v):
    return lax.optimization_barrier(v.astype(jnp.bfloat16)).astype(jnp.float32)

@jax.custom_vjp
def lower_precision_backward(v):
    return v

def low_keep(v):
    return (lower_precision(v), None)

def low_pass(kept, grad):
    return (grad,)

def back_keep(v):
    return (v, None)

def back_low(kept, grad):
    return (lower_precision(grad),)
lower_precision.defvjp(low_keep, low_pass)
lower_precision_backward.defvjp(back_keep, back_low)

def build_lists(random_blocks, blocks):
    middle_ids = jnp.arange(1, blocks - 1, dtype=jnp.int32)
    head_count = random_blocks.shape[0]
    window_ids = jnp.stack([middle_ids - 1, middle_ids, middle_ids + 1], axis=-1)
    global_ids = jnp.stack([jnp.zeros_like(middle_ids), jnp.full_like(middle_ids, blocks - 1)], axis=-1)
    block_list = jnp.concatenate([jnp.broadcast_to(window_ids, (head_count, blocks - 2, 3)), random_blocks.astype(jnp.int32), jnp.broadcast_to(global_ids, (head_count, blocks - 2, 2))], axis=-1)
    usable = jnp.concatenate([jnp.ones((blocks - 2, 3 + random_blocks.shape[2]), dtype=bool), (middle_ids != 1)[:, None], (middle_ids != blocks - 2)[:, None]], axis=-1)
    return (block_list, usable)

def masked_softmax(scores, allowed):
    shifted = jnp.where(allowed, scores, -1e+30)
    top_score = lax.optimization_barrier(jnp.max(shifted, axis=-1, keepdims=True))
    log_total = top_score + jnp.log(lax.optimization_barrier(jnp.sum(jnp.exp(shifted - top_score), axis=-1, keepdims=True)))
    return (jnp.exp(shifted - log_total), log_total)

def layer_norm(token_rows, gain_vec, bias_vec):
    center = token_rows - lax.optimization_barrier(jnp.mean(token_rows, axis=-1, keepdims=True))
    variance = lax.optimization_barrier(jnp.mean(center * center, axis=-1, keepdims=True))
    return center * lax.rsqrt(variance + 1e-05) * gain_vec + bias_vec

def gelu_tanh(pre_act):
    return 0.5 * pre_act * (1.0 + jnp.tanh(0.7978845608028654 * (pre_act + 0.044715 * pre_act * pre_act * pre_act)))

def head_attend(queries, keys_all, values_all, block_list, usable, segments):
    highest_precision = lax.Precision.HIGHEST
    length = queries.shape[0]
    blocks = length // BLK
    slot_count = block_list.shape[1]
    score_scale = 1.0 / math.sqrt(DH)
    blocked_queries = queries.reshape(blocks, BLK, DH)
    neighbour_keys = keys_all.reshape(blocks, BLK, DH)[block_list].reshape(blocks - 2, slot_count * BLK, DH)
    neighbour_values = values_all.reshape(blocks, BLK, DH)[block_list].reshape(blocks - 2, slot_count * BLK, DH)
    seg_blocks = segments.reshape(blocks, BLK)
    key_seg = seg_blocks[block_list].reshape(blocks - 2, slot_count * BLK)
    allowed = (seg_blocks[1:-1][:, :, None] == key_seg[:, None, :]) & jnp.repeat(usable, BLK, axis=1)[:, None, :]
    unscaled_scores = lower_precision_backward(jnp.einsum('vfn,vmn->vfm', blocked_queries[1:-1], neighbour_keys, precision=highest_precision))
    middle_probability, _ = masked_softmax(unscaled_scores * score_scale, allowed)
    middle_output = jnp.einsum('icf,ifl->icl', lower_precision(middle_probability), neighbour_values, precision=highest_precision)
    edge_queries = jnp.concatenate([blocked_queries[0], blocked_queries[-1]], axis=0)
    edge_seg = jnp.concatenate([seg_blocks[0], seg_blocks[-1]], axis=0)
    edge_allowed = edge_seg[:, None] == segments[None, :]
    edge_raw = lower_precision_backward(jnp.dot(edge_queries, keys_all.T, precision=highest_precision))
    prob_edge, _ = masked_softmax(edge_raw * score_scale, edge_allowed)
    out_edge = jnp.dot(lower_precision(prob_edge), values_all, precision=highest_precision)
    return jnp.concatenate([out_edge[:BLK], middle_output.reshape(-1, DH), out_edge[BLK:]], axis=0)

def attention(qkv_rows, segments, random_blocks):
    length = qkv_rows.shape[0]
    head_split = qkv_rows.reshape(length, 3, H, DH).transpose(1, 2, 0, 3)
    block_list, usable = build_lists(random_blocks, length // BLK)
    merged = jax.vmap(head_attend, in_axes=(0, 0, 0, 0, None, None))(head_split[0], head_split[1], head_split[2], block_list, usable, segments)
    return merged.transpose(1, 0, 2).reshape(length, H * DH)

def forward_sequence(token_rows, segments, random_blocks, weights):
    gain_one, bias_one, qkv_weight, out_weight, gain_two, bias_two, in_weight, in_bias, down_weight, down_bias = weights
    highest_precision = lax.Precision.HIGHEST
    normed_one = lower_precision(layer_norm(token_rows, gain_one, bias_one))
    qkv_rows = lower_precision_backward(lower_precision(jnp.dot(normed_one, qkv_weight, precision=highest_precision)))
    att_rows = lower_precision_backward(lower_precision(attention(qkv_rows, segments, random_blocks)))
    branch = lower_precision_backward(jnp.dot(att_rows, out_weight, precision=highest_precision))
    hidden = token_rows + branch
    normed_two = lower_precision(layer_norm(hidden, gain_two, bias_two))
    pre_act = lower_precision_backward(jnp.dot(normed_two, in_weight, precision=highest_precision) + in_bias)
    act_low = lower_precision(gelu_tanh(pre_act))
    return hidden + jnp.dot(act_low, down_weight, precision=highest_precision) + down_bias

def reference(tokens, segment_ids, random_blocks, ln1_gain, ln1_bias, w_qkv, w_out, ln2_gain, ln2_bias, w_in, b_in, w_down, b_down, cotangent):
    params = tuple((weight_item.astype(jnp.float32) for weight_item in (ln1_gain, ln1_bias, w_qkv, w_out, ln2_gain, ln2_bias, w_in, b_in, w_down, b_down)))

    def one_sequence(totals, item):
        seq_tokens, seq_ids, seq_cot = item

        def forward(inputs, weights):
            return forward_sequence(inputs, seq_ids, random_blocks, weights)
        result, pullback = jax.vjp(forward, seq_tokens.astype(jnp.float32), params)
        grad_inputs, grad_params = pullback(seq_cot.astype(jnp.float32))
        totals = jax.tree.map(jnp.add, totals, grad_params)
        return (totals, (result.astype(jnp.bfloat16), grad_inputs.astype(jnp.bfloat16)))
    start = tuple((jnp.zeros(weight_item.shape, jnp.float32) for weight_item in params))
    totals, outs_pair = lax.scan(one_sequence, start, (tokens, segment_ids, cotangent))
    return (outs_pair[0], outs_pair[1], totals[0], totals[1], totals[2], totals[3], totals[4], totals[5], totals[6], totals[7], totals[8], totals[9])
```

```python
import functools
import math

import jax
import jax.numpy as jnp
from jax import lax
from jax.experimental import pallas as pl
from jax.experimental.pallas import tpu as pltpu
from jax.sharding import PartitionSpec as P

DH = 64
BLK = 64
LANES = 128
NEG = -1e30
F32 = jnp.float32
BF16 = jnp.bfloat16


def layer_norm_parts(rows):
    center = rows - jnp.mean(rows, axis=-1, keepdims=True)
    variance = jnp.mean(center * center, axis=-1, keepdims=True)
    inv = lax.rsqrt(variance + 1e-05)
    return center * inv, inv


def gelu_tanh(pre_act):
    return (
        0.5
        * pre_act
        * (1.0 + jnp.tanh(0.7978845608028654 * (pre_act + 0.044715 * pre_act * pre_act * pre_act)))
    )


def dot_nn(a, b):
    return jnp.dot(a, b, preferred_element_type=F32)


def dot_nt(a, b):
    return lax.dot_general(a, b, (((1,), (1,)), ((), ())), preferred_element_type=F32)


def dot_tn(a, b):
    return lax.dot_general(a, b, (((0,), (0,)), ((), ())), preferred_element_type=F32)


def mask_features(random_blocks, seq_ids, docs):
    heads, inner, _ = random_blocks.shape
    blocks = inner + 2
    length = seq_ids.shape[0]
    ids = jnp.arange(blocks, dtype=jnp.int32)
    near = jnp.abs(ids[:, None] - ids[None, :]) <= 1
    edge = (ids == 0) | (ids == blocks - 1)
    fixed = near | edge[:, None] | edge[None, :]
    picked = jnp.any(random_blocks[:, :, :, None] == ids, axis=2)
    picked = jnp.pad(picked, ((0, 0), (1, 1), (0, 0)))
    used = fixed[None] | picked
    block_part = jnp.where(used, 0.0, NEG).astype(BF16)
    block_part = jnp.repeat(block_part, length // blocks, axis=1)
    doc_ids = jnp.arange(docs, dtype=jnp.int32)
    own_doc = seq_ids[:, None] == doc_ids[None, :]
    doc_part = jnp.where(own_doc, NEG, 0.0).astype(BF16)
    doc_part = jnp.broadcast_to(doc_part, (heads,) + doc_part.shape)
    spare = jnp.zeros((heads, length, DH - blocks - docs), BF16)
    query_half = jnp.concatenate([block_part, doc_part, spare], axis=-1)
    block_hot = (jnp.arange(length, dtype=jnp.int32)[:, None] // (length // blocks)) == ids[None, :]
    key_half = jnp.concatenate(
        [
            block_hot.astype(BF16),
            jnp.where(own_doc, 0.0, 1.0).astype(BF16),
            jnp.zeros((length, DH - blocks - docs), BF16),
        ],
        axis=-1,
    )
    return (
        jnp.concatenate([query_half, query_half], axis=-1),
        jnp.concatenate([key_half, key_half], axis=-1),
    )


def own_lanes(odd, shape):
    lane = lax.broadcasted_iota(jnp.int32, shape, 1)
    return (lane >= DH) if odd else (lane < DH)


def attend_forward(tile, q_ref, k_ref, v_ref, qf_ref, kf_ref, out_ref, lse_ref):
    length = k_ref.shape[0]
    scale = jnp.asarray(1.0 / math.sqrt(DH), BF16)
    values_t = v_ref[...].T
    for odd in (0, 1):
        mine = own_lanes(odd, (length, LANES))
        keys = jnp.where(mine, k_ref[...], kf_ref[...])
        for start in range(0, length, tile):
            rows = pl.ds(start, tile)
            lanes = own_lanes(odd, (tile, LANES))
            queries = jnp.where(lanes, q_ref[rows, :] * scale, qf_ref[odd, rows, :])
            scores = dot_nt(keys, queries)
            top = jnp.max(scores, axis=0, keepdims=True)
            prob = jnp.exp(scores - top)
            total = jnp.sum(prob, axis=0, keepdims=True)
            mixed = dot_nn(values_t, prob.astype(BF16)) / total
            lse_ref[0, odd, rows] = (top + jnp.log(total))[0]
            result = mixed.T.astype(BF16)
            if odd:
                out_ref[rows, :] = jnp.where(lanes, result, out_ref[rows, :])
            else:
                out_ref[rows, :] = result


def attend_backward(
    tile, q_ref, k_ref, v_ref, qf_ref, kf_ref, go_ref, lse_ref, dq_ref, dk_ref, dv_ref, p_sc, s_sc
):
    length = k_ref.shape[0]
    scale = jnp.asarray(1.0 / math.sqrt(DH), BF16)
    keys_t = k_ref[...].T
    for odd in (0, 1):
        mine = own_lanes(odd, (length, LANES))
        keys = jnp.where(mine, k_ref[...], kf_ref[...])
        values = jnp.where(mine, v_ref[...], jnp.zeros((), BF16))
        for start in range(0, length, tile):
            rows = pl.ds(start, tile)
            lanes = own_lanes(odd, (tile, LANES))
            queries = jnp.where(lanes, q_ref[rows, :] * scale, qf_ref[odd, rows, :])
            prob = jnp.exp(dot_nt(keys, queries) - lse_ref[0, odd, rows][None, :])
            grad_prob = dot_nt(values, go_ref[rows, :])
            delta = jnp.sum(prob * grad_prob, axis=0, keepdims=True)
            p_sc[:, rows] = prob.astype(BF16)
            s_sc[:, rows] = (prob * (grad_prob - delta)).astype(BF16)
        grad_v = dot_nn(p_sc[...], go_ref[...]).astype(BF16)
        grad_k = dot_nn(s_sc[...], q_ref[...] * scale).astype(BF16)
        grad_q = (dot_nn(keys_t, s_sc[...]) * (1.0 / math.sqrt(DH))).T.astype(BF16)
        if odd:
            dv_ref[...] = jnp.where(mine, grad_v, dv_ref[...])
            dk_ref[...] = jnp.where(mine, grad_k, dk_ref[...])
            dq_ref[...] = jnp.where(mine, grad_q, dq_ref[...])
        else:
            dv_ref[...] = grad_v
            dk_ref[...] = grad_k
            dq_ref[...] = grad_q


def column_spec(length, offset):
    return pl.BlockSpec((length, LANES), lambda p: (0, p + offset))


def attention_forward(by_heads, query_feats, key_feats):
    length = by_heads.shape[0]
    heads = query_feats.shape[0]
    pairs = heads // 2
    return pl.pallas_call(
        functools.partial(attend_forward, 256),
        grid=(pairs,),
        out_shape=(
            jax.ShapeDtypeStruct((length, heads * DH), BF16),
            jax.ShapeDtypeStruct((pairs, 2, length), F32),
        ),
        in_specs=[
            column_spec(length, 0),
            column_spec(length, pairs),
            column_spec(length, 2 * pairs),
            pl.BlockSpec((2, length, LANES), lambda p: (p, 0, 0)),
            pl.BlockSpec((length, LANES), lambda p: (0, 0)),
        ],
        out_specs=(
            column_spec(length, 0),
            pl.BlockSpec((1, 2, length), lambda p: (p, 0, 0)),
        ),
        compiler_params=pltpu.CompilerParams(vmem_limit_bytes=56 << 20),
        cost_estimate=pl.CostEstimate(
            flops=heads * length * length * 512, bytes_accessed=8 << 20, transcendentals=heads * length * length
        ),
    )(by_heads, by_heads, by_heads, query_feats, key_feats)


def attention_backward(by_heads, query_feats, key_feats, grad_out, lse):
    length = by_heads.shape[0]
    heads = query_feats.shape[0]
    pairs = heads // 2
    shape = jax.ShapeDtypeStruct((length, heads * DH), BF16)
    return pl.pallas_call(
        functools.partial(attend_backward, 256),
        grid=(pairs,),
        out_shape=(shape, shape, shape),
        in_specs=[
            column_spec(length, 0),
            column_spec(length, pairs),
            column_spec(length, 2 * pairs),
            pl.BlockSpec((2, length, LANES), lambda p: (p, 0, 0)),
            pl.BlockSpec((length, LANES), lambda p: (0, 0)),
            column_spec(length, 0),
            pl.BlockSpec((1, 2, length), lambda p: (p, 0, 0)),
        ],
        out_specs=(column_spec(length, 0), column_spec(length, 0), column_spec(length, 0)),
        scratch_shapes=[pltpu.VMEM((length, length), BF16), pltpu.VMEM((length, length), BF16)],
        compiler_params=pltpu.CompilerParams(vmem_limit_bytes=56 << 20),
        cost_estimate=pl.CostEstimate(
            flops=heads * length * length * 1280, bytes_accessed=12 << 20, transcendentals=heads * length * length
        ),
    )(by_heads, by_heads, by_heads, query_feats, key_feats, grad_out, lse)


def swap_thirds(rows, outer, inner):
    count, width = rows.shape
    return rows.reshape(count, outer, inner, width // (outer * inner)).swapaxes(1, 2).reshape(count, width)


def per_device(
    seq_count,
    fsdp_count,
    tokens,
    segment_ids,
    random_blocks,
    ln1_gain,
    ln1_bias,
    w_qkv,
    w_out,
    ln2_gain,
    ln2_bias,
    w_in,
    b_in,
    w_down,
    b_down,
    cotangent,
):
    gather = functools.partial(lax.all_gather, axis_name="fsdp", axis=0, tiled=True)
    width = w_qkv.shape[1] // 3
    share = ln1_gain.shape[0]
    packed = jnp.concatenate([ln1_gain, ln1_bias, ln2_gain, ln2_bias, b_down, b_in])[None]
    packed = gather(packed).astype(F32)
    gain_one, bias_one, gain_two, bias_two, down_bias = (
        packed[:, i * share : (i + 1) * share].reshape(-1) for i in range(5)
    )
    in_bias = packed[:, 5 * share :].reshape(-1)
    qkv_weight = gather(swap_thirds(w_qkv, 3, seq_count))
    seq_ids = lax.all_gather(segment_ids[0], "seq", axis=0, tiled=True)
    out_weight = gather(w_out)
    in_weight = gather(w_in)
    down_weight = gather(w_down)
    query_feats, key_feats = mask_features(random_blocks, seq_ids, 6)

    token_rows = tokens[0].astype(F32)
    hat_one, inv_one = layer_norm_parts(token_rows)
    normed_one = (hat_one * gain_one + bias_one).astype(BF16)
    qkv_rows = dot_nn(normed_one, qkv_weight).astype(BF16)
    by_heads = lax.all_to_all(qkv_rows, "seq", split_axis=1, concat_axis=0, tiled=True)
    att_heads, lse = attention_forward(by_heads, query_feats, key_feats)
    att_rows = lax.all_to_all(att_heads, "seq", split_axis=0, concat_axis=1, tiled=True)
    hidden = token_rows + dot_nn(att_rows, out_weight)
    hat_two, inv_two = layer_norm_parts(hidden)
    normed_two = (hat_two * gain_two + bias_two).astype(BF16)
    pre_act = dot_nn(normed_two, in_weight) + in_bias
    act_value, pull_gelu = jax.vjp(gelu_tanh, pre_act)
    act_low = act_value.astype(BF16)
    result = hidden + dot_nn(act_low, down_weight) + down_bias

    cot_low = cotangent[0]
    cot_rows = cot_low.astype(F32)
    grad_pre = pull_gelu(dot_nt(cot_low, down_weight))[0].astype(BF16)
    grad_norm_two = dot_nt(grad_pre, in_weight)
    scaled = grad_norm_two * gain_two
    grad_hidden = cot_rows + inv_two * (
        scaled
        - jnp.mean(scaled, axis=-1, keepdims=True)
        - hat_two * jnp.mean(scaled * hat_two, axis=-1, keepdims=True)
    )
    hidden_low = grad_hidden.astype(BF16)
    grad_att = dot_nt(hidden_low, out_weight).astype(BF16)
    grad_att_heads = lax.all_to_all(grad_att, "seq", split_axis=1, concat_axis=0, tiled=True)
    scatter = functools.partial(
        lax.psum_scatter, axis_name="fsdp", scatter_dimension=0, tiled=True
    )
    share_down = scatter(dot_tn(act_low, cot_low).astype(BF16))
    share_in = scatter(dot_tn(normed_two, grad_pre).astype(BF16))
    share_out = scatter(dot_tn(att_rows, hidden_low).astype(BF16))
    grad_heads = jnp.concatenate(
        attention_backward(by_heads, query_feats, key_feats, grad_att_heads, lse), axis=1
    )
    grad_qkv_rows = lax.all_to_all(grad_heads, "seq", split_axis=0, concat_axis=1, tiled=True)
    share_qkv = scatter(dot_tn(normed_one, grad_qkv_rows).astype(BF16))
    grad_norm_one = dot_nt(grad_qkv_rows, qkv_weight)
    scaled_one = grad_norm_one * gain_one
    grad_tokens = (
        grad_hidden
        + inv_one
        * (
            scaled_one
            - jnp.mean(scaled_one, axis=-1, keepdims=True)
            - hat_one * jnp.mean(scaled_one * hat_one, axis=-1, keepdims=True)
        )
    ).astype(BF16)

    small = [
        jnp.sum(grad_norm_one * hat_one, axis=0),
        jnp.sum(grad_norm_one, axis=0),
        jnp.sum(grad_norm_two * hat_two, axis=0),
        jnp.sum(grad_norm_two, axis=0),
        jnp.sum(cot_rows, axis=0),
        jnp.sum(grad_pre.astype(F32), axis=0),
    ]
    small = jnp.concatenate([v.reshape(fsdp_count, -1) for v in small], axis=1)
    small = lax.psum(small, ("seq", "fsdp"))
    small = lax.dynamic_index_in_dim(small, lax.axis_index("fsdp"), 0, keepdims=False)
    parts = [small[i * share : (i + 1) * share] for i in range(5)] + [small[5 * share :]]
    total_down, total_in, total_out, total_qkv = lax.psum(
        (share_down, share_in, share_out, share_qkv), "seq"
    )
    return (
        result.astype(BF16)[None],
        grad_tokens[None],
        parts[0],
        parts[1],
        swap_thirds(total_qkv, seq_count, 3).astype(F32),
        total_out.astype(F32),
        parts[2],
        parts[3],
        total_in.astype(F32),
        parts[5],
        total_down.astype(F32),
        parts[4],
    )


def solution(mesh):
    return jax.shard_map(
        functools.partial(per_device, mesh.shape["seq"], mesh.shape["fsdp"]),
        mesh=mesh,
        in_specs=(
            P("fsdp", "seq", None),
            P("fsdp", "seq"),
            P("seq", None, None),
            P("fsdp"),
            P("fsdp"),
            P("fsdp", None),
            P("fsdp", None),
            P("fsdp"),
            P("fsdp"),
            P("fsdp", None),
            P("fsdp"),
            P("fsdp", None),
            P("fsdp"),
            P("fsdp", "seq", None),
        ),
        out_specs=(
            P("fsdp", "seq", None),
            P("fsdp", "seq", None),
            P("fsdp"),
            P("fsdp"),
            P("fsdp", None),
            P("fsdp", None),
            P("fsdp"),
            P("fsdp"),
            P("fsdp", None),
            P("fsdp"),
            P("fsdp", None),
            P("fsdp"),
        ),
        check_vma=False,
    )
```

```python
import functools
import math

import jax
import jax.numpy as jnp
from jax import lax
from jax.experimental import pallas as pl
from jax.experimental.pallas import tpu as pltpu
from jax.sharding import PartitionSpec as P

DH = 64
BLK = 64
LANES = 128
NEG = -1e30
F32 = jnp.float32
BF16 = jnp.bfloat16


def layer_norm_parts(rows):
    center = rows - jnp.mean(rows, axis=-1, keepdims=True)
    variance = jnp.mean(center * center, axis=-1, keepdims=True)
    inv = lax.rsqrt(variance + 1e-05)
    return center * inv, inv


def gelu_tanh(pre_act):
    return (
        0.5
        * pre_act
        * (1.0 + jnp.tanh(0.7978845608028654 * (pre_act + 0.044715 * pre_act * pre_act * pre_act)))
    )


def dot_nn(a, b):
    return jnp.dot(a, b, preferred_element_type=F32)


def dot_nt(a, b):
    return lax.dot_general(a, b, (((1,), (1,)), ((), ())), preferred_element_type=F32)


def dot_tn(a, b):
    return lax.dot_general(a, b, (((0,), (0,)), ((), ())), preferred_element_type=F32)


def mask_features(random_blocks, seq_ids, docs):
    heads, inner, _ = random_blocks.shape
    blocks = inner + 2
    length = seq_ids.shape[0]
    ids = jnp.arange(blocks, dtype=jnp.int32)
    near = jnp.abs(ids[:, None] - ids[None, :]) <= 1
    edge = (ids == 0) | (ids == blocks - 1)
    fixed = near | edge[:, None] | edge[None, :]
    picked = jnp.any(random_blocks[:, :, :, None] == ids, axis=2)
    picked = jnp.pad(picked, ((0, 0), (1, 1), (0, 0)))
    used = fixed[None] | picked
    block_part = jnp.where(used, 0.0, NEG).astype(BF16)
    block_part = jnp.repeat(block_part, length // blocks, axis=1)
    doc_ids = jnp.arange(docs, dtype=jnp.int32)
    own_doc = seq_ids[:, None] == doc_ids[None, :]
    doc_part = jnp.where(own_doc, NEG, 0.0).astype(BF16)
    doc_part = jnp.broadcast_to(doc_part, (heads,) + doc_part.shape)
    spare = jnp.zeros((heads, length, DH - blocks - docs), BF16)
    query_half = jnp.concatenate([block_part, doc_part, spare], axis=-1)
    block_hot = (jnp.arange(length, dtype=jnp.int32)[:, None] // (length // blocks)) == ids[None, :]
    key_half = jnp.concatenate(
        [
            block_hot.astype(BF16),
            jnp.where(own_doc, 0.0, 1.0).astype(BF16),
            jnp.zeros((length, DH - blocks - docs), BF16),
        ],
        axis=-1,
    )
    return (
        jnp.concatenate([query_half, query_half], axis=-1),
        jnp.concatenate([key_half, key_half], axis=-1),
    )


def own_lanes(odd, shape):
    lane = lax.broadcasted_iota(jnp.int32, shape, 1)
    return (lane >= DH) if odd else (lane < DH)


MESH = pl.DeviceIdType.MESH


class Place:
    def __init__(self, fsdp_count):
        self.depth = fsdp_count // 2
        self.s = lax.axis_index("seq")
        self.f = lax.axis_index("fsdp")
        self.z = lax.div(self.f, 2)
        self.c = lax.rem(self.f, 2)
        self.s1 = self.s + 1 - 2 * lax.rem(self.s, 2)
        self.s2 = self.s + 2 - 4 * lax.div(self.s, 2)
        self.s3 = 3 - self.s
        self.beside = (self.s, self.f + 1 - 2 * self.c)

    def across(self, index):
        return ((self.s1, self.s2, self.s3)[index], self.f)

    def far(self, step):
        return lax.rem(self.z + step, self.depth)

    def back(self, step):
        return lax.rem(self.z + self.depth - step, self.depth)

    def along(self, z):
        return (self.s, 2 * z + self.c)

    def meet(self):
        barrier = pltpu.get_barrier_semaphore()
        peers = [self.beside] + [self.across(i) for i in range(3)]
        for peer in peers:
            pl.semaphore_signal(barrier, inc=1, device_id=peer, device_id_type=MESH)
        self.each(1, self.depth, lambda step: pl.semaphore_signal(
            barrier, inc=1, device_id=self.along(self.far(step)), device_id_type=MESH
        ))
        pl.semaphore_wait(barrier, len(peers) + self.depth - 1)

    def each(self, start, stop, body):
        if stop - start <= 8:
            for step in range(start, stop):
                body(step)
        else:
            lax.fori_loop(start, stop, lambda step, carry: (body(step), carry)[1], 0)


def send(src, dst, sems, index, device):
    sent, got = sems
    return pltpu.make_async_remote_copy(
        src_ref=src,
        dst_ref=dst,
        send_sem=sent.at[index],
        recv_sem=got.at[index],
        device_id=device,
        device_id_type=MESH,
    )


def aligned(start, size):
    return pl.ds(pl.multiple_of(start, size), size)


class Gather:
    def __init__(self, place, src, dst, split, sems):
        self.place, self.src, self.dst, self.split = place, src, dst, split
        self.rows, self.cols = src.shape
        self.local, self.zs, self.xs, self.rs, self.cs = sems

    def block(self, f, quarter=None, half=None):
        rows = aligned(f * self.rows, self.rows)
        if quarter is None:
            return self.dst.at[rows]
        wide = self.cols // 4
        if half is None:
            return self.dst.at[rows, aligned(quarter * wide, wide)]
        return self.dst.at[rows, aligned(quarter * wide + half * (wide // 2), wide // 2)]

    def own_copy(self):
        return pltpu.make_async_copy(self.src, self.block(self.place.f), self.local)

    def core_copy(self, step):
        p = self.place
        f = 2 * p.far(step) + p.c
        src = self.src if isinstance(step, int) and step == 0 else self.block(f)
        return send(src, self.block(f), self.cs, step, p.beside)

    def core_arrival(self, step):
        p = self.place
        there = self.block(2 * p.far(step) + 1 - p.c)
        return send(there, there, self.cs, step, p.beside)

    def z_copy(self, step):
        p = self.place
        if self.split:
            wide = self.cols // 4
            src, dst = self.src.at[:, aligned(p.s * wide, wide)], self.block(p.f, p.s)
        else:
            src, dst = self.src, self.block(p.f)
        return send(src, dst, self.zs, step, p.along(p.back(step)))

    def z_arrival(self, step):
        p = self.place
        f = 2 * p.far(step) + p.c
        there = self.block(f, p.s) if self.split else self.block(f)
        return send(there, there, self.zs, step, p.along(p.far(step)))

    def x_copy(self, step, way):
        p = self.place
        there = self.block(2 * p.far(step) + p.c, p.s)
        return send(there, there, self.xs[way], step, p.across(way))

    def x_arrival(self, step, way):
        p = self.place
        there = self.block(2 * p.far(step) + p.c, (p.s1, p.s2)[way])
        return send(there, there, self.xs[way], step, p.across(way))

    def relay_copy(self, step, way):
        p = self.place
        there = self.block(2 * p.far(step) + p.c, (p.s2, p.s1)[way], 1 - way)
        return send(there, there, self.rs[way], step, p.across(way))

    def relay_arrival(self, step, way):
        p = self.place
        there = self.block(2 * p.far(step) + p.c, p.s3, 1 - way)
        return send(there, there, self.rs[way], step, p.across(way))

    def begin(self):
        self.place.each(1, self.place.depth, lambda step: self.z_copy(step).start())
        self.own_copy().start()
        self.core_copy(0).start()

    def swap(self, step):
        self.z_arrival(step).wait_recv()
        if self.split:
            for way in (0, 1):
                self.x_copy(step, way).start()
        else:
            self.core_copy(step).start()

    def relay(self, step):
        if self.split:
            for way in (0, 1):
                self.x_arrival(step, way).wait_recv()
            for way in (0, 1):
                self.relay_copy(step, way).start()

    def share(self, step):
        if self.split:
            for way in (0, 1):
                self.relay_arrival(step, way).wait_recv()
            self.core_copy(step).start()

    def finish(self):
        self.own_copy().wait()
        self.core_copy(0).wait_send()
        self.core_arrival(0).wait_recv()

        def close(step):
            self.z_copy(step).wait_send()
            if self.split:
                for way in (0, 1):
                    self.x_copy(step, way).wait_send()
                    self.relay_copy(step, way).wait_send()
            self.core_copy(step).wait_send()
            self.core_arrival(step).wait_recv()

        self.place.each(1, self.place.depth, close)

    @staticmethod
    def scratch(depth):
        pair = [pltpu.SemaphoreType.DMA((depth,))] * 2
        return [pltpu.SemaphoreType.DMA] + pair * 6

    @staticmethod
    def take(refs):
        pairs = [(refs[i], refs[i + 1]) for i in range(1, 13, 2)]
        return (refs[0], pairs[0], pairs[1:3], pairs[3:5], pairs[5])


GATHER_SEMS = 13


def gather_steps(place, gathers, between):
    depth = place.depth
    work = list(between)

    def stage(step, swap, relay, share):
        for one in gathers:
            if swap:
                one.swap(step)
        for one in gathers:
            if relay:
                one.relay(step - 1)
        for one in gathers:
            if share:
                one.share(step - 2)

    if depth <= 8:
        for step in range(1, depth + 2):
            stage(step, step < depth, 2 <= step <= depth, step >= 3)
            if work:
                work.pop(0)()
    else:
        stage(1, True, False, False)
        stage(2, True, True, False)
        lax.fori_loop(3, depth, lambda step, carry: (stage(step, True, True, True), carry)[1], 0)
        stage(depth, False, True, True)
        stage(depth + 1, False, False, True)
    for rest in work:
        rest()


def first_gather_kernel(fsdp_count, w_ref, vec_ref, seg_ref, w_all, vec_all, seg_all, *sems):
    place = Place(fsdp_count)
    weight = Gather(place, w_ref, w_all, True, Gather.take(sems[:GATHER_SEMS]))
    vector = Gather(place, vec_ref, vec_all, False, Gather.take(sems[GATHER_SEMS : 2 * GATHER_SEMS]))
    local, sent, got = sems[2 * GATHER_SEMS :]
    rows = seg_ref.shape[0]
    place.meet()
    weight.begin()
    vector.begin()
    own = pltpu.make_async_copy(seg_ref, seg_all.at[aligned(place.s * rows, rows)], local)
    own.start()
    for way in range(3):
        send(seg_ref, seg_all.at[aligned(place.s * rows, rows)], (sent, got), way, place.across(way)).start()
    gather_steps(place, [vector, weight], [])
    own.wait()
    for way in range(3):
        there = seg_all.at[aligned((place.s1, place.s2, place.s3)[way] * rows, rows)]
        arrival = send(there, there, (sent, got), way, place.across(way))
        arrival.wait_recv()
        send(seg_ref, seg_all.at[aligned(place.s * rows, rows)], (sent, got), way, place.across(way)).wait_send()
    vector.finish()
    weight.finish()


def first_gather(fsdp_count, w_shard, vec, seg):
    anywhere = pl.BlockSpec(memory_space=pl.ANY)
    return pl.pallas_call(
        functools.partial(first_gather_kernel, fsdp_count),
        out_shape=(
            jax.ShapeDtypeStruct((fsdp_count * w_shard.shape[0], w_shard.shape[1]), w_shard.dtype),
            jax.ShapeDtypeStruct((fsdp_count * vec.shape[0], vec.shape[1]), vec.dtype),
            jax.ShapeDtypeStruct((4 * seg.shape[0], seg.shape[1]), seg.dtype),
        ),
        in_specs=[anywhere] * 3,
        out_specs=(anywhere,) * 3,
        scratch_shapes=Gather.scratch(fsdp_count // 2) * 2
        + [pltpu.SemaphoreType.DMA, pltpu.SemaphoreType.DMA((3,)), pltpu.SemaphoreType.DMA((3,))],
        compiler_params=pltpu.CompilerParams(collective_id=1, has_side_effects=True),
    )(w_shard, vec, seg)


def attend_unit(pair, odd, tile, heads_ref, qf_ref, kf_ref, keys_sc, values_t, out_ref, lse_ref):
    length = heads_ref.shape[0]
    third = heads_ref.shape[1] // 3
    scale = jnp.asarray(1.0 / math.sqrt(DH), BF16)
    cols = pl.ds(pair * LANES, LANES)
    if not odd:
        values_t[...] = heads_ref[:, pl.ds(2 * third + pair * LANES, LANES)].T
    mine = own_lanes(odd, (length, LANES))
    keys_sc[...] = jnp.where(mine, heads_ref[:, pl.ds(third + pair * LANES, LANES)], kf_ref[...])

    def one_tile(index, carry):
        rows = aligned(index * tile, tile)
        lanes = own_lanes(odd, (tile, LANES))
        queries = jnp.where(lanes, heads_ref[rows, cols] * scale, qf_ref[2 * pair + odd, rows, :])
        scores = dot_nt(keys_sc[...], queries)
        top = jnp.max(scores, axis=0, keepdims=True)
        prob = jnp.exp(scores - top)
        total = jnp.sum(prob, axis=0, keepdims=True)
        mixed = dot_nn(values_t[...], prob.astype(BF16)) / total
        lse_ref[pair, pl.ds(odd, 1), rows] = top + jnp.log(total)
        result = mixed.T.astype(BF16)
        if odd:
            out_ref[rows, cols] = jnp.where(lanes, result, out_ref[rows, cols])
        else:
            out_ref[rows, cols] = result
        return carry

    lax.fori_loop(0, length // tile, one_tile, 0, unroll=2)


def forward_kernel(
    fsdp_count,
    qkv_ref,
    qf_ref,
    kf_ref,
    out_w_ref,
    down_w_ref,
    in_w_ref,
    heads_all,
    lse_ref,
    att_all,
    out_w_all,
    down_w_all,
    in_w_all,
    heads_sc,
    att_sc,
    keys_sc,
    values_t,
    *sems,
):
    place = Place(fsdp_count)
    rows, width = qkv_ref.shape[0], heads_sc.shape[1]
    gathers = [
        Gather(place, src, dst, True, Gather.take(sems[i * GATHER_SEMS : (i + 1) * GATHER_SEMS]))
        for i, (src, dst) in enumerate(
            ((out_w_ref, out_w_all), (in_w_ref, in_w_all), (down_w_ref, down_w_all))
        )
    ]
    own_sem, q_sent, q_got, copy_sem, a_sent, a_got, a_own = sems[3 * GATHER_SEMS :]
    seats = (place.s1, place.s2, place.s3)

    def part(seat):
        return qkv_ref.at[:, aligned(seat * width, width)]

    def slot(seat):
        return heads_sc.at[aligned(seat * rows, rows)]

    place.meet()
    for way in range(3):
        send(part(seats[way]), slot(place.s), (q_sent, q_got), way, place.across(way)).start()
    own = pltpu.make_async_copy(part(place.s), slot(place.s), own_sem)
    own.start()
    for one in gathers:
        one.begin()
    own.wait()
    for way in range(3):
        send(slot(seats[way]), slot(seats[way]), (q_sent, q_got), way, place.across(way)).wait_recv()
    keep = pltpu.make_async_copy(heads_sc, heads_all, copy_sem)
    keep.start()

    pairs = att_sc.shape[1] // LANES

    def att_copy(pair, way):
        cols = aligned((place.s * pairs + pair) * LANES, LANES)
        return send(
            att_sc.at[aligned(seats[way] * rows, rows), pl.ds(pair * LANES, LANES)],
            att_all.at[:, cols],
            (a_sent, a_got),
            pair * 3 + way,
            place.across(way),
        )

    def att_own(pair):
        cols = aligned((place.s * pairs + pair) * LANES, LANES)
        return pltpu.make_async_copy(
            att_sc.at[aligned(place.s * rows, rows), pl.ds(pair * LANES, LANES)],
            att_all.at[:, cols],
            a_own.at[pair],
        )

    def att_arrival(pair, way):
        there = att_all.at[:, aligned((seats[way] * pairs + pair) * LANES, LANES)]
        return send(there, there, (a_sent, a_got), pair * 3 + way, place.across(way))

    def unit(pair, odd):
        attend_unit(pair, odd, 256, heads_sc, qf_ref, kf_ref, keys_sc, values_t, att_sc, lse_ref)
        if odd:
            for way in range(3):
                att_copy(pair, way).start()
            att_own(pair).start()

    gather_steps(
        place,
        gathers,
        [functools.partial(unit, pair, odd) for pair in range(pairs) for odd in (0, 1)],
    )
    keep.wait()
    for way in range(3):
        send(part(seats[way]), slot(place.s), (q_sent, q_got), way, place.across(way)).wait_send()
        for pair in range(pairs):
            att_copy(pair, way).wait_send()
            att_arrival(pair, way).wait_recv()
    for pair in range(pairs):
        att_own(pair).wait()
    for one in gathers:
        one.finish()


def forward_attention(fsdp_count, qkv_rows, query_feats, key_feats, w_out, w_down, w_in):
    rows, width = qkv_rows.shape
    length = 4 * rows
    heads = query_feats.shape[0]
    pairs = heads // 2
    depth = fsdp_count // 2
    anywhere = pl.BlockSpec(memory_space=pl.ANY)
    vmem = pl.BlockSpec(memory_space=pltpu.VMEM)

    def whole(shard):
        return jax.ShapeDtypeStruct((fsdp_count * shard.shape[0], shard.shape[1]), shard.dtype)

    return pl.pallas_call(
        functools.partial(forward_kernel, fsdp_count),
        out_shape=(
            jax.ShapeDtypeStruct((length, width // 4), BF16),
            jax.ShapeDtypeStruct((pairs, 2, length), F32),
            jax.ShapeDtypeStruct((rows, width // 3), BF16),
            whole(w_out),
            whole(w_down),
            whole(w_in),
        ),
        in_specs=[anywhere, vmem, vmem, anywhere, anywhere, anywhere],
        out_specs=(anywhere, vmem, anywhere, anywhere, anywhere, anywhere),
        scratch_shapes=[
            pltpu.VMEM((length, width // 4), BF16),
            pltpu.VMEM((length, heads * DH), BF16),
            pltpu.VMEM((length, LANES), BF16),
            pltpu.VMEM((LANES, length), BF16),
        ]
        + Gather.scratch(depth) * 3
        + [
            pltpu.SemaphoreType.DMA,
            pltpu.SemaphoreType.DMA((3,)),
            pltpu.SemaphoreType.DMA((3,)),
            pltpu.SemaphoreType.DMA,
            pltpu.SemaphoreType.DMA((3 * pairs,)),
            pltpu.SemaphoreType.DMA((3 * pairs,)),
            pltpu.SemaphoreType.DMA((pairs,)),
        ],
        compiler_params=pltpu.CompilerParams(
            collective_id=2, has_side_effects=True, vmem_limit_bytes=40 << 20
        ),
    )(qkv_rows, query_feats, key_feats, w_out, w_down, w_in)


def attend_backward(
    tile, q_ref, k_ref, v_ref, qf_ref, kf_ref, go_ref, lse_ref, dq_ref, dk_ref, dv_ref, p_sc, s_sc
):
    length = k_ref.shape[0]
    scale = jnp.asarray(1.0 / math.sqrt(DH), BF16)
    keys_t = k_ref[...].T
    for odd in (0, 1):
        mine = own_lanes(odd, (length, LANES))
        keys = jnp.where(mine, k_ref[...], kf_ref[...])
        values = jnp.where(mine, v_ref[...], jnp.zeros((), BF16))
        for start in range(0, length, tile):
            rows = pl.ds(start, tile)
            lanes = own_lanes(odd, (tile, LANES))
            queries = jnp.where(lanes, q_ref[rows, :] * scale, qf_ref[odd, rows, :])
            prob = jnp.exp(dot_nt(keys, queries) - lse_ref[0, odd, rows][None, :])
            grad_prob = dot_nt(values, go_ref[rows, :])
            delta = jnp.sum(prob * grad_prob, axis=0, keepdims=True)
            p_sc[:, rows] = prob.astype(BF16)
            s_sc[:, rows] = (prob * (grad_prob - delta)).astype(BF16)
        grad_v = dot_nn(p_sc[...], go_ref[...]).astype(BF16)
        grad_k = dot_nn(s_sc[...], q_ref[...] * scale).astype(BF16)
        grad_q = (dot_nn(keys_t, s_sc[...]) * (1.0 / math.sqrt(DH))).T.astype(BF16)
        if odd:
            dv_ref[...] = jnp.where(mine, grad_v, dv_ref[...])
            dk_ref[...] = jnp.where(mine, grad_k, dk_ref[...])
            dq_ref[...] = jnp.where(mine, grad_q, dq_ref[...])
        else:
            dv_ref[...] = grad_v
            dk_ref[...] = grad_k
            dq_ref[...] = grad_q


def column_spec(length, offset):
    return pl.BlockSpec((length, LANES), lambda p: (0, p + offset))


def attention_backward(by_heads, query_feats, key_feats, grad_out, lse):
    length = by_heads.shape[0]
    heads = query_feats.shape[0]
    pairs = heads // 2
    shape = jax.ShapeDtypeStruct((length, heads * DH), BF16)
    return pl.pallas_call(
        functools.partial(attend_backward, 256),
        grid=(pairs,),
        out_shape=(shape, shape, shape),
        in_specs=[
            column_spec(length, 0),
            column_spec(length, pairs),
            column_spec(length, 2 * pairs),
            pl.BlockSpec((2, length, LANES), lambda p: (p, 0, 0)),
            pl.BlockSpec((length, LANES), lambda p: (0, 0)),
            column_spec(length, 0),
            pl.BlockSpec((1, 2, length), lambda p: (p, 0, 0)),
        ],
        out_specs=(column_spec(length, 0), column_spec(length, 0), column_spec(length, 0)),
        scratch_shapes=[pltpu.VMEM((length, length), BF16), pltpu.VMEM((length, length), BF16)],
        compiler_params=pltpu.CompilerParams(vmem_limit_bytes=56 << 20),
        cost_estimate=pl.CostEstimate(
            flops=heads * length * length * 1280, bytes_accessed=12 << 20, transcendentals=heads * length * length
        ),
    )(by_heads, by_heads, by_heads, query_feats, key_feats, grad_out, lse)


def swap_thirds(rows, outer, inner):
    count, width = rows.shape
    return rows.reshape(count, outer, inner, width // (outer * inner)).swapaxes(1, 2).reshape(count, width)


def per_device(
    seq_count,
    fsdp_count,
    tokens,
    segment_ids,
    random_blocks,
    ln1_gain,
    ln1_bias,
    w_qkv,
    w_out,
    ln2_gain,
    ln2_bias,
    w_in,
    b_in,
    w_down,
    b_down,
    cotangent,
):
    width = w_qkv.shape[1] // 3
    share = ln1_gain.shape[0]
    packed = jnp.concatenate([ln1_gain, ln1_bias, ln2_gain, ln2_bias, b_down, b_in])
    packed_rows = -(-packed.shape[0] // (16 * LANES)) * 16
    packed = jnp.pad(packed, (0, packed_rows * LANES - packed.shape[0])).reshape(packed_rows, LANES)
    tok_count = segment_ids.shape[1]
    seg_rows = -(-tok_count // (8 * LANES)) * 8
    seg = jnp.pad(segment_ids[0], (0, seg_rows * LANES - tok_count)).reshape(seg_rows, LANES)
    qkv_weight, packed, seg = first_gather(fsdp_count, swap_thirds(w_qkv, 3, seq_count), packed, seg)
    packed = packed.reshape(fsdp_count, packed_rows * LANES).astype(F32)
    gain_one, bias_one, gain_two, bias_two, down_bias = (
        packed[:, i * share : (i + 1) * share].reshape(-1) for i in range(5)
    )
    in_bias = packed[:, 5 * share : 5 * share + b_in.shape[0]].reshape(-1)
    seq_ids = seg.reshape(seq_count, seg_rows * LANES)[:, :tok_count].reshape(-1)
    query_feats, key_feats = mask_features(random_blocks, seq_ids, 6)

    token_rows = tokens[0].astype(F32)
    hat_one, inv_one = layer_norm_parts(token_rows)
    normed_one = (hat_one * gain_one + bias_one).astype(BF16)
    qkv_rows = dot_nn(normed_one, qkv_weight).astype(BF16)
    by_heads, lse, att_rows, out_weight, down_weight, in_weight = forward_attention(
        fsdp_count, qkv_rows, query_feats, key_feats, w_out, w_down, w_in
    )
    hidden = token_rows + dot_nn(att_rows, out_weight)
    hat_two, inv_two = layer_norm_parts(hidden)
    normed_two = (hat_two * gain_two + bias_two).astype(BF16)
    pre_act = dot_nn(normed_two, in_weight) + in_bias
    act_value, pull_gelu = jax.vjp(gelu_tanh, pre_act)
    act_low = act_value.astype(BF16)
    result = hidden + dot_nn(act_low, down_weight) + down_bias

    cot_low = cotangent[0]
    cot_rows = cot_low.astype(F32)
    grad_pre = pull_gelu(dot_nt(cot_low, down_weight))[0].astype(BF16)
    grad_norm_two = dot_nt(grad_pre, in_weight)
    scaled = grad_norm_two * gain_two
    grad_hidden = cot_rows + inv_two * (
        scaled
        - jnp.mean(scaled, axis=-1, keepdims=True)
        - hat_two * jnp.mean(scaled * hat_two, axis=-1, keepdims=True)
    )
    hidden_low = grad_hidden.astype(BF16)
    grad_att = dot_nt(hidden_low, out_weight).astype(BF16)
    grad_att_heads = lax.all_to_all(grad_att, "seq", split_axis=1, concat_axis=0, tiled=True)
    scatter = functools.partial(
        lax.psum_scatter, axis_name="fsdp", scatter_dimension=0, tiled=True
    )
    share_down = scatter(dot_tn(act_low, cot_low).astype(BF16))
    share_in = scatter(dot_tn(normed_two, grad_pre).astype(BF16))
    share_out = scatter(dot_tn(att_rows, hidden_low).astype(BF16))
    grad_heads = jnp.concatenate(
        attention_backward(by_heads, query_feats, key_feats, grad_att_heads, lse), axis=1
    )
    grad_qkv_rows = lax.all_to_all(grad_heads, "seq", split_axis=0, concat_axis=1, tiled=True)
    share_qkv = scatter(dot_tn(normed_one, grad_qkv_rows).astype(BF16))
    grad_norm_one = dot_nt(grad_qkv_rows, qkv_weight)
    scaled_one = grad_norm_one * gain_one
    grad_tokens = (
        grad_hidden
        + inv_one
        * (
            scaled_one
            - jnp.mean(scaled_one, axis=-1, keepdims=True)
            - hat_one * jnp.mean(scaled_one * hat_one, axis=-1, keepdims=True)
        )
    ).astype(BF16)

    small = [
        jnp.sum(grad_norm_one * hat_one, axis=0),
        jnp.sum(grad_norm_one, axis=0),
        jnp.sum(grad_norm_two * hat_two, axis=0),
        jnp.sum(grad_norm_two, axis=0),
        jnp.sum(cot_rows, axis=0),
        jnp.sum(grad_pre.astype(F32), axis=0),
    ]
    small = jnp.concatenate([v.reshape(fsdp_count, -1) for v in small], axis=1)
    small = lax.psum(small, ("seq", "fsdp"))
    small = lax.dynamic_index_in_dim(small, lax.axis_index("fsdp"), 0, keepdims=False)
    parts = [small[i * share : (i + 1) * share] for i in range(5)] + [small[5 * share :]]
    total_down, total_in, total_out, total_qkv = lax.psum(
        (share_down, share_in, share_out, share_qkv), "seq"
    )
    return (
        result.astype(BF16)[None],
        grad_tokens[None],
        parts[0],
        parts[1],
        swap_thirds(total_qkv, seq_count, 3).astype(F32),
        total_out.astype(F32),
        parts[2],
        parts[3],
        total_in.astype(F32),
        parts[5],
        total_down.astype(F32),
        parts[4],
    )


def solution(mesh):
    return jax.shard_map(
        functools.partial(per_device, mesh.shape["seq"], mesh.shape["fsdp"]),
        mesh=mesh,
        in_specs=(
            P("fsdp", "seq", None),
            P("fsdp", "seq"),
            P("seq", None, None),
            P("fsdp"),
            P("fsdp"),
            P("fsdp", None),
            P("fsdp", None),
            P("fsdp"),
            P("fsdp"),
            P("fsdp", None),
            P("fsdp"),
            P("fsdp", None),
            P("fsdp"),
            P("fsdp", "seq", None),
        ),
        out_specs=(
            P("fsdp", "seq", None),
            P("fsdp", "seq", None),
            P("fsdp"),
            P("fsdp"),
            P("fsdp", None),
            P("fsdp", None),
            P("fsdp"),
            P("fsdp"),
            P("fsdp", None),
            P("fsdp"),
            P("fsdp", None),
            P("fsdp"),
        ),
        check_vma=False,
    )
```

```python
import functools
import math

import jax
import jax.numpy as jnp
from jax import lax
from jax.experimental import pallas as pl
from jax.experimental.pallas import tpu as pltpu
from jax.sharding import PartitionSpec as P

DH = 64
BLK = 64
LANES = 128
NEG = -1e30
F32 = jnp.float32
BF16 = jnp.bfloat16


def layer_norm_parts(rows):
    center = rows - jnp.mean(rows, axis=-1, keepdims=True)
    variance = jnp.mean(center * center, axis=-1, keepdims=True)
    inv = lax.rsqrt(variance + 1e-05)
    return center * inv, inv


def gelu_tanh(pre_act):
    return (
        0.5
        * pre_act
        * (1.0 + jnp.tanh(0.7978845608028654 * (pre_act + 0.044715 * pre_act * pre_act * pre_act)))
    )


def dot_nn(a, b):
    return jnp.dot(a, b, preferred_element_type=F32)


def dot_nt(a, b):
    return lax.dot_general(a, b, (((1,), (1,)), ((), ())), preferred_element_type=F32)


def dot_tn(a, b):
    return lax.dot_general(a, b, (((0,), (0,)), ((), ())), preferred_element_type=F32)


def mask_features(random_blocks, seq_ids, docs):
    heads, inner, _ = random_blocks.shape
    blocks = inner + 2
    length = seq_ids.shape[0]
    ids = jnp.arange(blocks, dtype=jnp.int32)
    near = jnp.abs(ids[:, None] - ids[None, :]) <= 1
    edge = (ids == 0) | (ids == blocks - 1)
    fixed = near | edge[:, None] | edge[None, :]
    picked = jnp.any(random_blocks[:, :, :, None] == ids, axis=2)
    picked = jnp.pad(picked, ((0, 0), (1, 1), (0, 0)))
    used = fixed[None] | picked
    block_part = jnp.where(used, 0.0, NEG).astype(BF16)
    block_part = jnp.repeat(block_part, length // blocks, axis=1)
    doc_ids = jnp.arange(docs, dtype=jnp.int32)
    own_doc = seq_ids[:, None] == doc_ids[None, :]
    doc_part = jnp.where(own_doc, NEG, 0.0).astype(BF16)
    doc_part = jnp.broadcast_to(doc_part, (heads,) + doc_part.shape)
    spare = jnp.zeros((heads, length, DH - blocks - docs), BF16)
    query_half = jnp.concatenate([block_part, doc_part, spare], axis=-1)
    block_hot = (jnp.arange(length, dtype=jnp.int32)[:, None] // (length // blocks)) == ids[None, :]
    key_half = jnp.concatenate(
        [
            block_hot.astype(BF16),
            jnp.where(own_doc, 0.0, 1.0).astype(BF16),
            jnp.zeros((length, DH - blocks - docs), BF16),
        ],
        axis=-1,
    )
    return (
        jnp.concatenate([query_half, query_half], axis=-1),
        jnp.concatenate([key_half, key_half], axis=-1),
    )


def own_lanes(odd, shape):
    lane = lax.broadcasted_iota(jnp.int32, shape, 1)
    return (lane >= DH) if odd else (lane < DH)


MESH = pl.DeviceIdType.MESH


class Place:
    def __init__(self, fsdp_count):
        self.depth = fsdp_count // 2
        self.s = lax.axis_index("seq")
        self.f = lax.axis_index("fsdp")
        self.z = lax.div(self.f, 2)
        self.c = lax.rem(self.f, 2)
        self.s1 = self.s + 1 - 2 * lax.rem(self.s, 2)
        self.s2 = self.s + 2 - 4 * lax.div(self.s, 2)
        self.s3 = 3 - self.s
        self.beside = (self.s, self.f + 1 - 2 * self.c)

    def across(self, index):
        return ((self.s1, self.s2, self.s3)[index], self.f)

    def far(self, step):
        return lax.rem(self.z + step, self.depth)

    def back(self, step):
        return lax.rem(self.z + self.depth - step, self.depth)

    def along(self, z):
        return (self.s, 2 * z + self.c)

    def meet(self):
        barrier = pltpu.get_barrier_semaphore()
        peers = [self.beside] + [self.across(i) for i in range(3)]
        for peer in peers:
            pl.semaphore_signal(barrier, inc=1, device_id=peer, device_id_type=MESH)
        self.each(1, self.depth, lambda step: pl.semaphore_signal(
            barrier, inc=1, device_id=self.along(self.far(step)), device_id_type=MESH
        ))
        pl.semaphore_wait(barrier, len(peers) + self.depth - 1)

    def each(self, start, stop, body):
        if stop - start <= 8:
            for step in range(start, stop):
                body(step)
        else:
            lax.fori_loop(start, stop, lambda step, carry: (body(step), carry)[1], 0)


def send(src, dst, sems, index, device):
    sent, got = sems
    return pltpu.make_async_remote_copy(
        src_ref=src,
        dst_ref=dst,
        send_sem=sent.at[index],
        recv_sem=got.at[index],
        device_id=device,
        device_id_type=MESH,
    )


def aligned(start, size):
    return pl.ds(pl.multiple_of(start, size), size)


class Gather:
    def __init__(self, place, src, dst, split, sems):
        self.place, self.src, self.dst, self.split = place, src, dst, split
        self.rows, self.cols = src.shape
        self.local, self.zs, self.xs, self.rs, self.cs = sems

    def block(self, f, quarter=None, half=None):
        rows = aligned(f * self.rows, self.rows)
        if quarter is None:
            return self.dst.at[rows]
        wide = self.cols // 4
        if half is None:
            return self.dst.at[rows, aligned(quarter * wide, wide)]
        return self.dst.at[rows, aligned(quarter * wide + half * (wide // 2), wide // 2)]

    def own_copy(self):
        return pltpu.make_async_copy(self.src, self.block(self.place.f), self.local)

    def core_copy(self, step):
        p = self.place
        f = 2 * p.far(step) + p.c
        src = self.src if isinstance(step, int) and step == 0 else self.block(f)
        return send(src, self.block(f), self.cs, step, p.beside)

    def core_arrival(self, step):
        p = self.place
        there = self.block(2 * p.far(step) + 1 - p.c)
        return send(there, there, self.cs, step, p.beside)

    def z_copy(self, step):
        p = self.place
        if self.split:
            wide = self.cols // 4
            src, dst = self.src.at[:, aligned(p.s * wide, wide)], self.block(p.f, p.s)
        else:
            src, dst = self.src, self.block(p.f)
        return send(src, dst, self.zs, step, p.along(p.back(step)))

    def z_arrival(self, step):
        p = self.place
        f = 2 * p.far(step) + p.c
        there = self.block(f, p.s) if self.split else self.block(f)
        return send(there, there, self.zs, step, p.along(p.far(step)))

    def x_copy(self, step, way):
        p = self.place
        there = self.block(2 * p.far(step) + p.c, p.s)
        return send(there, there, self.xs[way], step, p.across(way))

    def x_arrival(self, step, way):
        p = self.place
        there = self.block(2 * p.far(step) + p.c, (p.s1, p.s2)[way])
        return send(there, there, self.xs[way], step, p.across(way))

    def relay_copy(self, step, way):
        p = self.place
        there = self.block(2 * p.far(step) + p.c, (p.s2, p.s1)[way], 1 - way)
        return send(there, there, self.rs[way], step, p.across(way))

    def relay_arrival(self, step, way):
        p = self.place
        there = self.block(2 * p.far(step) + p.c, p.s3, 1 - way)
        return send(there, there, self.rs[way], step, p.across(way))

    def begin(self):
        self.place.each(1, self.place.depth, lambda step: self.z_copy(step).start())
        self.own_copy().start()
        self.core_copy(0).start()

    def swap(self, step):
        self.z_arrival(step).wait_recv()
        if self.split:
            for way in (0, 1):
                self.x_copy(step, way).start()
        else:
            self.core_copy(step).start()

    def relay(self, step):
        if self.split:
            for way in (0, 1):
                self.x_arrival(step, way).wait_recv()
            for way in (0, 1):
                self.relay_copy(step, way).start()

    def share(self, step):
        if self.split:
            for way in (0, 1):
                self.relay_arrival(step, way).wait_recv()
            self.core_copy(step).start()

    def finish(self):
        self.own_copy().wait()
        self.core_copy(0).wait_send()
        self.core_arrival(0).wait_recv()

        def close(step):
            self.z_copy(step).wait_send()
            if self.split:
                for way in (0, 1):
                    self.x_copy(step, way).wait_send()
                    self.relay_copy(step, way).wait_send()
            self.core_copy(step).wait_send()
            self.core_arrival(step).wait_recv()

        self.place.each(1, self.place.depth, close)

    @staticmethod
    def scratch(depth):
        pair = [pltpu.SemaphoreType.DMA((depth,))] * 2
        return [pltpu.SemaphoreType.DMA] + pair * 6

    @staticmethod
    def take(refs):
        pairs = [(refs[i], refs[i + 1]) for i in range(1, 13, 2)]
        return (refs[0], pairs[0], pairs[1:3], pairs[3:5], pairs[5])


GATHER_SEMS = 13


def gather_steps(place, gathers, between):
    depth = place.depth
    work = list(between)

    def stage(step, swap, relay, share):
        for one in gathers:
            if swap:
                one.swap(step)
        for one in gathers:
            if relay:
                one.relay(step - 1)
        for one in gathers:
            if share:
                one.share(step - 2)

    if depth <= 8:
        for step in range(1, depth + 2):
            stage(step, step < depth, 2 <= step <= depth, step >= 3)
            if work:
                work.pop(0)()
    else:
        stage(1, True, False, False)
        stage(2, True, True, False)
        lax.fori_loop(3, depth, lambda step, carry: (stage(step, True, True, True), carry)[1], 0)
        stage(depth, False, True, True)
        stage(depth + 1, False, False, True)
    for rest in work:
        rest()


def first_gather_kernel(fsdp_count, w_ref, vec_ref, seg_ref, w_all, vec_all, seg_all, *sems):
    place = Place(fsdp_count)
    weight = Gather(place, w_ref, w_all, True, Gather.take(sems[:GATHER_SEMS]))
    vector = Gather(place, vec_ref, vec_all, False, Gather.take(sems[GATHER_SEMS : 2 * GATHER_SEMS]))
    local, sent, got = sems[2 * GATHER_SEMS :]
    rows = seg_ref.shape[0]
    place.meet()
    weight.begin()
    vector.begin()
    own = pltpu.make_async_copy(seg_ref, seg_all.at[aligned(place.s * rows, rows)], local)
    own.start()
    for way in range(3):
        send(seg_ref, seg_all.at[aligned(place.s * rows, rows)], (sent, got), way, place.across(way)).start()
    gather_steps(place, [vector, weight], [])
    own.wait()
    for way in range(3):
        there = seg_all.at[aligned((place.s1, place.s2, place.s3)[way] * rows, rows)]
        arrival = send(there, there, (sent, got), way, place.across(way))
        arrival.wait_recv()
        send(seg_ref, seg_all.at[aligned(place.s * rows, rows)], (sent, got), way, place.across(way)).wait_send()
    vector.finish()
    weight.finish()


def first_gather(fsdp_count, w_shard, vec, seg):
    anywhere = pl.BlockSpec(memory_space=pl.ANY)
    return pl.pallas_call(
        functools.partial(first_gather_kernel, fsdp_count),
        out_shape=(
            jax.ShapeDtypeStruct((fsdp_count * w_shard.shape[0], w_shard.shape[1]), w_shard.dtype),
            jax.ShapeDtypeStruct((fsdp_count * vec.shape[0], vec.shape[1]), vec.dtype),
            jax.ShapeDtypeStruct((4 * seg.shape[0], seg.shape[1]), seg.dtype),
        ),
        in_specs=[anywhere] * 3,
        out_specs=(anywhere,) * 3,
        scratch_shapes=Gather.scratch(fsdp_count // 2) * 2
        + [pltpu.SemaphoreType.DMA, pltpu.SemaphoreType.DMA((3,)), pltpu.SemaphoreType.DMA((3,))],
        compiler_params=pltpu.CompilerParams(collective_id=1, has_side_effects=True),
    )(w_shard, vec, seg)


def attend_unit(pair, odd, tile, heads_ref, qf_ref, kf_ref, keys_sc, values_t, out_ref, lse_ref):
    length = heads_ref.shape[0]
    scale = jnp.asarray(1.0 / math.sqrt(DH), BF16)
    cols = pl.ds(pair * LANES, LANES)
    q_cols, k_cols, v_cols = (pl.ds((3 * pair + i) * LANES, LANES) for i in range(3))
    if not odd:
        values_t[...] = heads_ref[:, v_cols].T
    mine = own_lanes(odd, (length, LANES))
    keys_sc[...] = jnp.where(mine, heads_ref[:, k_cols], kf_ref[...])

    def one_tile(index, carry):
        rows = aligned(index * tile, tile)
        lanes = own_lanes(odd, (tile, LANES))
        queries = jnp.where(lanes, heads_ref[rows, q_cols] * scale, qf_ref[2 * pair + odd, rows, :])
        scores = dot_nt(keys_sc[...], queries)
        top = jnp.max(scores, axis=0, keepdims=True)
        prob = jnp.exp(scores - top)
        total = jnp.sum(prob, axis=0, keepdims=True)
        mixed = dot_nn(values_t[...], prob.astype(BF16)) / total
        lse_ref[pair, pl.ds(odd, 1), rows] = top + jnp.log(total)
        result = mixed.T.astype(BF16)
        if odd:
            out_ref[rows, cols] = jnp.where(lanes, result, out_ref[rows, cols])
        else:
            out_ref[rows, cols] = result
        return carry

    lax.fori_loop(0, length // tile, one_tile, 0, unroll=2)


def forward_kernel(
    fsdp_count,
    qkv_ref,
    qf_ref,
    kf_ref,
    out_w_ref,
    down_w_ref,
    in_w_ref,
    heads_all,
    lse_ref,
    att_all,
    out_w_all,
    down_w_all,
    in_w_all,
    heads_sc,
    att_sc,
    keys_sc,
    values_t,
    *sems,
):
    place = Place(fsdp_count)
    rows, width = qkv_ref.shape[0], heads_sc.shape[1]
    gathers = [
        Gather(place, src, dst, True, Gather.take(sems[i * GATHER_SEMS : (i + 1) * GATHER_SEMS]))
        for i, (src, dst) in enumerate(
            ((out_w_ref, out_w_all), (in_w_ref, in_w_all), (down_w_ref, down_w_all))
        )
    ]
    own_sem, q_sent, q_got, copy_sem, a_sent, a_got, a_own = sems[3 * GATHER_SEMS :]
    seats = (place.s1, place.s2, place.s3)

    def part(seat):
        return qkv_ref.at[:, aligned(seat * width, width)]

    def slot(seat):
        return heads_sc.at[aligned(seat * rows, rows)]

    place.meet()
    for way in range(3):
        send(part(seats[way]), slot(place.s), (q_sent, q_got), way, place.across(way)).start()
    own = pltpu.make_async_copy(part(place.s), slot(place.s), own_sem)
    own.start()
    for one in gathers:
        one.begin()
    own.wait()
    for way in range(3):
        send(slot(seats[way]), slot(seats[way]), (q_sent, q_got), way, place.across(way)).wait_recv()
    keep = pltpu.make_async_copy(heads_sc, heads_all, copy_sem)
    keep.start()

    pairs = att_sc.shape[1] // LANES

    def att_copy(pair, way):
        cols = aligned((place.s * pairs + pair) * LANES, LANES)
        return send(
            att_sc.at[aligned(seats[way] * rows, rows), pl.ds(pair * LANES, LANES)],
            att_all.at[:, cols],
            (a_sent, a_got),
            pair * 3 + way,
            place.across(way),
        )

    def att_own(pair):
        cols = aligned((place.s * pairs + pair) * LANES, LANES)
        return pltpu.make_async_copy(
            att_sc.at[aligned(place.s * rows, rows), pl.ds(pair * LANES, LANES)],
            att_all.at[:, cols],
            a_own.at[pair],
        )

    def att_arrival(pair, way):
        there = att_all.at[:, aligned((seats[way] * pairs + pair) * LANES, LANES)]
        return send(there, there, (a_sent, a_got), pair * 3 + way, place.across(way))

    def unit(pair, odd):
        attend_unit(pair, odd, 256, heads_sc, qf_ref, kf_ref, keys_sc, values_t, att_sc, lse_ref)
        if odd:
            for way in range(3):
                att_copy(pair, way).start()
            att_own(pair).start()

    gather_steps(
        place,
        gathers,
        [functools.partial(unit, pair, odd) for pair in range(pairs) for odd in (0, 1)],
    )
    keep.wait()
    for way in range(3):
        send(part(seats[way]), slot(place.s), (q_sent, q_got), way, place.across(way)).wait_send()
        for pair in range(pairs):
            att_copy(pair, way).wait_send()
            att_arrival(pair, way).wait_recv()
    for pair in range(pairs):
        att_own(pair).wait()
    for one in gathers:
        one.finish()


def forward_attention(fsdp_count, qkv_rows, query_feats, key_feats, w_out, w_down, w_in):
    rows, width = qkv_rows.shape
    length = 4 * rows
    heads = query_feats.shape[0]
    pairs = heads // 2
    depth = fsdp_count // 2
    anywhere = pl.BlockSpec(memory_space=pl.ANY)
    vmem = pl.BlockSpec(memory_space=pltpu.VMEM)

    def whole(shard):
        return jax.ShapeDtypeStruct((fsdp_count * shard.shape[0], shard.shape[1]), shard.dtype)

    return pl.pallas_call(
        functools.partial(forward_kernel, fsdp_count),
        out_shape=(
            jax.ShapeDtypeStruct((length, width // 4), BF16),
            jax.ShapeDtypeStruct((pairs, 2, length), F32),
            jax.ShapeDtypeStruct((rows, width // 3), BF16),
            whole(w_out),
            whole(w_down),
            whole(w_in),
        ),
        in_specs=[anywhere, vmem, vmem, anywhere, anywhere, anywhere],
        out_specs=(anywhere, vmem, anywhere, anywhere, anywhere, anywhere),
        scratch_shapes=[
            pltpu.VMEM((length, width // 4), BF16),
            pltpu.VMEM((length, heads * DH), BF16),
            pltpu.VMEM((length, LANES), BF16),
            pltpu.VMEM((LANES, length), BF16),
        ]
        + Gather.scratch(depth) * 3
        + [
            pltpu.SemaphoreType.DMA,
            pltpu.SemaphoreType.DMA((3,)),
            pltpu.SemaphoreType.DMA((3,)),
            pltpu.SemaphoreType.DMA,
            pltpu.SemaphoreType.DMA((3 * pairs,)),
            pltpu.SemaphoreType.DMA((3 * pairs,)),
            pltpu.SemaphoreType.DMA((pairs,)),
        ],
        compiler_params=pltpu.CompilerParams(
            collective_id=2, has_side_effects=True, vmem_limit_bytes=40 << 20
        ),
    )(qkv_rows, query_feats, key_feats, w_out, w_down, w_in)


def by_rows(count, body):
    lax.fori_loop(0, count // 16, lambda i, carry: (body(aligned(i * 16, 16)), carry)[1], 0)


class Reduce:
    def __init__(self, place, grad, out, bufs, sems):
        self.place, self.grad, self.out = place, grad, out
        self.rows, self.cols = out.shape
        self.wide = self.cols // 4
        self.acc, self.own, self.relay_in, self.quarter_in, self.z_in, self.total = bufs
        self.own_sem, self.cs, self.rs, self.qs, self.zs, self.fs, self.gs = sems

    @staticmethod
    def scratch(depth, rows, cols):
        pair = [pltpu.SemaphoreType.DMA((depth,))] * 2
        single = [pltpu.SemaphoreType.DMA((2,))] * 2
        return [
            pltpu.VMEM((depth, rows, cols), BF16),
            pltpu.VMEM((rows, cols), BF16),
            pltpu.VMEM((2, depth, rows, cols // 8), BF16),
            pltpu.VMEM((2, depth, rows, cols // 4), BF16),
            pltpu.VMEM((depth, rows, cols // 4), BF16),
            pltpu.VMEM((rows, cols), BF16),
            pltpu.SemaphoreType.DMA,
        ] + pair * 6 + single * 2

    @staticmethod
    def take(place, grad, out, refs):
        s = refs[7:]
        pairs = [(s[i], s[i + 1]) for i in range(0, 16, 2)]
        sems = (refs[6], pairs[0], pairs[1:3], pairs[3:5], pairs[5], pairs[6], pairs[7])
        return Reduce(place, grad, out, refs[:6], sems)

    def quarter(self, seat):
        return aligned(seat * self.wide, self.wide)

    def piece(self, seat, half):
        return aligned(seat * self.wide + half * (self.wide // 2), self.wide // 2)

    def own_copy(self, step):
        p = self.place
        rows = aligned((2 * p.far(step) + p.c) * self.rows, self.rows)
        return pltpu.make_async_copy(self.grad.at[rows], self.own, self.own_sem)

    def core_copy(self, step):
        p = self.place
        rows = aligned((2 * p.far(step) + 1 - p.c) * self.rows, self.rows)
        return send(self.grad.at[rows], self.acc.at[step], self.cs, step, p.beside)

    def relay_copy(self, step, way):
        p = self.place
        src = self.acc.at[step, :, self.piece(p.s3, way)]
        return send(src, self.relay_in.at[way, step], self.rs[way], step, p.across(way))

    def quarter_copy(self, step, way):
        p = self.place
        src = self.acc.at[step, :, self.quarter((p.s1, p.s2)[way])]
        return send(src, self.quarter_in.at[way, step], self.qs[way], step, p.across(way))

    def z_copy(self, step):
        p = self.place
        src = self.acc.at[step, :, self.quarter(p.s)]
        return send(src, self.z_in.at[step], self.zs, step, p.along(p.far(step)))

    def total_copy(self, way):
        p = self.place
        there = self.total.at[:, self.quarter(p.s)]
        return send(there, there, self.fs, way, p.across(way))

    def total_arrival(self, way):
        p = self.place
        there = self.total.at[:, self.quarter((p.s1, p.s2)[way])]
        return send(there, there, self.fs, way, p.across(way))

    def back_copy(self, way):
        p = self.place
        there = self.total.at[:, self.piece((p.s2, p.s1)[way], 1 - way)]
        return send(there, there, self.gs, way, p.across(way))

    def back_arrival(self, way):
        p = self.place
        there = self.total.at[:, self.piece(p.s3, 1 - way)]
        return send(there, there, self.gs, way, p.across(way))

    def begin(self):
        depth = self.place.depth
        self.place.each(1, depth, lambda step: self.core_copy(step).start())
        self.core_copy(0).start()
        self.own_copy(1).start()

    def fold(self, step, following):
        self.core_copy(step).wait_recv()
        self.own_copy(step).wait()
        acc, own = self.acc, self.own

        def body(rows):
            acc[step, rows, :] = (acc[step, rows, :].astype(F32) + own[rows, :].astype(F32)).astype(BF16)

        by_rows(self.rows, body)
        if following is not None:
            self.own_copy(following).start()
        for way in (0, 1):
            self.relay_copy(step, way).start()

    def swap(self, step):
        p, acc, half = self.place, self.acc, self.wide // 2
        for way in (0, 1):
            self.relay_copy(step, way).wait_recv()
            cols = self.piece((p.s2, p.s1)[way], way)
            came = self.relay_in.at[way, step]

            def body(rows):
                acc[step, rows, cols] = (acc[step, rows, cols].astype(F32) + came[rows, :].astype(F32)).astype(BF16)

            by_rows(self.rows, body)
        for way in (0, 1):
            self.quarter_copy(step, way).start()

    def close(self, step, own):
        p, acc, came = self.place, self.acc, self.quarter_in
        for way in (0, 1):
            self.quarter_copy(step, way).wait_recv()
        cols = self.quarter(p.s)

        def body(rows):
            acc[step, rows, cols] = (
                acc[step, rows, cols].astype(F32)
                + came[0, step, rows, :].astype(F32)
                + came[1, step, rows, :].astype(F32)
            ).astype(BF16)

        by_rows(self.rows, body)
        if not own:
            self.z_copy(step).start()

    def collect(self):
        p, acc, came, total = self.place, self.acc, self.z_in, self.total
        p.each(1, p.depth, lambda step: self.z_copy(step).wait_recv())
        cols = self.quarter(p.s)

        def body(rows):
            start = acc[0, rows, cols].astype(F32)
            if p.depth <= 8:
                for step in range(1, p.depth):
                    start = start + came[step, rows, :].astype(F32)
            else:
                start = lax.fori_loop(1, p.depth, lambda step, sofar: sofar + came[step, rows, :].astype(F32), start)
            total[rows, cols] = start.astype(BF16)

        by_rows(self.rows, body)
        for way in (0, 1):
            self.total_copy(way).start()

    def spread(self):
        for way in (0, 1):
            self.total_arrival(way).wait_recv()
        for way in (0, 1):
            self.back_copy(way).start()

    def finish(self):
        for way in (0, 1):
            self.back_arrival(way).wait_recv()
        total, out = self.total, self.out

        def body(rows):
            out[rows, :] = total[rows, :].astype(F32)

        by_rows(self.rows, body)

        def done(step):
            self.core_copy(step).wait_send()
            for way in (0, 1):
                self.relay_copy(step, way).wait_send()
                self.quarter_copy(step, way).wait_send()

        self.place.each(0, self.place.depth, done)
        self.place.each(1, self.place.depth, lambda step: self.z_copy(step).wait_send())
        for way in (0, 1):
            self.total_copy(way).wait_send()
            self.back_copy(way).wait_send()


REDUCE_REFS = 23


def reduce_steps(place, reduces, between):
    depth = place.depth
    work = list(between)

    def gap():
        if work:
            work.pop(0)()

    if depth <= 8:
        order = [(t + 1) % depth for t in range(depth)]
        for t in range(depth + 2):
            for one in reduces:
                if t < depth:
                    one.fold(order[t], order[t + 1] if t + 1 < depth else None)
            for one in reduces:
                if 0 <= t - 1 < depth:
                    one.swap(order[t - 1])
            for one in reduces:
                if 0 <= t - 2 < depth:
                    one.close(order[t - 2], order[t - 2] == 0)
            gap()
    else:
        def run(first, last, body):
            lax.fori_loop(first, last, lambda step, carry: (body(step), carry)[1], 0)

        for one in reduces:
            run(1, depth, lambda step: one.fold(step, lax.rem(step + 1, depth)))
            one.fold(0, None)
            run(0, depth, one.swap)
            run(1, depth, lambda step: one.close(step, False))
            one.close(0, True)
    for one in reduces:
        one.collect()
    gap()
    for one in reduces:
        one.spread()
    gap()
    for rest in work:
        rest()


def backward_unit(
    pair, odd, half, tile, heads_ref, qf_ref, kf_ref, go_ref, lse_ref, out_ref, keys_sc, values_sc, keys_t, p_sc, s_sc, k_acc, v_acc
):
    length = heads_ref.shape[0]
    span = p_sc.shape[1]
    scale = jnp.asarray(1.0 / math.sqrt(DH), BF16)
    q_cols, k_cols, v_cols = (pl.ds((3 * pair + i) * LANES, LANES) for i in range(3))
    cols = pl.ds(pair * LANES, LANES)
    mine = own_lanes(odd, (length, LANES))
    if half == 0:
        keys_sc[...] = jnp.where(mine, heads_ref[:, k_cols], kf_ref[...])
        values_sc[...] = jnp.where(mine, heads_ref[:, v_cols], jnp.zeros((), BF16))
        if not odd:
            keys_t[...] = heads_ref[:, k_cols].T

    def one_tile(index, carry):
        here = aligned(index * tile, tile)
        rows = aligned(half * span + index * tile, tile)
        lanes = own_lanes(odd, (tile, LANES))
        queries = jnp.where(lanes, heads_ref[rows, q_cols] * scale, qf_ref[2 * pair + odd, rows, :])
        prob = jnp.exp(dot_nt(keys_sc[...], queries) - lse_ref[pair, pl.ds(odd, 1), rows])
        grad_prob = dot_nt(values_sc[...], go_ref[rows, cols])
        delta = jnp.sum(prob * grad_prob, axis=0, keepdims=True)
        p_sc[:, here] = prob.astype(BF16)
        s_sc[:, here] = (prob * (grad_prob - delta)).astype(BF16)
        return carry

    lax.fori_loop(0, span // tile, one_tile, 0)
    part = pl.ds(half * span, span)
    grad_v = dot_nn(p_sc[...], go_ref[part, cols])
    grad_k = dot_nn(s_sc[...], heads_ref[part, q_cols] * scale)
    grad_q = (dot_nn(keys_t[...], s_sc[...]) * (1.0 / math.sqrt(DH))).T.astype(BF16)
    last = half * span + span == length

    def put(rows, columns, value, keep):
        if odd:
            value = jnp.where(keep, value, out_ref[rows, columns])
        out_ref[rows, columns] = value

    put(part, q_cols, grad_q, own_lanes(odd, (span, LANES)))
    if half > 0:
        grad_v, grad_k = grad_v + v_acc[...], grad_k + k_acc[...]
    if last:
        put(pl.ds(0, length), k_cols, grad_k.astype(BF16), mine)
        put(pl.ds(0, length), v_cols, grad_v.astype(BF16), mine)
    else:
        v_acc[...], k_acc[...] = grad_v, grad_k


def backward_kernel(
    fsdp_count,
    go_rows_ref,
    heads_ref,
    qf_ref,
    kf_ref,
    lse_ref,
    out_g_ref,
    down_g_ref,
    in_g_ref,
    dqkv_all,
    out_total,
    down_total,
    in_total,
    go_sc,
    grads_sc,
    keys_sc,
    values_sc,
    keys_t,
    p_sc,
    s_sc,
    k_acc,
    v_acc,
    *rest,
):
    place = Place(fsdp_count)
    rows = go_rows_ref.shape[0]
    reduces = [
        Reduce.take(place, grad, out, rest[i * REDUCE_REFS : (i + 1) * REDUCE_REFS])
        for i, (grad, out) in enumerate(
            ((out_g_ref, out_total), (in_g_ref, in_total), (down_g_ref, down_total))
        )
    ]
    g_own, g_sent, g_got, d_sent, d_got, d_own = rest[3 * REDUCE_REFS :]
    seats = (place.s1, place.s2, place.s3)
    width = go_sc.shape[1]
    pairs = width // LANES
    block = 3 * LANES

    def part(seat):
        return go_rows_ref.at[:, aligned(seat * width, width)]

    def slot(seat):
        return go_sc.at[aligned(seat * rows, rows)]

    def grad_copy(pair, way):
        src = grads_sc.at[aligned(seats[way] * rows, rows), pl.ds(pair * block, block)]
        dst = dqkv_all.at[:, aligned((place.s * pairs + pair) * block, block)]
        return send(src, dst, (d_sent, d_got), pair * 3 + way, place.across(way))

    def grad_own(pair):
        src = grads_sc.at[aligned(place.s * rows, rows), pl.ds(pair * block, block)]
        dst = dqkv_all.at[:, aligned((place.s * pairs + pair) * block, block)]
        return pltpu.make_async_copy(src, dst, d_own.at[pair])

    def grad_arrival(pair, way):
        there = dqkv_all.at[:, aligned((seats[way] * pairs + pair) * block, block)]
        return send(there, there, (d_sent, d_got), pair * 3 + way, place.across(way))

    place.meet()
    for way in range(3):
        send(part(seats[way]), slot(place.s), (g_sent, g_got), way, place.across(way)).start()
    own = pltpu.make_async_copy(part(place.s), slot(place.s), g_own)
    own.start()
    for one in reduces:
        one.begin()
    own.wait()
    for way in range(3):
        send(slot(seats[way]), slot(seats[way]), (g_sent, g_got), way, place.across(way)).wait_recv()

    def unit(pair, odd, half):
        backward_unit(
            pair, odd, half, 256, heads_ref, qf_ref, kf_ref, go_sc, lse_ref, grads_sc,
            keys_sc, values_sc, keys_t, p_sc, s_sc, k_acc, v_acc,
        )
        if odd and half:
            for way in range(3):
                grad_copy(pair, way).start()
            grad_own(pair).start()

    reduce_steps(
        place,
        reduces,
        [functools.partial(unit, pair, odd, half) for pair in range(pairs) for odd in (0, 1) for half in (0, 1)],
    )
    for way in range(3):
        send(part(seats[way]), slot(place.s), (g_sent, g_got), way, place.across(way)).wait_send()
        for pair in range(pairs):
            grad_copy(pair, way).wait_send()
            grad_arrival(pair, way).wait_recv()
    for pair in range(pairs):
        grad_own(pair).wait()
    for one in reduces:
        one.finish()


def backward_attention(fsdp_count, grad_att, by_heads, query_feats, key_feats, lse, grad_out, grad_down, grad_in):
    rows, width = grad_att.shape
    length = by_heads.shape[0]
    own_width = width // 4
    depth = fsdp_count // 2
    span = length // 2
    anywhere = pl.BlockSpec(memory_space=pl.ANY)
    vmem = pl.BlockSpec(memory_space=pltpu.VMEM)
    grads = (grad_out, grad_in, grad_down)

    def kept(grad):
        return jax.ShapeDtypeStruct((grad.shape[0] // fsdp_count, grad.shape[1]), F32)

    reduce_scratch = []
    for grad in grads:
        reduce_scratch += Reduce.scratch(depth, *kept(grad).shape)
    return pl.pallas_call(
        functools.partial(backward_kernel, fsdp_count),
        out_shape=(
            jax.ShapeDtypeStruct((rows, 3 * width), BF16),
            kept(grad_out),
            kept(grad_down),
            kept(grad_in),
        ),
        in_specs=[anywhere, vmem, vmem, vmem, vmem, anywhere, anywhere, anywhere],
        out_specs=(anywhere, vmem, vmem, vmem),
        scratch_shapes=[
            pltpu.VMEM((length, own_width), BF16),
            pltpu.VMEM((length, 3 * own_width), BF16),
            pltpu.VMEM((length, LANES), BF16),
            pltpu.VMEM((length, LANES), BF16),
            pltpu.VMEM((LANES, length), BF16),
            pltpu.VMEM((length, span), BF16),
            pltpu.VMEM((length, span), BF16),
            pltpu.VMEM((length, LANES), F32),
            pltpu.VMEM((length, LANES), F32),
        ]
        + reduce_scratch
        + [
            pltpu.SemaphoreType.DMA,
            pltpu.SemaphoreType.DMA((3,)),
            pltpu.SemaphoreType.DMA((3,)),
            pltpu.SemaphoreType.DMA((3 * own_width // LANES,)),
            pltpu.SemaphoreType.DMA((3 * own_width // LANES,)),
            pltpu.SemaphoreType.DMA((own_width // LANES,)),
        ],
        compiler_params=pltpu.CompilerParams(
            collective_id=3, has_side_effects=True, vmem_limit_bytes=60 << 20
        ),
    )(grad_att, by_heads, query_feats, key_feats, lse, grad_out, grad_down, grad_in)


def last_reduce_kernel(fsdp_count, grad_ref, small_ref, total_ref, small_total, mine_in, z_in, x_in, own_sc, *rest):
    place = Place(fsdp_count)
    big = Reduce.take(place, grad_ref, total_ref, rest[:REDUCE_REFS])
    c_sent, c_got, z_sent, z_got, x_sent, x_got = rest[REDUCE_REFS:]
    size = small_total.shape[0]
    depth = place.depth

    def rows_of(z, core):
        return aligned((2 * z + core) * size, size)

    def core_copy(step):
        src = small_ref.at[rows_of(place.far(step), 1 - place.c)]
        return send(src, mine_in.at[step], (c_sent, c_got), step, place.beside)

    def z_copy(step):
        return send(own_sc.at[step], z_in.at[step], (z_sent, z_got), step, place.along(place.far(step)))

    def x_copy(way):
        return send(own_sc.at[0], x_in.at[way], (x_sent, x_got), way, place.across(way))

    def fold(step):
        core_copy(step).wait_recv()
        own_sc[step] = small_ref[rows_of(place.far(step), place.c), :] + mine_in[step]

    def along(step):
        fold(step)
        z_copy(step).start()

    def gather_z(step):
        z_copy(step).wait_recv()
        own_sc[0] = own_sc[0] + z_in[step]

    place.meet()
    place.each(0, depth, lambda step: core_copy(step).start())
    big.begin()
    fold(0)
    place.each(1, depth, along)

    def small_middle():
        place.each(1, depth, gather_z)
        for way in range(3):
            x_copy(way).start()

    def small_end():
        for way in range(3):
            x_copy(way).wait_recv()
        small_total[...] = own_sc[0] + x_in[0] + x_in[1] + x_in[2]

    reduce_steps(place, [big], [small_middle, small_end])
    place.each(0, depth, lambda step: core_copy(step).wait_send())
    place.each(1, depth, lambda step: z_copy(step).wait_send())
    for way in range(3):
        x_copy(way).wait_send()
    big.finish()


def last_reduce(fsdp_count, grad, small):
    anywhere = pl.BlockSpec(memory_space=pl.ANY)
    vmem = pl.BlockSpec(memory_space=pltpu.VMEM)
    depth = fsdp_count // 2
    size = small.shape[0] // fsdp_count
    kept = (grad.shape[0] // fsdp_count, grad.shape[1])
    return pl.pallas_call(
        functools.partial(last_reduce_kernel, fsdp_count),
        out_shape=(jax.ShapeDtypeStruct(kept, F32), jax.ShapeDtypeStruct((size, LANES), F32)),
        in_specs=[anywhere, vmem],
        out_specs=(vmem, vmem),
        scratch_shapes=[
            pltpu.VMEM((depth, size, LANES), F32),
            pltpu.VMEM((depth, size, LANES), F32),
            pltpu.VMEM((3, size, LANES), F32),
            pltpu.VMEM((depth, size, LANES), F32),
        ]
        + Reduce.scratch(depth, *kept)
        + [
            pltpu.SemaphoreType.DMA((depth,)),
            pltpu.SemaphoreType.DMA((depth,)),
            pltpu.SemaphoreType.DMA((depth,)),
            pltpu.SemaphoreType.DMA((depth,)),
            pltpu.SemaphoreType.DMA((3,)),
            pltpu.SemaphoreType.DMA((3,)),
        ],
        compiler_params=pltpu.CompilerParams(
            collective_id=4, has_side_effects=True, vmem_limit_bytes=48 << 20
        ),
    )(grad, small)


def swap_thirds(rows, outer, inner):
    count, width = rows.shape
    return rows.reshape(count, outer, inner, width // (outer * inner)).swapaxes(1, 2).reshape(count, width)


def per_device(
    seq_count,
    fsdp_count,
    tokens,
    segment_ids,
    random_blocks,
    ln1_gain,
    ln1_bias,
    w_qkv,
    w_out,
    ln2_gain,
    ln2_bias,
    w_in,
    b_in,
    w_down,
    b_down,
    cotangent,
):
    groups = w_qkv.shape[1] // (3 * LANES)
    share = ln1_gain.shape[0]
    packed = jnp.concatenate([ln1_gain, ln1_bias, ln2_gain, ln2_bias, b_down, b_in])
    packed_rows = -(-packed.shape[0] // (16 * LANES)) * 16
    packed = jnp.pad(packed, (0, packed_rows * LANES - packed.shape[0])).reshape(packed_rows, LANES)
    tok_count = segment_ids.shape[1]
    seg_rows = -(-tok_count // (8 * LANES)) * 8
    seg = jnp.pad(segment_ids[0], (0, seg_rows * LANES - tok_count)).reshape(seg_rows, LANES)
    qkv_weight, packed, seg = first_gather(fsdp_count, swap_thirds(w_qkv, 3, groups), packed, seg)
    packed = packed.reshape(fsdp_count, packed_rows * LANES).astype(F32)
    gain_one, bias_one, gain_two, bias_two, down_bias = (
        packed[:, i * share : (i + 1) * share].reshape(-1) for i in range(5)
    )
    in_bias = packed[:, 5 * share : 5 * share + b_in.shape[0]].reshape(-1)
    seq_ids = seg.reshape(seq_count, seg_rows * LANES)[:, :tok_count].reshape(-1)
    query_feats, key_feats = mask_features(random_blocks, seq_ids, 6)

    token_rows = tokens[0].astype(F32)
    hat_one, inv_one = layer_norm_parts(token_rows)
    normed_one = (hat_one * gain_one + bias_one).astype(BF16)
    qkv_rows = dot_nn(normed_one, qkv_weight).astype(BF16)
    by_heads, lse, att_rows, out_weight, down_weight, in_weight = forward_attention(
        fsdp_count, qkv_rows, query_feats, key_feats, w_out, w_down, w_in
    )
    hidden = token_rows + dot_nn(att_rows, out_weight)
    hat_two, inv_two = layer_norm_parts(hidden)
    normed_two = (hat_two * gain_two + bias_two).astype(BF16)
    pre_act = dot_nn(normed_two, in_weight) + in_bias
    act_value, pull_gelu = jax.vjp(gelu_tanh, pre_act)
    act_low = act_value.astype(BF16)
    result = hidden + dot_nn(act_low, down_weight) + down_bias

    cot_low = cotangent[0]
    cot_rows = cot_low.astype(F32)
    grad_pre = pull_gelu(dot_nt(cot_low, down_weight))[0].astype(BF16)
    grad_norm_two = dot_nt(grad_pre, in_weight)
    scaled = grad_norm_two * gain_two
    grad_hidden = cot_rows + inv_two * (
        scaled
        - jnp.mean(scaled, axis=-1, keepdims=True)
        - hat_two * jnp.mean(scaled * hat_two, axis=-1, keepdims=True)
    )
    hidden_low = grad_hidden.astype(BF16)
    grad_att = dot_nt(hidden_low, out_weight).astype(BF16)
    grad_qkv_rows, total_out, total_down, total_in = backward_attention(
        fsdp_count,
        grad_att,
        by_heads,
        query_feats,
        key_feats,
        lse,
        dot_tn(att_rows, hidden_low).astype(BF16),
        dot_tn(act_low, cot_low).astype(BF16),
        dot_tn(normed_two, grad_pre).astype(BF16),
    )
    grad_qkv = dot_tn(normed_one, grad_qkv_rows).astype(BF16)
    grad_norm_one = dot_nt(grad_qkv_rows, qkv_weight)
    scaled_one = grad_norm_one * gain_one
    grad_tokens = (
        grad_hidden
        + inv_one
        * (
            scaled_one
            - jnp.mean(scaled_one, axis=-1, keepdims=True)
            - hat_one * jnp.mean(scaled_one * hat_one, axis=-1, keepdims=True)
        )
    ).astype(BF16)

    small = [
        jnp.sum(grad_norm_one * hat_one, axis=0),
        jnp.sum(grad_norm_one, axis=0),
        jnp.sum(grad_norm_two * hat_two, axis=0),
        jnp.sum(grad_norm_two, axis=0),
        jnp.sum(cot_rows, axis=0),
        jnp.sum(grad_pre.astype(F32), axis=0),
    ]
    small = jnp.concatenate([v.reshape(fsdp_count, -1) for v in small], axis=1)
    small = jnp.pad(small, ((0, 0), (0, packed_rows * LANES - small.shape[1])))
    total_qkv, small = last_reduce(fsdp_count, grad_qkv, small.reshape(-1, LANES))
    small = small.reshape(-1)
    parts = [small[i * share : (i + 1) * share] for i in range(5)]
    parts.append(small[5 * share : 5 * share + b_in.shape[0]])
    return (
        result.astype(BF16)[None],
        grad_tokens[None],
        parts[0],
        parts[1],
        swap_thirds(total_qkv, groups, 3),
        total_out,
        parts[2],
        parts[3],
        total_in,
        parts[5],
        total_down,
        parts[4],
    )


def solution(mesh):
    return jax.shard_map(
        functools.partial(per_device, mesh.shape["seq"], mesh.shape["fsdp"]),
        mesh=mesh,
        in_specs=(
            P("fsdp", "seq", None),
            P("fsdp", "seq"),
            P("seq", None, None),
            P("fsdp"),
            P("fsdp"),
            P("fsdp", None),
            P("fsdp", None),
            P("fsdp"),
            P("fsdp"),
            P("fsdp", None),
            P("fsdp"),
            P("fsdp", None),
            P("fsdp"),
            P("fsdp", "seq", None),
        ),
        out_specs=(
            P("fsdp", "seq", None),
            P("fsdp", "seq", None),
            P("fsdp"),
            P("fsdp"),
            P("fsdp", None),
            P("fsdp", None),
            P("fsdp"),
            P("fsdp"),
            P("fsdp", None),
            P("fsdp"),
            P("fsdp", None),
            P("fsdp"),
        ),
        check_vma=False,
    )
```

```python
import functools
import math

import jax
import jax.numpy as jnp
from jax import lax
from jax.experimental import pallas as pl
from jax.experimental.pallas import tpu as pltpu
from jax.sharding import PartitionSpec as P

DH = 64
BLK = 64
LANES = 128
NEG = -1e30
F32 = jnp.float32
BF16 = jnp.bfloat16


def layer_norm_parts(rows):
    center = rows - jnp.mean(rows, axis=-1, keepdims=True)
    variance = jnp.mean(center * center, axis=-1, keepdims=True)
    inv = lax.rsqrt(variance + 1e-05)
    return center * inv, inv


def gelu_tanh(pre_act):
    return (
        0.5
        * pre_act
        * (1.0 + jnp.tanh(0.7978845608028654 * (pre_act + 0.044715 * pre_act * pre_act * pre_act)))
    )


def dot_nn(a, b):
    return jnp.dot(a, b, preferred_element_type=F32)


def dot_nt(a, b):
    return lax.dot_general(a, b, (((1,), (1,)), ((), ())), preferred_element_type=F32)


def dot_tn(a, b):
    return lax.dot_general(a, b, (((0,), (0,)), ((), ())), preferred_element_type=F32)


DOCS = 6


def block_mask(random_blocks):
    heads, inner, _ = random_blocks.shape
    blocks = inner + 2
    ids = jnp.arange(blocks, dtype=jnp.int32)
    near = jnp.abs(ids[:, None] - ids[None, :]) <= 1
    edge = (ids == 0) | (ids == blocks - 1)
    fixed = near | edge[:, None] | edge[None, :]
    picked = jnp.any(random_blocks[:, :, :, None] == ids, axis=2)
    used = fixed[None] | jnp.pad(picked, ((0, 0), (1, 1), (0, 0)))
    row = jnp.pad(jnp.where(used, 0.0, NEG), ((0, 0), (0, 0), (0, DH - blocks)))
    return jnp.concatenate([row, row], axis=-1)


def token_features(start, docs, blocks):
    shape = (docs.shape[0], LANES)
    lane = lax.rem(lax.broadcasted_iota(jnp.int32, shape, 1), DH)
    block = lax.div(lax.broadcasted_iota(jnp.int32, shape, 0) + start, BLK)
    own = docs + blocks == lane
    other = jnp.where(own | (lane >= blocks + DOCS), 0.0, 1.0)
    key_part = jnp.where(lane < blocks, jnp.where(block == lane, 1.0, 0.0), other)
    return jnp.where(own, NEG, 0.0).astype(BF16), key_part.astype(BF16)


def query_tile(q_tile, doc_tile, mask_ref, head, first_block, lanes):
    scale = jnp.asarray(1.0 / math.sqrt(DH), BF16)
    count = q_tile.shape[0] // BLK
    mask = jnp.concatenate(
        [jnp.broadcast_to(mask_ref[head, pl.ds(first_block + i, 1), :], (BLK, LANES)) for i in range(count)], axis=0
    )
    return jnp.where(lanes, q_tile * scale, doc_tile + mask.astype(BF16))


def own_lanes(odd, shape):
    lane = lax.broadcasted_iota(jnp.int32, shape, 1)
    return (lane >= DH) if odd else (lane < DH)


MESH = pl.DeviceIdType.MESH


class Place:
    def __init__(self, fsdp_count):
        self.depth = fsdp_count // 2
        self.s = lax.axis_index("seq")
        self.f = lax.axis_index("fsdp")
        self.z = lax.div(self.f, 2)
        self.c = lax.rem(self.f, 2)
        self.s1 = self.s + 1 - 2 * lax.rem(self.s, 2)
        self.s2 = self.s + 2 - 4 * lax.div(self.s, 2)
        self.s3 = 3 - self.s
        self.beside = (self.s, self.f + 1 - 2 * self.c)

    def across(self, index):
        return ((self.s1, self.s2, self.s3)[index], self.f)

    def far(self, step):
        return lax.rem(self.z + step, self.depth)

    def back(self, step):
        return lax.rem(self.z + self.depth - step, self.depth)

    def along(self, z):
        return (self.s, 2 * z + self.c)

    def meet(self):
        barrier = pltpu.get_barrier_semaphore()
        peers = [self.beside] + [self.across(i) for i in range(3)]
        for peer in peers:
            pl.semaphore_signal(barrier, inc=1, device_id=peer, device_id_type=MESH)
        self.each(1, self.depth, lambda step: pl.semaphore_signal(
            barrier, inc=1, device_id=self.along(self.far(step)), device_id_type=MESH
        ))
        pl.semaphore_wait(barrier, len(peers) + self.depth - 1)

    def each(self, start, stop, body):
        if stop - start <= 8:
            for step in range(start, stop):
                body(step)
        else:
            lax.fori_loop(start, stop, lambda step, carry: (body(step), carry)[1], 0)


def send(src, dst, sems, index, device):
    sent, got = sems
    return pltpu.make_async_remote_copy(
        src_ref=src,
        dst_ref=dst,
        send_sem=sent.at[index],
        recv_sem=got.at[index],
        device_id=device,
        device_id_type=MESH,
    )


def aligned(start, size):
    return pl.ds(pl.multiple_of(start, size), size)


class Gather:
    def __init__(self, place, src, dst, split, sems):
        self.place, self.src, self.dst, self.split = place, src, dst, split
        self.rows, self.cols = src.shape
        self.local, self.zs, self.xs, self.rs, self.cs = sems

    def block(self, f, quarter=None, half=None):
        rows = aligned(f * self.rows, self.rows)
        if quarter is None:
            return self.dst.at[rows]
        wide = self.cols // 4
        if half is None:
            return self.dst.at[rows, aligned(quarter * wide, wide)]
        return self.dst.at[rows, aligned(quarter * wide + half * (wide // 2), wide // 2)]

    def own_copy(self):
        return pltpu.make_async_copy(self.src, self.block(self.place.f), self.local)

    def core_copy(self, step):
        p = self.place
        f = 2 * p.far(step) + p.c
        src = self.src if isinstance(step, int) and step == 0 else self.block(f)
        return send(src, self.block(f), self.cs, step, p.beside)

    def core_arrival(self, step):
        p = self.place
        there = self.block(2 * p.far(step) + 1 - p.c)
        return send(there, there, self.cs, step, p.beside)

    def z_copy(self, step):
        p = self.place
        if self.split:
            wide = self.cols // 4
            src, dst = self.src.at[:, aligned(p.s * wide, wide)], self.block(p.f, p.s)
        else:
            src, dst = self.src, self.block(p.f)
        return send(src, dst, self.zs, step, p.along(p.back(step)))

    def z_arrival(self, step):
        p = self.place
        f = 2 * p.far(step) + p.c
        there = self.block(f, p.s) if self.split else self.block(f)
        return send(there, there, self.zs, step, p.along(p.far(step)))

    def x_copy(self, step, way):
        p = self.place
        there = self.block(2 * p.far(step) + p.c, p.s)
        return send(there, there, self.xs[way], step, p.across(way))

    def x_arrival(self, step, way):
        p = self.place
        there = self.block(2 * p.far(step) + p.c, (p.s1, p.s2)[way])
        return send(there, there, self.xs[way], step, p.across(way))

    def relay_copy(self, step, way):
        p = self.place
        there = self.block(2 * p.far(step) + p.c, (p.s2, p.s1)[way], 1 - way)
        return send(there, there, self.rs[way], step, p.across(way))

    def relay_arrival(self, step, way):
        p = self.place
        there = self.block(2 * p.far(step) + p.c, p.s3, 1 - way)
        return send(there, there, self.rs[way], step, p.across(way))

    def begin(self):
        self.place.each(1, self.place.depth, lambda step: self.z_copy(step).start())
        self.own_copy().start()
        self.core_copy(0).start()

    def swap(self, step):
        self.z_arrival(step).wait_recv()
        if self.split:
            for way in (0, 1):
                self.x_copy(step, way).start()
        else:
            self.core_copy(step).start()

    def relay(self, step):
        if self.split:
            for way in (0, 1):
                self.x_arrival(step, way).wait_recv()
            for way in (0, 1):
                self.relay_copy(step, way).start()

    def share(self, step):
        if self.split:
            for way in (0, 1):
                self.relay_arrival(step, way).wait_recv()
            self.core_copy(step).start()

    def finish(self):
        self.own_copy().wait()
        self.core_copy(0).wait_send()
        self.core_arrival(0).wait_recv()

        def close(step):
            self.z_copy(step).wait_send()
            if self.split:
                for way in (0, 1):
                    self.x_copy(step, way).wait_send()
                    self.relay_copy(step, way).wait_send()
            self.core_copy(step).wait_send()
            self.core_arrival(step).wait_recv()

        self.place.each(1, self.place.depth, close)

    @staticmethod
    def scratch(depth):
        pair = [pltpu.SemaphoreType.DMA((depth,))] * 2
        return [pltpu.SemaphoreType.DMA] + pair * 6

    @staticmethod
    def take(refs):
        pairs = [(refs[i], refs[i + 1]) for i in range(1, 13, 2)]
        return (refs[0], pairs[0], pairs[1:3], pairs[3:5], pairs[5])


GATHER_SEMS = 13


def gather_steps(place, gathers, between):
    depth = place.depth
    work = list(between)

    def stage(step, swap, relay, share):
        for one in gathers:
            if swap:
                one.swap(step)
        for one in gathers:
            if relay:
                one.relay(step - 1)
        for one in gathers:
            if share:
                one.share(step - 2)

    if depth <= 8:
        for step in range(1, depth + 2):
            stage(step, step < depth, 2 <= step <= depth, step >= 3)
            if work:
                work.pop(0)()
    else:
        stage(1, True, False, False)
        stage(2, True, True, False)
        lax.fori_loop(3, depth, lambda step, carry: (stage(step, True, True, True), carry)[1], 0)
        stage(depth, False, True, True)
        stage(depth + 1, False, False, True)
    for rest in work:
        rest()


def attend_unit(pair, odd, tile, heads_ref, mask_ref, qd_ref, kf_ref, keys_sc, values_t, out_ref, lse_ref):
    length = heads_ref.shape[0]
    cols = pl.ds(pair * LANES, LANES)
    q_cols, k_cols, v_cols = (pl.ds((3 * pair + i) * LANES, LANES) for i in range(3))
    if not odd:
        values_t[...] = heads_ref[:, v_cols].T
    mine = own_lanes(odd, (length, LANES))
    keys_sc[...] = jnp.where(mine, heads_ref[:, k_cols], kf_ref[...])

    def one_tile(index, carry):
        rows = aligned(index * tile, tile)
        lanes = own_lanes(odd, (tile, LANES))
        queries = query_tile(
            heads_ref[rows, q_cols], qd_ref[rows, :], mask_ref, 2 * pair + odd, index * (tile // BLK), lanes
        )
        scores = dot_nt(keys_sc[...], queries)
        top = jnp.max(scores, axis=0, keepdims=True)
        prob = jnp.exp(scores - top)
        total = jnp.sum(prob, axis=0, keepdims=True)
        mixed = dot_nn(values_t[...], prob.astype(BF16)) / total
        lse_ref[pair, pl.ds(odd, 1), rows] = top + jnp.log(total)
        result = mixed.T.astype(BF16)
        if odd:
            out_ref[rows, cols] = jnp.where(lanes, result, out_ref[rows, cols])
        else:
            out_ref[rows, cols] = result
        return carry

    lax.fori_loop(0, length // tile, one_tile, 0, unroll=2)


def forward_kernel(
    fsdp_count,
    x_ref,
    wq_ref,
    vec_ref,
    seg_ref,
    mask_ref,
    out_w_ref,
    down_w_ref,
    in_w_ref,
    heads_all,
    lse_ref,
    att_all,
    out_w_all,
    down_w_all,
    in_w_all,
    vec_sum,
    n1_all,
    wq_all,
    qd_ref,
    kf_ref,
    x_sc,
    n1_sc,
    wq_sc,
    vec_sc,
    seg_sc,
    heads_sc,
    att_sc,
    keys_sc,
    values_t,
    *sems,
):
    place = Place(fsdp_count)
    rows, width = x_ref.shape
    own_width = wq_sc.shape[1]
    seats = (place.s1, place.s2, place.s3)

    def taken(i):
        return Gather.take(sems[i * GATHER_SEMS : (i + 1) * GATHER_SEMS])

    gathers = [
        Gather(place, src, dst, True, taken(i))
        for i, (src, dst) in enumerate(
            ((out_w_ref, out_w_all), (in_w_ref, in_w_all), (down_w_ref, down_w_all))
        )
    ]
    weight = Gather(place, wq_ref.at[:, aligned(place.s * own_width, own_width)], wq_sc, False, taken(3))
    vector = Gather(place, vec_ref, vec_sc, False, taken(4))
    x_own, seg_own, keep_sems, x_sent, x_got, r_sent, r_got, g_sent, g_got, a_sent, a_got, a_own = sems[5 * GATHER_SEMS :]
    half = rows // 2

    def x_rows(seat):
        return x_sc.at[aligned(seat * rows, rows)]

    def x_half(seat, part):
        return x_sc.at[aligned(seat * rows + part * half, half)]

    def x_copy(way):
        return send(x_ref, x_rows(place.s), (x_sent, x_got), way, place.across(way))

    def x_arrival(way):
        there = x_rows(seats[way])
        return send(there, there, (x_sent, x_got), way, place.across(way))

    def x_relay(way):
        there = x_half((place.s2, place.s1)[way], 1 - way)
        return send(there, there, (r_sent, r_got), way, place.across(way))

    def x_relayed(way):
        there = x_half(place.s3, 1 - way)
        return send(there, there, (r_sent, r_got), way, place.across(way))

    def seg_copy(way):
        return send(seg_ref, seg_sc.at[place.s], (g_sent, g_got), way, place.across(way))

    def seg_arrival(way):
        there = seg_sc.at[seats[way]]
        return send(there, there, (g_sent, g_got), way, place.across(way))

    place.meet()
    vector.begin()
    weight.begin()
    for way in range(2):
        x_copy(way).start()
    for way in range(3):
        seg_copy(way).start()
    own_x = pltpu.make_async_copy(x_ref, x_rows(place.s), x_own)
    own_x.start()
    own_seg = pltpu.make_async_copy(seg_ref, seg_sc.at[place.s], seg_own)
    own_seg.start()
    place.each(1, place.depth, vector.swap)
    vector.finish()
    vec_rows = vec_ref.shape[0]
    total = vec_sc[pl.ds(0, vec_rows), :].astype(F32)
    if fsdp_count <= 8:
        for f in range(1, fsdp_count):
            total = total + vec_sc[pl.ds(f * vec_rows, vec_rows), :].astype(F32)
    else:
        total = lax.fori_loop(
            1, fsdp_count, lambda f, sofar: sofar + vec_sc[aligned(f * vec_rows, vec_rows), :].astype(F32), total
        )
    vec_sum[...] = total
    place.each(1, place.depth, weight.swap)

    def normalise(seat):
        def body(part):
            token_rows = x_sc[aligned(seat * rows + part * 32, 32), :].astype(F32)
            center = token_rows - jnp.mean(token_rows, axis=-1, keepdims=True)
            variance = jnp.mean(center * center, axis=-1, keepdims=True)
            normed = center * lax.rsqrt(variance + 1e-05) * vec_sum[0:1, :] + vec_sum[1:2, :]
            n1_sc[aligned(seat * rows + part * 32, 32), :] = normed.astype(BF16)

        lax.fori_loop(0, rows // 32, lambda part, carry: (body(part), carry)[1], 0)

    def project(seat):
        here = aligned(seat * rows, rows)

        def body(part):
            cols = aligned(part * 256, 256)
            heads_sc[here, cols] = dot_nn(n1_sc[here, :], wq_sc[:, cols]).astype(BF16)

        lax.fori_loop(0, own_width // 256, lambda part, carry: (body(part), carry)[1], 0)

    own_x.wait()
    normalise(place.s)
    for way in range(2):
        x_arrival(way).wait_recv()
    for way in range(2):
        x_relay(way).start()
    for one in gathers:
        one.begin()
    for way in range(2):
        normalise(seats[way])
    weight.finish()
    project(place.s)
    for way in range(2):
        project(seats[way])
    own_seg.wait()
    for way in range(3):
        seg_arrival(way).wait_recv()
    blocks = mask_ref.shape[1]
    for seat in range(4):
        columns = seg_sc[seat].T
        for part in range(rows // LANES):
            here = pl.ds(seat * rows + part * LANES, LANES)
            qd_ref[here, :], kf_ref[here, :] = token_features(
                seat * rows + part * LANES, columns[:, part : part + 1], blocks
            )
    for way in range(2):
        x_relayed(way).wait_recv()
    normalise(place.s3)
    project(place.s3)
    keeps = [
        pltpu.make_async_copy(src, dst, keep_sems.at[i])
        for i, (src, dst) in enumerate(((heads_sc, heads_all), (n1_sc, n1_all), (wq_sc, wq_all)))
    ]
    for keep in keeps:
        keep.start()

    pairs = att_sc.shape[1] // LANES

    def att_copy(pair, way):
        cols = aligned((place.s * pairs + pair) * LANES, LANES)
        return send(
            att_sc.at[aligned(seats[way] * rows, rows), pl.ds(pair * LANES, LANES)],
            att_all.at[:, cols],
            (a_sent, a_got),
            pair * 3 + way,
            place.across(way),
        )

    def att_own(pair):
        cols = aligned((place.s * pairs + pair) * LANES, LANES)
        return pltpu.make_async_copy(
            att_sc.at[aligned(place.s * rows, rows), pl.ds(pair * LANES, LANES)],
            att_all.at[:, cols],
            a_own.at[pair],
        )

    def att_arrival(pair, way):
        there = att_all.at[:, aligned((seats[way] * pairs + pair) * LANES, LANES)]
        return send(there, there, (a_sent, a_got), pair * 3 + way, place.across(way))

    def unit(pair, odd):
        attend_unit(pair, odd, 256, heads_sc, mask_ref, qd_ref, kf_ref, keys_sc, values_t, att_sc, lse_ref)
        if odd:
            for way in range(3):
                att_copy(pair, way).start()
            att_own(pair).start()

    gather_steps(
        place,
        gathers,
        [functools.partial(unit, pair, odd) for pair in range(pairs) for odd in (0, 1)],
    )
    for keep in keeps:
        keep.wait()
    for way in range(3):
        seg_copy(way).wait_send()
        if way < 2:
            x_copy(way).wait_send()
            x_relay(way).wait_send()
        for pair in range(pairs):
            att_copy(pair, way).wait_send()
            att_arrival(pair, way).wait_recv()
    for pair in range(pairs):
        att_own(pair).wait()
    for one in gathers:
        one.finish()


def dma(*shape):
    return pltpu.SemaphoreType.DMA(shape) if shape else pltpu.SemaphoreType.DMA


def forward_attention(fsdp_count, x, w_qkv, vec, seg, mask, w_out, w_down, w_in):
    rows, width = x.shape
    length = 4 * rows
    heads = mask.shape[0]
    pairs = heads // 2
    depth = fsdp_count // 2
    own_width = w_qkv.shape[1] // 4
    full = fsdp_count * w_qkv.shape[0]
    anywhere = pl.BlockSpec(memory_space=pl.ANY)
    vmem = pl.BlockSpec(memory_space=pltpu.VMEM)
    shape = jax.ShapeDtypeStruct

    def whole(shard):
        return shape((fsdp_count * shard.shape[0], shard.shape[1]), shard.dtype)

    return pl.pallas_call(
        functools.partial(forward_kernel, fsdp_count),
        out_shape=(
            shape((length, own_width), BF16),
            shape((pairs, 2, length), F32),
            shape((rows, heads * DH * 4), BF16),
            whole(w_out),
            whole(w_down),
            whole(w_in),
            shape(vec.shape, F32),
            shape((length, width), BF16),
            shape((full, own_width), BF16),
            shape((length, LANES), BF16),
            shape((length, LANES), BF16),
        ),
        in_specs=[anywhere] * 4 + [vmem] + [anywhere] * 3,
        out_specs=(anywhere, vmem, anywhere, anywhere, anywhere, anywhere, vmem, anywhere, anywhere, vmem, vmem),
        scratch_shapes=[
            pltpu.VMEM((length, width), BF16),
            pltpu.VMEM((length, width), BF16),
            pltpu.VMEM((full, own_width), BF16),
            pltpu.VMEM((fsdp_count * vec.shape[0], vec.shape[1]), BF16),
            pltpu.VMEM((4,) + seg.shape, jnp.int32),
            pltpu.VMEM((length, own_width), BF16),
            pltpu.VMEM((length, heads * DH), BF16),
            pltpu.VMEM((length, LANES), BF16),
            pltpu.VMEM((LANES, length), BF16),
        ]
        + Gather.scratch(depth) * 5
        + [dma(), dma(), dma(3), dma(2), dma(2), dma(2), dma(2), dma(3), dma(3)]
        + [dma(3 * pairs), dma(3 * pairs), dma(pairs)],
        compiler_params=pltpu.CompilerParams(
            collective_id=2, has_side_effects=True, vmem_limit_bytes=48 << 20
        ),
    )(x, w_qkv, vec, seg, mask, w_out, w_down, w_in)


def by_rows(count, body):
    lax.fori_loop(0, count // 16, lambda i, carry: (body(aligned(i * 16, 16)), carry)[1], 0)


class Reduce:
    def __init__(self, place, grad, out, quartered, bufs, sems):
        self.place, self.grad, self.out, self.quartered = place, grad, out, quartered
        self.rows, self.cols = out.shape
        self.wide = self.cols // 4
        self.acc, self.own, self.relay_in, self.quarter_in, self.z_in, self.total = bufs
        self.own_sem, self.put_sem, self.cs, self.rs, self.qs, self.zs, self.fs, self.gs = sems

    @staticmethod
    def scratch(depth, rows, cols, quartered):
        held = cols // 4 if quartered else cols
        side = (1, 1, 16, LANES) if quartered else None
        return [
            pltpu.VMEM((depth, rows, held), BF16),
            pltpu.VMEM((rows, held), BF16),
            pltpu.VMEM(side or (2, depth, rows, cols // 8), BF16),
            pltpu.VMEM(side or (2, depth, rows, cols // 4), BF16),
            pltpu.VMEM((depth, rows, cols // 4), BF16),
            pltpu.VMEM((rows, cols // 4), BF16),
            dma(),
            dma(),
        ] + [dma(depth)] * 12 + [dma(2)] * 4

    @staticmethod
    def take(place, grad, out, quartered, refs):
        s = refs[8:]
        pairs = [(s[i], s[i + 1]) for i in range(0, 16, 2)]
        sems = (refs[6], refs[7], pairs[0], pairs[1:3], pairs[3:5], pairs[5], pairs[6], pairs[7])
        return Reduce(place, grad, out, quartered, refs[:6], sems)

    def quarter(self, seat):
        return aligned(seat * self.wide, self.wide)

    def mine(self):
        return pl.ds(0, self.wide) if self.quartered else self.quarter(self.place.s)

    def piece(self, seat, half):
        return aligned(seat * self.wide + half * (self.wide // 2), self.wide // 2)

    def own_copy(self, step):
        p = self.place
        rows = aligned((2 * p.far(step) + p.c) * self.rows, self.rows)
        return pltpu.make_async_copy(self.grad.at[rows], self.own, self.own_sem)

    def core_copy(self, step):
        p = self.place
        rows = aligned((2 * p.far(step) + 1 - p.c) * self.rows, self.rows)
        return send(self.grad.at[rows], self.acc.at[step], self.cs, step, p.beside)

    def relay_copy(self, step, way):
        p = self.place
        src = self.acc.at[step, :, self.piece(p.s3, way)]
        return send(src, self.relay_in.at[way, step], self.rs[way], step, p.across(way))

    def quarter_copy(self, step, way):
        p = self.place
        src = self.acc.at[step, :, self.quarter((p.s1, p.s2)[way])]
        return send(src, self.quarter_in.at[way, step], self.qs[way], step, p.across(way))

    def z_copy(self, step):
        p = self.place
        src = self.acc.at[step, :, self.mine()]
        return send(src, self.z_in.at[step], self.zs, step, p.along(p.far(step)))

    def put_copy(self):
        return pltpu.make_async_copy(self.total, self.out.at[:, self.quarter(self.place.s)], self.put_sem)

    def total_copy(self, way):
        p = self.place
        return send(self.total, self.out.at[:, self.quarter(p.s)], self.fs, way, p.across(way))

    def total_arrival(self, way):
        p = self.place
        there = self.out.at[:, self.quarter((p.s1, p.s2)[way])]
        return send(there, there, self.fs, way, p.across(way))

    def back_copy(self, way):
        p = self.place
        there = self.out.at[:, self.piece((p.s2, p.s1)[way], 1 - way)]
        return send(there, there, self.gs, way, p.across(way))

    def back_arrival(self, way):
        p = self.place
        there = self.out.at[:, self.piece(p.s3, 1 - way)]
        return send(there, there, self.gs, way, p.across(way))

    def begin(self):
        depth = self.place.depth
        self.place.each(1, depth, lambda step: self.core_copy(step).start())
        self.core_copy(0).start()
        self.own_copy(1).start()

    def fold(self, step, following):
        self.core_copy(step).wait_recv()
        self.own_copy(step).wait()
        acc, own = self.acc, self.own

        def body(rows):
            acc[step, rows, :] = (acc[step, rows, :].astype(F32) + own[rows, :].astype(F32)).astype(BF16)

        by_rows(self.rows, body)
        if following is not None:
            self.own_copy(following).start()
        if not self.quartered:
            for way in (0, 1):
                self.relay_copy(step, way).start()
        elif not (isinstance(step, int) and step == 0):
            self.z_copy(step).start()

    def swap(self, step):
        if self.quartered:
            return
        p, acc = self.place, self.acc
        for way in (0, 1):
            self.relay_copy(step, way).wait_recv()
            cols = self.piece((p.s2, p.s1)[way], way)
            came = self.relay_in.at[way, step]

            def body(rows):
                acc[step, rows, cols] = (acc[step, rows, cols].astype(F32) + came[rows, :].astype(F32)).astype(BF16)

            by_rows(self.rows, body)
        for way in (0, 1):
            self.quarter_copy(step, way).start()

    def close(self, step, own):
        if self.quartered:
            return
        p, acc, came = self.place, self.acc, self.quarter_in
        for way in (0, 1):
            self.quarter_copy(step, way).wait_recv()
        cols = self.quarter(p.s)

        def body(rows):
            acc[step, rows, cols] = (
                acc[step, rows, cols].astype(F32)
                + came[0, step, rows, :].astype(F32)
                + came[1, step, rows, :].astype(F32)
            ).astype(BF16)

        by_rows(self.rows, body)
        if not own:
            self.z_copy(step).start()

    def collect(self):
        p, acc, came, total = self.place, self.acc, self.z_in, self.total
        p.each(1, p.depth, lambda step: self.z_copy(step).wait_recv())
        cols = self.mine()

        def body(rows):
            start = acc[0, rows, cols].astype(F32)
            if p.depth <= 8:
                for step in range(1, p.depth):
                    start = start + came[step, rows, :].astype(F32)
            else:
                start = lax.fori_loop(1, p.depth, lambda step, sofar: sofar + came[step, rows, :].astype(F32), start)
            total[rows, :] = start.astype(BF16)

        by_rows(self.rows, body)
        for way in (0, 1):
            self.total_copy(way).start()
        self.put_copy().start()

    def spread(self):
        for way in (0, 1):
            self.total_arrival(way).wait_recv()
        for way in (0, 1):
            self.back_copy(way).start()

    def finish(self):
        for way in (0, 1):
            self.back_arrival(way).wait_recv()
        self.put_copy().wait()

        def done(step):
            self.core_copy(step).wait_send()
            if not self.quartered:
                for way in (0, 1):
                    self.relay_copy(step, way).wait_send()
                    self.quarter_copy(step, way).wait_send()

        self.place.each(0, self.place.depth, done)
        self.place.each(1, self.place.depth, lambda step: self.z_copy(step).wait_send())
        for way in (0, 1):
            self.total_copy(way).wait_send()
            self.back_copy(way).wait_send()


REDUCE_REFS = 24


def reduce_steps(place, reduces, between):
    depth = place.depth
    work = list(between)

    def gap():
        if work:
            work.pop(0)()

    if depth <= 8:
        order = [(t + 1) % depth for t in range(depth)]
        for t in range(depth + 2):
            for one in reduces:
                if t < depth:
                    one.fold(order[t], order[t + 1] if t + 1 < depth else None)
                if 0 <= t - 1 < depth:
                    one.swap(order[t - 1])
                if 0 <= t - 2 < depth:
                    one.close(order[t - 2], order[t - 2] == 0)
                gap()
    else:
        def run(first, last, body):
            lax.fori_loop(first, last, lambda step, carry: (body(step), carry)[1], 0)

        for one in reduces:
            run(1, depth, lambda step: one.fold(step, lax.rem(step + 1, depth)))
            one.fold(0, None)
            run(0, depth, one.swap)
            run(1, depth, lambda step: one.close(step, False))
            one.close(0, True)
    for rest in work:
        rest()


def backward_unit(
    pair, odd, half, tile, heads_ref, mask_ref, qd_ref, kf_ref, go_ref, lse_ref, out_ref, keys_sc, values_sc, keys_t, p_sc, s_sc, k_acc, v_acc
):
    length = heads_ref.shape[0]
    span = p_sc.shape[1]
    scale = jnp.asarray(1.0 / math.sqrt(DH), BF16)
    q_cols, k_cols, v_cols = (pl.ds((3 * pair + i) * LANES, LANES) for i in range(3))
    cols = pl.ds(pair * LANES, LANES)
    mine = own_lanes(odd, (length, LANES))
    if half == 0:
        keys_sc[...] = jnp.where(mine, heads_ref[:, k_cols], kf_ref[...])
        values_sc[...] = jnp.where(mine, heads_ref[:, v_cols], jnp.zeros((), BF16))
        if not odd:
            keys_t[...] = heads_ref[:, k_cols].T

    def one_tile(index, carry):
        here = aligned(index * tile, tile)
        rows = aligned(half * span + index * tile, tile)
        lanes = own_lanes(odd, (tile, LANES))
        queries = query_tile(
            heads_ref[rows, q_cols],
            qd_ref[rows, :],
            mask_ref,
            2 * pair + odd,
            half * (span // BLK) + index * (tile // BLK),
            lanes,
        )
        prob = jnp.exp(dot_nt(keys_sc[...], queries) - lse_ref[pair, pl.ds(odd, 1), rows])
        grad_prob = dot_nt(values_sc[...], go_ref[rows, cols])
        delta = jnp.sum(prob * grad_prob, axis=0, keepdims=True)
        p_sc[:, here] = prob.astype(BF16)
        s_sc[:, here] = (prob * (grad_prob - delta)).astype(BF16)
        return carry

    lax.fori_loop(0, span // tile, one_tile, 0)
    part = pl.ds(half * span, span)
    grad_v = dot_nn(p_sc[...], go_ref[part, cols])
    grad_k = dot_nn(s_sc[...], heads_ref[part, q_cols] * scale)
    grad_q = (dot_nn(keys_t[...], s_sc[...]) * (1.0 / math.sqrt(DH))).T.astype(BF16)
    last = half * span + span == length

    def put(rows, columns, value, keep):
        if odd:
            value = jnp.where(keep, value, out_ref[rows, columns])
        out_ref[rows, columns] = value

    put(part, q_cols, grad_q, own_lanes(odd, (span, LANES)))
    if half > 0:
        grad_v, grad_k = grad_v + v_acc[...], grad_k + k_acc[...]
    if last:
        put(pl.ds(0, length), k_cols, grad_k.astype(BF16), mine)
        put(pl.ds(0, length), v_cols, grad_v.astype(BF16), mine)
    else:
        v_acc[...], k_acc[...] = grad_v, grad_k


def backward_kernel(
    fsdp_count,
    go_rows_ref,
    heads_ref,
    mask_ref,
    qd_ref,
    kf_ref,
    lse_ref,
    n1_ref,
    wq_ref,
    x_ref,
    hid_ref,
    vec_ref,
    small_ref,
    out_g_ref,
    down_g_ref,
    in_g_ref,
    tokens_out,
    small_out,
    qkv_total,
    out_total,
    down_total,
    in_total,
    go_sc,
    grads_sc,
    keys_sc,
    values_sc,
    keys_t,
    p_sc,
    s_sc,
    k_acc,
    v_acc,
    n1_sc,
    qkv_g,
    part_sc,
    part_in,
    half_in,
    small_sc,
    small_in,
    *rest,
):
    place = Place(fsdp_count)
    rows = go_rows_ref.shape[0]
    reduces = [
        Reduce.take(place, grad, out, False, rest[i * REDUCE_REFS : (i + 1) * REDUCE_REFS])
        for i, (grad, out) in enumerate(
            ((out_g_ref, out_total), (in_g_ref, in_total), (down_g_ref, down_total))
        )
    ]
    first = Reduce.take(place, qkv_g, qkv_total, True, rest[3 * REDUCE_REFS : 4 * REDUCE_REFS])
    g_own, n_own, g_sent, g_got, h_sent, h_got, p_sent, p_got, c_sent, c_got, z_sent, z_got, x_sent, x_got = rest[
        4 * REDUCE_REFS :
    ]
    seats = (place.s1, place.s2, place.s3)
    width = go_sc.shape[1]
    pairs = width // LANES
    half = rows // 2

    def part(seat):
        return go_rows_ref.at[:, aligned(seat * width, width)]

    def slot(seat):
        return go_sc.at[aligned(seat * rows, rows)]

    place.meet()
    for way in range(3):
        send(part(seats[way]), slot(place.s), (g_sent, g_got), way, place.across(way)).start()
    own = pltpu.make_async_copy(part(place.s), slot(place.s), g_own)
    own.start()
    for one in reduces:
        one.begin()
    n1_copy = pltpu.make_async_copy(n1_ref, n1_sc, n_own)
    n1_copy.start()
    own.wait()
    for way in range(3):
        send(slot(seats[way]), slot(seats[way]), (g_sent, g_got), way, place.across(way)).wait_recv()

    def unit(pair, odd, side):
        backward_unit(
            pair, odd, side, 256, heads_ref, mask_ref, qd_ref, kf_ref, go_sc, lse_ref, grads_sc,
            keys_sc, values_sc, keys_t, p_sc, s_sc, k_acc, v_acc,
        )

    def half_copy(way):
        src = part_sc.at[aligned(place.s3 * rows + way * half, half)]
        return send(src, half_in.at[way], (h_sent, h_got), way, place.across(way))

    def part_copy(way):
        src = part_sc.at[aligned(seats[way] * rows, rows)]
        return send(src, part_in.at[way], (p_sent, p_got), way, place.across(way))

    def partial_dn1():
        def body(index):
            here = aligned(index * rows, rows)
            part_sc[here, :] = dot_nt(grads_sc[here, :], wq_ref[...]).astype(BF16)

        lax.fori_loop(0, 4, lambda index, carry: (body(index), carry)[1], 0)
        for way in (0, 1):
            half_copy(way).start()

    def weight_grad():
        n1_copy.wait()

        def body(index):
            cols = aligned(index * 256, 256)
            qkv_g[cols, :] = dot_tn(n1_sc[:, cols], grads_sc[...]).astype(BF16)

        lax.fori_loop(0, qkv_g.shape[0] // 256, lambda index, carry: (body(index), carry)[1], 0)
        first.begin()

    def swap_dn1():
        for way in (0, 1):
            half_copy(way).wait_recv()
            base = (place.s2, place.s1)[way] * rows + way * half

            def body(index):
                here = aligned(base + index * 32, 32)
                came = half_in[way, aligned(index * 32, 32), :]
                part_sc[here, :] = (part_sc[here, :].astype(F32) + came.astype(F32)).astype(BF16)

            lax.fori_loop(0, half // 32, lambda index, carry: (body(index), carry)[1], 0)
        for way in (0, 1):
            part_copy(way).start()

    def fold_first():
        depth = place.depth
        place.each(1, depth, lambda step: first.fold(step, lax.rem(step + 1, depth)))
        first.fold(0, None)

    def core_small():
        return send(small_sc.at[0], small_sc.at[1], (c_sent, c_got), 0, place.beside)

    def z_small(step):
        return send(small_sc.at[2], small_in.at[step], (z_sent, z_got), step, place.along(place.far(step)))

    def x_small(way):
        return send(small_sc.at[3], small_sc.at[4 + way], (x_sent, x_got), way, place.across(way))

    def close_dn1():
        for way in (0, 1):
            part_copy(way).wait_recv()
        gain = vec_ref[0:1, :]

        def body(index, sums):
            here = aligned(index * 32, 32)
            mine = aligned(place.s * rows + index * 32, 32)
            dn1 = (
                part_sc[mine, :].astype(F32)
                + part_in[0, here, :].astype(F32)
                + part_in[1, here, :].astype(F32)
            )
            token_rows = x_ref[here, :].astype(F32)
            center = token_rows - jnp.mean(token_rows, axis=-1, keepdims=True)
            inv = lax.rsqrt(jnp.mean(center * center, axis=-1, keepdims=True) + 1e-05)
            hat = center * inv
            scaled = dn1 * gain
            grad = hid_ref[here, :] + inv * (
                scaled
                - jnp.mean(scaled, axis=-1, keepdims=True)
                - hat * jnp.mean(scaled * hat, axis=-1, keepdims=True)
            )
            tokens_out[here, :] = grad.astype(BF16)
            return (
                sums[0] + jnp.sum(dn1 * hat, axis=0, keepdims=True),
                sums[1] + jnp.sum(dn1, axis=0, keepdims=True),
            )

        none = jnp.zeros((1, x_ref.shape[1]), F32)
        gain_sum, bias_sum = lax.fori_loop(0, rows // 32, body, (none, none))
        small_sc[0] = small_ref[...]
        small_sc[0, 0:1, :] = gain_sum
        small_sc[0, 1:2, :] = bias_sum
        core_small().start()

    def small_z():
        core_small().wait_recv()
        small_sc[2] = small_sc[0] + small_sc[1]
        place.each(1, place.depth, lambda step: z_small(step).start())

    def small_x():
        place.each(1, place.depth, lambda step: z_small(step).wait_recv())
        small_in[0] = small_sc[2]
        if place.depth <= 8:
            total = small_in[place.back(0)]
            for z in range(1, place.depth):
                total = total + small_in[place.back(z)]
        else:
            total = lax.fori_loop(
                1, place.depth, lambda z, sofar: sofar + small_in[place.back(z)], small_in[place.back(0)]
            )
        small_sc[3] = total
        for way in range(3):
            x_small(way).start()

    def small_end():
        for way in range(3):
            x_small(way).wait_recv()
        small_out[...] = (small_sc[3] + small_sc[4]) + (small_sc[5] + small_sc[6])

    units = [
        functools.partial(unit, pair, odd, side) for pair in range(pairs) for odd in (0, 1) for side in (0, 1)
    ]
    reduce_steps(
        place,
        reduces,
        units + [partial_dn1, weight_grad, swap_dn1, fold_first, close_dn1, small_z],
    )
    for one in [first] + reduces:
        one.collect()
    small_x()
    for one in [first] + reduces:
        one.spread()
    small_end()
    core_small().wait_send()
    place.each(1, place.depth, lambda step: z_small(step).wait_send())
    for way in range(3):
        send(part(seats[way]), slot(place.s), (g_sent, g_got), way, place.across(way)).wait_send()
        x_small(way).wait_send()
        if way < 2:
            half_copy(way).wait_send()
            part_copy(way).wait_send()
    for one in [first] + reduces:
        one.finish()


def backward_attention(fsdp_count, grad_att, saved, x, hid, small, grads):
    heads, mask, qd, kf, lse, n1, wq, vec = saved
    rows, width = grad_att.shape
    length = heads.shape[0]
    own_width = width // 4
    depth = fsdp_count // 2
    span = length // 2
    anywhere = pl.BlockSpec(memory_space=pl.ANY)
    vmem = pl.BlockSpec(memory_space=pltpu.VMEM)
    share = wq.shape[0] // fsdp_count
    kept = [(grad.shape[0] // fsdp_count, grad.shape[1]) for grad in grads]
    kept_qkv = (share, 4 * wq.shape[1])
    shape = jax.ShapeDtypeStruct

    reduce_scratch = []
    for one in (kept[0], kept[2], kept[1]):
        reduce_scratch += Reduce.scratch(depth, *one, False)
    reduce_scratch += Reduce.scratch(depth, *kept_qkv, True)
    return pl.pallas_call(
        functools.partial(backward_kernel, fsdp_count),
        out_shape=(shape(x.shape, BF16), shape(small.shape, F32), shape(kept_qkv, BF16))
        + tuple(shape(one, BF16) for one in kept),
        in_specs=[anywhere] + [vmem] * 5 + [anywhere] + [vmem] * 5 + [anywhere] * 3,
        out_specs=(vmem, vmem, anywhere, anywhere, anywhere, anywhere),
        scratch_shapes=[
            pltpu.VMEM((length, own_width), BF16),
            pltpu.VMEM((length, 3 * own_width), BF16),
            pltpu.VMEM((length, LANES), BF16),
            pltpu.VMEM((length, LANES), BF16),
            pltpu.VMEM((LANES, length), BF16),
            pltpu.VMEM((length, span), BF16),
            pltpu.VMEM((length, span), BF16),
            pltpu.VMEM((length, LANES), F32),
            pltpu.VMEM((length, LANES), F32),
            pltpu.VMEM((length, width), BF16),
            pltpu.VMEM(wq.shape, BF16),
            pltpu.VMEM((length, width), BF16),
            pltpu.VMEM((2, rows, width), BF16),
            pltpu.VMEM((2, rows // 2, width), BF16),
            pltpu.VMEM((7,) + small.shape, F32),
            pltpu.VMEM((depth,) + small.shape, F32),
        ]
        + reduce_scratch
        + [dma(), dma(), dma(3), dma(3), dma(2), dma(2), dma(2), dma(2)]
        + [dma(1), dma(1), dma(depth), dma(depth), dma(3), dma(3)],
        compiler_params=pltpu.CompilerParams(
            collective_id=3, has_side_effects=True, vmem_limit_bytes=60 << 20
        ),
    )(grad_att, heads, mask, qd, kf, lse, n1, wq, x, hid, vec, small, *grads)


def swap_thirds(rows, outer, inner):
    count, width = rows.shape
    return rows.reshape(count, outer, inner, width // (outer * inner)).swapaxes(1, 2).reshape(count, width)


def per_device(
    seq_count,
    fsdp_count,
    tokens,
    segment_ids,
    random_blocks,
    ln1_gain,
    ln1_bias,
    w_qkv,
    w_out,
    ln2_gain,
    ln2_bias,
    w_in,
    b_in,
    w_down,
    b_down,
    cotangent,
):
    groups = w_qkv.shape[1] // (3 * LANES)
    width = tokens.shape[2]
    share = ln1_gain.shape[0]
    position = lax.axis_index("fsdp")

    def placed(vector):
        held = vector.shape[0]
        spread = jnp.tile(vector, fsdp_count).reshape(-1, width)
        owner = jnp.arange(fsdp_count * held, dtype=jnp.int32).reshape(-1, width) // held
        return jnp.where(owner == position, spread, jnp.zeros((), BF16))

    vec = jnp.concatenate(
        [placed(v) for v in (ln1_gain, ln1_bias, ln2_gain, ln2_bias, b_down, b_in)], axis=0
    )
    vec = jnp.pad(vec, ((0, -vec.shape[0] % 16), (0, 0)))
    tok_count = segment_ids.shape[1]
    seg_rows = -(-tok_count // (8 * LANES)) * 8
    seg = jnp.pad(segment_ids[0], (0, seg_rows * LANES - tok_count)).reshape(seg_rows, LANES)
    mask = block_mask(random_blocks)
    by_heads, lse, att_rows, out_weight, down_weight, in_weight, vec, normed_one, own_qkv, query_docs, key_feats = (
        forward_attention(
            fsdp_count, tokens[0], swap_thirds(w_qkv, 3, groups), vec, seg, mask, w_out, w_down, w_in
        )
    )
    gain_two, bias_two, down_bias, in_bias = vec[2], vec[3], vec[4], vec[5 : 5 + in_weight.shape[1] // width].reshape(-1)
    token_rows = tokens[0].astype(F32)
    hidden = token_rows + dot_nn(att_rows, out_weight)
    hat_two, inv_two = layer_norm_parts(hidden)
    normed_two = (hat_two * gain_two + bias_two).astype(BF16)
    pre_act = dot_nn(normed_two, in_weight) + in_bias
    act_value, pull_gelu = jax.vjp(gelu_tanh, pre_act)
    act_low = act_value.astype(BF16)
    result = hidden + dot_nn(act_low, down_weight) + down_bias

    cot_low = cotangent[0]
    cot_rows = cot_low.astype(F32)
    grad_pre = pull_gelu(dot_nt(cot_low, down_weight))[0].astype(BF16)
    grad_norm_two = dot_nt(grad_pre, in_weight)
    scaled = grad_norm_two * gain_two
    grad_hidden = cot_rows + inv_two * (
        scaled
        - jnp.mean(scaled, axis=-1, keepdims=True)
        - hat_two * jnp.mean(scaled * hat_two, axis=-1, keepdims=True)
    )
    hidden_low = grad_hidden.astype(BF16)
    grad_att = dot_nt(hidden_low, out_weight).astype(BF16)
    small = jnp.concatenate(
        [
            jnp.zeros((2, width), F32),
            jnp.sum(grad_norm_two * hat_two, axis=0)[None],
            jnp.sum(grad_norm_two, axis=0)[None],
            jnp.sum(cot_rows, axis=0)[None],
            jnp.sum(grad_pre.astype(F32), axis=0).reshape(-1, width),
        ],
        axis=0,
    )
    small = jnp.pad(small, ((0, vec.shape[0] - small.shape[0]), (0, 0)))
    grad_tokens, small, total_qkv, total_out, total_down, total_in = backward_attention(
        fsdp_count,
        grad_att,
        (by_heads, mask, query_docs, key_feats, lse, normed_one, own_qkv, vec),
        tokens[0],
        grad_hidden,
        small,
        (
            dot_tn(att_rows, hidden_low).astype(BF16),
            dot_tn(act_low, cot_low).astype(BF16),
            dot_tn(normed_two, grad_pre).astype(BF16),
        ),
    )
    parts = [lax.dynamic_slice_in_dim(small[i], position * share, share) for i in range(5)]
    held = b_in.shape[0]
    parts.append(lax.dynamic_slice_in_dim(small[5 : 5 + fsdp_count * held // width].reshape(-1), position * held, held))
    return (
        result.astype(BF16)[None],
        grad_tokens[None],
        parts[0],
        parts[1],
        swap_thirds(total_qkv, groups, 3).astype(F32),
        total_out.astype(F32),
        parts[2],
        parts[3],
        total_in.astype(F32),
        parts[5],
        total_down.astype(F32),
        parts[4],
    )


def solution(mesh):
    return jax.shard_map(
        functools.partial(per_device, mesh.shape["seq"], mesh.shape["fsdp"]),
        mesh=mesh,
        in_specs=(
            P("fsdp", "seq", None),
            P("fsdp", "seq"),
            P("seq", None, None),
            P("fsdp"),
            P("fsdp"),
            P("fsdp", None),
            P("fsdp", None),
            P("fsdp"),
            P("fsdp"),
            P("fsdp", None),
            P("fsdp"),
            P("fsdp", None),
            P("fsdp"),
            P("fsdp", "seq", None),
        ),
        out_specs=(
            P("fsdp", "seq", None),
            P("fsdp", "seq", None),
            P("fsdp"),
            P("fsdp"),
            P("fsdp", None),
            P("fsdp", None),
            P("fsdp"),
            P("fsdp"),
            P("fsdp", None),
            P("fsdp"),
            P("fsdp", None),
            P("fsdp"),
        ),
        check_vma=False,
    )
```

```python
import functools
import math

import jax
import jax.numpy as jnp
from jax import lax
from jax.experimental import pallas as pl
from jax.experimental.pallas import tpu as pltpu
from jax.sharding import PartitionSpec as P

DH = 64
BLK = 64
LANES = 128
NEG = -1e30
F32 = jnp.float32
BF16 = jnp.bfloat16


def layer_norm_parts(rows):
    center = rows - jnp.mean(rows, axis=-1, keepdims=True)
    variance = jnp.mean(center * center, axis=-1, keepdims=True)
    inv = lax.rsqrt(variance + 1e-05)
    return center * inv, inv


def gelu_tanh(pre_act):
    return (
        0.5
        * pre_act
        * (1.0 + jnp.tanh(0.7978845608028654 * (pre_act + 0.044715 * pre_act * pre_act * pre_act)))
    )


def dot_nn(a, b):
    return jnp.dot(a, b, preferred_element_type=F32)


def dot_nt(a, b):
    return lax.dot_general(a, b, (((1,), (1,)), ((), ())), preferred_element_type=F32)


def dot_tn(a, b):
    return lax.dot_general(a, b, (((0,), (0,)), ((), ())), preferred_element_type=F32)


DOCS = 6


def block_mask(random_blocks):
    heads, inner, _ = random_blocks.shape
    blocks = inner + 2
    ids = jnp.arange(blocks, dtype=jnp.int32)
    near = jnp.abs(ids[:, None] - ids[None, :]) <= 1
    edge = (ids == 0) | (ids == blocks - 1)
    fixed = near | edge[:, None] | edge[None, :]
    picked = jnp.any(random_blocks[:, :, :, None] == ids, axis=2)
    used = fixed[None] | jnp.pad(picked, ((0, 0), (1, 1), (0, 0)))
    row = jnp.pad(jnp.where(used, 0.0, NEG), ((0, 0), (0, 0), (0, DH - blocks)))
    return jnp.concatenate([row, row], axis=-1)


def token_features(start, docs, blocks):
    shape = (docs.shape[0], LANES)
    lane = lax.rem(lax.broadcasted_iota(jnp.int32, shape, 1), DH)
    block = lax.div(lax.broadcasted_iota(jnp.int32, shape, 0) + start, BLK)
    own = docs + blocks == lane
    other = jnp.where(own | (lane >= blocks + DOCS), 0.0, 1.0)
    key_part = jnp.where(lane < blocks, jnp.where(block == lane, 1.0, 0.0), other)
    return jnp.where(own, NEG, 0.0).astype(BF16), key_part.astype(BF16)


def query_tile(q_tile, doc_tile, mask_ref, head, first_block, lanes):
    scale = jnp.asarray(1.0 / math.sqrt(DH), BF16)
    count = q_tile.shape[0] // BLK
    mask = jnp.concatenate(
        [jnp.broadcast_to(mask_ref[head, pl.ds(first_block + i, 1), :], (BLK, LANES)) for i in range(count)], axis=0
    )
    return jnp.where(lanes, q_tile * scale, doc_tile + mask.astype(BF16))


def own_lanes(odd, shape):
    lane = lax.broadcasted_iota(jnp.int32, shape, 1)
    return (lane >= DH) if odd else (lane < DH)


MESH = pl.DeviceIdType.MESH


class Place:
    def __init__(self, fsdp_count):
        self.depth = fsdp_count // 2
        self.s = lax.axis_index("seq")
        self.f = lax.axis_index("fsdp")
        self.z = lax.div(self.f, 2)
        self.c = lax.rem(self.f, 2)
        self.s1 = self.s + 1 - 2 * lax.rem(self.s, 2)
        self.s2 = self.s + 2 - 4 * lax.div(self.s, 2)
        self.s3 = 3 - self.s
        self.beside = (self.s, self.f + 1 - 2 * self.c)

    def across(self, index):
        return ((self.s1, self.s2, self.s3)[index], self.f)

    def far(self, step):
        return lax.rem(self.z + step, self.depth)

    def back(self, step):
        return lax.rem(self.z + self.depth - step, self.depth)

    def along(self, z):
        return (self.s, 2 * z + self.c)

    def meet(self):
        barrier = pltpu.get_barrier_semaphore()
        peers = [self.beside] + [self.across(i) for i in range(3)]
        for peer in peers:
            pl.semaphore_signal(barrier, inc=1, device_id=peer, device_id_type=MESH)
        self.each(1, self.depth, lambda step: pl.semaphore_signal(
            barrier, inc=1, device_id=self.along(self.far(step)), device_id_type=MESH
        ))
        pl.semaphore_wait(barrier, len(peers) + self.depth - 1)

    def each(self, start, stop, body):
        if stop - start <= 8:
            for step in range(start, stop):
                body(step)
        else:
            lax.fori_loop(start, stop, lambda step, carry: (body(step), carry)[1], 0)


def send(src, dst, sems, index, device):
    sent, got = sems
    return pltpu.make_async_remote_copy(
        src_ref=src,
        dst_ref=dst,
        send_sem=sent.at[index],
        recv_sem=got.at[index],
        device_id=device,
        device_id_type=MESH,
    )


def aligned(start, size):
    return pl.ds(pl.multiple_of(start, size), size)


class Gather:
    def __init__(self, place, src, dst, split, sems):
        self.place, self.src, self.dst, self.split = place, src, dst, split
        self.rows, self.cols = src.shape
        self.local, self.zs, self.xs, self.rs, self.cs = sems

    def block(self, z, core, quarter=None, half=None):
        rows = aligned((2 * z + core) * self.rows, self.rows)
        if quarter is None:
            return self.dst.at[rows]
        wide = self.cols // 4
        if half is None:
            return self.dst.at[rows, aligned(quarter * wide, wide)]
        return self.dst.at[rows, aligned(quarter * wide + half * (wide // 2), wide // 2)]

    def source(self, step, side):
        return self.place.z - step if side == 0 else self.place.z + step

    def has(self, step, side):
        z = self.source(step, side)
        return z >= 0 if side == 0 else z < self.place.depth

    def sends(self, step, side):
        p = self.place
        onward = p.z + 1 < p.depth if side == 0 else p.z > 0
        return jnp.logical_and(self.has(step - 1, side), onward)

    def slot(self, step, side):
        return 2 * step + side

    def own_copy(self):
        return pltpu.make_async_copy(self.src, self.block(self.place.z, self.place.c), self.local)

    def own_core(self):
        p = self.place
        return send(self.src, self.block(p.z, p.c), self.cs, 0, p.beside)

    def own_arrival(self):
        p = self.place
        there = self.block(p.z, 1 - p.c)
        return send(there, there, self.cs, 0, p.beside)

    def core_copy(self, step, side):
        p = self.place
        there = self.block(self.source(step, side), p.c)
        return send(there, there, self.cs, self.slot(step, side), p.beside)

    def core_arrival(self, step, side):
        p = self.place
        there = self.block(self.source(step, side), 1 - p.c)
        return send(there, there, self.cs, self.slot(step, side), p.beside)

    def z_copy(self, step, side):
        p = self.place
        z = self.source(step - 1, side)
        there = self.block(z, p.c, p.s) if self.split else self.block(z, p.c)
        src = there
        if isinstance(step, int) and step == 1:
            wide = self.cols // 4
            src = self.src.at[:, aligned(p.s * wide, wide)] if self.split else self.src
        return send(src, there, self.zs, self.slot(step, side), p.along(p.z + 1 - 2 * side))

    def z_arrival(self, step, side):
        p = self.place
        z = self.source(step, side)
        there = self.block(z, p.c, p.s) if self.split else self.block(z, p.c)
        return send(there, there, self.zs, self.slot(step, side), p.along(p.z - 1 + 2 * side))

    def x_copy(self, step, side, way):
        p = self.place
        there = self.block(self.source(step, side), p.c, p.s)
        return send(there, there, self.xs[way], self.slot(step, side), p.across(way))

    def x_arrival(self, step, side, way):
        p = self.place
        there = self.block(self.source(step, side), p.c, (p.s1, p.s2)[way])
        return send(there, there, self.xs[way], self.slot(step, side), p.across(way))

    def relay_copy(self, step, side, way):
        p = self.place
        there = self.block(self.source(step, side), p.c, (p.s2, p.s1)[way], 1 - way)
        return send(there, there, self.rs[way], self.slot(step, side), p.across(way))

    def relay_arrival(self, step, side, way):
        p = self.place
        there = self.block(self.source(step, side), p.c, p.s3, 1 - way)
        return send(there, there, self.rs[way], self.slot(step, side), p.across(way))

    def both(self, step, body, test=None):
        for side in (0, 1):
            pl.when((test or self.has)(step, side))(functools.partial(body, step, side))

    def begin(self):
        self.both(1, lambda step, side: self.z_copy(step, side).start(), self.sends)
        self.own_copy().start()
        self.own_core().start()

    def swap(self, step):
        def body(step, side):
            self.z_arrival(step, side).wait_recv()
            pl.when(self.sends(step + 1, side))(lambda: self.z_copy(step + 1, side).start())
            if self.split:
                for way in (0, 1):
                    self.x_copy(step, side, way).start()
            else:
                self.core_copy(step, side).start()

        self.both(step, body)

    def relay(self, step):
        def body(step, side):
            for way in (0, 1):
                self.x_arrival(step, side, way).wait_recv()
            for way in (0, 1):
                self.relay_copy(step, side, way).start()

        if self.split:
            self.both(step, body)

    def share(self, step):
        def body(step, side):
            for way in (0, 1):
                self.relay_arrival(step, side, way).wait_recv()
            self.core_copy(step, side).start()

        if self.split:
            self.both(step, body)

    def finish(self):
        self.own_copy().wait()
        self.own_core().wait_send()
        self.own_arrival().wait_recv()

        def close(step, side):
            if self.split:
                for way in (0, 1):
                    self.x_copy(step, side, way).wait_send()
                    self.relay_copy(step, side, way).wait_send()
            self.core_copy(step, side).wait_send()
            self.core_arrival(step, side).wait_recv()

        self.place.each(1, self.place.depth, lambda step: self.both(step, close))
        self.place.each(
            1,
            self.place.depth,
            lambda step: self.both(step, lambda step, side: self.z_copy(step, side).wait_send(), self.sends),
        )

    @staticmethod
    def scratch(depth, split):
        held = 2 * depth if split else 1
        return [dma()] + [dma(2 * depth)] * 2 + [dma(held)] * 8 + [dma(2 * depth)] * 2

    @staticmethod
    def take(refs):
        pairs = [(refs[i], refs[i + 1]) for i in range(1, 13, 2)]
        return (refs[0], pairs[0], pairs[1:3], pairs[3:5], pairs[5])


GATHER_SEMS = 13


def gather_steps(place, gathers, late, between):
    depth = place.depth
    work = list(between)

    def gap():
        if work:
            work.pop(0)()

    def stage(step, swap, relay, share, gap):
        if swap:
            for one in gathers:
                one.swap(step)
        if relay:
            for one in gathers:
                one.relay(step - 1)
            gap()
        if swap:
            for one in late:
                one.swap(step - 1)
        if share:
            for one in gathers:
                one.share(step - 2)

    for one in late:
        one.begin()
    gap()
    if depth <= 8:
        for step in range(2, depth + 2):
            stage(step, step < depth, step <= depth, step >= 3, gap)
    else:
        stage(2, True, True, False, gap)
        lax.fori_loop(3, depth, lambda step, carry: (stage(step, True, True, True, lambda: None), carry)[1], 0)
        stage(depth, False, True, True, gap)
        stage(depth + 1, False, False, True, gap)
    for one in late:
        one.swap(depth - 1)
    for rest in work:
        rest()


def dma(*shape):
    return pltpu.SemaphoreType.DMA(shape) if shape else pltpu.SemaphoreType.DMA


def attend_unit(pair, odd, tile, heads_ref, mask_ref, qd_ref, kf_ref, keys_sc, values_t, out_ref, lse_ref):
    length = heads_ref.shape[0]
    cols = pl.ds(pair * LANES, LANES)
    q_cols, k_cols, v_cols = (pl.ds((3 * pair + i) * LANES, LANES) for i in range(3))
    if not odd:
        values_t[...] = heads_ref[:, v_cols].T
    mine = own_lanes(odd, (length, LANES))
    keys_sc[...] = jnp.where(mine, heads_ref[:, k_cols], kf_ref[...])

    def one_tile(index, carry):
        rows = aligned(index * tile, tile)
        lanes = own_lanes(odd, (tile, LANES))
        queries = query_tile(
            heads_ref[rows, q_cols], qd_ref[rows, :], mask_ref, 2 * pair + odd, index * (tile // BLK), lanes
        )
        scores = dot_nt(keys_sc[...], queries)
        top = jnp.max(scores, axis=0, keepdims=True)
        prob = jnp.exp(scores - top)
        total = jnp.sum(prob, axis=0, keepdims=True)
        mixed = dot_nn(values_t[...], prob.astype(BF16)) / total
        lse_ref[pair, pl.ds(odd, 1), rows] = top + jnp.log(total)
        result = mixed.T.astype(BF16)
        if odd:
            out_ref[rows, cols] = jnp.where(lanes, result, out_ref[rows, cols])
        else:
            out_ref[rows, cols] = result
        return carry

    lax.fori_loop(0, length // tile, one_tile, 0, unroll=2)


def forward_kernel(
    fsdp_count,
    x_ref,
    wq_ref,
    vec_ref,
    seg_ref,
    mask_ref,
    out_w_ref,
    down_w_ref,
    in_w_ref,
    heads_all,
    lse_ref,
    att_all,
    out_w_all,
    down_w_all,
    in_w_all,
    vec_sum,
    n1_all,
    wq_all,
    qd_ref,
    kf_ref,
    x_sc,
    n1_sc,
    wq_sc,
    vec_sc,
    seg_sc,
    heads_sc,
    att_sc,
    keys_sc,
    values_t,
    *sems,
):
    place = Place(fsdp_count)
    rows, width = x_ref.shape
    own_width = wq_sc.shape[1]
    seats = (place.s1, place.s2, place.s3)

    def taken(i):
        return Gather.take(sems[i * GATHER_SEMS : (i + 1) * GATHER_SEMS])

    lone = pl.ds(0, in_w_ref.shape[1] // 2)
    shared = pl.ds(in_w_ref.shape[1] // 2, in_w_ref.shape[1] // 2)
    gathers = [
        Gather(place, src, dst, split, taken(i))
        for i, (src, dst, split) in enumerate(
            (
                (out_w_ref, out_w_all, True),
                (in_w_ref.at[:, shared], in_w_all.at[:, shared], True),
                (down_w_ref, down_w_all, True),
                (in_w_ref.at[:, lone], in_w_all.at[:, lone], False),
            )
        )
    ]
    late = [gathers.pop()]
    weight = Gather(place, wq_ref.at[:, aligned(place.s * own_width, own_width)], wq_sc, False, taken(4))
    vector = Gather(place, vec_ref, vec_sc, False, taken(5))
    x_own, seg_own, keep_sems, x_sent, x_got, r_sent, r_got, g_sent, g_got, a_sent, a_got, a_own = sems[6 * GATHER_SEMS :]
    half = rows // 2

    def x_rows(seat):
        return x_sc.at[aligned(seat * rows, rows)]

    def x_half(seat, part):
        return x_sc.at[aligned(seat * rows + part * half, half)]

    def x_copy(way):
        return send(x_ref, x_rows(place.s), (x_sent, x_got), way, place.across(way))

    def x_arrival(way):
        there = x_rows(seats[way])
        return send(there, there, (x_sent, x_got), way, place.across(way))

    def x_relay(way):
        there = x_half((place.s2, place.s1)[way], 1 - way)
        return send(there, there, (r_sent, r_got), way, place.across(way))

    def x_relayed(way):
        there = x_half(place.s3, 1 - way)
        return send(there, there, (r_sent, r_got), way, place.across(way))

    def seg_copy(way):
        return send(seg_ref, seg_sc.at[place.s], (g_sent, g_got), way, place.across(way))

    def seg_arrival(way):
        there = seg_sc.at[seats[way]]
        return send(there, there, (g_sent, g_got), way, place.across(way))

    place.meet()
    vector.begin()
    weight.begin()
    for way in range(2):
        x_copy(way).start()
    for way in range(3):
        seg_copy(way).start()
    own_x = pltpu.make_async_copy(x_ref, x_rows(place.s), x_own)
    own_x.start()
    own_seg = pltpu.make_async_copy(seg_ref, seg_sc.at[place.s], seg_own)
    own_seg.start()
    def start_rest():
        for one in gathers:
            one.begin()

    if place.depth <= 8:
        for step in range(1, place.depth):
            vector.swap(step)
            weight.swap(step)
            if step == max(1, place.depth - 2):
                start_rest()
    else:
        place.each(1, place.depth, vector.swap)
        place.each(1, place.depth, weight.swap)
        start_rest()
    vector.finish()
    vec_rows = vec_ref.shape[0]
    total = vec_sc[pl.ds(0, vec_rows), :].astype(F32)
    if fsdp_count <= 8:
        for f in range(1, fsdp_count):
            total = total + vec_sc[pl.ds(f * vec_rows, vec_rows), :].astype(F32)
    else:
        total = lax.fori_loop(
            1, fsdp_count, lambda f, sofar: sofar + vec_sc[aligned(f * vec_rows, vec_rows), :].astype(F32), total
        )
    vec_sum[...] = total

    def normalise(seat):
        def body(part):
            token_rows = x_sc[aligned(seat * rows + part * 32, 32), :].astype(F32)
            center = token_rows - jnp.mean(token_rows, axis=-1, keepdims=True)
            variance = jnp.mean(center * center, axis=-1, keepdims=True)
            normed = center * lax.rsqrt(variance + 1e-05) * vec_sum[0:1, :] + vec_sum[1:2, :]
            n1_sc[aligned(seat * rows + part * 32, 32), :] = normed.astype(BF16)

        lax.fori_loop(0, rows // 32, lambda part, carry: (body(part), carry)[1], 0)

    def project(seat):
        here = aligned(seat * rows, rows)

        def body(part):
            cols = aligned(part * 256, 256)
            heads_sc[here, cols] = dot_nn(n1_sc[here, :], wq_sc[:, cols]).astype(BF16)

        lax.fori_loop(0, own_width // 256, lambda part, carry: (body(part), carry)[1], 0)

    own_x.wait()
    normalise(place.s)
    for way in range(2):
        x_arrival(way).wait_recv()
    for way in range(2):
        x_relay(way).start()
    for way in range(2):
        normalise(seats[way])
    weight.finish()
    project(place.s)
    for way in range(2):
        project(seats[way])
    for one in gathers:
        one.swap(1)
    for way in range(2):
        x_relayed(way).wait_recv()
    normalise(place.s3)
    project(place.s3)
    own_seg.wait()
    for way in range(3):
        seg_arrival(way).wait_recv()
    blocks = mask_ref.shape[1]
    for seat in range(4):
        columns = seg_sc[seat].T
        for part in range(rows // LANES):
            here = pl.ds(seat * rows + part * LANES, LANES)
            qd_ref[here, :], kf_ref[here, :] = token_features(
                seat * rows + part * LANES, columns[:, part : part + 1], blocks
            )
    keeps = [
        pltpu.make_async_copy(src, dst, keep_sems.at[i])
        for i, (src, dst) in enumerate(((heads_sc, heads_all), (n1_sc, n1_all), (wq_sc, wq_all)))
    ]
    for keep in keeps:
        keep.start()

    pairs = att_sc.shape[1] // LANES

    def att_copy(pair, way):
        cols = aligned((place.s * pairs + pair) * LANES, LANES)
        return send(
            att_sc.at[aligned(seats[way] * rows, rows), pl.ds(pair * LANES, LANES)],
            att_all.at[:, cols],
            (a_sent, a_got),
            pair * 3 + way,
            place.across(way),
        )

    def att_own(pair):
        cols = aligned((place.s * pairs + pair) * LANES, LANES)
        return pltpu.make_async_copy(
            att_sc.at[aligned(place.s * rows, rows), pl.ds(pair * LANES, LANES)],
            att_all.at[:, cols],
            a_own.at[pair],
        )

    def att_arrival(pair, way):
        there = att_all.at[:, aligned((seats[way] * pairs + pair) * LANES, LANES)]
        return send(there, there, (a_sent, a_got), pair * 3 + way, place.across(way))

    def unit(pair, odd):
        attend_unit(pair, odd, 256, heads_sc, mask_ref, qd_ref, kf_ref, keys_sc, values_t, att_sc, lse_ref)
        if odd:
            for way in range(3):
                att_copy(pair, way).start()
            att_own(pair).start()

    gather_steps(
        place,
        gathers,
        late,
        [functools.partial(unit, pair, odd) for pair in range(pairs) for odd in (0, 1)],
    )
    for keep in keeps:
        keep.wait()
    for way in range(3):
        seg_copy(way).wait_send()
        if way < 2:
            x_copy(way).wait_send()
            x_relay(way).wait_send()
        for pair in range(pairs):
            att_copy(pair, way).wait_send()
            att_arrival(pair, way).wait_recv()
    for pair in range(pairs):
        att_own(pair).wait()
    for one in gathers + late:
        one.finish()


def forward_attention(fsdp_count, x, w_qkv, vec, seg, mask, w_out, w_down, w_in):
    rows, width = x.shape
    length = 4 * rows
    heads = mask.shape[0]
    pairs = heads // 2
    depth = fsdp_count // 2
    own_width = w_qkv.shape[1] // 4
    full = fsdp_count * w_qkv.shape[0]
    anywhere = pl.BlockSpec(memory_space=pl.ANY)
    vmem = pl.BlockSpec(memory_space=pltpu.VMEM)
    shape = jax.ShapeDtypeStruct

    def whole(shard):
        return shape((fsdp_count * shard.shape[0], shard.shape[1]), shard.dtype)

    return pl.pallas_call(
        functools.partial(forward_kernel, fsdp_count),
        out_shape=(
            shape((length, own_width), BF16),
            shape((pairs, 2, length), F32),
            shape((rows, heads * DH * 4), BF16),
            whole(w_out),
            whole(w_down),
            whole(w_in),
            shape(vec.shape, F32),
            shape((length, width), BF16),
            shape((full, own_width), BF16),
            shape((length, LANES), BF16),
            shape((length, LANES), BF16),
        ),
        in_specs=[anywhere] * 4 + [vmem] + [anywhere] * 3,
        out_specs=(anywhere, vmem, anywhere, anywhere, anywhere, anywhere, vmem, anywhere, anywhere, vmem, vmem),
        scratch_shapes=[
            pltpu.VMEM((length, width), BF16),
            pltpu.VMEM((length, width), BF16),
            pltpu.VMEM((full, own_width), BF16),
            pltpu.VMEM((fsdp_count * vec.shape[0], vec.shape[1]), BF16),
            pltpu.VMEM((4,) + seg.shape, jnp.int32),
            pltpu.VMEM((length, own_width), BF16),
            pltpu.VMEM((length, heads * DH), BF16),
            pltpu.VMEM((length, LANES), BF16),
            pltpu.VMEM((LANES, length), BF16),
        ]
        + Gather.scratch(depth, True) * 3
        + Gather.scratch(depth, False) * 3
        + [dma(), dma(), dma(3), dma(2), dma(2), dma(2), dma(2), dma(3), dma(3)]
        + [dma(3 * pairs), dma(3 * pairs), dma(pairs)],
        compiler_params=pltpu.CompilerParams(
            collective_id=2, has_side_effects=True, vmem_limit_bytes=48 << 20
        ),
    )(x, w_qkv, vec, seg, mask, w_out, w_down, w_in)


def by_rows(count, body):
    lax.fori_loop(0, count // 16, lambda i, carry: (body(aligned(i * 16, 16)), carry)[1], 0)


class Reduce:
    def __init__(self, place, grad, out, quartered, bufs, sems):
        self.place, self.grad, self.out, self.quartered = place, grad, out, quartered
        self.rows, self.cols = out.shape
        self.wide = self.cols // 4
        self.acc, self.own, self.relay_in, self.quarter_in, self.z_in, self.total = bufs
        self.own_sem, self.put_sem, self.cs, self.rs, self.qs, self.zs, self.fs, self.gs = sems

    @staticmethod
    def scratch(depth, rows, cols, quartered):
        held = cols // 4 if quartered else cols
        side = (1, 1, 16, LANES) if quartered else None
        return [
            pltpu.VMEM((depth, rows, held), BF16),
            pltpu.VMEM((rows, held), BF16),
            pltpu.VMEM(side or (2, depth, rows, cols // 8), BF16),
            pltpu.VMEM(side or (2, depth, rows, cols // 4), BF16),
            pltpu.VMEM((depth, rows, cols // 4), BF16),
            pltpu.VMEM((rows, cols // 4), BF16),
            dma(),
            dma(),
        ] + [dma(depth)] * 12 + [dma(2)] * 4

    @staticmethod
    def take(place, grad, out, quartered, refs):
        s = refs[8:]
        pairs = [(s[i], s[i + 1]) for i in range(0, 16, 2)]
        sems = (refs[6], refs[7], pairs[0], pairs[1:3], pairs[3:5], pairs[5], pairs[6], pairs[7])
        return Reduce(place, grad, out, quartered, refs[:6], sems)

    def quarter(self, seat):
        return aligned(seat * self.wide, self.wide)

    def mine(self):
        return pl.ds(0, self.wide) if self.quartered else self.quarter(self.place.s)

    def piece(self, seat, half):
        return aligned(seat * self.wide + half * (self.wide // 2), self.wide // 2)

    def own_copy(self, step):
        p = self.place
        rows = aligned((2 * p.far(step) + p.c) * self.rows, self.rows)
        return pltpu.make_async_copy(self.grad.at[rows], self.own, self.own_sem)

    def core_copy(self, step):
        p = self.place
        rows = aligned((2 * p.far(step) + 1 - p.c) * self.rows, self.rows)
        return send(self.grad.at[rows], self.acc.at[step], self.cs, step, p.beside)

    def relay_copy(self, step, way):
        p = self.place
        src = self.acc.at[step, :, self.piece(p.s3, way)]
        return send(src, self.relay_in.at[way, step], self.rs[way], step, p.across(way))

    def quarter_copy(self, step, way):
        p = self.place
        src = self.acc.at[step, :, self.quarter((p.s1, p.s2)[way])]
        return send(src, self.quarter_in.at[way, step], self.qs[way], step, p.across(way))

    def z_copy(self, step):
        p = self.place
        src = self.acc.at[step, :, self.mine()]
        return send(src, self.z_in.at[step], self.zs, step, p.along(p.far(step)))

    def put_copy(self):
        return pltpu.make_async_copy(self.total, self.out.at[:, self.quarter(self.place.s)], self.put_sem)

    def total_copy(self, way):
        p = self.place
        return send(self.total, self.out.at[:, self.quarter(p.s)], self.fs, way, p.across(way))

    def total_arrival(self, way):
        p = self.place
        there = self.out.at[:, self.quarter((p.s1, p.s2)[way])]
        return send(there, there, self.fs, way, p.across(way))

    def back_copy(self, way):
        p = self.place
        there = self.out.at[:, self.piece((p.s2, p.s1)[way], 1 - way)]
        return send(there, there, self.gs, way, p.across(way))

    def back_arrival(self, way):
        p = self.place
        there = self.out.at[:, self.piece(p.s3, 1 - way)]
        return send(there, there, self.gs, way, p.across(way))

    def begin(self):
        depth = self.place.depth
        self.place.each(1, depth, lambda step: self.core_copy(step).start())
        self.core_copy(0).start()
        self.own_copy(1).start()

    def fold(self, step, following):
        self.core_copy(step).wait_recv()
        self.own_copy(step).wait()
        acc, own = self.acc, self.own

        def body(rows):
            acc[step, rows, :] = (acc[step, rows, :].astype(F32) + own[rows, :].astype(F32)).astype(BF16)

        by_rows(self.rows, body)
        if following is not None:
            self.own_copy(following).start()
        if not self.quartered:
            for way in (0, 1):
                self.relay_copy(step, way).start()
        elif not (isinstance(step, int) and step == 0):
            self.z_copy(step).start()

    def swap(self, step):
        if self.quartered:
            return
        p, acc = self.place, self.acc
        for way in (0, 1):
            self.relay_copy(step, way).wait_recv()
            cols = self.piece((p.s2, p.s1)[way], way)
            came = self.relay_in.at[way, step]

            def body(rows):
                acc[step, rows, cols] = (acc[step, rows, cols].astype(F32) + came[rows, :].astype(F32)).astype(BF16)

            by_rows(self.rows, body)
        for way in (0, 1):
            self.quarter_copy(step, way).start()

    def close(self, step, own):
        if self.quartered:
            return
        p, acc, came = self.place, self.acc, self.quarter_in
        for way in (0, 1):
            self.quarter_copy(step, way).wait_recv()
        cols = self.quarter(p.s)

        def body(rows):
            acc[step, rows, cols] = (
                acc[step, rows, cols].astype(F32)
                + came[0, step, rows, :].astype(F32)
                + came[1, step, rows, :].astype(F32)
            ).astype(BF16)

        by_rows(self.rows, body)
        if not own:
            self.z_copy(step).start()

    def collect(self):
        p, acc, came, total = self.place, self.acc, self.z_in, self.total
        p.each(1, p.depth, lambda step: self.z_copy(step).wait_recv())
        cols = self.mine()

        def body(rows):
            start = acc[0, rows, cols].astype(F32)
            if p.depth <= 8:
                for step in range(1, p.depth):
                    start = start + came[step, rows, :].astype(F32)
            else:
                start = lax.fori_loop(1, p.depth, lambda step, sofar: sofar + came[step, rows, :].astype(F32), start)
            total[rows, :] = start.astype(BF16)

        by_rows(self.rows, body)
        for way in (0, 1):
            self.total_copy(way).start()
        self.put_copy().start()

    def spread(self):
        for way in (0, 1):
            self.total_arrival(way).wait_recv()
        for way in (0, 1):
            self.back_copy(way).start()

    def finish(self):
        for way in (0, 1):
            self.back_arrival(way).wait_recv()
        self.put_copy().wait()

        def done(step):
            self.core_copy(step).wait_send()
            if not self.quartered:
                for way in (0, 1):
                    self.relay_copy(step, way).wait_send()
                    self.quarter_copy(step, way).wait_send()

        self.place.each(0, self.place.depth, done)
        self.place.each(1, self.place.depth, lambda step: self.z_copy(step).wait_send())
        for way in (0, 1):
            self.total_copy(way).wait_send()
            self.back_copy(way).wait_send()


REDUCE_REFS = 24


def reduce_steps(place, reduces, between):
    depth = place.depth
    work = list(between)

    def gap():
        if work:
            work.pop(0)()

    if depth <= 8:
        order = [(t + 1) % depth for t in range(depth)]
        for t in range(depth + 2):
            for one in reduces:
                if t < depth:
                    one.fold(order[t], order[t + 1] if t + 1 < depth else None)
                if 0 <= t - 1 < depth:
                    one.swap(order[t - 1])
                if 0 <= t - 2 < depth:
                    one.close(order[t - 2], order[t - 2] == 0)
                gap()
    else:
        def run(first, last, body):
            lax.fori_loop(first, last, lambda step, carry: (body(step), carry)[1], 0)

        for one in reduces:
            run(1, depth, lambda step: one.fold(step, lax.rem(step + 1, depth)))
            one.fold(0, None)
            run(0, depth, one.swap)
            run(1, depth, lambda step: one.close(step, False))
            one.close(0, True)
    for rest in work:
        rest()


def backward_unit(
    pair, odd, half, tile, heads_ref, mask_ref, qd_ref, kf_ref, go_ref, lse_ref, out_ref, keys_sc, values_sc, keys_t, p_sc, s_sc, k_acc, v_acc
):
    length = heads_ref.shape[0]
    span = p_sc.shape[1]
    scale = jnp.asarray(1.0 / math.sqrt(DH), BF16)
    q_cols, k_cols, v_cols = (pl.ds((3 * pair + i) * LANES, LANES) for i in range(3))
    cols = pl.ds(pair * LANES, LANES)
    mine = own_lanes(odd, (length, LANES))
    if half == 0:
        keys_sc[...] = jnp.where(mine, heads_ref[:, k_cols], kf_ref[...])
        values_sc[...] = jnp.where(mine, heads_ref[:, v_cols], jnp.zeros((), BF16))
        if not odd:
            keys_t[...] = heads_ref[:, k_cols].T

    def one_tile(index, carry):
        here = aligned(index * tile, tile)
        rows = aligned(half * span + index * tile, tile)
        lanes = own_lanes(odd, (tile, LANES))
        queries = query_tile(
            heads_ref[rows, q_cols],
            qd_ref[rows, :],
            mask_ref,
            2 * pair + odd,
            half * (span // BLK) + index * (tile // BLK),
            lanes,
        )
        prob = jnp.exp(dot_nt(keys_sc[...], queries) - lse_ref[pair, pl.ds(odd, 1), rows])
        grad_prob = dot_nt(values_sc[...], go_ref[rows, cols])
        delta = jnp.sum(prob * grad_prob, axis=0, keepdims=True)
        p_sc[:, here] = prob.astype(BF16)
        s_sc[:, here] = (prob * (grad_prob - delta)).astype(BF16)
        return carry

    lax.fori_loop(0, span // tile, one_tile, 0)
    part = pl.ds(half * span, span)
    grad_v = dot_nn(p_sc[...], go_ref[part, cols])
    grad_k = dot_nn(s_sc[...], heads_ref[part, q_cols] * scale)
    grad_q = (dot_nn(keys_t[...], s_sc[...]) * (1.0 / math.sqrt(DH))).T.astype(BF16)
    last = half * span + span == length

    def put(rows, columns, value, keep):
        if odd:
            value = jnp.where(keep, value, out_ref[rows, columns])
        out_ref[rows, columns] = value

    put(part, q_cols, grad_q, own_lanes(odd, (span, LANES)))
    if half > 0:
        grad_v, grad_k = grad_v + v_acc[...], grad_k + k_acc[...]
    if last:
        put(pl.ds(0, length), k_cols, grad_k.astype(BF16), mine)
        put(pl.ds(0, length), v_cols, grad_v.astype(BF16), mine)
    else:
        v_acc[...], k_acc[...] = grad_v, grad_k


def backward_kernel(
    fsdp_count,
    go_rows_ref,
    heads_ref,
    mask_ref,
    qd_ref,
    kf_ref,
    lse_ref,
    n1_ref,
    wq_ref,
    x_ref,
    hid_ref,
    vec_ref,
    small_ref,
    out_g_ref,
    down_g_ref,
    in_g_ref,
    tokens_out,
    small_out,
    qkv_total,
    out_total,
    down_total,
    in_total,
    go_sc,
    grads_sc,
    keys_sc,
    values_sc,
    keys_t,
    p_sc,
    s_sc,
    k_acc,
    v_acc,
    n1_sc,
    qkv_g,
    part_sc,
    part_in,
    half_in,
    small_sc,
    small_in,
    *rest,
):
    place = Place(fsdp_count)
    rows = go_rows_ref.shape[0]
    reduces = [
        Reduce.take(place, grad, out, False, rest[i * REDUCE_REFS : (i + 1) * REDUCE_REFS])
        for i, (grad, out) in enumerate(
            ((out_g_ref, out_total), (in_g_ref, in_total), (down_g_ref, down_total))
        )
    ]
    first = Reduce.take(place, qkv_g, qkv_total, True, rest[3 * REDUCE_REFS : 4 * REDUCE_REFS])
    g_own, n_own, g_sent, g_got, h_sent, h_got, p_sent, p_got, c_sent, c_got, z_sent, z_got, x_sent, x_got = rest[
        4 * REDUCE_REFS :
    ]
    seats = (place.s1, place.s2, place.s3)
    width = go_sc.shape[1]
    pairs = width // LANES
    half = rows // 2

    def part(seat):
        return go_rows_ref.at[:, aligned(seat * width, width)]

    def slot(seat):
        return go_sc.at[aligned(seat * rows, rows)]

    place.meet()
    for way in range(3):
        send(part(seats[way]), slot(place.s), (g_sent, g_got), way, place.across(way)).start()
    own = pltpu.make_async_copy(part(place.s), slot(place.s), g_own)
    own.start()
    for one in reduces:
        one.begin()
    n1_copy = pltpu.make_async_copy(n1_ref, n1_sc, n_own)
    n1_copy.start()
    own.wait()
    for way in range(3):
        send(slot(seats[way]), slot(seats[way]), (g_sent, g_got), way, place.across(way)).wait_recv()

    def unit(pair, odd, side):
        backward_unit(
            pair, odd, side, 256, heads_ref, mask_ref, qd_ref, kf_ref, go_sc, lse_ref, grads_sc,
            keys_sc, values_sc, keys_t, p_sc, s_sc, k_acc, v_acc,
        )

    def half_copy(way):
        src = part_sc.at[aligned(place.s3 * rows + way * half, half)]
        return send(src, half_in.at[way], (h_sent, h_got), way, place.across(way))

    def part_copy(way):
        src = part_sc.at[aligned(seats[way] * rows, rows)]
        return send(src, part_in.at[way], (p_sent, p_got), way, place.across(way))

    def partial_dn1():
        def body(index):
            here = aligned(index * rows, rows)
            part_sc[here, :] = dot_nt(grads_sc[here, :], wq_ref[...]).astype(BF16)

        lax.fori_loop(0, 4, lambda index, carry: (body(index), carry)[1], 0)
        for way in (0, 1):
            half_copy(way).start()

    def weight_grad():
        n1_copy.wait()

        def body(index):
            cols = aligned(index * 256, 256)
            qkv_g[cols, :] = dot_tn(n1_sc[:, cols], grads_sc[...]).astype(BF16)

        lax.fori_loop(0, qkv_g.shape[0] // 256, lambda index, carry: (body(index), carry)[1], 0)
        first.begin()

    def swap_dn1():
        for way in (0, 1):
            half_copy(way).wait_recv()
            base = (place.s2, place.s1)[way] * rows + way * half

            def body(index):
                here = aligned(base + index * 32, 32)
                came = half_in[way, aligned(index * 32, 32), :]
                part_sc[here, :] = (part_sc[here, :].astype(F32) + came.astype(F32)).astype(BF16)

            lax.fori_loop(0, half // 32, lambda index, carry: (body(index), carry)[1], 0)
        for way in (0, 1):
            part_copy(way).start()

    def fold_first():
        depth = place.depth
        place.each(1, depth, lambda step: first.fold(step, lax.rem(step + 1, depth)))
        first.fold(0, None)

    def core_small():
        return send(small_sc.at[0], small_sc.at[1], (c_sent, c_got), 0, place.beside)

    def z_small(step):
        return send(small_sc.at[2], small_in.at[step], (z_sent, z_got), step, place.along(place.far(step)))

    def x_small(way):
        return send(small_sc.at[3], small_sc.at[4 + way], (x_sent, x_got), way, place.across(way))

    def close_dn1():
        for way in (0, 1):
            part_copy(way).wait_recv()
        gain = vec_ref[0:1, :]

        def body(index, sums):
            here = aligned(index * 32, 32)
            mine = aligned(place.s * rows + index * 32, 32)
            dn1 = (
                part_sc[mine, :].astype(F32)
                + part_in[0, here, :].astype(F32)
                + part_in[1, here, :].astype(F32)
            )
            token_rows = x_ref[here, :].astype(F32)
            center = token_rows - jnp.mean(token_rows, axis=-1, keepdims=True)
            inv = lax.rsqrt(jnp.mean(center * center, axis=-1, keepdims=True) + 1e-05)
            hat = center * inv
            scaled = dn1 * gain
            grad = hid_ref[here, :] + inv * (
                scaled
                - jnp.mean(scaled, axis=-1, keepdims=True)
                - hat * jnp.mean(scaled * hat, axis=-1, keepdims=True)
            )
            tokens_out[here, :] = grad.astype(BF16)
            return (
                sums[0] + jnp.sum(dn1 * hat, axis=0, keepdims=True),
                sums[1] + jnp.sum(dn1, axis=0, keepdims=True),
            )

        none = jnp.zeros((1, x_ref.shape[1]), F32)
        gain_sum, bias_sum = lax.fori_loop(0, rows // 32, body, (none, none))
        small_sc[0] = small_ref[...]
        small_sc[0, 0:1, :] = gain_sum
        small_sc[0, 1:2, :] = bias_sum
        core_small().start()

    def small_z():
        core_small().wait_recv()
        small_sc[2] = small_sc[0] + small_sc[1]
        place.each(1, place.depth, lambda step: z_small(step).start())

    def small_x():
        place.each(1, place.depth, lambda step: z_small(step).wait_recv())
        small_in[0] = small_sc[2]
        if place.depth <= 8:
            total = small_in[place.back(0)]
            for z in range(1, place.depth):
                total = total + small_in[place.back(z)]
        else:
            total = lax.fori_loop(
                1, place.depth, lambda z, sofar: sofar + small_in[place.back(z)], small_in[place.back(0)]
            )
        small_sc[3] = total
        for way in range(3):
            x_small(way).start()

    def small_end():
        for way in range(3):
            x_small(way).wait_recv()
        small_out[...] = (small_sc[3] + small_sc[4]) + (small_sc[5] + small_sc[6])

    units = [
        functools.partial(unit, pair, odd, side) for pair in range(pairs) for odd in (0, 1) for side in (0, 1)
    ]
    reduce_steps(
        place,
        reduces,
        units + [partial_dn1, weight_grad, swap_dn1, fold_first, close_dn1, small_z],
    )
    for one in [first] + reduces:
        one.collect()
    small_x()
    for one in [first] + reduces:
        one.spread()
    small_end()
    core_small().wait_send()
    place.each(1, place.depth, lambda step: z_small(step).wait_send())
    for way in range(3):
        send(part(seats[way]), slot(place.s), (g_sent, g_got), way, place.across(way)).wait_send()
        x_small(way).wait_send()
        if way < 2:
            half_copy(way).wait_send()
            part_copy(way).wait_send()
    for one in [first] + reduces:
        one.finish()


def backward_attention(fsdp_count, grad_att, saved, x, hid, small, grads):
    heads, mask, qd, kf, lse, n1, wq, vec = saved
    rows, width = grad_att.shape
    length = heads.shape[0]
    own_width = width // 4
    depth = fsdp_count // 2
    span = length // 2
    anywhere = pl.BlockSpec(memory_space=pl.ANY)
    vmem = pl.BlockSpec(memory_space=pltpu.VMEM)
    share = wq.shape[0] // fsdp_count
    kept = [(grad.shape[0] // fsdp_count, grad.shape[1]) for grad in grads]
    kept_qkv = (share, 4 * wq.shape[1])
    shape = jax.ShapeDtypeStruct

    reduce_scratch = []
    for one in (kept[0], kept[2], kept[1]):
        reduce_scratch += Reduce.scratch(depth, *one, False)
    reduce_scratch += Reduce.scratch(depth, *kept_qkv, True)
    return pl.pallas_call(
        functools.partial(backward_kernel, fsdp_count),
        out_shape=(shape(x.shape, BF16), shape(small.shape, F32), shape(kept_qkv, BF16))
        + tuple(shape(one, BF16) for one in kept),
        in_specs=[anywhere] + [vmem] * 5 + [anywhere] + [vmem] * 5 + [anywhere] * 3,
        out_specs=(vmem, vmem, anywhere, anywhere, anywhere, anywhere),
        scratch_shapes=[
            pltpu.VMEM((length, own_width), BF16),
            pltpu.VMEM((length, 3 * own_width), BF16),
            pltpu.VMEM((length, LANES), BF16),
            pltpu.VMEM((length, LANES), BF16),
            pltpu.VMEM((LANES, length), BF16),
            pltpu.VMEM((length, span), BF16),
            pltpu.VMEM((length, span), BF16),
            pltpu.VMEM((length, LANES), F32),
            pltpu.VMEM((length, LANES), F32),
            pltpu.VMEM((length, width), BF16),
            pltpu.VMEM(wq.shape, BF16),
            pltpu.VMEM((length, width), BF16),
            pltpu.VMEM((2, rows, width), BF16),
            pltpu.VMEM((2, rows // 2, width), BF16),
            pltpu.VMEM((7,) + small.shape, F32),
            pltpu.VMEM((depth,) + small.shape, F32),
        ]
        + reduce_scratch
        + [dma(), dma(), dma(3), dma(3), dma(2), dma(2), dma(2), dma(2)]
        + [dma(1), dma(1), dma(depth), dma(depth), dma(3), dma(3)],
        compiler_params=pltpu.CompilerParams(
            collective_id=3, has_side_effects=True, vmem_limit_bytes=60 << 20
        ),
    )(grad_att, heads, mask, qd, kf, lse, n1, wq, x, hid, vec, small, *grads)


def swap_thirds(rows, outer, inner):
    count, width = rows.shape
    return rows.reshape(count, outer, inner, width // (outer * inner)).swapaxes(1, 2).reshape(count, width)


def per_device(
    seq_count,
    fsdp_count,
    tokens,
    segment_ids,
    random_blocks,
    ln1_gain,
    ln1_bias,
    w_qkv,
    w_out,
    ln2_gain,
    ln2_bias,
    w_in,
    b_in,
    w_down,
    b_down,
    cotangent,
):
    groups = w_qkv.shape[1] // (3 * LANES)
    width = tokens.shape[2]
    share = ln1_gain.shape[0]
    position = lax.axis_index("fsdp")

    def placed(vector):
        held = vector.shape[0]
        spread = jnp.tile(vector, fsdp_count).reshape(-1, width)
        owner = jnp.arange(fsdp_count * held, dtype=jnp.int32).reshape(-1, width) // held
        return jnp.where(owner == position, spread, jnp.zeros((), BF16))

    vec = jnp.concatenate(
        [placed(v) for v in (ln1_gain, ln1_bias, ln2_gain, ln2_bias, b_down, b_in)], axis=0
    )
    vec = jnp.pad(vec, ((0, -vec.shape[0] % 16), (0, 0)))
    tok_count = segment_ids.shape[1]
    seg_rows = -(-tok_count // (8 * LANES)) * 8
    seg = jnp.pad(segment_ids[0], (0, seg_rows * LANES - tok_count)).reshape(seg_rows, LANES)
    mask = block_mask(random_blocks)
    by_heads, lse, att_rows, out_weight, down_weight, in_weight, vec, normed_one, own_qkv, query_docs, key_feats = (
        forward_attention(
            fsdp_count, tokens[0], swap_thirds(w_qkv, 3, groups), vec, seg, mask, w_out, w_down, w_in
        )
    )
    gain_two, bias_two, down_bias, in_bias = vec[2], vec[3], vec[4], vec[5 : 5 + in_weight.shape[1] // width].reshape(-1)
    token_rows = tokens[0].astype(F32)
    hidden = token_rows + dot_nn(att_rows, out_weight)
    hat_two, inv_two = layer_norm_parts(hidden)
    normed_two = (hat_two * gain_two + bias_two).astype(BF16)
    pre_act = dot_nn(normed_two, in_weight) + in_bias
    act_value, pull_gelu = jax.vjp(gelu_tanh, pre_act)
    act_low = act_value.astype(BF16)
    result = hidden + dot_nn(act_low, down_weight) + down_bias

    cot_low = cotangent[0]
    cot_rows = cot_low.astype(F32)
    grad_pre = pull_gelu(dot_nt(cot_low, down_weight))[0].astype(BF16)
    grad_norm_two = dot_nt(grad_pre, in_weight)
    scaled = grad_norm_two * gain_two
    grad_hidden = cot_rows + inv_two * (
        scaled
        - jnp.mean(scaled, axis=-1, keepdims=True)
        - hat_two * jnp.mean(scaled * hat_two, axis=-1, keepdims=True)
    )
    hidden_low = grad_hidden.astype(BF16)
    grad_att = dot_nt(hidden_low, out_weight).astype(BF16)
    small = jnp.concatenate(
        [
            jnp.zeros((2, width), F32),
            jnp.sum(grad_norm_two * hat_two, axis=0)[None],
            jnp.sum(grad_norm_two, axis=0)[None],
            jnp.sum(cot_rows, axis=0)[None],
            jnp.sum(grad_pre.astype(F32), axis=0).reshape(-1, width),
        ],
        axis=0,
    )
    small = jnp.pad(small, ((0, vec.shape[0] - small.shape[0]), (0, 0)))
    grad_tokens, small, total_qkv, total_out, total_down, total_in = backward_attention(
        fsdp_count,
        grad_att,
        (by_heads, mask, query_docs, key_feats, lse, normed_one, own_qkv, vec),
        tokens[0],
        grad_hidden,
        small,
        (
            dot_tn(att_rows, hidden_low).astype(BF16),
            dot_tn(act_low, cot_low).astype(BF16),
            dot_tn(normed_two, grad_pre).astype(BF16),
        ),
    )
    parts = [lax.dynamic_slice_in_dim(small[i], position * share, share) for i in range(5)]
    held = b_in.shape[0]
    parts.append(lax.dynamic_slice_in_dim(small[5 : 5 + fsdp_count * held // width].reshape(-1), position * held, held))
    return (
        result.astype(BF16)[None],
        grad_tokens[None],
        parts[0],
        parts[1],
        swap_thirds(total_qkv, groups, 3).astype(F32),
        total_out.astype(F32),
        parts[2],
        parts[3],
        total_in.astype(F32),
        parts[5],
        total_down.astype(F32),
        parts[4],
    )


def solution(mesh):
    return jax.shard_map(
        functools.partial(per_device, mesh.shape["seq"], mesh.shape["fsdp"]),
        mesh=mesh,
        in_specs=(
            P("fsdp", "seq", None),
            P("fsdp", "seq"),
            P("seq", None, None),
            P("fsdp"),
            P("fsdp"),
            P("fsdp", None),
            P("fsdp", None),
            P("fsdp"),
            P("fsdp"),
            P("fsdp", None),
            P("fsdp"),
            P("fsdp", None),
            P("fsdp"),
            P("fsdp", "seq", None),
        ),
        out_specs=(
            P("fsdp", "seq", None),
            P("fsdp", "seq", None),
            P("fsdp"),
            P("fsdp"),
            P("fsdp", None),
            P("fsdp", None),
            P("fsdp"),
            P("fsdp"),
            P("fsdp", None),
            P("fsdp"),
            P("fsdp", None),
            P("fsdp"),
        ),
        check_vma=False,
    )
```

```python
import functools
import math

import jax
import jax.numpy as jnp
from jax import lax
from jax.experimental import pallas as pl
from jax.experimental.pallas import tpu as pltpu
from jax.sharding import PartitionSpec as P

DH = 64
BLK = 64
LANES = 128
NEG = -1e30
F32 = jnp.float32
BF16 = jnp.bfloat16


def dot_nn(a, b):
    return jnp.dot(a, b, preferred_element_type=F32)


def dot_nt(a, b):
    return lax.dot_general(a, b, (((1,), (1,)), ((), ())), preferred_element_type=F32)


def dot_tn(a, b):
    return lax.dot_general(a, b, (((0,), (0,)), ((), ())), preferred_element_type=F32)


DOCS = 6


def block_mask(random_blocks):
    heads, inner, _ = random_blocks.shape
    blocks = inner + 2
    ids = jnp.arange(blocks, dtype=jnp.int32)
    near = jnp.abs(ids[:, None] - ids[None, :]) <= 1
    edge = (ids == 0) | (ids == blocks - 1)
    fixed = near | edge[:, None] | edge[None, :]
    picked = jnp.any(random_blocks[:, :, :, None] == ids, axis=2)
    used = fixed[None] | jnp.pad(picked, ((0, 0), (1, 1), (0, 0)))
    row = jnp.pad(jnp.where(used, 0.0, NEG), ((0, 0), (0, 0), (0, DH - blocks)))
    return jnp.concatenate([row, row], axis=-1)


def token_features(start, docs, blocks):
    shape = (docs.shape[0], LANES)
    lane = lax.rem(lax.broadcasted_iota(jnp.int32, shape, 1), DH)
    block = lax.div(lax.broadcasted_iota(jnp.int32, shape, 0) + start, BLK)
    own = docs + blocks == lane
    other = jnp.where(own | (lane >= blocks + DOCS), 0.0, 1.0)
    key_part = jnp.where(lane < blocks, jnp.where(block == lane, 1.0, 0.0), other)
    return jnp.where(own, NEG, 0.0).astype(BF16), key_part.astype(BF16)


def query_tile(q_tile, doc_tile, mask_ref, head, first_block, lanes):
    scale = jnp.asarray(1.0 / math.sqrt(DH), BF16)
    count = q_tile.shape[0] // BLK
    mask = jnp.concatenate(
        [jnp.broadcast_to(mask_ref[head, pl.ds(first_block + i, 1), :], (BLK, LANES)) for i in range(count)], axis=0
    )
    return jnp.where(lanes, q_tile * scale, doc_tile + mask.astype(BF16))


def own_lanes(odd, shape):
    lane = lax.broadcasted_iota(jnp.int32, shape, 1)
    return (lane >= DH) if odd else (lane < DH)


MESH = pl.DeviceIdType.MESH


class Place:
    def __init__(self, fsdp_count):
        self.depth = fsdp_count // 2
        self.s = lax.axis_index("seq")
        self.f = lax.axis_index("fsdp")
        self.z = lax.div(self.f, 2)
        self.c = lax.rem(self.f, 2)
        self.s1 = self.s + 1 - 2 * lax.rem(self.s, 2)
        self.s2 = self.s + 2 - 4 * lax.div(self.s, 2)
        self.s3 = 3 - self.s
        self.beside = (self.s, self.f + 1 - 2 * self.c)

    def across(self, index):
        return ((self.s1, self.s2, self.s3)[index], self.f)

    def far(self, step):
        return lax.rem(self.z + step, self.depth)

    def back(self, step):
        return lax.rem(self.z + self.depth - step, self.depth)

    def along(self, z):
        return (self.s, 2 * z + self.c)

    def meet(self):
        barrier = pltpu.get_barrier_semaphore()
        peers = [self.beside] + [self.across(i) for i in range(3)]
        for peer in peers:
            pl.semaphore_signal(barrier, inc=1, device_id=peer, device_id_type=MESH)
        self.each(1, self.depth, lambda step: pl.semaphore_signal(
            barrier, inc=1, device_id=self.along(self.far(step)), device_id_type=MESH
        ))
        pl.semaphore_wait(barrier, len(peers) + self.depth - 1)

    def each(self, start, stop, body):
        if stop - start <= 8:
            for step in range(start, stop):
                body(step)
        else:
            lax.fori_loop(start, stop, lambda step, carry: (body(step), carry)[1], 0)


def send(src, dst, sems, index, device):
    sent, got = sems
    return pltpu.make_async_remote_copy(
        src_ref=src,
        dst_ref=dst,
        send_sem=sent.at[index],
        recv_sem=got.at[index],
        device_id=device,
        device_id_type=MESH,
    )


def aligned(start, size):
    return pl.ds(pl.multiple_of(start, size), size)


class Gather:
    def __init__(self, place, src, dst, split, sems):
        self.place, self.src, self.dst, self.split = place, src, dst, split
        self.rows, self.cols = src.shape
        self.local, self.zs, self.xs, self.rs, self.cs = sems

    def block(self, z, core, quarter=None, half=None):
        rows = aligned((2 * z + core) * self.rows, self.rows)
        if quarter is None:
            return self.dst.at[rows]
        wide = self.cols // 4
        if half is None:
            return self.dst.at[rows, aligned(quarter * wide, wide)]
        return self.dst.at[rows, aligned(quarter * wide + half * (wide // 2), wide // 2)]

    def source(self, step, side):
        return self.place.z - step if side == 0 else self.place.z + step

    def has(self, step, side):
        z = self.source(step, side)
        return z >= 0 if side == 0 else z < self.place.depth

    def sends(self, step, side):
        p = self.place
        onward = p.z + 1 < p.depth if side == 0 else p.z > 0
        return jnp.logical_and(self.has(step - 1, side), onward)

    def slot(self, step, side):
        return 2 * step + side

    def own_copy(self):
        return pltpu.make_async_copy(self.src, self.block(self.place.z, self.place.c), self.local)

    def own_core(self):
        p = self.place
        return send(self.src, self.block(p.z, p.c), self.cs, 0, p.beside)

    def own_arrival(self):
        p = self.place
        there = self.block(p.z, 1 - p.c)
        return send(there, there, self.cs, 0, p.beside)

    def core_copy(self, step, side):
        p = self.place
        there = self.block(self.source(step, side), p.c)
        return send(there, there, self.cs, self.slot(step, side), p.beside)

    def core_arrival(self, step, side):
        p = self.place
        there = self.block(self.source(step, side), 1 - p.c)
        return send(there, there, self.cs, self.slot(step, side), p.beside)

    def z_copy(self, step, side):
        p = self.place
        z = self.source(step - 1, side)
        there = self.block(z, p.c, p.s) if self.split else self.block(z, p.c)
        src = there
        if isinstance(step, int) and step == 1:
            wide = self.cols // 4
            src = self.src.at[:, aligned(p.s * wide, wide)] if self.split else self.src
        return send(src, there, self.zs, self.slot(step, side), p.along(p.z + 1 - 2 * side))

    def z_arrival(self, step, side):
        p = self.place
        z = self.source(step, side)
        there = self.block(z, p.c, p.s) if self.split else self.block(z, p.c)
        return send(there, there, self.zs, self.slot(step, side), p.along(p.z - 1 + 2 * side))

    def x_copy(self, step, side, way):
        p = self.place
        there = self.block(self.source(step, side), p.c, p.s)
        return send(there, there, self.xs[way], self.slot(step, side), p.across(way))

    def x_arrival(self, step, side, way):
        p = self.place
        there = self.block(self.source(step, side), p.c, (p.s1, p.s2)[way])
        return send(there, there, self.xs[way], self.slot(step, side), p.across(way))

    def relay_copy(self, step, side, way):
        p = self.place
        there = self.block(self.source(step, side), p.c, (p.s2, p.s1)[way], 1 - way)
        return send(there, there, self.rs[way], self.slot(step, side), p.across(way))

    def relay_arrival(self, step, side, way):
        p = self.place
        there = self.block(self.source(step, side), p.c, p.s3, 1 - way)
        return send(there, there, self.rs[way], self.slot(step, side), p.across(way))

    def both(self, step, body, test=None):
        for side in (0, 1):
            pl.when((test or self.has)(step, side))(functools.partial(body, step, side))

    def begin(self):
        self.both(1, lambda step, side: self.z_copy(step, side).start(), self.sends)
        self.own_copy().start()
        self.own_core().start()

    def swap(self, step):
        def body(step, side):
            self.z_arrival(step, side).wait_recv()
            pl.when(self.sends(step + 1, side))(lambda: self.z_copy(step + 1, side).start())
            if self.split:
                for way in (0, 1):
                    self.x_copy(step, side, way).start()
            else:
                self.core_copy(step, side).start()

        self.both(step, body)

    def relay(self, step):
        def body(step, side):
            for way in (0, 1):
                self.x_arrival(step, side, way).wait_recv()
            for way in (0, 1):
                self.relay_copy(step, side, way).start()

        if self.split:
            self.both(step, body)

    def share(self, step):
        def body(step, side):
            for way in (0, 1):
                self.relay_arrival(step, side, way).wait_recv()
            self.core_copy(step, side).start()

        if self.split:
            self.both(step, body)

    def finish(self):
        self.own_copy().wait()
        self.own_core().wait_send()
        self.own_arrival().wait_recv()

        def close(step, side):
            if self.split:
                for way in (0, 1):
                    self.x_copy(step, side, way).wait_send()
                    self.relay_copy(step, side, way).wait_send()
            self.core_copy(step, side).wait_send()
            self.core_arrival(step, side).wait_recv()

        self.place.each(1, self.place.depth, lambda step: self.both(step, close))
        self.place.each(
            1,
            self.place.depth,
            lambda step: self.both(step, lambda step, side: self.z_copy(step, side).wait_send(), self.sends),
        )

    @staticmethod
    def scratch(depth, split):
        held = 2 * depth if split else 1
        return [dma()] + [dma(2 * depth)] * 2 + [dma(held)] * 8 + [dma(2 * depth)] * 2

    @staticmethod
    def take(refs):
        pairs = [(refs[i], refs[i + 1]) for i in range(1, 13, 2)]
        return (refs[0], pairs[0], pairs[1:3], pairs[3:5], pairs[5])


GATHER_SEMS = 13


def gather_steps(place, gathers, late, between):
    depth = place.depth
    work = list(between)

    def gap():
        if work:
            work.pop(0)()

    def stage(step, swap, relay, share, gap):
        if swap:
            for one in gathers:
                one.swap(step)
        if relay:
            for one in gathers:
                one.relay(step - 1)
            gap()
        if swap:
            for one in late:
                one.swap(step - 1)
        if share:
            for one in gathers:
                one.share(step - 2)

    for one in late:
        one.begin()
    gap()
    if depth <= 8:
        for step in range(2, depth + 2):
            stage(step, step < depth, step <= depth, step >= 3, gap)
    else:
        stage(2, True, True, False, gap)
        lax.fori_loop(3, depth, lambda step, carry: (stage(step, True, True, True, lambda: None), carry)[1], 0)
        stage(depth, False, True, True, gap)
        stage(depth + 1, False, False, True, gap)
    for one in late:
        one.swap(depth - 1)
    for rest in work:
        rest()


def dma(*shape):
    return pltpu.SemaphoreType.DMA(shape) if shape else pltpu.SemaphoreType.DMA


def attend_unit(pair, odd, tile, heads_ref, mask_ref, qd_ref, kf_ref, keys_sc, values_t, out_ref, lse_ref):
    length = heads_ref.shape[0]
    cols = pl.ds(pair * LANES, LANES)
    q_cols, k_cols, v_cols = (pl.ds((3 * pair + i) * LANES, LANES) for i in range(3))
    if not odd:
        values_t[...] = heads_ref[:, v_cols].T
    mine = own_lanes(odd, (length, LANES))
    keys_sc[...] = jnp.where(mine, heads_ref[:, k_cols], kf_ref[...])

    def one_tile(index, carry):
        rows = aligned(index * tile, tile)
        lanes = own_lanes(odd, (tile, LANES))
        queries = query_tile(
            heads_ref[rows, q_cols], qd_ref[rows, :], mask_ref, 2 * pair + odd, index * (tile // BLK), lanes
        )
        scores = dot_nt(keys_sc[...], queries)
        top = jnp.max(scores, axis=0, keepdims=True)
        prob = jnp.exp(scores - top)
        total = jnp.sum(prob, axis=0, keepdims=True)
        mixed = dot_nn(values_t[...], prob.astype(BF16)) / total
        lse_ref[pair, pl.ds(odd, 1), rows] = top + jnp.log(total)
        result = mixed.T.astype(BF16)
        if odd:
            out_ref[rows, cols] = jnp.where(lanes, result, out_ref[rows, cols])
        else:
            out_ref[rows, cols] = result
        return carry

    lax.fori_loop(0, length // tile, one_tile, 0, unroll=2)


def forward_kernel(
    fsdp_count,
    x_ref,
    wq_ref,
    vec_ref,
    seg_ref,
    mask_ref,
    out_w_ref,
    down_w_ref,
    in_w_ref,
    heads_all,
    lse_ref,
    att_all,
    out_w_all,
    down_w_all,
    in_w_all,
    vec_sum,
    n1_all,
    wq_all,
    qd_ref,
    kf_ref,
    x_sc,
    n1_sc,
    wq_sc,
    vec_sc,
    seg_sc,
    heads_sc,
    att_sc,
    keys_sc,
    values_t,
    *sems,
):
    place = Place(fsdp_count)
    rows, width = x_ref.shape
    own_width = wq_sc.shape[1]
    seats = (place.s1, place.s2, place.s3)

    def taken(i):
        return Gather.take(sems[i * GATHER_SEMS : (i + 1) * GATHER_SEMS])

    lone = pl.ds(0, in_w_ref.shape[1] // 2)
    shared = pl.ds(in_w_ref.shape[1] // 2, in_w_ref.shape[1] // 2)
    gathers = [
        Gather(place, src, dst, split, taken(i))
        for i, (src, dst, split) in enumerate(
            (
                (out_w_ref, out_w_all, True),
                (in_w_ref.at[:, shared], in_w_all.at[:, shared], True),
                (down_w_ref, down_w_all, True),
                (in_w_ref.at[:, lone], in_w_all.at[:, lone], False),
            )
        )
    ]
    late = [gathers.pop()]
    weight = Gather(place, wq_ref.at[:, aligned(place.s * own_width, own_width)], wq_sc, False, taken(4))
    vector = Gather(place, vec_ref, vec_sc, False, taken(5))
    x_own, seg_own, keep_sems, x_sent, x_got, r_sent, r_got, g_sent, g_got, a_sent, a_got, a_own = sems[6 * GATHER_SEMS :]
    half = rows // 2

    def x_rows(seat):
        return x_sc.at[aligned(seat * rows, rows)]

    def x_half(seat, part):
        return x_sc.at[aligned(seat * rows + part * half, half)]

    def x_copy(way):
        return send(x_ref, x_rows(place.s), (x_sent, x_got), way, place.across(way))

    def x_arrival(way):
        there = x_rows(seats[way])
        return send(there, there, (x_sent, x_got), way, place.across(way))

    def x_relay(way):
        there = x_half((place.s2, place.s1)[way], 1 - way)
        return send(there, there, (r_sent, r_got), way, place.across(way))

    def x_relayed(way):
        there = x_half(place.s3, 1 - way)
        return send(there, there, (r_sent, r_got), way, place.across(way))

    def seg_copy(way):
        return send(seg_ref, seg_sc.at[place.s], (g_sent, g_got), way, place.across(way))

    def seg_arrival(way):
        there = seg_sc.at[seats[way]]
        return send(there, there, (g_sent, g_got), way, place.across(way))

    place.meet()
    vector.begin()
    weight.begin()
    for way in range(2):
        x_copy(way).start()
    for way in range(3):
        seg_copy(way).start()
    own_x = pltpu.make_async_copy(x_ref, x_rows(place.s), x_own)
    own_x.start()
    own_seg = pltpu.make_async_copy(seg_ref, seg_sc.at[place.s], seg_own)
    own_seg.start()
    def start_rest():
        for one in gathers:
            one.begin()

    if place.depth <= 8:
        for step in range(1, place.depth):
            vector.swap(step)
            weight.swap(step)
            if step == max(1, place.depth - 2):
                start_rest()
    else:
        place.each(1, place.depth, vector.swap)
        place.each(1, place.depth, weight.swap)
        start_rest()
    vector.finish()
    vec_rows = vec_ref.shape[0]
    total = vec_sc[pl.ds(0, vec_rows), :].astype(F32)
    if fsdp_count <= 8:
        for f in range(1, fsdp_count):
            total = total + vec_sc[pl.ds(f * vec_rows, vec_rows), :].astype(F32)
    else:
        total = lax.fori_loop(
            1, fsdp_count, lambda f, sofar: sofar + vec_sc[aligned(f * vec_rows, vec_rows), :].astype(F32), total
        )
    vec_sum[...] = total

    def normalise(seat):
        def body(part):
            token_rows = x_sc[aligned(seat * rows + part * 32, 32), :].astype(F32)
            center = token_rows - jnp.mean(token_rows, axis=-1, keepdims=True)
            variance = jnp.mean(center * center, axis=-1, keepdims=True)
            normed = center * lax.rsqrt(variance + 1e-05) * vec_sum[0:1, :] + vec_sum[1:2, :]
            n1_sc[aligned(seat * rows + part * 32, 32), :] = normed.astype(BF16)

        lax.fori_loop(0, rows // 32, lambda part, carry: (body(part), carry)[1], 0)

    def project(seat):
        here = aligned(seat * rows, rows)

        def body(part):
            cols = aligned(part * 256, 256)
            heads_sc[here, cols] = dot_nn(n1_sc[here, :], wq_sc[:, cols]).astype(BF16)

        lax.fori_loop(0, own_width // 256, lambda part, carry: (body(part), carry)[1], 0)

    own_x.wait()
    normalise(place.s)
    for way in range(2):
        x_arrival(way).wait_recv()
    for way in range(2):
        x_relay(way).start()
    for way in range(2):
        normalise(seats[way])
    weight.finish()
    project(place.s)
    for way in range(2):
        project(seats[way])
    for one in gathers:
        one.swap(1)
    for way in range(2):
        x_relayed(way).wait_recv()
    normalise(place.s3)
    project(place.s3)
    own_seg.wait()
    for way in range(3):
        seg_arrival(way).wait_recv()
    blocks = mask_ref.shape[1]
    for seat in range(4):
        columns = seg_sc[seat].T
        for part in range(rows // LANES):
            here = pl.ds(seat * rows + part * LANES, LANES)
            qd_ref[here, :], kf_ref[here, :] = token_features(
                seat * rows + part * LANES, columns[:, part : part + 1], blocks
            )
    keeps = [
        pltpu.make_async_copy(src, dst, keep_sems.at[i])
        for i, (src, dst) in enumerate(((heads_sc, heads_all), (n1_sc, n1_all), (wq_sc, wq_all)))
    ]
    for keep in keeps:
        keep.start()

    pairs = att_sc.shape[1] // LANES

    def att_copy(pair, way):
        cols = aligned((place.s * pairs + pair) * LANES, LANES)
        return send(
            att_sc.at[aligned(seats[way] * rows, rows), pl.ds(pair * LANES, LANES)],
            att_all.at[:, cols],
            (a_sent, a_got),
            pair * 3 + way,
            place.across(way),
        )

    def att_own(pair):
        cols = aligned((place.s * pairs + pair) * LANES, LANES)
        return pltpu.make_async_copy(
            att_sc.at[aligned(place.s * rows, rows), pl.ds(pair * LANES, LANES)],
            att_all.at[:, cols],
            a_own.at[pair],
        )

    def att_arrival(pair, way):
        there = att_all.at[:, aligned((seats[way] * pairs + pair) * LANES, LANES)]
        return send(there, there, (a_sent, a_got), pair * 3 + way, place.across(way))

    def unit(pair, odd):
        attend_unit(pair, odd, 256, heads_sc, mask_ref, qd_ref, kf_ref, keys_sc, values_t, att_sc, lse_ref)
        if odd:
            for way in range(3):
                att_copy(pair, way).start()
            att_own(pair).start()

    gather_steps(
        place,
        gathers,
        late,
        [functools.partial(unit, pair, odd) for pair in range(pairs) for odd in (0, 1)],
    )
    for keep in keeps:
        keep.wait()
    for way in range(3):
        seg_copy(way).wait_send()
        if way < 2:
            x_copy(way).wait_send()
            x_relay(way).wait_send()
        for pair in range(pairs):
            att_copy(pair, way).wait_send()
            att_arrival(pair, way).wait_recv()
    for pair in range(pairs):
        att_own(pair).wait()
    for one in gathers + late:
        one.finish()


def forward_attention(fsdp_count, x, w_qkv, vec, seg, mask, w_out, w_down, w_in):
    rows, width = x.shape
    length = 4 * rows
    heads = mask.shape[0]
    pairs = heads // 2
    depth = fsdp_count // 2
    own_width = w_qkv.shape[1] // 4
    full = fsdp_count * w_qkv.shape[0]
    anywhere = pl.BlockSpec(memory_space=pl.ANY)
    vmem = pl.BlockSpec(memory_space=pltpu.VMEM)
    shape = jax.ShapeDtypeStruct

    def whole(shard):
        return shape((fsdp_count * shard.shape[0], shard.shape[1]), shard.dtype)

    return pl.pallas_call(
        functools.partial(forward_kernel, fsdp_count),
        out_shape=(
            shape((length, own_width), BF16),
            shape((pairs, 2, length), F32),
            shape((rows, heads * DH * 4), BF16),
            whole(w_out),
            whole(w_down),
            whole(w_in),
            shape(vec.shape, F32),
            shape((length, width), BF16),
            shape((full, own_width), BF16),
            shape((length, LANES), BF16),
            shape((length, LANES), BF16),
        ),
        in_specs=[anywhere] * 4 + [vmem] + [anywhere] * 3,
        out_specs=(anywhere, vmem, anywhere, anywhere, anywhere, anywhere, vmem, anywhere, anywhere, vmem, vmem),
        scratch_shapes=[
            pltpu.VMEM((length, width), BF16),
            pltpu.VMEM((length, width), BF16),
            pltpu.VMEM((full, own_width), BF16),
            pltpu.VMEM((fsdp_count * vec.shape[0], vec.shape[1]), BF16),
            pltpu.VMEM((4,) + seg.shape, jnp.int32),
            pltpu.VMEM((length, own_width), BF16),
            pltpu.VMEM((length, heads * DH), BF16),
            pltpu.VMEM((length, LANES), BF16),
            pltpu.VMEM((LANES, length), BF16),
        ]
        + Gather.scratch(depth, True) * 3
        + Gather.scratch(depth, False) * 3
        + [dma(), dma(), dma(3), dma(2), dma(2), dma(2), dma(2), dma(3), dma(3)]
        + [dma(3 * pairs), dma(3 * pairs), dma(pairs)],
        compiler_params=pltpu.CompilerParams(
            collective_id=2, has_side_effects=True, vmem_limit_bytes=48 << 20
        ),
    )(x, w_qkv, vec, seg, mask, w_out, w_down, w_in)


def by_rows(count, body):
    lax.fori_loop(0, count // 16, lambda i, carry: (body(aligned(i * 16, 16)), carry)[1], 0)


class Reduce:
    def __init__(self, place, grad, out, quartered, bufs, sems, direct=False):
        self.place, self.grad, self.out, self.quartered, self.direct = place, grad, out, quartered, direct
        self.rows, self.cols = out.shape
        self.wide = self.cols // 4
        self.acc, self.own, self.relay_in, self.quarter_in, self.z_in, self.total = bufs
        self.own_sem, self.put_sem, self.cs, self.rs, self.qs, self.zs, self.fs, self.gs = sems

    @staticmethod
    def scratch(depth, rows, cols, quartered, direct=False):
        held = cols // 4 if quartered else cols
        side = (1, 1, 16, LANES) if quartered else None
        return [
            pltpu.VMEM((depth, rows, held), BF16),
            pltpu.VMEM((16, LANES) if direct else (rows, held), BF16),
            pltpu.VMEM(side or (2, depth, rows, cols // 8), BF16),
            pltpu.VMEM(side or (2, depth, rows, cols // 4), BF16),
            pltpu.VMEM((depth, rows, cols // 4), BF16),
            pltpu.VMEM((rows, cols // 4), BF16),
            dma(),
            dma(),
        ] + [dma(depth)] * 12 + [dma(2)] * 4

    @staticmethod
    def take(place, grad, out, quartered, refs, direct=False):
        s = refs[8:]
        pairs = [(s[i], s[i + 1]) for i in range(0, 16, 2)]
        sems = (refs[6], refs[7], pairs[0], pairs[1:3], pairs[3:5], pairs[5], pairs[6], pairs[7])
        return Reduce(place, grad, out, quartered, refs[:6], sems, direct)

    def quarter(self, seat):
        return aligned(seat * self.wide, self.wide)

    def mine(self):
        return pl.ds(0, self.wide) if self.quartered else self.quarter(self.place.s)

    def piece(self, seat, half):
        return aligned(seat * self.wide + half * (self.wide // 2), self.wide // 2)

    def own_copy(self, step):
        p = self.place
        rows = aligned((2 * p.far(step) + p.c) * self.rows, self.rows)
        return pltpu.make_async_copy(self.grad.at[rows], self.own, self.own_sem)

    def core_copy(self, step):
        p = self.place
        rows = aligned((2 * p.far(step) + 1 - p.c) * self.rows, self.rows)
        return send(self.grad.at[rows], self.acc.at[step], self.cs, step, p.beside)

    def relay_copy(self, step, way):
        p = self.place
        src = self.acc.at[step, :, self.piece(p.s3, way)]
        return send(src, self.relay_in.at[way, step], self.rs[way], step, p.across(way))

    def quarter_copy(self, step, way):
        p = self.place
        src = self.acc.at[step, :, self.quarter((p.s1, p.s2)[way])]
        return send(src, self.quarter_in.at[way, step], self.qs[way], step, p.across(way))

    def z_copy(self, step):
        p = self.place
        src = self.acc.at[step, :, self.mine()]
        return send(src, self.z_in.at[step], self.zs, step, p.along(p.far(step)))

    def put_copy(self):
        return pltpu.make_async_copy(self.total, self.out.at[:, self.quarter(self.place.s)], self.put_sem)

    def total_copy(self, way):
        p = self.place
        return send(self.total, self.out.at[:, self.quarter(p.s)], self.fs, way, p.across(way))

    def total_arrival(self, way):
        p = self.place
        there = self.out.at[:, self.quarter((p.s1, p.s2)[way])]
        return send(there, there, self.fs, way, p.across(way))

    def back_copy(self, way):
        p = self.place
        there = self.out.at[:, self.piece((p.s2, p.s1)[way], 1 - way)]
        return send(there, there, self.gs, way, p.across(way))

    def back_arrival(self, way):
        p = self.place
        there = self.out.at[:, self.piece(p.s3, 1 - way)]
        return send(there, there, self.gs, way, p.across(way))

    def begin(self):
        depth = self.place.depth
        self.place.each(1, depth, lambda step: self.core_copy(step).start())
        self.core_copy(0).start()
        self.own_copy(1).start()

    def fold(self, step, following):
        p, acc, own = self.place, self.acc, self.own
        self.core_copy(step).wait_recv()
        if not self.direct:
            self.own_copy(step).wait()
        base = (2 * p.far(step) + p.c) * self.rows

        def body(index, carry):
            rows = aligned(index * 16, 16)
            added = self.grad[aligned(base + index * 16, 16), :] if self.direct else own[rows, :]
            acc[step, rows, :] = (acc[step, rows, :].astype(F32) + added.astype(F32)).astype(BF16)
            return carry

        lax.fori_loop(0, self.rows // 16, body, 0)
        if following is not None:
            self.own_copy(following).start()
        if not self.quartered:
            for way in (0, 1):
                self.relay_copy(step, way).start()
        elif not (isinstance(step, int) and step == 0):
            self.z_copy(step).start()

    def swap(self, step):
        if self.quartered:
            return
        p, acc = self.place, self.acc
        for way in (0, 1):
            self.relay_copy(step, way).wait_recv()
            cols = self.piece((p.s2, p.s1)[way], way)
            came = self.relay_in.at[way, step]

            def body(rows):
                acc[step, rows, cols] = (acc[step, rows, cols].astype(F32) + came[rows, :].astype(F32)).astype(BF16)

            by_rows(self.rows, body)
        for way in (0, 1):
            self.quarter_copy(step, way).start()

    def close(self, step, own):
        if self.quartered:
            return
        p, acc, came = self.place, self.acc, self.quarter_in
        for way in (0, 1):
            self.quarter_copy(step, way).wait_recv()
        cols = self.quarter(p.s)

        def body(rows):
            acc[step, rows, cols] = (
                acc[step, rows, cols].astype(F32)
                + came[0, step, rows, :].astype(F32)
                + came[1, step, rows, :].astype(F32)
            ).astype(BF16)

        by_rows(self.rows, body)
        pl.when(jnp.logical_not(own))(lambda: self.z_copy(step).start())

    def collect(self):
        p, acc, came, total = self.place, self.acc, self.z_in, self.total
        p.each(1, p.depth, lambda step: self.z_copy(step).wait_recv())
        cols = self.mine()

        def body(rows):
            start = acc[0, rows, cols].astype(F32)
            if p.depth <= 8:
                for step in range(1, p.depth):
                    start = start + came[step, rows, :].astype(F32)
            else:
                start = lax.fori_loop(1, p.depth, lambda step, sofar: sofar + came[step, rows, :].astype(F32), start)
            total[rows, :] = start.astype(BF16)

        by_rows(self.rows, body)
        for way in (0, 1):
            self.total_copy(way).start()
        self.put_copy().start()

    def spread(self):
        for way in (0, 1):
            self.total_arrival(way).wait_recv()
        for way in (0, 1):
            self.back_copy(way).start()

    def finish(self):
        for way in (0, 1):
            self.back_arrival(way).wait_recv()
        self.put_copy().wait()

        def done(step):
            self.core_copy(step).wait_send()
            if not self.quartered:
                for way in (0, 1):
                    self.relay_copy(step, way).wait_send()
                    self.quarter_copy(step, way).wait_send()

        self.place.each(0, self.place.depth, done)
        self.place.each(1, self.place.depth, lambda step: self.z_copy(step).wait_send())
        for way in (0, 1):
            self.total_copy(way).wait_send()
            self.back_copy(way).wait_send()


REDUCE_REFS = 24


def reduce_steps(place, reduces, between):
    depth = place.depth
    work = list(between)

    def gap():
        if work:
            work.pop(0)()

    if depth <= 8:
        order = [(t + 1) % depth for t in range(depth)]
        for t in range(depth + 2):
            for one in reduces:
                if t < depth:
                    one.fold(order[t], order[t + 1] if t + 1 < depth else None)
                if 0 <= t - 1 < depth:
                    one.swap(order[t - 1])
                if 0 <= t - 2 < depth:
                    one.close(order[t - 2], order[t - 2] == 0)
                gap()
    else:
        def run(first, last, body):
            lax.fori_loop(first, last, lambda step, carry: (body(step), carry)[1], 0)

        for one in reduces:
            run(1, depth, lambda step: one.fold(step, lax.rem(step + 1, depth)))
            one.fold(0, None)
            run(0, depth, one.swap)
            run(1, depth, lambda step: one.close(step, False))
            one.close(0, True)
    for rest in work:
        rest()


def backward_unit(
    pair, odd, half, tile, heads_ref, mask_ref, qd_ref, kf_ref, go_ref, lse_ref, out_ref, keys_sc, values_sc, keys_t, p_sc, s_sc, k_acc, v_acc
):
    length = heads_ref.shape[0]
    span = p_sc.shape[1]
    scale = jnp.asarray(1.0 / math.sqrt(DH), BF16)
    q_cols, k_cols, v_cols = (pl.ds((3 * pair + i) * LANES, LANES) for i in range(3))
    cols = pl.ds(pair * LANES, LANES)
    mine = own_lanes(odd, (length, LANES))
    if half == 0:
        keys_sc[...] = jnp.where(mine, heads_ref[:, k_cols], kf_ref[...])
        values_sc[...] = jnp.where(mine, heads_ref[:, v_cols], jnp.zeros((), BF16))
        if not odd:
            keys_t[...] = heads_ref[:, k_cols].T

    def one_tile(index, carry):
        here = aligned(index * tile, tile)
        rows = aligned(half * span + index * tile, tile)
        lanes = own_lanes(odd, (tile, LANES))
        queries = query_tile(
            heads_ref[rows, q_cols],
            qd_ref[rows, :],
            mask_ref,
            2 * pair + odd,
            half * (span // BLK) + index * (tile // BLK),
            lanes,
        )
        prob = jnp.exp(dot_nt(keys_sc[...], queries) - lse_ref[pair, pl.ds(odd, 1), rows])
        grad_prob = dot_nt(values_sc[...], go_ref[rows, cols])
        delta = jnp.sum(prob * grad_prob, axis=0, keepdims=True)
        p_sc[:, here] = prob.astype(BF16)
        s_sc[:, here] = (prob * (grad_prob - delta)).astype(BF16)
        return carry

    lax.fori_loop(0, span // tile, one_tile, 0)
    part = pl.ds(half * span, span)
    grad_v = dot_nn(p_sc[...], go_ref[part, cols])
    grad_k = dot_nn(s_sc[...], heads_ref[part, q_cols] * scale)
    grad_q = (dot_nn(keys_t[...], s_sc[...]) * (1.0 / math.sqrt(DH))).T.astype(BF16)
    last = half * span + span == length

    def put(rows, columns, value, keep):
        if odd:
            value = jnp.where(keep, value, out_ref[rows, columns])
        out_ref[rows, columns] = value

    put(part, q_cols, grad_q, own_lanes(odd, (span, LANES)))
    if half > 0:
        grad_v, grad_k = grad_v + v_acc[...], grad_k + k_acc[...]
    if last:
        put(pl.ds(0, length), k_cols, grad_k.astype(BF16), mine)
        put(pl.ds(0, length), v_cols, grad_v.astype(BF16), mine)
    else:
        v_acc[...], k_acc[...] = grad_v, grad_k


def backward_kernel(
    fsdp_count,
    go_rows_ref,
    heads_ref,
    mask_ref,
    qd_ref,
    kf_ref,
    lse_ref,
    n1_ref,
    wq_ref,
    x_ref,
    hid_ref,
    vec_ref,
    small_ref,
    out_g_ref,
    in_g_ref,
    tokens_out,
    small_out,
    qkv_total,
    out_total,
    in_total,
    go_sc,
    grads_sc,
    keys_sc,
    values_sc,
    keys_t,
    p_sc,
    s_sc,
    k_acc,
    v_acc,
    n1_sc,
    qkv_g,
    part_sc,
    part_in,
    half_in,
    small_sc,
    small_in,
    *rest,
):
    place = Place(fsdp_count)
    rows = go_rows_ref.shape[0]
    reduces = [
        Reduce.take(place, grad, out, False, rest[i * REDUCE_REFS : (i + 1) * REDUCE_REFS])
        for i, (grad, out) in enumerate(
            ((out_g_ref, out_total), (in_g_ref, in_total))
        )
    ]
    first = Reduce.take(place, qkv_g, qkv_total, True, rest[2 * REDUCE_REFS : 3 * REDUCE_REFS])
    g_own, n_own, g_sent, g_got, h_sent, h_got, p_sent, p_got, c_sent, c_got, z_sent, z_got, x_sent, x_got = rest[
        3 * REDUCE_REFS :
    ]
    seats = (place.s1, place.s2, place.s3)
    width = go_sc.shape[1]
    pairs = width // LANES
    half = rows // 2

    def part(seat):
        return go_rows_ref.at[:, aligned(seat * width, width)]

    def slot(seat):
        return go_sc.at[aligned(seat * rows, rows)]

    place.meet()
    for way in range(3):
        send(part(seats[way]), slot(place.s), (g_sent, g_got), way, place.across(way)).start()
    own = pltpu.make_async_copy(part(place.s), slot(place.s), g_own)
    own.start()
    for one in reduces:
        one.begin()
    n1_copy = pltpu.make_async_copy(n1_ref, n1_sc, n_own)
    n1_copy.start()
    own.wait()
    for way in range(3):
        send(slot(seats[way]), slot(seats[way]), (g_sent, g_got), way, place.across(way)).wait_recv()

    def unit(pair, odd, side):
        backward_unit(
            pair, odd, side, 256, heads_ref, mask_ref, qd_ref, kf_ref, go_sc, lse_ref, grads_sc,
            keys_sc, values_sc, keys_t, p_sc, s_sc, k_acc, v_acc,
        )

    def half_copy(way):
        src = part_sc.at[aligned(place.s3 * rows + way * half, half)]
        return send(src, half_in.at[way], (h_sent, h_got), way, place.across(way))

    def part_copy(way):
        src = part_sc.at[aligned(seats[way] * rows, rows)]
        return send(src, part_in.at[way], (p_sent, p_got), way, place.across(way))

    def partial_dn1():
        def body(index):
            here = aligned(index * rows, rows)
            part_sc[here, :] = dot_nt(grads_sc[here, :], wq_ref[...]).astype(BF16)

        lax.fori_loop(0, 4, lambda index, carry: (body(index), carry)[1], 0)
        for way in (0, 1):
            half_copy(way).start()

    def weight_grad():
        n1_copy.wait()

        def body(index):
            cols = aligned(index * 256, 256)
            qkv_g[cols, :] = dot_tn(n1_sc[:, cols], grads_sc[...]).astype(BF16)

        lax.fori_loop(0, qkv_g.shape[0] // 256, lambda index, carry: (body(index), carry)[1], 0)
        first.begin()

    def swap_dn1():
        for way in (0, 1):
            half_copy(way).wait_recv()
            base = (place.s2, place.s1)[way] * rows + way * half

            def body(index):
                here = aligned(base + index * 32, 32)
                came = half_in[way, aligned(index * 32, 32), :]
                part_sc[here, :] = (part_sc[here, :].astype(F32) + came.astype(F32)).astype(BF16)

            lax.fori_loop(0, half // 32, lambda index, carry: (body(index), carry)[1], 0)
        for way in (0, 1):
            part_copy(way).start()

    def fold_first():
        depth = place.depth
        place.each(1, depth, lambda step: first.fold(step, lax.rem(step + 1, depth)))
        first.fold(0, None)

    def core_small():
        return send(small_sc.at[0], small_sc.at[1], (c_sent, c_got), 0, place.beside)

    def z_small(step):
        return send(small_sc.at[2], small_in.at[step], (z_sent, z_got), step, place.along(place.far(step)))

    def x_small(way):
        return send(small_sc.at[3], small_sc.at[4 + way], (x_sent, x_got), way, place.across(way))

    def close_dn1():
        for way in (0, 1):
            part_copy(way).wait_recv()
        gain = vec_ref[0:1, :]

        def body(index, sums):
            here = aligned(index * 32, 32)
            mine = aligned(place.s * rows + index * 32, 32)
            dn1 = (
                part_sc[mine, :].astype(F32)
                + part_in[0, here, :].astype(F32)
                + part_in[1, here, :].astype(F32)
            )
            token_rows = x_ref[here, :].astype(F32)
            center = token_rows - jnp.mean(token_rows, axis=-1, keepdims=True)
            inv = lax.rsqrt(jnp.mean(center * center, axis=-1, keepdims=True) + 1e-05)
            hat = center * inv
            scaled = dn1 * gain
            grad = hid_ref[here, :] + inv * (
                scaled
                - jnp.mean(scaled, axis=-1, keepdims=True)
                - hat * jnp.mean(scaled * hat, axis=-1, keepdims=True)
            )
            tokens_out[here, :] = grad.astype(BF16)
            return (
                sums[0] + jnp.sum(dn1 * hat, axis=0, keepdims=True),
                sums[1] + jnp.sum(dn1, axis=0, keepdims=True),
            )

        none = jnp.zeros((1, x_ref.shape[1]), F32)
        gain_sum, bias_sum = lax.fori_loop(0, rows // 32, body, (none, none))
        small_sc[0] = small_ref[...]
        small_sc[0, 0:1, :] = gain_sum
        small_sc[0, 1:2, :] = bias_sum
        core_small().start()

    def small_z():
        core_small().wait_recv()
        small_sc[2] = small_sc[0] + small_sc[1]
        place.each(1, place.depth, lambda step: z_small(step).start())

    def small_x():
        place.each(1, place.depth, lambda step: z_small(step).wait_recv())
        small_in[0] = small_sc[2]
        if place.depth <= 8:
            total = small_in[place.back(0)]
            for z in range(1, place.depth):
                total = total + small_in[place.back(z)]
        else:
            total = lax.fori_loop(
                1, place.depth, lambda z, sofar: sofar + small_in[place.back(z)], small_in[place.back(0)]
            )
        small_sc[3] = total
        for way in range(3):
            x_small(way).start()

    def small_end():
        for way in range(3):
            x_small(way).wait_recv()
        small_out[...] = (small_sc[3] + small_sc[4]) + (small_sc[5] + small_sc[6])

    units = [
        functools.partial(unit, pair, odd, side) for pair in range(pairs) for odd in (0, 1) for side in (0, 1)
    ]
    reduce_steps(
        place,
        reduces,
        units + [partial_dn1, weight_grad, swap_dn1, fold_first, close_dn1, small_z],
    )
    for one in [first] + reduces:
        one.collect()
    small_x()
    for one in [first] + reduces:
        one.spread()
    small_end()
    core_small().wait_send()
    place.each(1, place.depth, lambda step: z_small(step).wait_send())
    for way in range(3):
        send(part(seats[way]), slot(place.s), (g_sent, g_got), way, place.across(way)).wait_send()
        x_small(way).wait_send()
        if way < 2:
            half_copy(way).wait_send()
            part_copy(way).wait_send()
    for one in [first] + reduces:
        one.finish()


def backward_attention(fsdp_count, grad_att, saved, x, hid, small, grads):
    heads, mask, qd, kf, lse, n1, wq, vec = saved
    rows, width = grad_att.shape
    length = heads.shape[0]
    own_width = width // 4
    depth = fsdp_count // 2
    span = length // 2
    anywhere = pl.BlockSpec(memory_space=pl.ANY)
    vmem = pl.BlockSpec(memory_space=pltpu.VMEM)
    share = wq.shape[0] // fsdp_count
    kept = [(grad.shape[0] // fsdp_count, grad.shape[1]) for grad in grads]
    kept_qkv = (share, 4 * wq.shape[1])
    shape = jax.ShapeDtypeStruct

    reduce_scratch = []
    for one in kept:
        reduce_scratch += Reduce.scratch(depth, *one, False)
    reduce_scratch += Reduce.scratch(depth, *kept_qkv, True)
    return pl.pallas_call(
        functools.partial(backward_kernel, fsdp_count),
        out_shape=(shape(x.shape, BF16), shape(small.shape, F32), shape(kept_qkv, BF16))
        + tuple(shape(one, BF16) for one in kept),
        in_specs=[anywhere] + [vmem] * 5 + [anywhere] + [vmem] * 5 + [anywhere] * 2,
        out_specs=(vmem, vmem, anywhere, anywhere, anywhere),
        scratch_shapes=[
            pltpu.VMEM((length, own_width), BF16),
            pltpu.VMEM((length, 3 * own_width), BF16),
            pltpu.VMEM((length, LANES), BF16),
            pltpu.VMEM((length, LANES), BF16),
            pltpu.VMEM((LANES, length), BF16),
            pltpu.VMEM((length, span), BF16),
            pltpu.VMEM((length, span), BF16),
            pltpu.VMEM((length, LANES), F32),
            pltpu.VMEM((length, LANES), F32),
            pltpu.VMEM((length, width), BF16),
            pltpu.VMEM(wq.shape, BF16),
            pltpu.VMEM((length, width), BF16),
            pltpu.VMEM((2, rows, width), BF16),
            pltpu.VMEM((2, rows // 2, width), BF16),
            pltpu.VMEM((7,) + small.shape, F32),
            pltpu.VMEM((depth,) + small.shape, F32),
        ]
        + reduce_scratch
        + [dma(), dma(), dma(3), dma(3), dma(2), dma(2), dma(2), dma(2)]
        + [dma(1), dma(1), dma(depth), dma(depth), dma(3), dma(3)],
        compiler_params=pltpu.CompilerParams(
            collective_id=3, has_side_effects=True, vmem_limit_bytes=60 << 20
        ),
    )(grad_att, heads, mask, qd, kf, lse, n1, wq, x, hid, vec, small, *grads)


def middle_kernel(
    fsdp_count,
    att_ref,
    x_ref,
    cot_ref,
    vec_ref,
    out_w_ref,
    in_w_ref,
    down_w_ref,
    result_ref,
    datt_ref,
    hid_ref,
    small_ref,
    out_g_ref,
    in_g_ref,
    down_total,
    hidden_sc,
    n2_sc,
    n2_t,
    out_acc,
    dn2_acc,
    in_buf,
    down_buf,
    grad_buf,
    down_g,
    in_sems,
    down_sems,
    grad_sems,
    *rest,
):
    place = Place(fsdp_count)
    depth = place.depth
    total = Reduce.take(place, down_g, down_total, False, rest, True)
    rows, width = x_ref.shape
    span = down_buf.shape[1]
    hidden_units = down_g.shape[0]
    chunks = hidden_units // span
    paired = total.rows == span
    lines = rows // 32

    def order(index):
        if not paired:
            return index
        z = place.far(lax.rem(lax.div(index, 2) + 1, depth))
        return 2 * z + jnp.where(lax.rem(index, 2) == 0, 1 - place.c, place.c)

    def in_load(index):
        slot = lax.rem(index, 2)
        return pltpu.make_async_copy(
            in_w_ref.at[:, aligned(order(index) * span, span)], in_buf.at[slot], in_sems.at[slot]
        )

    def down_load(index):
        slot = lax.rem(index, 2)
        return pltpu.make_async_copy(
            down_w_ref.at[aligned(order(index) * span, span)], down_buf.at[slot], down_sems.at[slot]
        )

    def grad_store(index):
        slot = lax.rem(index, 2)
        return pltpu.make_async_copy(
            grad_buf.at[slot], in_g_ref.at[:, aligned(order(index) * span, span)], grad_sems.at[slot]
        )

    def over_rows(body, start=0):
        return lax.fori_loop(0, lines, lambda index, carry: body(aligned(index * 32, 32), carry), start)

    in_load(0).start()
    down_load(0).start()
    place.meet()
    hidden_sc[...] = x_ref[...].astype(F32) + dot_nn(att_ref[...], out_w_ref[...])

    def normalise(here, carry):
        token_rows = hidden_sc[here, :]
        center = token_rows - jnp.mean(token_rows, axis=-1, keepdims=True)
        variance = jnp.mean(center * center, axis=-1, keepdims=True)
        normed = center * lax.rsqrt(variance + 1e-05) * vec_ref[2:3, :] + vec_ref[3:4, :]
        n2_sc[here, :] = normed.astype(BF16)
        out_acc[here, :] = token_rows + vec_ref[4:5, :]
        return carry

    over_rows(normalise)
    n2_t[...] = n2_sc[...].T
    dn2_acc[...] = jnp.zeros_like(dn2_acc)
    small_ref[...] = jnp.zeros_like(small_ref)

    def chunk(index):
        slot = lax.rem(index, 2)
        which = order(index)
        in_load(index).wait()
        down_load(index).wait()

        def ahead():
            in_load(index + 1).start()
            down_load(index + 1).start()

        pl.when(index + 1 < chunks)(ahead)
        per = width // span
        line = pl.ds(5 + lax.div(which, per), 1)
        cols = aligned(lax.rem(which, per) * span, span)
        pre = dot_nn(n2_sc[...], in_buf[slot]) + vec_ref[line, cols]
        inner = jnp.tanh(0.7978845608028654 * (pre + 0.044715 * pre * pre * pre))
        act = (0.5 * pre * (1.0 + inner)).astype(BF16)
        slope = 0.5 * (1.0 + inner) + (0.5 * 0.7978845608028654) * pre * (1.0 - inner * inner) * (
            1.0 + (3.0 * 0.044715) * pre * pre
        )
        grad = dot_nt(cot_ref[...], down_buf[slot]) * slope
        low = grad.astype(BF16)
        small_ref[line, cols] = jnp.sum(low.astype(F32), axis=0, keepdims=True)
        down_g[aligned(which * span, span), :] = dot_tn(act, cot_ref[...]).astype(BF16)
        out_acc[...] += dot_nn(act, down_buf[slot])
        dn2_acc[...] += dot_nt(low, in_buf[slot])
        pl.when(index >= 2)(lambda: grad_store(index - 2).wait())
        grad_buf[slot] = dot_nn(n2_t[...], low).astype(BF16)
        grad_store(index).start()

    def later(t):
        pl.when(jnp.logical_and(t >= 1, t <= depth))(lambda: total.swap(lax.rem(t, depth)))
        pl.when(t >= 2)(lambda: total.close(lax.rem(t + depth - 1, depth), t == depth + 1))

    if paired:

        def step(t, carry):
            dest = lax.rem(t + 1, depth)

            def one(side, carry):
                chunk(2 * t + side)
                pl.when(side == 0)(lambda: total.core_copy(dest).start())
                return carry

            lax.fori_loop(0, 2, one, 0)
            total.fold(dest, None)
            later(t)
            return carry

        lax.fori_loop(0, depth, step, 0)
    else:
        lax.fori_loop(0, chunks, lambda index, carry: (chunk(index), carry)[1], 0)
        place.each(0, depth, lambda step: total.core_copy(step).start())

        def step(t, carry):
            total.fold(lax.rem(t + 1, depth), None)
            later(t)
            return carry

        lax.fori_loop(0, depth, step, 0)

    def finish(here, sums):
        token_rows = hidden_sc[here, :]
        center = token_rows - jnp.mean(token_rows, axis=-1, keepdims=True)
        inv = lax.rsqrt(jnp.mean(center * center, axis=-1, keepdims=True) + 1e-05)
        hat = center * inv
        dn2 = dn2_acc[here, :]
        cot = cot_ref[here, :].astype(F32)
        scaled = dn2 * vec_ref[2:3, :]
        grad = cot + inv * (
            scaled
            - jnp.mean(scaled, axis=-1, keepdims=True)
            - hat * jnp.mean(scaled * hat, axis=-1, keepdims=True)
        )
        hid_ref[here, :] = grad
        n2_sc[here, :] = grad.astype(BF16)
        result_ref[here, :] = out_acc[here, :].astype(BF16)
        return (
            sums[0] + jnp.sum(dn2 * hat, axis=0, keepdims=True),
            sums[1] + jnp.sum(dn2, axis=0, keepdims=True),
            sums[2] + jnp.sum(cot, axis=0, keepdims=True),
        )

    none = jnp.zeros((1, width), F32)
    gain_sum, bias_sum, cot_sum = over_rows(finish, (none, none, none))
    small_ref[2:3, :] = gain_sum
    small_ref[3:4, :] = bias_sum
    small_ref[4:5, :] = cot_sum
    later(depth)
    datt_ref[...] = dot_nt(n2_sc[...], out_w_ref[...]).astype(BF16)
    later(depth + 1)
    total.collect()
    out_g_ref[...] = dot_tn(att_ref[...], n2_sc[...]).astype(BF16)
    total.spread()
    for index in (chunks - 2, chunks - 1):
        grad_store(index).wait()
    total.finish()


def middle(fsdp_count, att, x, cot, vec, w_out, w_in, w_down):
    rows, width = x.shape
    hidden_units = w_in.shape[1]
    span = 512
    depth = fsdp_count // 2
    anywhere = pl.BlockSpec(memory_space=pl.ANY)
    vmem = pl.BlockSpec(memory_space=pltpu.VMEM)
    shape = jax.ShapeDtypeStruct
    kept = (hidden_units // fsdp_count, width)
    return pl.pallas_call(
        functools.partial(middle_kernel, fsdp_count),
        out_shape=(
            shape((rows, width), BF16),
            shape((rows, width), BF16),
            shape((rows, width), F32),
            shape(vec.shape, F32),
            shape(w_out.shape, BF16),
            shape(w_in.shape, BF16),
            shape(kept, BF16),
        ),
        in_specs=[vmem] * 5 + [anywhere] * 2,
        out_specs=(vmem,) * 5 + (anywhere,) * 2,
        scratch_shapes=[
            pltpu.VMEM((rows, width), F32),
            pltpu.VMEM((rows, width), BF16),
            pltpu.VMEM((width, rows), BF16),
            pltpu.VMEM((rows, width), F32),
            pltpu.VMEM((rows, width), F32),
            pltpu.VMEM((2, width, span), BF16),
            pltpu.VMEM((2, span, width), BF16),
            pltpu.VMEM((2, width, span), BF16),
            pltpu.VMEM((hidden_units, width), BF16),
            dma(2),
            dma(2),
            dma(2),
        ]
        + Reduce.scratch(depth, *kept, False, True),
        compiler_params=pltpu.CompilerParams(
            collective_id=5, has_side_effects=True, vmem_limit_bytes=58 << 20
        ),
    )(att, x, cot, vec, w_out, w_in, w_down)


def swap_thirds(rows, outer, inner):
    count, width = rows.shape
    return rows.reshape(count, outer, inner, width // (outer * inner)).swapaxes(1, 2).reshape(count, width)


def per_device(
    seq_count,
    fsdp_count,
    tokens,
    segment_ids,
    random_blocks,
    ln1_gain,
    ln1_bias,
    w_qkv,
    w_out,
    ln2_gain,
    ln2_bias,
    w_in,
    b_in,
    w_down,
    b_down,
    cotangent,
):
    groups = w_qkv.shape[1] // (3 * LANES)
    width = tokens.shape[2]
    share = ln1_gain.shape[0]
    position = lax.axis_index("fsdp")

    def placed(vector):
        held = vector.shape[0]
        spread = jnp.tile(vector, fsdp_count).reshape(-1, width)
        owner = jnp.arange(fsdp_count * held, dtype=jnp.int32).reshape(-1, width) // held
        return jnp.where(owner == position, spread, jnp.zeros((), BF16))

    vec = jnp.concatenate(
        [placed(v) for v in (ln1_gain, ln1_bias, ln2_gain, ln2_bias, b_down, b_in)], axis=0
    )
    vec = jnp.pad(vec, ((0, -vec.shape[0] % 16), (0, 0)))
    tok_count = segment_ids.shape[1]
    seg_rows = -(-tok_count // (8 * LANES)) * 8
    seg = jnp.pad(segment_ids[0], (0, seg_rows * LANES - tok_count)).reshape(seg_rows, LANES)
    mask = block_mask(random_blocks)
    by_heads, lse, att_rows, out_weight, down_weight, in_weight, vec, normed_one, own_qkv, query_docs, key_feats = (
        forward_attention(
            fsdp_count, tokens[0], swap_thirds(w_qkv, 3, groups), vec, seg, mask, w_out, w_down, w_in
        )
    )
    result, grad_att, grad_hidden, small, grad_out, grad_in, total_down = middle(
        fsdp_count, att_rows, tokens[0], cotangent[0], vec, out_weight, in_weight, down_weight
    )
    grad_tokens, small, total_qkv, total_out, total_in = backward_attention(
        fsdp_count,
        grad_att,
        (by_heads, mask, query_docs, key_feats, lse, normed_one, own_qkv, vec),
        tokens[0],
        grad_hidden,
        small,
        (grad_out, grad_in),
    )
    parts = [lax.dynamic_slice_in_dim(small[i], position * share, share) for i in range(5)]
    held = b_in.shape[0]
    parts.append(lax.dynamic_slice_in_dim(small[5 : 5 + fsdp_count * held // width].reshape(-1), position * held, held))
    return (
        result[None],
        grad_tokens[None],
        parts[0],
        parts[1],
        swap_thirds(total_qkv, groups, 3).astype(F32),
        total_out.astype(F32),
        parts[2],
        parts[3],
        total_in.astype(F32),
        parts[5],
        total_down.astype(F32),
        parts[4],
    )


def solution(mesh):
    return jax.shard_map(
        functools.partial(per_device, mesh.shape["seq"], mesh.shape["fsdp"]),
        mesh=mesh,
        in_specs=(
            P("fsdp", "seq", None),
            P("fsdp", "seq"),
            P("seq", None, None),
            P("fsdp"),
            P("fsdp"),
            P("fsdp", None),
            P("fsdp", None),
            P("fsdp"),
            P("fsdp"),
            P("fsdp", None),
            P("fsdp"),
            P("fsdp", None),
            P("fsdp"),
            P("fsdp", "seq", None),
        ),
        out_specs=(
            P("fsdp", "seq", None),
            P("fsdp", "seq", None),
            P("fsdp"),
            P("fsdp"),
            P("fsdp", None),
            P("fsdp", None),
            P("fsdp"),
            P("fsdp"),
            P("fsdp", None),
            P("fsdp"),
            P("fsdp", None),
            P("fsdp"),
        ),
        check_vma=False,
    )
```

```python
import functools
import math

import jax
import jax.numpy as jnp
from jax import lax
from jax.experimental import pallas as pl
from jax.experimental.pallas import tpu as pltpu
from jax.sharding import PartitionSpec as P

DH = 64
BLK = 64
LANES = 128
NEG = -1e30
F32 = jnp.float32
BF16 = jnp.bfloat16


def dot_nn(a, b):
    return jnp.dot(a, b, preferred_element_type=F32)


def dot_nt(a, b):
    return lax.dot_general(a, b, (((1,), (1,)), ((), ())), preferred_element_type=F32)


def dot_tn(a, b):
    return lax.dot_general(a, b, (((0,), (0,)), ((), ())), preferred_element_type=F32)


DOCS = 6


def block_mask(random_blocks):
    heads, inner, _ = random_blocks.shape
    blocks = inner + 2
    ids = jnp.arange(blocks, dtype=jnp.int32)
    near = jnp.abs(ids[:, None] - ids[None, :]) <= 1
    edge = (ids == 0) | (ids == blocks - 1)
    fixed = near | edge[:, None] | edge[None, :]
    picked = jnp.any(random_blocks[:, :, :, None] == ids, axis=2)
    used = fixed[None] | jnp.pad(picked, ((0, 0), (1, 1), (0, 0)))
    row = jnp.pad(jnp.where(used, 0.0, NEG), ((0, 0), (0, 0), (0, DH - blocks)))
    return jnp.concatenate([row, row], axis=-1)


def token_features(start, docs, blocks):
    shape = (docs.shape[0], LANES)
    lane = lax.rem(lax.broadcasted_iota(jnp.int32, shape, 1), DH)
    block = lax.div(lax.broadcasted_iota(jnp.int32, shape, 0) + start, BLK)
    own = docs + blocks == lane
    other = jnp.where(own | (lane >= blocks + DOCS), 0.0, 1.0)
    key_part = jnp.where(lane < blocks, jnp.where(block == lane, 1.0, 0.0), other)
    return jnp.where(own, NEG, 0.0).astype(BF16), key_part.astype(BF16)


def query_tile(q_tile, doc_tile, mask_ref, head, first_block, lanes):
    scale = jnp.asarray(1.0 / math.sqrt(DH), BF16)
    count = q_tile.shape[0] // BLK
    mask = jnp.concatenate(
        [jnp.broadcast_to(mask_ref[head, pl.ds(first_block + i, 1), :], (BLK, LANES)) for i in range(count)], axis=0
    )
    return jnp.where(lanes, q_tile * scale, doc_tile + mask.astype(BF16))


def own_lanes(odd, shape):
    lane = lax.broadcasted_iota(jnp.int32, shape, 1)
    return (lane >= DH) if odd else (lane < DH)


MESH = pl.DeviceIdType.MESH


class Place:
    def __init__(self, fsdp_count):
        self.depth = fsdp_count // 2
        self.s = lax.axis_index("seq")
        self.f = lax.axis_index("fsdp")
        self.z = lax.div(self.f, 2)
        self.c = lax.rem(self.f, 2)
        self.s1 = self.s + 1 - 2 * lax.rem(self.s, 2)
        self.s2 = self.s + 2 - 4 * lax.div(self.s, 2)
        self.s3 = 3 - self.s
        self.beside = (self.s, self.f + 1 - 2 * self.c)

    def across(self, index):
        return ((self.s1, self.s2, self.s3)[index], self.f)

    def far(self, step):
        return lax.rem(self.z + step, self.depth)

    def back(self, step):
        return lax.rem(self.z + self.depth - step, self.depth)

    def along(self, z):
        return (self.s, 2 * z + self.c)

    def meet(self):
        barrier = pltpu.get_barrier_semaphore()
        peers = [self.beside] + [self.across(i) for i in range(3)]
        for peer in peers:
            pl.semaphore_signal(barrier, inc=1, device_id=peer, device_id_type=MESH)
        self.each(1, self.depth, lambda step: pl.semaphore_signal(
            barrier, inc=1, device_id=self.along(self.far(step)), device_id_type=MESH
        ))
        pl.semaphore_wait(barrier, len(peers) + self.depth - 1)

    def each(self, start, stop, body):
        if stop - start <= 8:
            for step in range(start, stop):
                body(step)
        else:
            lax.fori_loop(start, stop, lambda step, carry: (body(step), carry)[1], 0)


def send(src, dst, sems, index, device):
    sent, got = sems
    return pltpu.make_async_remote_copy(
        src_ref=src,
        dst_ref=dst,
        send_sem=sent.at[index],
        recv_sem=got.at[index],
        device_id=device,
        device_id_type=MESH,
    )


def aligned(start, size):
    return pl.ds(pl.multiple_of(start, size), size)


class Gather:
    def __init__(self, place, src, dst, split, sems):
        self.place, self.src, self.dst, self.split = place, src, dst, split
        self.rows, self.cols = src.shape
        self.local, self.zs, self.xs, self.rs, self.cs = sems

    def block(self, z, core, quarter=None, half=None):
        rows = aligned((2 * z + core) * self.rows, self.rows)
        if quarter is None:
            return self.dst.at[rows]
        wide = self.cols // 4
        if half is None:
            return self.dst.at[rows, aligned(quarter * wide, wide)]
        return self.dst.at[rows, aligned(quarter * wide + half * (wide // 2), wide // 2)]

    def source(self, step, side):
        return self.place.z - step if side == 0 else self.place.z + step

    def has(self, step, side):
        z = self.source(step, side)
        return z >= 0 if side == 0 else z < self.place.depth

    def sends(self, step, side):
        p = self.place
        onward = p.z + 1 < p.depth if side == 0 else p.z > 0
        return jnp.logical_and(self.has(step - 1, side), onward)

    def slot(self, step, side):
        return 2 * step + side

    def own_copy(self):
        return pltpu.make_async_copy(self.src, self.block(self.place.z, self.place.c), self.local)

    def own_core(self):
        p = self.place
        return send(self.src, self.block(p.z, p.c), self.cs, 0, p.beside)

    def own_arrival(self):
        p = self.place
        there = self.block(p.z, 1 - p.c)
        return send(there, there, self.cs, 0, p.beside)

    def core_copy(self, step, side):
        p = self.place
        there = self.block(self.source(step, side), p.c)
        return send(there, there, self.cs, self.slot(step, side), p.beside)

    def core_arrival(self, step, side):
        p = self.place
        there = self.block(self.source(step, side), 1 - p.c)
        return send(there, there, self.cs, self.slot(step, side), p.beside)

    def z_copy(self, step, side):
        p = self.place
        z = self.source(step - 1, side)
        there = self.block(z, p.c, p.s) if self.split else self.block(z, p.c)
        src = there
        if isinstance(step, int) and step == 1:
            wide = self.cols // 4
            src = self.src.at[:, aligned(p.s * wide, wide)] if self.split else self.src
        return send(src, there, self.zs, self.slot(step, side), p.along(p.z + 1 - 2 * side))

    def z_arrival(self, step, side):
        p = self.place
        z = self.source(step, side)
        there = self.block(z, p.c, p.s) if self.split else self.block(z, p.c)
        return send(there, there, self.zs, self.slot(step, side), p.along(p.z - 1 + 2 * side))

    def x_copy(self, step, side, way):
        p = self.place
        there = self.block(self.source(step, side), p.c, p.s)
        return send(there, there, self.xs[way], self.slot(step, side), p.across(way))

    def x_arrival(self, step, side, way):
        p = self.place
        there = self.block(self.source(step, side), p.c, (p.s1, p.s2)[way])
        return send(there, there, self.xs[way], self.slot(step, side), p.across(way))

    def relay_copy(self, step, side, way):
        p = self.place
        there = self.block(self.source(step, side), p.c, (p.s2, p.s1)[way], 1 - way)
        return send(there, there, self.rs[way], self.slot(step, side), p.across(way))

    def relay_arrival(self, step, side, way):
        p = self.place
        there = self.block(self.source(step, side), p.c, p.s3, 1 - way)
        return send(there, there, self.rs[way], self.slot(step, side), p.across(way))

    def both(self, step, body, test=None):
        for side in (0, 1):
            pl.when((test or self.has)(step, side))(functools.partial(body, step, side))

    def begin(self):
        self.both(1, lambda step, side: self.z_copy(step, side).start(), self.sends)
        self.own_copy().start()
        self.own_core().start()

    def swap(self, step):
        def body(step, side):
            self.z_arrival(step, side).wait_recv()
            pl.when(self.sends(step + 1, side))(lambda: self.z_copy(step + 1, side).start())
            if self.split:
                for way in (0, 1):
                    self.x_copy(step, side, way).start()
            else:
                self.core_copy(step, side).start()

        self.both(step, body)

    def relay(self, step):
        def body(step, side):
            for way in (0, 1):
                self.x_arrival(step, side, way).wait_recv()
            for way in (0, 1):
                self.relay_copy(step, side, way).start()

        if self.split:
            self.both(step, body)

    def share(self, step):
        def body(step, side):
            for way in (0, 1):
                self.relay_arrival(step, side, way).wait_recv()
            self.core_copy(step, side).start()

        if self.split:
            self.both(step, body)

    def finish(self):
        self.own_copy().wait()
        self.own_core().wait_send()
        self.own_arrival().wait_recv()

        def close(step, side):
            if self.split:
                for way in (0, 1):
                    self.x_copy(step, side, way).wait_send()
                    self.relay_copy(step, side, way).wait_send()
            self.core_copy(step, side).wait_send()
            self.core_arrival(step, side).wait_recv()

        self.place.each(1, self.place.depth, lambda step: self.both(step, close))
        self.place.each(
            1,
            self.place.depth,
            lambda step: self.both(step, lambda step, side: self.z_copy(step, side).wait_send(), self.sends),
        )

    @staticmethod
    def scratch(depth, split):
        held = 2 * depth if split else 1
        return [dma()] + [dma(2 * depth)] * 2 + [dma(held)] * 8 + [dma(2 * depth)] * 2

    @staticmethod
    def take(refs):
        pairs = [(refs[i], refs[i + 1]) for i in range(1, 13, 2)]
        return (refs[0], pairs[0], pairs[1:3], pairs[3:5], pairs[5])


GATHER_SEMS = 13


def gather_steps(place, gathers, late, between):
    depth = place.depth
    work = list(between)

    def gap():
        if work:
            work.pop(0)()

    def stage(step, swap, relay, share, gap):
        if swap:
            for one in gathers:
                one.swap(step)
        if relay:
            for one in gathers:
                one.relay(step - 1)
            gap()
        if swap:
            for one in late:
                one.swap(step - 1)
        if share:
            for one in gathers:
                one.share(step - 2)

    for one in late:
        one.begin()
    gap()
    if depth <= 8:
        for step in range(2, depth + 2):
            stage(step, step < depth, step <= depth, step >= 3, gap)
    else:
        stage(2, True, True, False, gap)
        lax.fori_loop(3, depth, lambda step, carry: (stage(step, True, True, True, lambda: None), carry)[1], 0)
        stage(depth, False, True, True, gap)
        stage(depth + 1, False, False, True, gap)
    for one in late:
        one.swap(depth - 1)
    for rest in work:
        rest()


def dma(*shape):
    return pltpu.SemaphoreType.DMA(shape) if shape else pltpu.SemaphoreType.DMA


def attend_unit(pair, odd, tile, heads_ref, mask_ref, qd_ref, kf_ref, keys_sc, values_t, out_ref, lse_ref):
    length = heads_ref.shape[0]
    cols = pl.ds(pair * LANES, LANES)
    q_cols, k_cols, v_cols = (pl.ds(i * heads_ref.shape[1] // 3 + pair * LANES, LANES) for i in range(3))
    if not odd:
        values_t[...] = heads_ref[:, v_cols].T
    mine = own_lanes(odd, (length, LANES))
    keys_sc[...] = jnp.where(mine, heads_ref[:, k_cols], kf_ref[...])

    def one_tile(index, carry):
        rows = aligned(index * tile, tile)
        lanes = own_lanes(odd, (tile, LANES))
        queries = query_tile(
            heads_ref[rows, q_cols], qd_ref[rows, :], mask_ref, 2 * pair + odd, index * (tile // BLK), lanes
        )
        scores = dot_nt(keys_sc[...], queries)
        top = jnp.max(scores, axis=0, keepdims=True)
        prob = jnp.exp(scores - top)
        total = jnp.sum(prob, axis=0, keepdims=True)
        mixed = dot_nn(values_t[...], prob.astype(BF16)) / total
        lse_ref[pair, pl.ds(odd, 1), rows] = top + jnp.log(total)
        result = mixed.T.astype(BF16)
        if odd:
            out_ref[rows, cols] = jnp.where(lanes, result, out_ref[rows, cols])
        else:
            out_ref[rows, cols] = result
        return carry

    lax.fori_loop(0, length // tile, one_tile, 0, unroll=2)


def forward_kernel(
    fsdp_count,
    x_ref,
    wq_ref,
    vec_ref,
    seg_ref,
    mask_ref,
    out_w_ref,
    down_w_ref,
    in_w_ref,
    heads_all,
    lse_ref,
    att_all,
    out_w_all,
    down_w_all,
    in_w_all,
    vec_sum,
    n1_all,
    wq_all,
    qd_ref,
    kf_ref,
    x_sc,
    n1_sc,
    wq_own,
    wq_sc,
    vec_sc,
    seg_sc,
    heads_sc,
    att_sc,
    keys_sc,
    values_t,
    *sems,
):
    place = Place(fsdp_count)
    rows, width = x_ref.shape
    own_width = wq_sc.shape[1]
    seats = (place.s1, place.s2, place.s3)

    def taken(i):
        return Gather.take(sems[i * GATHER_SEMS : (i + 1) * GATHER_SEMS])

    x_own, seg_own, keep_sems, pick_sems, x_sent, x_got, r_sent, r_got, g_sent, g_got, a_sent, a_got, a_own = sems[6 * GATHER_SEMS :]
    lone = pl.ds(0, in_w_ref.shape[1] // 2)
    shared = pl.ds(in_w_ref.shape[1] // 2, in_w_ref.shape[1] // 2)
    gathers = [
        Gather(place, src, dst, split, taken(i))
        for i, (src, dst, split) in enumerate(
            (
                (out_w_ref, out_w_all, True),
                (in_w_ref.at[:, shared], in_w_all.at[:, shared], True),
                (down_w_ref, down_w_all, True),
                (in_w_ref.at[:, lone], in_w_all.at[:, lone], False),
            )
        )
    ]
    late = [gathers.pop()]
    third = own_width // 3
    picks = [
        pltpu.make_async_copy(
            wq_ref.at[:, aligned((4 * i + place.s) * third, third)], wq_own.at[:, pl.ds(i * third, third)], pick_sems.at[i]
        )
        for i in range(3)
    ]
    for pick in picks:
        pick.start()
    weight = Gather(place, wq_own, wq_sc, False, taken(4))
    vector = Gather(place, vec_ref, vec_sc, False, taken(5))
    half = rows // 2

    def x_rows(seat):
        return x_sc.at[aligned(seat * rows, rows)]

    def x_half(seat, part):
        return x_sc.at[aligned(seat * rows + part * half, half)]

    def x_copy(way):
        return send(x_ref, x_rows(place.s), (x_sent, x_got), way, place.across(way))

    def x_arrival(way):
        there = x_rows(seats[way])
        return send(there, there, (x_sent, x_got), way, place.across(way))

    def x_relay(way):
        there = x_half((place.s2, place.s1)[way], 1 - way)
        return send(there, there, (r_sent, r_got), way, place.across(way))

    def x_relayed(way):
        there = x_half(place.s3, 1 - way)
        return send(there, there, (r_sent, r_got), way, place.across(way))

    def seg_copy(way):
        return send(seg_ref, seg_sc.at[place.s], (g_sent, g_got), way, place.across(way))

    def seg_arrival(way):
        there = seg_sc.at[seats[way]]
        return send(there, there, (g_sent, g_got), way, place.across(way))

    place.meet()
    vector.begin()
    for pick in picks:
        pick.wait()
    weight.begin()
    for way in range(2):
        x_copy(way).start()
    for way in range(3):
        seg_copy(way).start()
    own_x = pltpu.make_async_copy(x_ref, x_rows(place.s), x_own)
    own_x.start()
    own_seg = pltpu.make_async_copy(seg_ref, seg_sc.at[place.s], seg_own)
    own_seg.start()
    def start_rest():
        for one in gathers:
            one.begin()

    if place.depth <= 8:
        for step in range(1, place.depth):
            vector.swap(step)
            weight.swap(step)
            if step == max(1, place.depth - 2):
                start_rest()
    else:
        place.each(1, place.depth, vector.swap)
        place.each(1, place.depth, weight.swap)
        start_rest()
    vector.finish()
    vec_rows = vec_ref.shape[0]
    total = vec_sc[pl.ds(0, vec_rows), :].astype(F32)
    if fsdp_count <= 8:
        for f in range(1, fsdp_count):
            total = total + vec_sc[pl.ds(f * vec_rows, vec_rows), :].astype(F32)
    else:
        total = lax.fori_loop(
            1, fsdp_count, lambda f, sofar: sofar + vec_sc[aligned(f * vec_rows, vec_rows), :].astype(F32), total
        )
    vec_sum[...] = total

    def normalise(seat):
        def body(part):
            token_rows = x_sc[aligned(seat * rows + part * 32, 32), :].astype(F32)
            center = token_rows - jnp.mean(token_rows, axis=-1, keepdims=True)
            variance = jnp.mean(center * center, axis=-1, keepdims=True)
            normed = center * lax.rsqrt(variance + 1e-05) * vec_sum[0:1, :] + vec_sum[1:2, :]
            n1_sc[aligned(seat * rows + part * 32, 32), :] = normed.astype(BF16)

        lax.fori_loop(0, rows // 32, lambda part, carry: (body(part), carry)[1], 0)

    def project(seat):
        here = aligned(seat * rows, rows)

        def body(part):
            cols = aligned(part * 256, 256)
            heads_sc[here, cols] = dot_nn(n1_sc[here, :], wq_sc[:, cols]).astype(BF16)

        lax.fori_loop(0, own_width // 256, lambda part, carry: (body(part), carry)[1], 0)

    own_x.wait()
    normalise(place.s)
    for way in range(2):
        x_arrival(way).wait_recv()
    for way in range(2):
        x_relay(way).start()
    for way in range(2):
        normalise(seats[way])
    weight.finish()
    project(place.s)
    for way in range(2):
        project(seats[way])
    for one in gathers:
        one.swap(1)
    for way in range(2):
        x_relayed(way).wait_recv()
    normalise(place.s3)
    project(place.s3)
    own_seg.wait()
    for way in range(3):
        seg_arrival(way).wait_recv()
    blocks = mask_ref.shape[1]
    for seat in range(4):
        columns = seg_sc[seat].T
        for part in range(rows // LANES):
            here = pl.ds(seat * rows + part * LANES, LANES)
            qd_ref[here, :], kf_ref[here, :] = token_features(
                seat * rows + part * LANES, columns[:, part : part + 1], blocks
            )
    keeps = [
        pltpu.make_async_copy(src, dst, keep_sems.at[i])
        for i, (src, dst) in enumerate(((heads_sc, heads_all), (n1_sc, n1_all), (wq_sc, wq_all)))
    ]
    for keep in keeps:
        keep.start()

    pairs = att_sc.shape[1] // LANES

    def att_copy(pair, way):
        cols = aligned((place.s * pairs + pair) * LANES, LANES)
        return send(
            att_sc.at[aligned(seats[way] * rows, rows), pl.ds(pair * LANES, LANES)],
            att_all.at[:, cols],
            (a_sent, a_got),
            pair * 3 + way,
            place.across(way),
        )

    def att_own(pair):
        cols = aligned((place.s * pairs + pair) * LANES, LANES)
        return pltpu.make_async_copy(
            att_sc.at[aligned(place.s * rows, rows), pl.ds(pair * LANES, LANES)],
            att_all.at[:, cols],
            a_own.at[pair],
        )

    def att_arrival(pair, way):
        there = att_all.at[:, aligned((seats[way] * pairs + pair) * LANES, LANES)]
        return send(there, there, (a_sent, a_got), pair * 3 + way, place.across(way))

    def unit(pair, odd):
        attend_unit(pair, odd, 256, heads_sc, mask_ref, qd_ref, kf_ref, keys_sc, values_t, att_sc, lse_ref)
        if odd:
            for way in range(3):
                att_copy(pair, way).start()
            att_own(pair).start()

    gather_steps(
        place,
        gathers,
        late,
        [functools.partial(unit, pair, odd) for pair in range(pairs) for odd in (0, 1)],
    )
    for keep in keeps:
        keep.wait()
    for way in range(3):
        seg_copy(way).wait_send()
        if way < 2:
            x_copy(way).wait_send()
            x_relay(way).wait_send()
        for pair in range(pairs):
            att_copy(pair, way).wait_send()
            att_arrival(pair, way).wait_recv()
    for pair in range(pairs):
        att_own(pair).wait()
    for one in gathers + late:
        one.finish()


def forward_attention(fsdp_count, x, w_qkv, vec, seg, mask, w_out, w_down, w_in):
    rows, width = x.shape
    length = 4 * rows
    heads = mask.shape[0]
    pairs = heads // 2
    depth = fsdp_count // 2
    own_width = w_qkv.shape[1] // 4
    full = fsdp_count * w_qkv.shape[0]
    anywhere = pl.BlockSpec(memory_space=pltpu.HBM)
    vmem = pl.BlockSpec(memory_space=pltpu.VMEM)
    shape = jax.ShapeDtypeStruct

    def whole(shard):
        return shape((fsdp_count * shard.shape[0], shard.shape[1]), shard.dtype)

    return pl.pallas_call(
        functools.partial(forward_kernel, fsdp_count),
        out_shape=(
            shape((length, own_width), BF16),
            shape((pairs, 2, length), F32),
            shape((rows, heads * DH * 4), BF16),
            whole(w_out),
            whole(w_down),
            whole(w_in),
            shape(vec.shape, F32),
            shape((length, width), BF16),
            shape((full, own_width), BF16),
            shape((length, LANES), BF16),
            shape((length, LANES), BF16),
        ),
        in_specs=[anywhere] * 4 + [vmem] + [anywhere] * 3,
        out_specs=(anywhere, vmem, anywhere, anywhere, anywhere, anywhere, vmem, anywhere, anywhere, vmem, vmem),
        scratch_shapes=[
            pltpu.VMEM((length, width), BF16),
            pltpu.VMEM((length, width), BF16),
            pltpu.VMEM((w_qkv.shape[0], own_width), BF16),
            pltpu.VMEM((full, own_width), BF16),
            pltpu.VMEM((fsdp_count * vec.shape[0], vec.shape[1]), BF16),
            pltpu.VMEM((4,) + seg.shape, jnp.int32),
            pltpu.VMEM((length, own_width), BF16),
            pltpu.VMEM((length, heads * DH), BF16),
            pltpu.VMEM((length, LANES), BF16),
            pltpu.VMEM((LANES, length), BF16),
        ]
        + Gather.scratch(depth, True) * 3
        + Gather.scratch(depth, False) * 3
        + [dma(), dma(), dma(3), dma(3), dma(2), dma(2), dma(2), dma(2), dma(3), dma(3)]
        + [dma(3 * pairs), dma(3 * pairs), dma(pairs)],
        compiler_params=pltpu.CompilerParams(
            collective_id=2, has_side_effects=True, vmem_limit_bytes=60 << 20
        ),
    )(x, w_qkv, vec, seg, mask, w_out, w_down, w_in)


def by_rows(count, body):
    lax.fori_loop(0, count // 16, lambda i, carry: (body(aligned(i * 16, 16)), carry)[1], 0)


class Reduce:
    def __init__(self, place, grad, out, quartered, bufs, sems, direct=False, thirds=False, late=False, far_first=False):
        self.far_first = far_first
        self.place, self.grad, self.out, self.quartered, self.direct = place, grad, out, quartered, direct
        self.thirds, self.late = thirds, late
        self.rows, self.cols = out.shape
        self.wide = self.cols // 4
        self.acc, self.own, self.relay_in, self.quarter_in, self.z_in, self.total = bufs
        self.own_sem, self.put_sem, self.cs, self.rs, self.qs, self.zs, self.fs, self.gs = sems

    @staticmethod
    def scratch(depth, rows, cols, quartered, direct=False, far_first=False):
        held = cols // 4 if quartered else cols
        near = 1 if far_first else depth
        side = (1, 1, 16, LANES) if quartered else None
        return [
            pltpu.VMEM((depth, rows, held), BF16),
            pltpu.VMEM((16, LANES) if direct else (rows, held), BF16),
            pltpu.VMEM(side or (2, near, rows, cols // 8), BF16),
            pltpu.VMEM(side or (2, near, rows, cols // 4), BF16),
            pltpu.VMEM((depth, rows, cols if far_first else cols // 4), BF16),
            pltpu.VMEM((rows, cols // 4), BF16),
            dma(),
            dma(3),
        ] + [dma(depth)] * 12 + [dma(9)] * 2 + [dma(2)] * 2

    @staticmethod
    def take(place, grad, out, quartered, refs, direct=False, thirds=False, far_first=False):
        s = refs[8:]
        pairs = [(s[i], s[i + 1]) for i in range(0, 16, 2)]
        sems = (refs[6], refs[7], pairs[0], pairs[1:3], pairs[3:5], pairs[5], pairs[6], pairs[7])
        return Reduce(place, grad, out, quartered, refs[:6], sems, direct, thirds, False, far_first)

    def quarter(self, seat):
        return aligned(seat * self.wide, self.wide)

    def mine(self):
        if self.far_first:
            return pl.ds(0, self.cols)
        return pl.ds(0, self.wide) if self.quartered else self.quarter(self.place.s)

    def piece(self, seat, half):
        return aligned(seat * self.wide + half * (self.wide // 2), self.wide // 2)

    def own_copy(self, step):
        p = self.place
        rows = aligned((2 * p.far(step) + p.c) * self.rows, self.rows)
        return pltpu.make_async_copy(self.grad.at[rows], self.own, self.own_sem)

    def core_copy(self, step):
        p = self.place
        rows = aligned((2 * p.far(step) + 1 - p.c) * self.rows, self.rows)
        return send(self.grad.at[rows], self.acc.at[step], self.cs, step, p.beside)

    def relay_copy(self, step, way):
        p = self.place
        src = self.acc.at[step, :, self.piece(p.s3, way)]
        return send(src, self.relay_in.at[way, step], self.rs[way], step, p.across(way))

    def quarter_copy(self, step, way):
        p = self.place
        src = self.acc.at[step, :, self.quarter((p.s1, p.s2)[way])]
        return send(src, self.quarter_in.at[way, step], self.qs[way], step, p.across(way))

    def z_copy(self, step):
        p = self.place
        src = self.acc.at[step, :, self.mine()]
        return send(src, self.z_in.at[step], self.zs, step, p.along(p.far(step)))

    def columns(self, seat, part):
        if not self.thirds:
            return self.quarter(seat), pl.ds(0, self.wide)
        third = self.wide // 3
        return aligned((4 * part + seat) * third, third), pl.ds(part * third, third)

    @property
    def parts(self):
        return 3 if self.thirds else 1

    def put_copy(self, part):
        there, here = self.columns(self.place.s, part)
        return pltpu.make_async_copy(self.total.at[:, here], self.out.at[:, there], self.put_sem.at[part])

    def total_copy(self, way, part):
        p = self.place
        there, here = self.columns(p.s, part)
        return send(self.total.at[:, here], self.out.at[:, there], self.fs, 3 * way + part, p.across(way))

    def total_arrival(self, way, part):
        p = self.place
        there = self.out.at[:, self.columns((p.s1, p.s2, p.s3)[way], part)[0]]
        return send(there, there, self.fs, 3 * way + part, p.across(way))

    def totals(self):
        return [(way, part) for way in range(3 if self.thirds else 2) for part in range(self.parts)]

    def back_copy(self, way):
        p = self.place
        there = self.out.at[:, self.piece((p.s2, p.s1)[way], 1 - way)]
        return send(there, there, self.gs, way, p.across(way))

    def back_arrival(self, way):
        p = self.place
        there = self.out.at[:, self.piece(p.s3, 1 - way)]
        return send(there, there, self.gs, way, p.across(way))

    def begin(self):
        depth = self.place.depth
        self.place.each(1, depth, lambda step: self.core_copy(step).start())
        self.core_copy(0).start()
        self.own_copy(1).start()

    def fold(self, step, following):
        p, acc, own = self.place, self.acc, self.own
        self.core_copy(step).wait_recv()
        if not self.direct:
            self.own_copy(step).wait()
        base = (2 * p.far(step) + p.c) * self.rows

        def body(index, carry):
            rows = aligned(index * 16, 16)
            added = self.grad[aligned(base + index * 16, 16), :] if self.direct else own[rows, :]
            acc[step, rows, :] = acc[step, rows, :] + added
            return carry

        lax.fori_loop(0, self.rows // 16, body, 0)
        if following is not None:
            self.own_copy(following).start()
        if not (self.quartered or self.far_first):
            for way in (0, 1):
                self.relay_copy(step, way).start()
        elif not (isinstance(step, int) and step == 0):
            self.z_copy(step).start()

    def swap(self, step):
        if self.quartered:
            return
        p, acc = self.place, self.acc
        for way in (0, 1):
            self.relay_copy(step, way).wait_recv()
            cols = self.piece((p.s2, p.s1)[way], way)
            came = self.relay_in.at[way, step]

            def body(rows):
                acc[step, rows, cols] = acc[step, rows, cols] + came[rows, :]

            by_rows(self.rows, body)
        for way in (0, 1):
            self.quarter_copy(step, way).start()

    def close(self, step, own):
        if self.quartered:
            return
        p, acc, came = self.place, self.acc, self.quarter_in
        for way in (0, 1):
            self.quarter_copy(step, way).wait_recv()
        cols = self.quarter(p.s)

        def body(rows):
            acc[step, rows, cols] = (
                acc[step, rows, cols].astype(F32)
                + came[0, step, rows, :].astype(F32)
                + came[1, step, rows, :].astype(F32)
            ).astype(BF16)

        by_rows(self.rows, body)
        if not self.far_first:
            pl.when(jnp.logical_not(own))(lambda: self.z_copy(step).start())

    def far_sum(self):
        p, acc, came = self.place, self.acc, self.z_in
        p.each(1, p.depth, lambda step: self.z_copy(step).wait_recv())

        def body(rows):
            start = acc[0, rows, :].astype(F32)
            if p.depth <= 8:
                for step in range(1, p.depth):
                    start = start + came[step, rows, :].astype(F32)
            else:
                start = lax.fori_loop(1, p.depth, lambda step, sofar: sofar + came[step, rows, :].astype(F32), start)
            acc[0, rows, :] = start.astype(BF16)

        by_rows(self.rows, body)
        for way in (0, 1):
            self.relay_copy(0, way).start()

    def near_sum(self):
        self.close(0, True)
        total, acc, cols = self.total, self.acc, self.quarter(self.place.s)

        def body(rows):
            total[rows, :] = acc[0, rows, cols]

        by_rows(self.rows, body)
        self.give()

    def collect(self):
        p, acc, came, total = self.place, self.acc, self.z_in, self.total
        p.each(1, p.depth, lambda step: self.z_copy(step).wait_recv())
        cols = self.mine()

        def body(rows):
            start = acc[0, rows, cols].astype(F32)
            if p.depth <= 8:
                for step in range(1, p.depth):
                    start = start + came[step, rows, :].astype(F32)
            else:
                start = lax.fori_loop(1, p.depth, lambda step, sofar: sofar + came[step, rows, :].astype(F32), start)
            total[rows, :] = start.astype(BF16)

        by_rows(self.rows, body)
        if not self.direct:
            self.give()

    def give(self):
        for way, part in self.totals():
            self.total_copy(way, part).start()
        for part in range(self.parts):
            self.put_copy(part).start()

    def spread(self):
        for way, part in self.totals():
            self.total_arrival(way, part).wait_recv()
        if not self.thirds:
            for way in (0, 1):
                self.back_copy(way).start()

    def sent(self):
        def done(step):
            self.core_copy(step).wait_send()
            if not (self.quartered or self.far_first):
                for way in (0, 1):
                    self.relay_copy(step, way).wait_send()
                    self.quarter_copy(step, way).wait_send()

        self.place.each(0, self.place.depth, done)
        if self.far_first:
            for way in (0, 1):
                self.relay_copy(0, way).wait_send()
                self.quarter_copy(0, way).wait_send()

    def finish(self):
        for part in range(self.parts):
            self.put_copy(part).wait()
        if not self.late:
            self.sent()
            self.place.each(1, self.place.depth, lambda step: self.z_copy(step).wait_send())
        for way, part in self.totals():
            self.total_copy(way, part).wait_send()
        if not self.thirds:
            for way in (0, 1):
                self.back_arrival(way).wait_recv()
                self.back_copy(way).wait_send()


REDUCE_REFS = 24


def backward_unit(
    pair, odd, half, tile, heads_ref, mask_ref, qd_ref, kf_ref, go_ref, lse_ref, out_ref, keys_sc, values_sc, keys_t, p_sc, s_sc, k_acc, v_acc
):
    length = heads_ref.shape[0]
    span = p_sc.shape[1]
    scale = jnp.asarray(1.0 / math.sqrt(DH), BF16)
    q_cols, k_cols, v_cols = (pl.ds(i * heads_ref.shape[1] // 3 + pair * LANES, LANES) for i in range(3))
    cols = pl.ds(pair * LANES, LANES)
    mine = own_lanes(odd, (length, LANES))
    if half == 0:
        keys_sc[...] = jnp.where(mine, heads_ref[:, k_cols], kf_ref[...])
        values_sc[...] = jnp.where(mine, heads_ref[:, v_cols], jnp.zeros((), BF16))
        if not odd:
            keys_t[...] = heads_ref[:, k_cols].T

    def one_tile(index, carry):
        here = aligned(index * tile, tile)
        rows = aligned(half * span + index * tile, tile)
        lanes = own_lanes(odd, (tile, LANES))
        queries = query_tile(
            heads_ref[rows, q_cols],
            qd_ref[rows, :],
            mask_ref,
            2 * pair + odd,
            half * (span // BLK) + index * (tile // BLK),
            lanes,
        )
        prob = jnp.exp(dot_nt(keys_sc[...], queries) - lse_ref[pair, pl.ds(odd, 1), rows])
        grad_prob = dot_nt(values_sc[...], go_ref[rows, cols])
        delta = jnp.sum(prob * grad_prob, axis=0, keepdims=True)
        p_sc[:, here] = prob.astype(BF16)
        s_sc[:, here] = (prob * (grad_prob - delta)).astype(BF16)
        return carry

    lax.fori_loop(0, span // tile, one_tile, 0, unroll=True)
    part = pl.ds(half * span, span)
    grad_v = dot_nn(p_sc[...], go_ref[part, cols])
    grad_k = dot_nn(s_sc[...], heads_ref[part, q_cols] * scale)
    grad_q = (dot_nn(keys_t[...], s_sc[...]) * (1.0 / math.sqrt(DH))).T.astype(BF16)
    last = half * span + span == length

    def put(rows, columns, value, keep):
        if odd:
            value = jnp.where(keep, value, out_ref[rows, columns])
        out_ref[rows, columns] = value

    put(part, q_cols, grad_q, own_lanes(odd, (span, LANES)))
    if half > 0:
        grad_v, grad_k = grad_v + v_acc[...], grad_k + k_acc[...]
    if last:
        put(pl.ds(0, length), k_cols, grad_k.astype(BF16), mine)
        put(pl.ds(0, length), v_cols, grad_v.astype(BF16), mine)
    else:
        v_acc[...], k_acc[...] = grad_v, grad_k


def backward_kernel(
    fsdp_count,
    go_hbm,
    heads_hbm,
    mask_ref,
    qd_hbm,
    kf_hbm,
    lse_ref,
    n1_ref,
    wq_hbm,
    x_hbm,
    hid_hbm,
    vec_ref,
    small_ref,
    out_g_ref,
    in_g_ref,
    down_part,
    tokens_out,
    small_out,
    qkv_total,
    out_total,
    in_total,
    down_total,
    go_sc,
    heads_ref,
    qd_ref,
    kf_ref,
    wq_ref,
    x_ref,
    hid_ref,
    load_sems,
    grads_sc,
    keys_sc,
    values_sc,
    keys_t,
    p_sc,
    s_sc,
    k_acc,
    v_acc,
    n1_sc,
    qkv_g,
    part_sc,
    part_in,
    half_in,
    small_sc,
    small_in,
    *rest,
):
    place = Place(fsdp_count)
    rows = x_ref.shape[0]
    shared = pl.ds(0, in_g_ref.shape[1] // 2)
    apart = pl.ds(in_g_ref.shape[1] // 2, in_g_ref.shape[1] // 2)
    reduces = [
        Reduce.take(place, grad, out, False, rest[i * REDUCE_REFS : (i + 1) * REDUCE_REFS])
        for i, (grad, out) in enumerate(
            ((out_g_ref, out_total), (in_g_ref.at[:, shared], in_total.at[:, shared]))
        )
    ]
    lone = Reduce.take(
        place,
        in_g_ref.at[:, apart],
        in_total.at[:, apart],
        False,
        rest[3 * REDUCE_REFS : 4 * REDUCE_REFS],
        far_first=True,
    )
    first = Reduce.take(place, qkv_g, qkv_total, True, rest[2 * REDUCE_REFS : 3 * REDUCE_REFS], thirds=True)
    put_sem, f_pair, g_pair = (
        rest[4 * REDUCE_REFS],
        rest[4 * REDUCE_REFS + 1 : 4 * REDUCE_REFS + 3],
        rest[4 * REDUCE_REFS + 3 : 4 * REDUCE_REFS + 5],
    )
    down = Reduce(
        place,
        None,
        down_total,
        True,
        (None, None, None, None, None, down_part),
        (None, put_sem, None, None, None, None, f_pair, g_pair),
        late=True,
    )
    n_own, h_sent, h_got, p_sent, p_got, c_sent, c_got, z_sent, z_got, x_sent, x_got = rest[
        4 * REDUCE_REFS + 5 :
    ]
    seats = (place.s1, place.s2, place.s3)
    width = go_sc.shape[1]
    pairs = width // LANES
    half = rows // 2

    loads = [
        pltpu.make_async_copy(src, dst, load_sems.at[i])
        for i, (src, dst) in enumerate(
            (
                (heads_hbm, heads_ref),
                (qd_hbm, qd_ref),
                (kf_hbm, kf_ref),
                (go_hbm, go_sc),
                (wq_hbm, wq_ref),
                (x_hbm, x_ref),
                (hid_hbm, hid_ref),
            )
        )
    ]
    for load in loads:
        load.start()
    later_loads = loads[4:]
    place.meet()
    for one in reduces:
        one.begin()
    lone.begin()
    down.give()
    n1_copy = pltpu.make_async_copy(n1_ref, n1_sc, n_own)
    n1_copy.start()

    def unit(pair, odd, side):
        backward_unit(
            pair, odd, side, 256, heads_ref, mask_ref, qd_ref, kf_ref, go_sc, lse_ref, grads_sc,
            keys_sc, values_sc, keys_t, p_sc, s_sc, k_acc, v_acc,
        )

    def half_copy(way):
        src = part_sc.at[aligned(place.s3 * rows + way * half, half)]
        return send(src, half_in.at[way], (h_sent, h_got), way, place.across(way))

    def part_copy(way, late):
        side = 1 - way if late else way
        src = part_sc.at[aligned(seats[way] * rows + side * half, half)]
        dst = part_in.at[way, pl.ds(side * half, half)]
        return send(src, dst, (p_sent, p_got), 2 * way + late, place.across(way))

    def partial_dn1():
        later_loads[0].wait()
        for seat in (place.s3, place.s1, place.s2, place.s):
            here = aligned(seat * rows, rows)
            part_sc[here, :] = dot_nt(grads_sc[here, :], wq_ref[...]).astype(BF16)
            for way in (0, 1):
                if seat is place.s3:
                    half_copy(way).start()
                elif seat is seats[way]:
                    part_copy(way, 0).start()

    def weight_grad():
        n1_copy.wait()

        def body(index):
            cols = aligned(index * 256, 256)
            qkv_g[cols, :] = dot_tn(n1_sc[:, cols], grads_sc[...]).astype(BF16)

        lax.fori_loop(0, qkv_g.shape[0] // 256, lambda index, carry: (body(index), carry)[1], 0)
        first.begin()

    def swap_dn1():
        for way in (0, 1):
            half_copy(way).wait_recv()
            base = (place.s2, place.s1)[way] * rows + way * half

            def body(index):
                here = aligned(base + index * 32, 32)
                came = half_in[way, aligned(index * 32, 32), :]
                part_sc[here, :] = (part_sc[here, :].astype(F32) + came.astype(F32)).astype(BF16)

            lax.fori_loop(0, half // 32, lambda index, carry: (body(index), carry)[1], 0)
        for way in (0, 1):
            part_copy(way, 1).start()

    def fold_first():
        depth = place.depth
        place.each(1, depth, lambda step: first.fold(step, lax.rem(step + 1, depth)))
        first.fold(0, None)

    def core_small():
        return send(small_sc.at[0], small_sc.at[1], (c_sent, c_got), 0, place.beside)

    def z_small(step):
        return send(small_sc.at[2], small_in.at[step], (z_sent, z_got), step, place.along(place.far(step)))

    def x_small(way):
        return send(small_sc.at[3], small_sc.at[4 + way], (x_sent, x_got), way, place.across(way))

    def close_dn1():
        for way in (0, 1):
            for late in (0, 1):
                part_copy(way, late).wait_recv()
        for load in later_loads[1:]:
            load.wait()
        gain = vec_ref[0:1, :]

        def body(index, sums):
            here = aligned(index * 32, 32)
            mine = aligned(place.s * rows + index * 32, 32)
            dn1 = (
                part_sc[mine, :].astype(F32)
                + part_in[0, here, :].astype(F32)
                + part_in[1, here, :].astype(F32)
            )
            token_rows = x_ref[here, :].astype(F32)
            center = token_rows - jnp.mean(token_rows, axis=-1, keepdims=True)
            inv = lax.rsqrt(jnp.mean(center * center, axis=-1, keepdims=True) + 1e-05)
            hat = center * inv
            scaled = dn1 * gain
            grad = hid_ref[here, :] + inv * (
                scaled
                - jnp.mean(scaled, axis=-1, keepdims=True)
                - hat * jnp.mean(scaled * hat, axis=-1, keepdims=True)
            )
            tokens_out[here, :] = grad.astype(BF16)
            return (
                sums[0] + jnp.sum(dn1 * hat, axis=0, keepdims=True),
                sums[1] + jnp.sum(dn1, axis=0, keepdims=True),
            )

        none = jnp.zeros((1, x_ref.shape[1]), F32)
        gain_sum, bias_sum = lax.fori_loop(0, rows // 32, body, (none, none))
        small_sc[0] = small_ref[...]
        small_sc[0, 0:1, :] = gain_sum
        small_sc[0, 1:2, :] = bias_sum
        core_small().start()

    def small_z():
        core_small().wait_recv()
        small_sc[2] = small_sc[0] + small_sc[1]
        place.each(1, place.depth, lambda step: z_small(step).start())

    def small_x():
        place.each(1, place.depth, lambda step: z_small(step).wait_recv())
        small_in[0] = small_sc[2]
        if place.depth <= 8:
            total = small_in[place.back(0)]
            for z in range(1, place.depth):
                total = total + small_in[place.back(z)]
        else:
            total = lax.fori_loop(
                1, place.depth, lambda z, sofar: sofar + small_in[place.back(z)], small_in[place.back(0)]
            )
        small_sc[3] = total
        for way in range(3):
            x_small(way).start()

    def small_end():
        for way in range(3):
            x_small(way).wait_recv()
        small_out[...] = (small_sc[3] + small_sc[4]) + (small_sc[5] + small_sc[6])

    units = [
        functools.partial(unit, pair, odd, side) for pair in range(pairs) for odd in (0, 1) for side in (0, 1)
    ]
    depth = place.depth
    loose = depth > 8

    def run(count, body):
        lax.fori_loop(1, count, lambda step, carry: (body(step), carry)[1], 0)

    def fold(index):
        for one in [lone] + reduces:
            if not loose:
                step = (index + 1) % depth
                one.fold(step, (step + 1) % depth if step else None)
            elif index == 0:
                run(depth, lambda step: one.fold(step, lax.rem(step + 1, depth)))
                one.fold(0, None)

    def swap(index):
        for one in reduces:
            if not loose:
                one.swap((index + 1) % depth)
            elif index == 0:
                run(depth, one.swap)
                one.swap(0)

    def close(index):
        for one in reduces:
            if not loose:
                one.close((index + 1) % depth, (index + 1) % depth == 0)
            elif index == 0:
                run(depth, lambda step: one.close(step, False))
                one.close(0, True)

    rounds = 1 if loose else depth
    fold(0)
    if rounds > 1:
        fold(1)
    for load in loads[:4]:
        load.wait()
    steps = []
    for index in range(rounds + 2):
        if 2 <= index < rounds:
            steps.append(functools.partial(fold, index))
        if index < rounds:
            steps.append(functools.partial(swap, index))
        if 0 <= index - 1 < rounds:
            steps.append(functools.partial(close, index - 1))
    steps.insert(len(steps) // 2, down.spread)
    for index, one in enumerate(units):
        one()
        for step in steps[index * len(steps) // len(units) : (index + 1) * len(steps) // len(units)]:
            step()
    partial_dn1()
    weight_grad()
    lone.far_sum()
    swap_dn1()
    lone.swap(0)
    for one in reduces:
        one.collect()
    fold_first()
    lone.near_sum()
    close_dn1()
    small_z()
    for one in reduces + [lone]:
        one.spread()
    first.collect()
    small_x()
    first.spread()
    small_end()
    core_small().wait_send()
    place.each(1, place.depth, lambda step: z_small(step).wait_send())
    for way in range(3):
        x_small(way).wait_send()
        if way < 2:
            half_copy(way).wait_send()
            for late in (0, 1):
                part_copy(way, late).wait_send()
    for one in [first, down, lone] + reduces:
        one.finish()


def backward_attention(fsdp_count, grad_heads, saved, x, hid, small, grads, down_part):
    heads, mask, qd, kf, lse, n1, wq, vec = saved
    rows, width = x.shape
    length, own_width = grad_heads.shape
    depth = fsdp_count // 2
    span = length // 2
    anywhere = pl.BlockSpec(memory_space=pltpu.HBM)
    vmem = pl.BlockSpec(memory_space=pltpu.VMEM)
    share = wq.shape[0] // fsdp_count
    kept = [(grad.shape[0] // fsdp_count, grad.shape[1]) for grad in grads]
    kept_qkv = (share, 4 * wq.shape[1])
    down_kept = (down_part.shape[0], 4 * down_part.shape[1])
    shape = jax.ShapeDtypeStruct

    reduce_scratch = []
    half_in = (kept[1][0], kept[1][1] // 2)
    for one in (kept[0], half_in):
        reduce_scratch += Reduce.scratch(depth, *one, False)
    reduce_scratch += Reduce.scratch(depth, *kept_qkv, True)
    reduce_scratch += Reduce.scratch(depth, *half_in, False, far_first=True)
    return pl.pallas_call(
        functools.partial(backward_kernel, fsdp_count),
        out_shape=(shape(x.shape, BF16), shape(small.shape, F32), shape(kept_qkv, BF16))
        + tuple(shape(one, BF16) for one in kept)
        + (shape(down_kept, BF16),),
        in_specs=[anywhere] * 2 + [vmem] + [anywhere] * 2 + [vmem] + [anywhere] * 4 + [vmem] * 2 + [anywhere] * 2 + [vmem],
        out_specs=(vmem, vmem, anywhere, anywhere, anywhere, anywhere),
        scratch_shapes=[
            pltpu.VMEM((length, own_width), BF16),
            pltpu.VMEM(heads.shape, BF16),
            pltpu.VMEM(qd.shape, BF16),
            pltpu.VMEM(kf.shape, BF16),
            pltpu.VMEM(wq.shape, BF16),
            pltpu.VMEM(x.shape, BF16),
            pltpu.VMEM(hid.shape, F32),
            dma(7),
            pltpu.VMEM((length, 3 * own_width), BF16),
            pltpu.VMEM((length, LANES), BF16),
            pltpu.VMEM((length, LANES), BF16),
            pltpu.VMEM((LANES, length), BF16),
            pltpu.VMEM((length, span), BF16),
            pltpu.VMEM((length, span), BF16),
            pltpu.VMEM((length, LANES), F32),
            pltpu.VMEM((length, LANES), F32),
            pltpu.VMEM((length, width), BF16),
            pltpu.VMEM(wq.shape, BF16),
            pltpu.VMEM((length, width), BF16),
            pltpu.VMEM((2, rows, width), BF16),
            pltpu.VMEM((2, rows // 2, width), BF16),
            pltpu.VMEM((7,) + small.shape, F32),
            pltpu.VMEM((depth,) + small.shape, F32),
        ]
        + reduce_scratch
        + [dma(3), dma(9), dma(9), dma(2), dma(2)]
        + [dma(), dma(2), dma(2), dma(4), dma(4)]
        + [dma(1), dma(1), dma(depth), dma(depth), dma(3), dma(3)],
        compiler_params=pltpu.CompilerParams(
            collective_id=3, has_side_effects=True, vmem_limit_bytes=60 << 20
        ),
    )(grad_heads, heads, mask, qd, kf, lse, n1, wq, x, hid, vec, small, *grads, down_part)


def middle_kernel(
    fsdp_count,
    att_hbm,
    x_hbm,
    cot_hbm,
    vec_ref,
    out_w_hbm,
    in_w_ref,
    down_w_ref,
    result_ref,
    go_all,
    hid_ref,
    small_ref,
    out_g_ref,
    in_g_ref,
    down_part,
    att_ref,
    x_ref,
    cot_ref,
    out_w_ref,
    fetch_sems,
    datt_ref,
    go_sems,
    go_sent,
    go_got,
    hidden_sc,
    n2_sc,
    n2_t,
    out_acc,
    dn2_acc,
    in_buf,
    down_buf,
    grad_buf,
    down_g,
    in_sems,
    down_sems,
    grad_sems,
    *rest,
):
    place = Place(fsdp_count)
    depth = place.depth
    down_like = rest[0]
    total = Reduce.take(place, down_g, down_like, False, rest[1:], True)
    rows, width = x_ref.shape
    span = down_buf.shape[1]
    hidden_units = down_g.shape[0]
    chunks = hidden_units // span
    paired = total.rows == span
    lines = rows // 32

    def order(index):
        if not paired:
            return index
        z = place.far(lax.rem(lax.div(index, 2) + 1, depth))
        return 2 * z + jnp.where(lax.rem(index, 2) == 0, 1 - place.c, place.c)

    def in_load(index):
        slot = lax.rem(index, 2)
        return pltpu.make_async_copy(
            in_w_ref.at[:, aligned(order(index) * span, span)], in_buf.at[slot], in_sems.at[slot]
        )

    def down_load(index):
        slot = lax.rem(index, 2)
        return pltpu.make_async_copy(
            down_w_ref.at[aligned(order(index) * span, span)], down_buf.at[slot], down_sems.at[slot]
        )

    def grad_store(index):
        slot = lax.rem(index, 2)
        return pltpu.make_async_copy(
            grad_buf.at[slot], in_g_ref.at[:, aligned(order(index) * span, span)], grad_sems.at[slot]
        )

    def over_rows(body, start=0):
        return lax.fori_loop(0, lines, lambda index, carry: body(aligned(index * 32, 32), carry), start)

    in_load(0).start()
    down_load(0).start()
    loads = [
        pltpu.make_async_copy(src, dst, fetch_sems.at[i])
        for i, (src, dst) in enumerate(((att_hbm, att_ref), (out_w_hbm, out_w_ref), (x_hbm, x_ref), (cot_hbm, cot_ref)))
    ]
    for load in loads:
        load.start()
    place.meet()
    for load in loads:
        load.wait()
    hidden_sc[...] = x_ref[...].astype(F32) + dot_nn(att_ref[...], out_w_ref[...])

    def normalise(here, carry):
        token_rows = hidden_sc[here, :]
        center = token_rows - jnp.mean(token_rows, axis=-1, keepdims=True)
        variance = jnp.mean(center * center, axis=-1, keepdims=True)
        normed = center * lax.rsqrt(variance + 1e-05) * vec_ref[2:3, :] + vec_ref[3:4, :]
        n2_sc[here, :] = normed.astype(BF16)
        out_acc[here, :] = token_rows + vec_ref[4:5, :]
        return carry

    over_rows(normalise)
    n2_t[...] = n2_sc[...].T
    dn2_acc[...] = jnp.zeros_like(dn2_acc)
    small_ref[...] = jnp.zeros_like(small_ref)

    def chunk(index):
        slot = lax.rem(index, 2)
        which = order(index)
        in_load(index).wait()
        down_load(index).wait()

        def ahead():
            in_load(index + 1).start()
            down_load(index + 1).start()

        pl.when(index + 1 < chunks)(ahead)
        per = width // span
        line = pl.ds(5 + lax.div(which, per), 1)
        cols = aligned(lax.rem(which, per) * span, span)
        pre = dot_nn(n2_sc[...], in_buf[slot]) + vec_ref[line, cols]
        inner = jnp.tanh(0.7978845608028654 * (pre + 0.044715 * pre * pre * pre))
        act = (0.5 * pre * (1.0 + inner)).astype(BF16)
        slope = 0.5 * (1.0 + inner) + (0.5 * 0.7978845608028654) * pre * (1.0 - inner * inner) * (
            1.0 + (3.0 * 0.044715) * pre * pre
        )
        grad = dot_nt(cot_ref[...], down_buf[slot]) * slope
        low = grad.astype(BF16)
        small_ref[line, cols] = jnp.sum(low.astype(F32), axis=0, keepdims=True)
        down_g[aligned(which * span, span), :] = dot_tn(act, cot_ref[...]).astype(BF16)
        out_acc[...] += dot_nn(act, down_buf[slot])
        dn2_acc[...] += dot_nt(low, in_buf[slot])
        pl.when(index >= 2)(lambda: grad_store(index - 2).wait())
        grad_buf[slot] = dot_nn(n2_t[...], low).astype(BF16)
        grad_store(index).start()

    def later(t):
        pl.when(jnp.logical_and(t >= 1, t <= depth))(lambda: total.swap(lax.rem(t, depth)))
        pl.when(t >= 2)(lambda: total.close(lax.rem(t + depth - 1, depth), t == depth + 1))

    if paired:

        def step(t, carry):
            dest = lax.rem(t + 1, depth)

            def one(side, carry):
                chunk(2 * t + side)
                pl.when(side == 0)(lambda: total.core_copy(dest).start())
                return carry

            lax.fori_loop(0, 2, one, 0)
            total.fold(dest, None)
            later(t)
            return carry

        lax.fori_loop(0, depth, step, 0)
    else:
        lax.fori_loop(0, chunks, lambda index, carry: (chunk(index), carry)[1], 0)
        place.each(0, depth, lambda step: total.core_copy(step).start())

        def step(t, carry):
            total.fold(lax.rem(t + 1, depth), None)
            later(t)
            return carry

        lax.fori_loop(0, depth, step, 0)

    def finish(here, sums):
        token_rows = hidden_sc[here, :]
        center = token_rows - jnp.mean(token_rows, axis=-1, keepdims=True)
        inv = lax.rsqrt(jnp.mean(center * center, axis=-1, keepdims=True) + 1e-05)
        hat = center * inv
        dn2 = dn2_acc[here, :]
        cot = cot_ref[here, :].astype(F32)
        scaled = dn2 * vec_ref[2:3, :]
        grad = cot + inv * (
            scaled
            - jnp.mean(scaled, axis=-1, keepdims=True)
            - hat * jnp.mean(scaled * hat, axis=-1, keepdims=True)
        )
        hid_ref[here, :] = grad
        n2_sc[here, :] = grad.astype(BF16)
        result_ref[here, :] = out_acc[here, :].astype(BF16)
        return (
            sums[0] + jnp.sum(dn2 * hat, axis=0, keepdims=True),
            sums[1] + jnp.sum(dn2, axis=0, keepdims=True),
            sums[2] + jnp.sum(cot, axis=0, keepdims=True),
        )

    none = jnp.zeros((1, width), F32)
    gain_sum, bias_sum, cot_sum = over_rows(finish, (none, none, none))
    small_ref[2:3, :] = gain_sum
    small_ref[3:4, :] = bias_sum
    small_ref[4:5, :] = cot_sum
    later(depth)
    datt_ref[...] = dot_nt(n2_sc[...], out_w_ref[...]).astype(BF16)
    seats = (place.s1, place.s2, place.s3)
    part = width // 4

    def go_copy(way):
        src = datt_ref.at[:, aligned(seats[way] * part, part)]
        return send(src, go_all.at[aligned(place.s * rows, rows)], (go_sent, go_got), way, place.across(way))

    def go_arrival(way):
        there = go_all.at[aligned(seats[way] * rows, rows)]
        return send(there, there, (go_sent, go_got), way, place.across(way))

    own_go = pltpu.make_async_copy(
        datt_ref.at[:, aligned(place.s * part, part)], go_all.at[aligned(place.s * rows, rows)], go_sems
    )
    for way in range(3):
        go_copy(way).start()
    own_go.start()
    out_g_ref[...] = dot_tn(att_ref[...], n2_sc[...]).astype(BF16)
    later(depth + 1)
    total.collect()
    down_part[...] = total.total[...]
    for index in (chunks - 2, chunks - 1):
        grad_store(index).wait()
    own_go.wait()
    for way in range(3):
        go_arrival(way).wait_recv()
        go_copy(way).wait_send()
    total.sent()
    place.each(1, depth, lambda step: total.z_copy(step).wait_send())


def middle(fsdp_count, att, x, cot, vec, w_out, w_in, w_down):
    rows, width = x.shape
    hidden_units = w_in.shape[1]
    span = 512
    depth = fsdp_count // 2
    anywhere = pl.BlockSpec(memory_space=pltpu.HBM)
    vmem = pl.BlockSpec(memory_space=pltpu.VMEM)
    shape = jax.ShapeDtypeStruct
    kept = (hidden_units // fsdp_count, width)
    return pl.pallas_call(
        functools.partial(middle_kernel, fsdp_count),
        out_shape=(
            shape((rows, width), BF16),
            shape((4 * rows, width // 4), BF16),
            shape((rows, width), F32),
            shape(vec.shape, F32),
            shape(w_out.shape, BF16),
            shape(w_in.shape, BF16),
            shape((kept[0], width // 4), BF16),
        ),
        in_specs=[anywhere] * 3 + [vmem] + [anywhere] * 3,
        out_specs=(vmem, anywhere, vmem, vmem, vmem, anywhere, vmem),
        scratch_shapes=[
            pltpu.VMEM((rows, width), BF16),
            pltpu.VMEM((rows, width), BF16),
            pltpu.VMEM((rows, width), BF16),
            pltpu.VMEM(w_out.shape, BF16),
            dma(4),
            pltpu.VMEM((rows, width), BF16),
            dma(),
            dma(3),
            dma(3),
            pltpu.VMEM((rows, width), F32),
            pltpu.VMEM((rows, width), BF16),
            pltpu.VMEM((width, rows), BF16),
            pltpu.VMEM((rows, width), F32),
            pltpu.VMEM((rows, width), F32),
            pltpu.VMEM((2, width, span), BF16),
            pltpu.VMEM((2, span, width), BF16),
            pltpu.VMEM((2, width, span), BF16),
            pltpu.VMEM((hidden_units, width), BF16),
            dma(2),
            dma(2),
            dma(2),
            pltpu.VMEM(kept, BF16),
        ]
        + Reduce.scratch(depth, *kept, False, True),
        compiler_params=pltpu.CompilerParams(
            collective_id=5, has_side_effects=True, vmem_limit_bytes=60 << 20
        ),
    )(att, x, cot, vec, w_out, w_in, w_down)


def results_kernel(share, held, *refs):
    sources, small, refs = refs[:6], refs[6], refs[7:]
    cut = len(refs) > 20
    count = 12 if cut else 6
    outs, refs = refs[:count], refs[count:]
    taken, given, in_sems, out_sems = refs[:6], refs[6:12], refs[12], refs[13]
    loads = [pltpu.make_async_copy(src, dst, in_sems.at[i]) for i, (src, dst) in enumerate(zip(sources, taken))]
    for load in loads:
        load.start()
    stores = []
    for i, load in enumerate(loads):
        load.wait()
        src, dst = taken[i], given[i]
        chunk = 32 if src.shape[0] % 32 == 0 else 16

        def body(index, carry):
            rows = aligned(index * chunk, chunk)
            dst[rows, :] = src[rows, :].astype(dst.dtype)
            return carry

        if dst.dtype == src.dtype:
            store = pltpu.make_async_copy(src, outs[i], out_sems.at[i])
        else:
            lax.fori_loop(0, src.shape[0] // chunk, body, 0)
            store = pltpu.make_async_copy(dst, outs[i], out_sems.at[i])
        store.start()
        stores.append(store)
    if cut:
        position = lax.axis_index("fsdp")
        cols = aligned(position * share, share)
        for line in range(5):
            outs[6 + line][...] = small[line : line + 1, cols]
        per = small.shape[1] // held
        outs[11][...] = small[pl.ds(5 + lax.div(position, per), 1), aligned(lax.rem(position, per) * held, held)]
    for store in stores:
        store.wait()


def write_results(share, held, arrays, small):
    shape = jax.ShapeDtypeStruct
    kinds = (F32, F32, F32, F32, BF16, BF16)
    shapes = [shape(a.shape, kind) for a, kind in zip(arrays, kinds)]
    cut = share % LANES == 0 and held % LANES == 0
    small_shapes = [shape((1, share), F32)] * 5 + [shape((1, held), F32)] if cut else []
    hbm = pl.BlockSpec(memory_space=pltpu.HBM)
    vmem = pl.BlockSpec(memory_space=pltpu.VMEM)
    outs = pl.pallas_call(
        functools.partial(results_kernel, share, held),
        out_shape=tuple(shapes + small_shapes),
        in_specs=[hbm] * 6 + [vmem],
        out_specs=tuple([hbm] * 6 + [vmem] * len(small_shapes)),
        scratch_shapes=[pltpu.VMEM(a.shape, BF16) for a in arrays]
        + [pltpu.VMEM(a.shape if kind == F32 else (16, LANES), kind) for a, kind in zip(arrays, kinds)]
        + [dma(6), dma(6)],
        compiler_params=pltpu.CompilerParams(vmem_limit_bytes=60 << 20),
    )(*arrays, small)
    if cut:
        return outs[:6], [part.reshape(-1) for part in outs[6:]]
    position = lax.axis_index("fsdp")
    lines = lax.dynamic_slice_in_dim(small[:5], position * share, share, axis=1)
    rest = small[5:].reshape(-1)
    return outs, [lines[i] for i in range(5)] + [lax.dynamic_slice_in_dim(rest, position * held, held)]


def per_device(
    fsdp_count,
    tokens,
    segment_ids,
    random_blocks,
    ln1_gain,
    ln1_bias,
    w_qkv,
    w_out,
    ln2_gain,
    ln2_bias,
    w_in,
    b_in,
    w_down,
    b_down,
    cotangent,
):
    width = tokens.shape[2]
    share, held = ln1_gain.shape[0], b_in.shape[0]
    lines = fsdp_count * held // width
    position = lax.axis_index("fsdp")
    column = jnp.arange(width, dtype=jnp.int32)
    narrow = jnp.tile(jnp.stack([ln1_gain, ln1_bias, ln2_gain, ln2_bias, b_down]), (1, fsdp_count))
    narrow = jnp.where(column // share == position, narrow, jnp.zeros((), BF16))
    line = jnp.arange(lines, dtype=jnp.int32)[:, None]
    broad = jnp.tile(b_in[None], (1, width // held))
    broad = jnp.where((line * width + column) // held == position, broad, jnp.zeros((), BF16))
    vec = jnp.concatenate([narrow, broad, jnp.zeros((-(5 + lines) % 16, width), BF16)], axis=0)
    tok_count = segment_ids.shape[1]
    seg_rows = -(-tok_count // (8 * LANES)) * 8
    seg = jnp.pad(segment_ids[0], (0, seg_rows * LANES - tok_count)).reshape(seg_rows, LANES)
    mask = block_mask(random_blocks)
    by_heads, lse, att_rows, out_weight, down_weight, in_weight, vec, normed_one, own_qkv, query_docs, key_feats = (
        forward_attention(fsdp_count, tokens[0], w_qkv, vec, seg, mask, w_out, w_down, w_in)
    )
    result, grad_att, grad_hidden, small, grad_out, grad_in, down_part = middle(
        fsdp_count, att_rows, tokens[0], cotangent[0], vec, out_weight, in_weight, down_weight
    )
    grad_tokens, small, total_qkv, total_out, total_in, total_down = backward_attention(
        fsdp_count,
        grad_att,
        (by_heads, mask, query_docs, key_feats, lse, normed_one, own_qkv, vec),
        tokens[0],
        grad_hidden,
        small,
        (grad_out, grad_in),
        down_part,
    )
    arrays, parts = write_results(
        share, held, (total_in, total_down, total_qkv, total_out, result, grad_tokens), small
    )
    return (
        arrays[4][None],
        arrays[5][None],
        parts[0],
        parts[1],
        arrays[2],
        arrays[3],
        parts[2],
        parts[3],
        arrays[0],
        parts[5],
        arrays[1],
        parts[4],
    )


def solution(mesh):
    return jax.shard_map(
        functools.partial(per_device, mesh.shape["fsdp"]),
        mesh=mesh,
        in_specs=(
            P("fsdp", "seq", None),
            P("fsdp", "seq"),
            P("seq", None, None),
            P("fsdp"),
            P("fsdp"),
            P("fsdp", None),
            P("fsdp", None),
            P("fsdp"),
            P("fsdp"),
            P("fsdp", None),
            P("fsdp"),
            P("fsdp", None),
            P("fsdp"),
            P("fsdp", "seq", None),
        ),
        out_specs=(
            P("fsdp", "seq", None),
            P("fsdp", "seq", None),
            P("fsdp"),
            P("fsdp"),
            P("fsdp", None),
            P("fsdp", None),
            P("fsdp"),
            P("fsdp"),
            P("fsdp", None),
            P("fsdp"),
            P("fsdp", None),
            P("fsdp"),
        ),
        check_vma=False,
    )
```

```python
import functools
import math

import jax
import jax.numpy as jnp
from jax import lax
from jax.experimental import pallas as pl
from jax.experimental.pallas import tpu as pltpu
from jax.sharding import PartitionSpec as P

DH = 64
BLK = 64
LANES = 128
NEG = -1e30
F32 = jnp.float32
BF16 = jnp.bfloat16


def dot_nn(a, b):
    return jnp.dot(a, b, preferred_element_type=F32)


def dot_nt(a, b):
    return lax.dot_general(a, b, (((1,), (1,)), ((), ())), preferred_element_type=F32)


def dot_tn(a, b):
    return lax.dot_general(a, b, (((0,), (0,)), ((), ())), preferred_element_type=F32)


DOCS = 6


def block_mask(random_blocks):
    heads, inner, _ = random_blocks.shape
    blocks = inner + 2
    ids = jnp.arange(blocks, dtype=jnp.int32)
    near = jnp.abs(ids[:, None] - ids[None, :]) <= 1
    edge = (ids == 0) | (ids == blocks - 1)
    fixed = near | edge[:, None] | edge[None, :]
    picked = jnp.any(random_blocks[:, :, :, None] == ids, axis=2)
    used = fixed[None] | jnp.pad(picked, ((0, 0), (1, 1), (0, 0)))
    row = jnp.pad(jnp.where(used, 0.0, NEG), ((0, 0), (0, 0), (0, DH - blocks)))
    return jnp.concatenate([row, row], axis=-1)


def token_features(start, docs, blocks):
    shape = (docs.shape[0], LANES)
    lane = lax.rem(lax.broadcasted_iota(jnp.int32, shape, 1), DH)
    block = lax.div(lax.broadcasted_iota(jnp.int32, shape, 0) + start, BLK)
    own = docs + blocks == lane
    other = jnp.where(own | (lane >= blocks + DOCS), 0.0, 1.0)
    key_part = jnp.where(lane < blocks, jnp.where(block == lane, 1.0, 0.0), other)
    return jnp.where(own, NEG, 0.0).astype(BF16), key_part.astype(BF16)


def query_tile(q_tile, doc_tile, mask_ref, head, first_block, lanes):
    scale = jnp.asarray(1.0 / math.sqrt(DH), BF16)
    count = q_tile.shape[0] // BLK
    mask = jnp.concatenate(
        [jnp.broadcast_to(mask_ref[head, pl.ds(first_block + i, 1), :], (BLK, LANES)) for i in range(count)], axis=0
    )
    return jnp.where(lanes, q_tile * scale, doc_tile + mask.astype(BF16))


def own_lanes(odd, shape):
    return lax.div(lax.broadcasted_iota(jnp.int32, shape, 1), DH) == odd


MESH = pl.DeviceIdType.MESH


class Place:
    def __init__(self, fsdp_count):
        self.depth = fsdp_count // 2
        self.s = lax.axis_index("seq")
        self.f = lax.axis_index("fsdp")
        self.z = lax.div(self.f, 2)
        self.c = lax.rem(self.f, 2)
        self.s1 = self.s + 1 - 2 * lax.rem(self.s, 2)
        self.s2 = self.s + 2 - 4 * lax.div(self.s, 2)
        self.s3 = 3 - self.s
        self.beside = (self.s, self.f + 1 - 2 * self.c)

    def across(self, index):
        return ((self.s1, self.s2, self.s3)[index], self.f)

    def far(self, step):
        return lax.rem(self.z + step, self.depth)

    def back(self, step):
        return lax.rem(self.z + self.depth - step, self.depth)

    def along(self, z):
        return (self.s, 2 * z + self.c)

    def meet(self):
        barrier = pltpu.get_barrier_semaphore()
        peers = [self.beside] + [self.across(i) for i in range(3)]
        for peer in peers:
            pl.semaphore_signal(barrier, inc=1, device_id=peer, device_id_type=MESH)
        self.each(1, self.depth, lambda step: pl.semaphore_signal(
            barrier, inc=1, device_id=self.along(self.far(step)), device_id_type=MESH
        ))
        pl.semaphore_wait(barrier, len(peers) + self.depth - 1)

    def each(self, start, stop, body):
        if stop - start <= 8:
            for step in range(start, stop):
                body(step)
        else:
            lax.fori_loop(start, stop, lambda step, carry: (body(step), carry)[1], 0)


def send(src, dst, sems, index, device):
    sent, got = sems
    return pltpu.make_async_remote_copy(
        src_ref=src,
        dst_ref=dst,
        send_sem=sent.at[index],
        recv_sem=got.at[index],
        device_id=device,
        device_id_type=MESH,
    )


def aligned(start, size):
    return pl.ds(pl.multiple_of(start, size), size)


class Gather:
    def __init__(self, place, src, dst, split, sems):
        self.place, self.src, self.dst, self.split = place, src, dst, split
        self.rows, self.cols = src.shape
        self.local, self.zs, self.xs, self.rs, self.cs = sems

    def block(self, z, core, quarter=None, half=None):
        rows = aligned((2 * z + core) * self.rows, self.rows)
        if quarter is None:
            return self.dst.at[rows]
        wide = self.cols // 4
        if half is None:
            return self.dst.at[rows, aligned(quarter * wide, wide)]
        return self.dst.at[rows, aligned(quarter * wide + half * (wide // 2), wide // 2)]

    def source(self, step, side):
        return self.place.z - step if side == 0 else self.place.z + step

    def has(self, step, side):
        z = self.source(step, side)
        return z >= 0 if side == 0 else z < self.place.depth

    def sends(self, step, side):
        p = self.place
        onward = p.z + 1 < p.depth if side == 0 else p.z > 0
        return jnp.logical_and(self.has(step - 1, side), onward)

    def slot(self, step, side):
        return 2 * step + side

    def own_copy(self):
        return pltpu.make_async_copy(self.src, self.block(self.place.z, self.place.c), self.local)

    def own_core(self):
        p = self.place
        return send(self.src, self.block(p.z, p.c), self.cs, 0, p.beside)

    def own_arrival(self):
        p = self.place
        there = self.block(p.z, 1 - p.c)
        return send(there, there, self.cs, 0, p.beside)

    def core_copy(self, step, side):
        p = self.place
        there = self.block(self.source(step, side), p.c)
        return send(there, there, self.cs, self.slot(step, side), p.beside)

    def core_arrival(self, step, side):
        p = self.place
        there = self.block(self.source(step, side), 1 - p.c)
        return send(there, there, self.cs, self.slot(step, side), p.beside)

    def z_copy(self, step, side):
        p = self.place
        z = self.source(step - 1, side)
        there = self.block(z, p.c, p.s) if self.split else self.block(z, p.c)
        src = there
        if isinstance(step, int) and step == 1:
            wide = self.cols // 4
            src = self.src.at[:, aligned(p.s * wide, wide)] if self.split else self.src
        return send(src, there, self.zs, self.slot(step, side), p.along(p.z + 1 - 2 * side))

    def z_arrival(self, step, side):
        p = self.place
        z = self.source(step, side)
        there = self.block(z, p.c, p.s) if self.split else self.block(z, p.c)
        return send(there, there, self.zs, self.slot(step, side), p.along(p.z - 1 + 2 * side))

    def x_copy(self, step, side, way):
        p = self.place
        there = self.block(self.source(step, side), p.c, p.s)
        return send(there, there, self.xs[way], self.slot(step, side), p.across(way))

    def x_arrival(self, step, side, way):
        p = self.place
        there = self.block(self.source(step, side), p.c, (p.s1, p.s2)[way])
        return send(there, there, self.xs[way], self.slot(step, side), p.across(way))

    def relay_copy(self, step, side, way):
        p = self.place
        there = self.block(self.source(step, side), p.c, (p.s2, p.s1)[way], 1 - way)
        return send(there, there, self.rs[way], self.slot(step, side), p.across(way))

    def relay_arrival(self, step, side, way):
        p = self.place
        there = self.block(self.source(step, side), p.c, p.s3, 1 - way)
        return send(there, there, self.rs[way], self.slot(step, side), p.across(way))

    def both(self, step, body, test=None):
        for side in (0, 1):
            pl.when((test or self.has)(step, side))(functools.partial(body, step, side))

    def begin(self):
        self.both(1, lambda step, side: self.z_copy(step, side).start(), self.sends)
        self.own_copy().start()
        self.own_core().start()

    def swap(self, step):
        def body(step, side):
            self.z_arrival(step, side).wait_recv()
            pl.when(self.sends(step + 1, side))(lambda: self.z_copy(step + 1, side).start())
            if self.split:
                for way in (0, 1):
                    self.x_copy(step, side, way).start()
            else:
                self.core_copy(step, side).start()

        self.both(step, body)

    def relay(self, step):
        def body(step, side):
            for way in (0, 1):
                self.x_arrival(step, side, way).wait_recv()
            for way in (0, 1):
                self.relay_copy(step, side, way).start()

        if self.split:
            self.both(step, body)

    def share(self, step):
        def body(step, side):
            for way in (0, 1):
                self.relay_arrival(step, side, way).wait_recv()
            self.core_copy(step, side).start()

        if self.split:
            self.both(step, body)

    def finish(self):
        self.own_copy().wait()
        self.own_core().wait_send()
        self.own_arrival().wait_recv()

        def close(step, side):
            if self.split:
                for way in (0, 1):
                    self.x_copy(step, side, way).wait_send()
                    self.relay_copy(step, side, way).wait_send()
            self.core_copy(step, side).wait_send()
            self.core_arrival(step, side).wait_recv()

        self.place.each(1, self.place.depth, lambda step: self.both(step, close))
        self.place.each(
            1,
            self.place.depth,
            lambda step: self.both(step, lambda step, side: self.z_copy(step, side).wait_send(), self.sends),
        )

    @staticmethod
    def scratch(depth, split):
        held = 2 * depth if split else 1
        return [dma()] + [dma(2 * depth)] * 2 + [dma(held)] * 8 + [dma(2 * depth)] * 2

    @staticmethod
    def take(refs):
        pairs = [(refs[i], refs[i + 1]) for i in range(1, 13, 2)]
        return (refs[0], pairs[0], pairs[1:3], pairs[3:5], pairs[5])


GATHER_SEMS = 13


def gather_steps(place, gathers, late, count, unit):
    depth = place.depth

    def swap(step):
        for one in gathers:
            one.swap(step)

    def relay(step):
        for one in gathers:
            one.relay(step)

    def share(step):
        for one in gathers:
            one.share(step)

    def late_swap(step):
        for one in late:
            one.swap(step)

    for one in late:
        one.begin()
    if depth <= 8:
        rounds = []
        for step in range(2, depth + 2):
            now = []
            if step <= depth:
                now.append(functools.partial(late_swap, step - 2)) if step > 2 else None
                now.append(functools.partial(share, step - 3)) if step > 3 else None
                now.append(functools.partial(swap, step)) if step < depth else None
                now.append(functools.partial(relay, step - 1))
            rounds.append(now)
        rounds[-1] = [functools.partial(share, step) for step in range(max(1, depth - 2), depth)]
        rounds[-1].append(functools.partial(late_swap, depth - 1))
        in_turn(count, unit, rounds[:count])
        for now in rounds[count:]:
            for one in now:
                one()
    else:
        in_turn(count, unit, [])
        swap(2)
        relay(1)

        def body(step, carry):
            late_swap(step - 2)
            share(step - 2)
            swap(step)
            relay(step - 1)
            return carry

        lax.fori_loop(3, depth, body, 0)
        late_swap(depth - 2)
        share(depth - 2)
        relay(depth - 1)
        share(depth - 1)
        late_swap(depth - 1)


def dma(*shape):
    return pltpu.SemaphoreType.DMA(shape) if shape else pltpu.SemaphoreType.DMA


def qkv_columns(heads_ref, pair):
    third = heads_ref.shape[1] // 3
    return tuple(aligned(i * third + pair * LANES, LANES) for i in range(3))


def attend_unit(pair, odd, tile, heads_ref, mask_ref, qd_ref, kf_ref, keys_sc, values_t, out_ref, lse_ref):
    length = heads_ref.shape[0]
    cols = aligned(pair * LANES, LANES)
    q_cols, k_cols, v_cols = qkv_columns(heads_ref, pair)
    mine = own_lanes(odd, (length, LANES))
    keys_sc[...] = jnp.where(mine, heads_ref[:, k_cols], kf_ref[...])

    @pl.when(odd == 0)
    def _():
        values_t[...] = heads_ref[:, v_cols].T
        out_ref[:, cols] = jnp.zeros((length, LANES), BF16)

    def one_tile(index, carry):
        rows = aligned(index * tile, tile)
        lanes = own_lanes(odd, (tile, LANES))
        queries = query_tile(
            heads_ref[rows, q_cols], qd_ref[rows, :], mask_ref, 2 * pair + odd, index * (tile // BLK), lanes
        )
        scores = dot_nt(keys_sc[...], queries)
        top = jnp.max(scores, axis=0, keepdims=True)
        prob = jnp.exp(scores - top)
        total = jnp.sum(prob, axis=0, keepdims=True)
        mixed = dot_nn(values_t[...], prob.astype(BF16)) / total
        lse_ref[pair, pl.ds(odd, 1), rows] = top + jnp.log(total)
        out_ref[rows, cols] = jnp.where(lanes, mixed.T.astype(BF16), out_ref[rows, cols])
        return carry

    lax.fori_loop(0, length // tile, one_tile, 0, unroll=2)


def in_turn(count, unit, actions):
    def body(index, carry):
        unit(index)
        for which, todo in enumerate(actions):
            if todo:

                @pl.when(index == which)
                def _(todo=todo):
                    for one in todo:
                        one()

        return carry

    lax.fori_loop(0, count, body, 0)


def forward_kernel(
    fsdp_count,
    x_ref,
    wq_ref,
    vec_ref,
    seg_ref,
    mask_ref,
    out_w_ref,
    down_w_ref,
    in_w_ref,
    heads_all,
    lse_ref,
    att_all,
    out_w_all,
    down_w_all,
    in_w_all,
    vec_sum,
    n1_all,
    wq_all,
    qd_ref,
    kf_ref,
    x_sc,
    n1_sc,
    wq_own,
    wq_sc,
    vec_sc,
    seg_sc,
    heads_sc,
    att_sc,
    keys_sc,
    values_t,
    *sems,
):
    place = Place(fsdp_count)
    rows, width = x_ref.shape
    own_width = wq_sc.shape[1]
    seats = (place.s1, place.s2, place.s3)

    def taken(i):
        return Gather.take(sems[i * GATHER_SEMS : (i + 1) * GATHER_SEMS])

    x_own, seg_own, keep_sems, pick_sems, x_sent, x_got, r_sent, r_got, g_sent, g_got, a_sent, a_got, a_own = sems[6 * GATHER_SEMS :]
    lone = pl.ds(0, in_w_ref.shape[1] // 2)
    shared = pl.ds(in_w_ref.shape[1] // 2, in_w_ref.shape[1] // 2)
    gathers = [
        Gather(place, src, dst, split, taken(i))
        for i, (src, dst, split) in enumerate(
            (
                (out_w_ref, out_w_all, True),
                (in_w_ref.at[:, shared], in_w_all.at[:, shared], True),
                (down_w_ref, down_w_all, True),
                (in_w_ref.at[:, lone], in_w_all.at[:, lone], False),
            )
        )
    ]
    late = [gathers.pop()]
    third = own_width // 3
    picks = [
        pltpu.make_async_copy(
            wq_ref.at[:, aligned((4 * i + place.s) * third, third)], wq_own.at[:, pl.ds(i * third, third)], pick_sems.at[i]
        )
        for i in range(3)
    ]
    for pick in picks:
        pick.start()
    weight = Gather(place, wq_own, wq_sc, False, taken(4))
    vector = Gather(place, vec_ref, vec_sc, False, taken(5))
    half = rows // 2

    def x_rows(seat):
        return x_sc.at[aligned(seat * rows, rows)]

    def x_half(seat, part):
        return x_sc.at[aligned(seat * rows + part * half, half)]

    def x_copy(way):
        return send(x_ref, x_rows(place.s), (x_sent, x_got), way, place.across(way))

    def x_arrival(way):
        there = x_rows(seats[way])
        return send(there, there, (x_sent, x_got), way, place.across(way))

    def x_relay(way):
        there = x_half((place.s2, place.s1)[way], 1 - way)
        return send(there, there, (r_sent, r_got), way, place.across(way))

    def x_relayed(way):
        there = x_half(place.s3, 1 - way)
        return send(there, there, (r_sent, r_got), way, place.across(way))

    def seg_copy(way):
        return send(seg_ref, seg_sc.at[place.s], (g_sent, g_got), way, place.across(way))

    def seg_arrival(way):
        there = seg_sc.at[seats[way]]
        return send(there, there, (g_sent, g_got), way, place.across(way))

    place.meet()
    vector.begin()
    for pick in picks:
        pick.wait()
    weight.begin()
    for way in range(2):
        x_copy(way).start()
    for way in range(3):
        seg_copy(way).start()
    own_x = pltpu.make_async_copy(x_ref, x_rows(place.s), x_own)
    own_x.start()
    own_seg = pltpu.make_async_copy(seg_ref, seg_sc.at[place.s], seg_own)
    own_seg.start()
    def start_rest():
        for one in gathers:
            one.begin()

    if place.depth <= 8:
        for step in range(1, place.depth):
            vector.swap(step)
            weight.swap(step)
            if step == max(1, place.depth - 2):
                start_rest()
    else:
        place.each(1, place.depth, vector.swap)
        place.each(1, place.depth, weight.swap)
        start_rest()
    vector.finish()
    vec_rows = vec_ref.shape[0]
    total = vec_sc[pl.ds(0, vec_rows), :].astype(F32)
    if fsdp_count <= 8:
        for f in range(1, fsdp_count):
            total = total + vec_sc[pl.ds(f * vec_rows, vec_rows), :].astype(F32)
    else:
        total = lax.fori_loop(
            1, fsdp_count, lambda f, sofar: sofar + vec_sc[aligned(f * vec_rows, vec_rows), :].astype(F32), total
        )
    vec_sum[...] = total

    def normalise(seat):
        def body(part):
            token_rows = x_sc[aligned(seat * rows + part * 32, 32), :].astype(F32)
            center = token_rows - jnp.mean(token_rows, axis=-1, keepdims=True)
            variance = jnp.mean(center * center, axis=-1, keepdims=True)
            normed = center * lax.rsqrt(variance + 1e-05) * vec_sum[0:1, :] + vec_sum[1:2, :]
            n1_sc[aligned(seat * rows + part * 32, 32), :] = normed.astype(BF16)

        lax.fori_loop(0, rows // 32, lambda part, carry: (body(part), carry)[1], 0)

    def project(seat):
        here = aligned(seat * rows, rows)

        def body(part):
            cols = aligned(part * 256, 256)
            heads_sc[here, cols] = dot_nn(n1_sc[here, :], wq_sc[:, cols]).astype(BF16)

        lax.fori_loop(0, own_width // 256, lambda part, carry: (body(part), carry)[1], 0)

    own_x.wait()
    normalise(place.s)
    for way in range(2):
        x_arrival(way).wait_recv()
    for way in range(2):
        x_relay(way).start()
    for way in range(2):
        normalise(seats[way])
    weight.finish()
    project(place.s)
    for way in range(2):
        project(seats[way])
    for one in gathers:
        one.swap(1)
    for way in range(2):
        x_relayed(way).wait_recv()
    normalise(place.s3)
    project(place.s3)
    own_seg.wait()
    for way in range(3):
        seg_arrival(way).wait_recv()
    blocks = mask_ref.shape[1]
    for seat in range(4):
        columns = seg_sc[seat].T
        for part in range(rows // LANES):
            here = pl.ds(seat * rows + part * LANES, LANES)
            qd_ref[here, :], kf_ref[here, :] = token_features(
                seat * rows + part * LANES, columns[:, part : part + 1], blocks
            )
    keeps = [
        pltpu.make_async_copy(src, dst, keep_sems.at[i])
        for i, (src, dst) in enumerate(((heads_sc, heads_all), (n1_sc, n1_all), (wq_sc, wq_all)))
    ]
    for keep in keeps:
        keep.start()

    pairs = att_sc.shape[1] // LANES

    def att_copy(pair, way):
        cols = aligned((place.s * pairs + pair) * LANES, LANES)
        return send(
            att_sc.at[aligned(seats[way] * rows, rows), aligned(pair * LANES, LANES)],
            att_all.at[:, cols],
            (a_sent, a_got),
            pair * 3 + way,
            place.across(way),
        )

    def att_own(pair):
        cols = aligned((place.s * pairs + pair) * LANES, LANES)
        return pltpu.make_async_copy(
            att_sc.at[aligned(place.s * rows, rows), aligned(pair * LANES, LANES)],
            att_all.at[:, cols],
            a_own.at[pair],
        )

    def att_arrival(pair, way):
        there = att_all.at[:, aligned((seats[way] * pairs + pair) * LANES, LANES)]
        return send(there, there, (a_sent, a_got), pair * 3 + way, place.across(way))

    def unit(index):
        pair, odd = lax.div(index, 2), lax.rem(index, 2)
        attend_unit(pair, odd, 256, heads_sc, mask_ref, qd_ref, kf_ref, keys_sc, values_t, att_sc, lse_ref)

        @pl.when(odd == 1)
        def _():
            for way in range(3):
                att_copy(pair, way).start()
            att_own(pair).start()

    gather_steps(place, gathers, late, 2 * pairs, unit)
    for keep in keeps:
        keep.wait()
    for way in range(3):
        seg_copy(way).wait_send()
        if way < 2:
            x_copy(way).wait_send()
            x_relay(way).wait_send()
        for pair in range(pairs):
            att_copy(pair, way).wait_send()
            att_arrival(pair, way).wait_recv()
    for pair in range(pairs):
        att_own(pair).wait()
    for one in gathers + late:
        one.finish()


def forward_attention(fsdp_count, x, w_qkv, vec, seg, mask, w_out, w_down, w_in):
    rows, width = x.shape
    length = 4 * rows
    heads = mask.shape[0]
    pairs = heads // 2
    depth = fsdp_count // 2
    own_width = w_qkv.shape[1] // 4
    full = fsdp_count * w_qkv.shape[0]
    anywhere = pl.BlockSpec(memory_space=pltpu.HBM)
    vmem = pl.BlockSpec(memory_space=pltpu.VMEM)
    shape = jax.ShapeDtypeStruct

    def whole(shard):
        return shape((fsdp_count * shard.shape[0], shard.shape[1]), shard.dtype)

    return pl.pallas_call(
        functools.partial(forward_kernel, fsdp_count),
        out_shape=(
            shape((length, own_width), BF16),
            shape((pairs, 2, length), F32),
            shape((rows, heads * DH * 4), BF16),
            whole(w_out),
            whole(w_down),
            whole(w_in),
            shape(vec.shape, F32),
            shape((length, width), BF16),
            shape((full, own_width), BF16),
            shape((length, LANES), BF16),
            shape((length, LANES), BF16),
        ),
        in_specs=[anywhere] * 4 + [vmem] + [anywhere] * 3,
        out_specs=(anywhere, vmem, anywhere, anywhere, anywhere, anywhere, vmem, anywhere, anywhere, vmem, vmem),
        scratch_shapes=[
            pltpu.VMEM((length, width), BF16),
            pltpu.VMEM((length, width), BF16),
            pltpu.VMEM((w_qkv.shape[0], own_width), BF16),
            pltpu.VMEM((full, own_width), BF16),
            pltpu.VMEM((fsdp_count * vec.shape[0], vec.shape[1]), BF16),
            pltpu.VMEM((4,) + seg.shape, jnp.int32),
            pltpu.VMEM((length, own_width), BF16),
            pltpu.VMEM((length, heads * DH), BF16),
            pltpu.VMEM((length, LANES), BF16),
            pltpu.VMEM((LANES, length), BF16),
        ]
        + Gather.scratch(depth, True) * 3
        + Gather.scratch(depth, False) * 3
        + [dma(), dma(), dma(3), dma(3), dma(2), dma(2), dma(2), dma(2), dma(3), dma(3)]
        + [dma(3 * pairs), dma(3 * pairs), dma(pairs)],
        compiler_params=pltpu.CompilerParams(
            collective_id=2, has_side_effects=True, vmem_limit_bytes=60 << 20
        ),
    )(x, w_qkv, vec, seg, mask, w_out, w_down, w_in)


def by_rows(count, body):
    lax.fori_loop(0, count // 16, lambda i, carry: (body(aligned(i * 16, 16)), carry)[1], 0)


class Reduce:
    def __init__(self, place, grad, out, quartered, bufs, sems, direct=False, thirds=False, late=False, far_first=False):
        self.far_first = far_first
        self.place, self.grad, self.out, self.quartered, self.direct = place, grad, out, quartered, direct
        self.thirds, self.late = thirds, late
        self.rows, self.cols = out.shape
        self.wide = self.cols // 4
        self.acc, self.own, self.relay_in, self.quarter_in, self.z_in, self.total = bufs
        self.own_sem, self.put_sem, self.cs, self.rs, self.qs, self.zs, self.fs, self.gs = sems

    @staticmethod
    def scratch(depth, rows, cols, quartered, direct=False, far_first=False):
        held = cols // 4 if quartered else cols
        near = 1 if far_first else depth
        side = (1, 1, 16, LANES) if quartered else None
        return [
            pltpu.VMEM((depth, rows, held), BF16),
            pltpu.VMEM((16, LANES) if direct else (rows, held), BF16),
            pltpu.VMEM(side or (2, near, rows, cols // 8), BF16),
            pltpu.VMEM(side or (2, near, rows, cols // 4), BF16),
            pltpu.VMEM((depth, rows, cols if far_first else cols // 4), BF16),
            pltpu.VMEM((rows, cols // 4), BF16),
            dma(),
            dma(3),
        ] + [dma(depth)] * 12 + [dma(9)] * 2 + [dma(2)] * 2

    @staticmethod
    def take(place, grad, out, quartered, refs, direct=False, thirds=False, far_first=False):
        s = refs[8:]
        pairs = [(s[i], s[i + 1]) for i in range(0, 16, 2)]
        sems = (refs[6], refs[7], pairs[0], pairs[1:3], pairs[3:5], pairs[5], pairs[6], pairs[7])
        return Reduce(place, grad, out, quartered, refs[:6], sems, direct, thirds, False, far_first)

    def quarter(self, seat):
        return aligned(seat * self.wide, self.wide)

    def mine(self):
        if self.far_first:
            return pl.ds(0, self.cols)
        return pl.ds(0, self.wide) if self.quartered else self.quarter(self.place.s)

    def piece(self, seat, half):
        return aligned(seat * self.wide + half * (self.wide // 2), self.wide // 2)

    def own_copy(self, step):
        p = self.place
        rows = aligned((2 * p.far(step) + p.c) * self.rows, self.rows)
        return pltpu.make_async_copy(self.grad.at[rows], self.own, self.own_sem)

    def core_copy(self, step):
        p = self.place
        rows = aligned((2 * p.far(step) + 1 - p.c) * self.rows, self.rows)
        return send(self.grad.at[rows], self.acc.at[step], self.cs, step, p.beside)

    def relay_copy(self, step, way):
        p = self.place
        src = self.acc.at[step, :, self.piece(p.s3, way)]
        return send(src, self.relay_in.at[way, step], self.rs[way], step, p.across(way))

    def quarter_copy(self, step, way):
        p = self.place
        src = self.acc.at[step, :, self.quarter((p.s1, p.s2)[way])]
        return send(src, self.quarter_in.at[way, step], self.qs[way], step, p.across(way))

    def z_copy(self, step):
        p = self.place
        src = self.acc.at[step, :, self.mine()]
        return send(src, self.z_in.at[step], self.zs, step, p.along(p.far(step)))

    def columns(self, seat, part):
        if not self.thirds:
            return self.quarter(seat), pl.ds(0, self.wide)
        third = self.wide // 3
        return aligned((4 * part + seat) * third, third), pl.ds(part * third, third)

    @property
    def parts(self):
        return 3 if self.thirds else 1

    def put_copy(self, part):
        there, here = self.columns(self.place.s, part)
        return pltpu.make_async_copy(self.total.at[:, here], self.out.at[:, there], self.put_sem.at[part])

    def total_copy(self, way, part):
        p = self.place
        there, here = self.columns(p.s, part)
        return send(self.total.at[:, here], self.out.at[:, there], self.fs, 3 * way + part, p.across(way))

    def total_arrival(self, way, part):
        p = self.place
        there = self.out.at[:, self.columns((p.s1, p.s2, p.s3)[way], part)[0]]
        return send(there, there, self.fs, 3 * way + part, p.across(way))

    def totals(self):
        return [(way, part) for way in range(3 if self.thirds else 2) for part in range(self.parts)]

    def back_copy(self, way):
        p = self.place
        there = self.out.at[:, self.piece((p.s2, p.s1)[way], 1 - way)]
        return send(there, there, self.gs, way, p.across(way))

    def back_arrival(self, way):
        p = self.place
        there = self.out.at[:, self.piece(p.s3, 1 - way)]
        return send(there, there, self.gs, way, p.across(way))

    def begin(self):
        depth = self.place.depth
        self.place.each(1, depth, lambda step: self.core_copy(step).start())
        self.core_copy(0).start()
        self.own_copy(1).start()

    def fold(self, step, following):
        p, acc, own = self.place, self.acc, self.own
        self.core_copy(step).wait_recv()
        if not self.direct:
            self.own_copy(step).wait()
        base = (2 * p.far(step) + p.c) * self.rows

        def body(index, carry):
            rows = aligned(index * 16, 16)
            added = self.grad[aligned(base + index * 16, 16), :] if self.direct else own[rows, :]
            acc[step, rows, :] = acc[step, rows, :] + added
            return carry

        lax.fori_loop(0, self.rows // 16, body, 0)
        if following is not None:
            self.own_copy(following).start()
        if not (self.quartered or self.far_first):
            for way in (0, 1):
                self.relay_copy(step, way).start()
        elif not (isinstance(step, int) and step == 0):
            self.z_copy(step).start()

    def swap(self, step):
        if self.quartered:
            return
        p, acc = self.place, self.acc
        for way in (0, 1):
            self.relay_copy(step, way).wait_recv()
            cols = self.piece((p.s2, p.s1)[way], way)
            came = self.relay_in.at[way, step]

            def body(rows):
                acc[step, rows, cols] = acc[step, rows, cols] + came[rows, :]

            by_rows(self.rows, body)
        for way in (0, 1):
            self.quarter_copy(step, way).start()

    def close(self, step, own):
        if self.quartered:
            return
        p, acc, came = self.place, self.acc, self.quarter_in
        for way in (0, 1):
            self.quarter_copy(step, way).wait_recv()
        cols = self.quarter(p.s)

        def body(rows):
            acc[step, rows, cols] = (
                acc[step, rows, cols].astype(F32)
                + came[0, step, rows, :].astype(F32)
                + came[1, step, rows, :].astype(F32)
            ).astype(BF16)

        by_rows(self.rows, body)
        if not self.far_first:
            pl.when(jnp.logical_not(own))(lambda: self.z_copy(step).start())

    def far_sum(self):
        p, acc, came = self.place, self.acc, self.z_in
        p.each(1, p.depth, lambda step: self.z_copy(step).wait_recv())

        def body(rows):
            start = acc[0, rows, :].astype(F32)
            if p.depth <= 8:
                for step in range(1, p.depth):
                    start = start + came[step, rows, :].astype(F32)
            else:
                start = lax.fori_loop(1, p.depth, lambda step, sofar: sofar + came[step, rows, :].astype(F32), start)
            acc[0, rows, :] = start.astype(BF16)

        by_rows(self.rows, body)
        for way in (0, 1):
            self.relay_copy(0, way).start()

    def near_sum(self):
        self.close(0, True)
        total, acc, cols = self.total, self.acc, self.quarter(self.place.s)

        def body(rows):
            total[rows, :] = acc[0, rows, cols]

        by_rows(self.rows, body)
        self.give()

    def collect(self):
        p, acc, came, total = self.place, self.acc, self.z_in, self.total
        p.each(1, p.depth, lambda step: self.z_copy(step).wait_recv())
        cols = self.mine()

        def body(rows):
            start = acc[0, rows, cols].astype(F32)
            if p.depth <= 8:
                for step in range(1, p.depth):
                    start = start + came[step, rows, :].astype(F32)
            else:
                start = lax.fori_loop(1, p.depth, lambda step, sofar: sofar + came[step, rows, :].astype(F32), start)
            total[rows, :] = start.astype(BF16)

        by_rows(self.rows, body)
        if not self.direct:
            self.give()

    def give(self):
        for way, part in self.totals():
            self.total_copy(way, part).start()
        for part in range(self.parts):
            self.put_copy(part).start()

    def spread(self):
        for way, part in self.totals():
            self.total_arrival(way, part).wait_recv()
        if not self.thirds:
            for way in (0, 1):
                self.back_copy(way).start()

    def sent(self):
        def done(step):
            self.core_copy(step).wait_send()
            if not (self.quartered or self.far_first):
                for way in (0, 1):
                    self.relay_copy(step, way).wait_send()
                    self.quarter_copy(step, way).wait_send()

        self.place.each(0, self.place.depth, done)
        if self.far_first:
            for way in (0, 1):
                self.relay_copy(0, way).wait_send()
                self.quarter_copy(0, way).wait_send()

    def finish(self):
        for part in range(self.parts):
            self.put_copy(part).wait()
        if not self.late:
            self.sent()
            self.place.each(1, self.place.depth, lambda step: self.z_copy(step).wait_send())
        for way, part in self.totals():
            self.total_copy(way, part).wait_send()
        if not self.thirds:
            for way in (0, 1):
                self.back_arrival(way).wait_recv()
                self.back_copy(way).wait_send()


REDUCE_REFS = 24


def backward_unit(
    pair, odd, half, tile, heads_ref, mask_ref, qd_ref, kf_ref, go_ref, lse_ref, out_ref, keys_sc, values_sc, keys_t, p_sc, s_sc, k_acc, v_acc
):
    length = heads_ref.shape[0]
    span = p_sc.shape[1]
    scale = jnp.asarray(1.0 / math.sqrt(DH), BF16)
    q_cols, k_cols, v_cols = qkv_columns(heads_ref, pair)
    cols = aligned(pair * LANES, LANES)
    mine = own_lanes(odd, (length, LANES))

    @pl.when(half == 0)
    def _():
        keys_sc[...] = jnp.where(mine, heads_ref[:, k_cols], kf_ref[...])
        values_sc[...] = jnp.where(mine, heads_ref[:, v_cols], jnp.zeros((), BF16))
        keys_t[...] = heads_ref[:, k_cols].T
        k_acc[...] = jnp.zeros_like(k_acc)
        v_acc[...] = jnp.zeros_like(v_acc)

    def one_tile(index, carry):
        here = aligned(index * tile, tile)
        rows = aligned(half * span + index * tile, tile)
        lanes = own_lanes(odd, (tile, LANES))
        queries = query_tile(
            heads_ref[rows, q_cols],
            qd_ref[rows, :],
            mask_ref,
            2 * pair + odd,
            half * (span // BLK) + index * (tile // BLK),
            lanes,
        )
        prob = jnp.exp(dot_nt(keys_sc[...], queries) - lse_ref[pair, pl.ds(odd, 1), rows])
        grad_prob = dot_nt(values_sc[...], go_ref[rows, cols])
        delta = jnp.sum(prob * grad_prob, axis=0, keepdims=True)
        p_sc[:, here] = prob.astype(BF16)
        s_sc[:, here] = (prob * (grad_prob - delta)).astype(BF16)
        return carry

    lax.fori_loop(0, span // tile, one_tile, 0, unroll=True)
    part = aligned(half * span, span)
    v_acc[...] += dot_nn(p_sc[...], go_ref[part, cols])
    k_acc[...] += dot_nn(s_sc[...], heads_ref[part, q_cols] * scale)
    grad_q = (dot_nn(keys_t[...], s_sc[...]) * (1.0 / math.sqrt(DH))).T.astype(BF16)
    out_ref[part, q_cols] = jnp.where(own_lanes(odd, (span, LANES)), grad_q, out_ref[part, q_cols])

    @pl.when(half == 1)
    def _():
        out_ref[:, k_cols] = jnp.where(mine, k_acc[...].astype(BF16), out_ref[:, k_cols])
        out_ref[:, v_cols] = jnp.where(mine, v_acc[...].astype(BF16), out_ref[:, v_cols])


def backward_kernel(
    fsdp_count,
    go_hbm,
    heads_hbm,
    mask_ref,
    qd_hbm,
    kf_hbm,
    lse_ref,
    n1_ref,
    wq_hbm,
    x_hbm,
    hid_hbm,
    vec_ref,
    small_ref,
    out_g_ref,
    in_g_ref,
    down_part,
    tokens_out,
    small_out,
    qkv_total,
    out_total,
    in_total,
    down_total,
    go_sc,
    heads_ref,
    qd_ref,
    kf_ref,
    wq_ref,
    x_ref,
    hid_ref,
    load_sems,
    grads_sc,
    keys_sc,
    values_sc,
    keys_t,
    p_sc,
    s_sc,
    k_acc,
    v_acc,
    n1_sc,
    qkv_g,
    part_sc,
    part_in,
    half_in,
    small_sc,
    small_in,
    *rest,
):
    place = Place(fsdp_count)
    rows = x_ref.shape[0]
    cut_at = in_g_ref.shape[1] * 3 // 4
    shared = pl.ds(0, cut_at)
    apart = pl.ds(cut_at, in_g_ref.shape[1] - cut_at)
    reduces = [
        Reduce.take(place, grad, out, False, rest[i * REDUCE_REFS : (i + 1) * REDUCE_REFS])
        for i, (grad, out) in enumerate(
            ((out_g_ref, out_total), (in_g_ref.at[:, shared], in_total.at[:, shared]))
        )
    ]
    lone = Reduce.take(
        place,
        in_g_ref.at[:, apart],
        in_total.at[:, apart],
        False,
        rest[3 * REDUCE_REFS : 4 * REDUCE_REFS],
        far_first=True,
    )
    first = Reduce.take(place, qkv_g, qkv_total, True, rest[2 * REDUCE_REFS : 3 * REDUCE_REFS], thirds=True)
    put_sem, f_pair, g_pair = (
        rest[4 * REDUCE_REFS],
        rest[4 * REDUCE_REFS + 1 : 4 * REDUCE_REFS + 3],
        rest[4 * REDUCE_REFS + 3 : 4 * REDUCE_REFS + 5],
    )
    down = Reduce(
        place,
        None,
        down_total,
        True,
        (None, None, None, None, None, down_part),
        (None, put_sem, None, None, None, None, f_pair, g_pair),
        late=True,
    )
    n_own, h_sent, h_got, p_sent, p_got, c_sent, c_got, z_sent, z_got, x_sent, x_got = rest[
        4 * REDUCE_REFS + 5 :
    ]
    seats = (place.s1, place.s2, place.s3)
    width = go_sc.shape[1]
    pairs = width // LANES
    half = rows // 2

    loads = [
        pltpu.make_async_copy(src, dst, load_sems.at[i])
        for i, (src, dst) in enumerate(
            (
                (heads_hbm, heads_ref),
                (qd_hbm, qd_ref),
                (kf_hbm, kf_ref),
                (go_hbm, go_sc),
                (wq_hbm, wq_ref),
                (x_hbm, x_ref),
                (hid_hbm, hid_ref),
            )
        )
    ]
    for load in loads:
        load.start()
    later_loads = loads[4:]
    place.meet()
    for one in reduces:
        one.begin()
    lone.begin()
    down.give()
    n1_copy = pltpu.make_async_copy(n1_ref, n1_sc, n_own)
    n1_copy.start()

    def unit(index):
        backward_unit(
            lax.div(index, 4), lax.rem(lax.div(index, 2), 2), lax.rem(index, 2), 256, heads_ref, mask_ref, qd_ref, kf_ref,
            go_sc, lse_ref, grads_sc, keys_sc, values_sc, keys_t, p_sc, s_sc, k_acc, v_acc,
        )

    def half_copy(way):
        src = part_sc.at[aligned(place.s3 * rows + way * half, half)]
        return send(src, half_in.at[way], (h_sent, h_got), way, place.across(way))

    def part_copy(way, late):
        side = 1 - way if late else way
        src = part_sc.at[aligned(seats[way] * rows + side * half, half)]
        dst = part_in.at[way, pl.ds(side * half, half)]
        return send(src, dst, (p_sent, p_got), 2 * way + late, place.across(way))

    def partial_dn1():
        later_loads[0].wait()
        for seat in (place.s3, place.s1, place.s2, place.s):
            here = aligned(seat * rows, rows)
            part_sc[here, :] = dot_nt(grads_sc[here, :], wq_ref[...]).astype(BF16)
            for way in (0, 1):
                if seat is place.s3:
                    half_copy(way).start()
                elif seat is seats[way]:
                    part_copy(way, 0).start()

    def weight_grad():
        n1_copy.wait()

        def body(index):
            cols = aligned(index * 256, 256)
            qkv_g[cols, :] = dot_tn(n1_sc[:, cols], grads_sc[...]).astype(BF16)

        lax.fori_loop(0, qkv_g.shape[0] // 256, lambda index, carry: (body(index), carry)[1], 0)
        first.begin()

    def swap_dn1():
        for way in (0, 1):
            half_copy(way).wait_recv()
            base = (place.s2, place.s1)[way] * rows + way * half

            def body(index):
                here = aligned(base + index * 32, 32)
                came = half_in[way, aligned(index * 32, 32), :]
                part_sc[here, :] = (part_sc[here, :].astype(F32) + came.astype(F32)).astype(BF16)

            lax.fori_loop(0, half // 32, lambda index, carry: (body(index), carry)[1], 0)
        for way in (0, 1):
            part_copy(way, 1).start()

    def fold_first():
        depth = place.depth
        place.each(1, depth, lambda step: first.fold(step, lax.rem(step + 1, depth)))
        first.fold(0, None)

    def core_small():
        return send(small_sc.at[0], small_sc.at[1], (c_sent, c_got), 0, place.beside)

    def z_small(step):
        return send(small_sc.at[2], small_in.at[step], (z_sent, z_got), step, place.along(place.far(step)))

    def x_small(way):
        return send(small_sc.at[3], small_sc.at[4 + way], (x_sent, x_got), way, place.across(way))

    def close_dn1():
        for way in (0, 1):
            for late in (0, 1):
                part_copy(way, late).wait_recv()
        for load in later_loads[1:]:
            load.wait()
        gain = vec_ref[0:1, :]

        def body(index, sums):
            here = aligned(index * 32, 32)
            mine = aligned(place.s * rows + index * 32, 32)
            dn1 = (
                part_sc[mine, :].astype(F32)
                + part_in[0, here, :].astype(F32)
                + part_in[1, here, :].astype(F32)
            )
            token_rows = x_ref[here, :].astype(F32)
            center = token_rows - jnp.mean(token_rows, axis=-1, keepdims=True)
            inv = lax.rsqrt(jnp.mean(center * center, axis=-1, keepdims=True) + 1e-05)
            hat = center * inv
            scaled = dn1 * gain
            grad = hid_ref[here, :] + inv * (
                scaled
                - jnp.mean(scaled, axis=-1, keepdims=True)
                - hat * jnp.mean(scaled * hat, axis=-1, keepdims=True)
            )
            tokens_out[here, :] = grad.astype(BF16)
            return (
                sums[0] + jnp.sum(dn1 * hat, axis=0, keepdims=True),
                sums[1] + jnp.sum(dn1, axis=0, keepdims=True),
            )

        none = jnp.zeros((1, x_ref.shape[1]), F32)
        gain_sum, bias_sum = lax.fori_loop(0, rows // 32, body, (none, none))
        small_sc[0] = small_ref[...]
        small_sc[0, 0:1, :] = gain_sum
        small_sc[0, 1:2, :] = bias_sum
        core_small().start()

    def small_z():
        core_small().wait_recv()
        small_sc[2] = small_sc[0] + small_sc[1]
        place.each(1, place.depth, lambda step: z_small(step).start())

    def small_x():
        place.each(1, place.depth, lambda step: z_small(step).wait_recv())
        small_in[0] = small_sc[2]
        if place.depth <= 8:
            total = small_in[place.back(0)]
            for z in range(1, place.depth):
                total = total + small_in[place.back(z)]
        else:
            total = lax.fori_loop(
                1, place.depth, lambda z, sofar: sofar + small_in[place.back(z)], small_in[place.back(0)]
            )
        small_sc[3] = total
        for way in range(3):
            x_small(way).start()

    def small_end():
        for way in range(3):
            x_small(way).wait_recv()
        small_out[...] = (small_sc[3] + small_sc[4]) + (small_sc[5] + small_sc[6])

    depth = place.depth
    loose = depth > 8

    def run(count, body):
        lax.fori_loop(1, count, lambda step, carry: (body(step), carry)[1], 0)

    def fold(index):
        for one in [lone] + reduces:
            if not loose:
                step = (index + 1) % depth
                one.fold(step, (step + 1) % depth if step else None)
            elif index == 0:
                run(depth, lambda step: one.fold(step, lax.rem(step + 1, depth)))
                one.fold(0, None)

    def swap(index):
        for one in reduces:
            if not loose:
                one.swap((index + 1) % depth)
            elif index == 0:
                run(depth, one.swap)
                one.swap(0)

    def close(index):
        for one in reduces:
            if not loose:
                one.close((index + 1) % depth, (index + 1) % depth == 0)
            elif index == 0:
                run(depth, lambda step: one.close(step, False))
                one.close(0, True)

    rounds = 1 if loose else depth
    fold(0)
    if rounds > 1:
        fold(1)
    for load in loads[:4]:
        load.wait()
    steps = []
    for index in range(rounds + 2):
        if 2 <= index < rounds:
            steps.append(functools.partial(fold, index))
        if index < rounds:
            steps.append(functools.partial(swap, index))
        if 0 <= index - 1 < rounds:
            steps.append(functools.partial(close, index - 1))
    steps.insert(len(steps) // 2, down.spread)
    count = 4 * pairs
    grads_sc[...] = jnp.zeros_like(grads_sc)
    in_turn(count, unit, [steps[i * len(steps) // count : (i + 1) * len(steps) // count] for i in range(count)])
    partial_dn1()
    weight_grad()
    lone.far_sum()
    swap_dn1()
    lone.swap(0)
    for one in reduces:
        one.collect()
    fold_first()
    lone.near_sum()
    close_dn1()
    small_z()
    for one in reduces + [lone]:
        one.spread()
    first.collect()
    small_x()
    first.spread()
    small_end()
    core_small().wait_send()
    place.each(1, place.depth, lambda step: z_small(step).wait_send())
    for way in range(3):
        x_small(way).wait_send()
        if way < 2:
            half_copy(way).wait_send()
            for late in (0, 1):
                part_copy(way, late).wait_send()
    for one in [first, down, lone] + reduces:
        one.finish()


def backward_attention(fsdp_count, grad_heads, saved, x, hid, small, grads, down_part):
    heads, mask, qd, kf, lse, n1, wq, vec = saved
    rows, width = x.shape
    length, own_width = grad_heads.shape
    depth = fsdp_count // 2
    span = length // 2
    anywhere = pl.BlockSpec(memory_space=pltpu.HBM)
    vmem = pl.BlockSpec(memory_space=pltpu.VMEM)
    share = wq.shape[0] // fsdp_count
    kept = [(grad.shape[0] // fsdp_count, grad.shape[1]) for grad in grads]
    kept_qkv = (share, 4 * wq.shape[1])
    down_kept = (down_part.shape[0], 4 * down_part.shape[1])
    shape = jax.ShapeDtypeStruct

    reduce_scratch = []
    cut_at = kept[1][1] * 3 // 4
    for one in (kept[0], (kept[1][0], cut_at)):
        reduce_scratch += Reduce.scratch(depth, *one, False)
    reduce_scratch += Reduce.scratch(depth, *kept_qkv, True)
    reduce_scratch += Reduce.scratch(depth, kept[1][0], kept[1][1] - cut_at, False, far_first=True)
    return pl.pallas_call(
        functools.partial(backward_kernel, fsdp_count),
        out_shape=(shape(x.shape, BF16), shape(small.shape, F32), shape(kept_qkv, BF16))
        + tuple(shape(one, BF16) for one in kept)
        + (shape(down_kept, BF16),),
        in_specs=[anywhere] * 2 + [vmem] + [anywhere] * 2 + [vmem] + [anywhere] * 4 + [vmem] * 2 + [anywhere] * 2 + [vmem],
        out_specs=(vmem, vmem, anywhere, anywhere, anywhere, anywhere),
        scratch_shapes=[
            pltpu.VMEM((length, own_width), BF16),
            pltpu.VMEM(heads.shape, BF16),
            pltpu.VMEM(qd.shape, BF16),
            pltpu.VMEM(kf.shape, BF16),
            pltpu.VMEM(wq.shape, BF16),
            pltpu.VMEM(x.shape, BF16),
            pltpu.VMEM(hid.shape, F32),
            dma(7),
            pltpu.VMEM((length, 3 * own_width), BF16),
            pltpu.VMEM((length, LANES), BF16),
            pltpu.VMEM((length, LANES), BF16),
            pltpu.VMEM((LANES, length), BF16),
            pltpu.VMEM((length, span), BF16),
            pltpu.VMEM((length, span), BF16),
            pltpu.VMEM((length, LANES), F32),
            pltpu.VMEM((length, LANES), F32),
            pltpu.VMEM((length, width), BF16),
            pltpu.VMEM(wq.shape, BF16),
            pltpu.VMEM((length, width), BF16),
            pltpu.VMEM((2, rows, width), BF16),
            pltpu.VMEM((2, rows // 2, width), BF16),
            pltpu.VMEM((7,) + small.shape, F32),
            pltpu.VMEM((depth,) + small.shape, F32),
        ]
        + reduce_scratch
        + [dma(3), dma(9), dma(9), dma(2), dma(2)]
        + [dma(), dma(2), dma(2), dma(4), dma(4)]
        + [dma(1), dma(1), dma(depth), dma(depth), dma(3), dma(3)],
        compiler_params=pltpu.CompilerParams(
            collective_id=3, has_side_effects=True, vmem_limit_bytes=60 << 20
        ),
    )(grad_heads, heads, mask, qd, kf, lse, n1, wq, x, hid, vec, small, *grads, down_part)


def middle_kernel(
    fsdp_count,
    att_hbm,
    x_hbm,
    cot_hbm,
    vec_ref,
    out_w_hbm,
    in_w_ref,
    down_w_ref,
    result_ref,
    go_all,
    hid_ref,
    small_ref,
    out_g_ref,
    in_g_ref,
    down_part,
    att_ref,
    x_ref,
    cot_ref,
    out_w_ref,
    fetch_sems,
    datt_ref,
    go_sems,
    go_sent,
    go_got,
    hidden_sc,
    n2_sc,
    n2_t,
    out_acc,
    dn2_acc,
    in_buf,
    down_buf,
    grad_buf,
    down_g,
    in_sems,
    down_sems,
    grad_sems,
    *rest,
):
    place = Place(fsdp_count)
    depth = place.depth
    down_like = rest[0]
    total = Reduce.take(place, down_g, down_like, False, rest[1:], True)
    rows, width = x_ref.shape
    span = down_buf.shape[1]
    hidden_units = down_g.shape[0]
    chunks = hidden_units // span
    paired = total.rows == span
    lines = rows // 32

    def order(index):
        if not paired:
            return index
        z = place.far(lax.rem(lax.div(index, 2) + 1, depth))
        return 2 * z + jnp.where(lax.rem(index, 2) == 0, 1 - place.c, place.c)

    def in_load(index):
        slot = lax.rem(index, 2)
        return pltpu.make_async_copy(
            in_w_ref.at[:, aligned(order(index) * span, span)], in_buf.at[slot], in_sems.at[slot]
        )

    def down_load(index):
        slot = lax.rem(index, 2)
        return pltpu.make_async_copy(
            down_w_ref.at[aligned(order(index) * span, span)], down_buf.at[slot], down_sems.at[slot]
        )

    def grad_store(index):
        slot = lax.rem(index, 2)
        return pltpu.make_async_copy(
            grad_buf.at[slot], in_g_ref.at[:, aligned(order(index) * span, span)], grad_sems.at[slot]
        )

    def over_rows(body, start=0):
        return lax.fori_loop(0, lines, lambda index, carry: body(aligned(index * 32, 32), carry), start)

    in_load(0).start()
    down_load(0).start()
    loads = [
        pltpu.make_async_copy(src, dst, fetch_sems.at[i])
        for i, (src, dst) in enumerate(((att_hbm, att_ref), (out_w_hbm, out_w_ref), (x_hbm, x_ref), (cot_hbm, cot_ref)))
    ]
    for load in loads:
        load.start()
    place.meet()
    for load in loads:
        load.wait()
    hidden_sc[...] = x_ref[...].astype(F32) + dot_nn(att_ref[...], out_w_ref[...])

    def normalise(here, carry):
        token_rows = hidden_sc[here, :]
        center = token_rows - jnp.mean(token_rows, axis=-1, keepdims=True)
        variance = jnp.mean(center * center, axis=-1, keepdims=True)
        normed = center * lax.rsqrt(variance + 1e-05) * vec_ref[2:3, :] + vec_ref[3:4, :]
        n2_sc[here, :] = normed.astype(BF16)
        out_acc[here, :] = token_rows + vec_ref[4:5, :]
        return carry

    over_rows(normalise)
    n2_t[...] = n2_sc[...].T
    dn2_acc[...] = jnp.zeros_like(dn2_acc)
    small_ref[...] = jnp.zeros_like(small_ref)

    def chunk(index):
        slot = lax.rem(index, 2)
        which = order(index)
        in_load(index).wait()
        down_load(index).wait()

        def ahead():
            in_load(index + 1).start()
            down_load(index + 1).start()

        pl.when(index + 1 < chunks)(ahead)
        per = width // span
        line = pl.ds(5 + lax.div(which, per), 1)
        cols = aligned(lax.rem(which, per) * span, span)
        pre = dot_nn(n2_sc[...], in_buf[slot]) + vec_ref[line, cols]
        inner = jnp.tanh(0.7978845608028654 * (pre + 0.044715 * pre * pre * pre))
        act = (0.5 * pre * (1.0 + inner)).astype(BF16)
        slope = 0.5 * (1.0 + inner) + (0.5 * 0.7978845608028654) * pre * (1.0 - inner * inner) * (
            1.0 + (3.0 * 0.044715) * pre * pre
        )
        grad = dot_nt(cot_ref[...], down_buf[slot]) * slope
        low = grad.astype(BF16)
        small_ref[line, cols] = jnp.sum(low.astype(F32), axis=0, keepdims=True)
        down_g[aligned(which * span, span), :] = dot_tn(act, cot_ref[...]).astype(BF16)
        out_acc[...] += dot_nn(act, down_buf[slot])
        dn2_acc[...] += dot_nt(low, in_buf[slot])
        pl.when(index >= 2)(lambda: grad_store(index - 2).wait())
        grad_buf[slot] = dot_nn(n2_t[...], low).astype(BF16)
        grad_store(index).start()

    def later(t):
        pl.when(jnp.logical_and(t >= 1, t <= depth))(lambda: total.swap(lax.rem(t, depth)))
        pl.when(t >= 2)(lambda: total.close(lax.rem(t + depth - 1, depth), t == depth + 1))

    if paired:

        def step(t, carry):
            dest = lax.rem(t + 1, depth)

            def one(side, carry):
                chunk(2 * t + side)
                pl.when(side == 0)(lambda: total.core_copy(dest).start())
                return carry

            lax.fori_loop(0, 2, one, 0)
            total.fold(dest, None)
            later(t)
            return carry

        lax.fori_loop(0, depth, step, 0)
    else:
        lax.fori_loop(0, chunks, lambda index, carry: (chunk(index), carry)[1], 0)
        place.each(0, depth, lambda step: total.core_copy(step).start())

        def step(t, carry):
            total.fold(lax.rem(t + 1, depth), None)
            later(t)
            return carry

        lax.fori_loop(0, depth, step, 0)

    def finish(here, sums):
        token_rows = hidden_sc[here, :]
        center = token_rows - jnp.mean(token_rows, axis=-1, keepdims=True)
        inv = lax.rsqrt(jnp.mean(center * center, axis=-1, keepdims=True) + 1e-05)
        hat = center * inv
        dn2 = dn2_acc[here, :]
        cot = cot_ref[here, :].astype(F32)
        scaled = dn2 * vec_ref[2:3, :]
        grad = cot + inv * (
            scaled
            - jnp.mean(scaled, axis=-1, keepdims=True)
            - hat * jnp.mean(scaled * hat, axis=-1, keepdims=True)
        )
        hid_ref[here, :] = grad
        n2_sc[here, :] = grad.astype(BF16)
        result_ref[here, :] = out_acc[here, :].astype(BF16)
        return (
            sums[0] + jnp.sum(dn2 * hat, axis=0, keepdims=True),
            sums[1] + jnp.sum(dn2, axis=0, keepdims=True),
            sums[2] + jnp.sum(cot, axis=0, keepdims=True),
        )

    none = jnp.zeros((1, width), F32)
    gain_sum, bias_sum, cot_sum = over_rows(finish, (none, none, none))
    small_ref[2:3, :] = gain_sum
    small_ref[3:4, :] = bias_sum
    small_ref[4:5, :] = cot_sum
    later(depth)
    datt_ref[...] = dot_nt(n2_sc[...], out_w_ref[...]).astype(BF16)
    seats = (place.s1, place.s2, place.s3)
    part = width // 4

    def go_copy(way):
        src = datt_ref.at[:, aligned(seats[way] * part, part)]
        return send(src, go_all.at[aligned(place.s * rows, rows)], (go_sent, go_got), way, place.across(way))

    def go_arrival(way):
        there = go_all.at[aligned(seats[way] * rows, rows)]
        return send(there, there, (go_sent, go_got), way, place.across(way))

    own_go = pltpu.make_async_copy(
        datt_ref.at[:, aligned(place.s * part, part)], go_all.at[aligned(place.s * rows, rows)], go_sems
    )
    for way in range(3):
        go_copy(way).start()
    own_go.start()
    out_g_ref[...] = dot_tn(att_ref[...], n2_sc[...]).astype(BF16)
    later(depth + 1)
    total.collect()
    down_part[...] = total.total[...]
    for index in (chunks - 2, chunks - 1):
        grad_store(index).wait()
    own_go.wait()
    for way in range(3):
        go_arrival(way).wait_recv()
        go_copy(way).wait_send()
    total.sent()
    place.each(1, depth, lambda step: total.z_copy(step).wait_send())


def middle(fsdp_count, att, x, cot, vec, w_out, w_in, w_down):
    rows, width = x.shape
    hidden_units = w_in.shape[1]
    span = 512
    depth = fsdp_count // 2
    anywhere = pl.BlockSpec(memory_space=pltpu.HBM)
    vmem = pl.BlockSpec(memory_space=pltpu.VMEM)
    shape = jax.ShapeDtypeStruct
    kept = (hidden_units // fsdp_count, width)
    return pl.pallas_call(
        functools.partial(middle_kernel, fsdp_count),
        out_shape=(
            shape((rows, width), BF16),
            shape((4 * rows, width // 4), BF16),
            shape((rows, width), F32),
            shape(vec.shape, F32),
            shape(w_out.shape, BF16),
            shape(w_in.shape, BF16),
            shape((kept[0], width // 4), BF16),
        ),
        in_specs=[anywhere] * 3 + [vmem] + [anywhere] * 3,
        out_specs=(vmem, anywhere, vmem, vmem, vmem, anywhere, vmem),
        scratch_shapes=[
            pltpu.VMEM((rows, width), BF16),
            pltpu.VMEM((rows, width), BF16),
            pltpu.VMEM((rows, width), BF16),
            pltpu.VMEM(w_out.shape, BF16),
            dma(4),
            pltpu.VMEM((rows, width), BF16),
            dma(),
            dma(3),
            dma(3),
            pltpu.VMEM((rows, width), F32),
            pltpu.VMEM((rows, width), BF16),
            pltpu.VMEM((width, rows), BF16),
            pltpu.VMEM((rows, width), F32),
            pltpu.VMEM((rows, width), F32),
            pltpu.VMEM((2, width, span), BF16),
            pltpu.VMEM((2, span, width), BF16),
            pltpu.VMEM((2, width, span), BF16),
            pltpu.VMEM((hidden_units, width), BF16),
            dma(2),
            dma(2),
            dma(2),
            pltpu.VMEM(kept, BF16),
        ]
        + Reduce.scratch(depth, *kept, False, True),
        compiler_params=pltpu.CompilerParams(
            collective_id=5, has_side_effects=True, vmem_limit_bytes=60 << 20
        ),
    )(att, x, cot, vec, w_out, w_in, w_down)


def results_kernel(share, held, *refs):
    sources, small, refs = refs[:6], refs[6], refs[7:]
    cut = len(refs) > 20
    count = 12 if cut else 6
    outs, refs = refs[:count], refs[count:]
    taken, given, in_sems, out_sems = refs[:6], refs[6:12], refs[12], refs[13]
    loads = [pltpu.make_async_copy(src, dst, in_sems.at[i]) for i, (src, dst) in enumerate(zip(sources, taken))]
    for load in loads:
        load.start()
    stores = []
    for i, load in enumerate(loads):
        load.wait()
        src, dst = taken[i], given[i]
        chunk = 32 if src.shape[0] % 32 == 0 else 16

        def body(index, carry):
            rows = aligned(index * chunk, chunk)
            dst[rows, :] = src[rows, :].astype(dst.dtype)
            return carry

        if dst.dtype == src.dtype:
            store = pltpu.make_async_copy(src, outs[i], out_sems.at[i])
        else:
            lax.fori_loop(0, src.shape[0] // chunk, body, 0)
            store = pltpu.make_async_copy(dst, outs[i], out_sems.at[i])
        store.start()
        stores.append(store)
    if cut:
        position = lax.axis_index("fsdp")
        cols = aligned(position * share, share)
        for line in range(5):
            outs[6 + line][...] = small[line : line + 1, cols]
        per = small.shape[1] // held
        outs[11][...] = small[pl.ds(5 + lax.div(position, per), 1), aligned(lax.rem(position, per) * held, held)]
    for store in stores:
        store.wait()


def write_results(share, held, arrays, small):
    shape = jax.ShapeDtypeStruct
    kinds = (F32, F32, F32, F32, BF16, BF16)
    shapes = [shape(a.shape, kind) for a, kind in zip(arrays, kinds)]
    cut = share % LANES == 0 and held % LANES == 0
    small_shapes = [shape((1, share), F32)] * 5 + [shape((1, held), F32)] if cut else []
    hbm = pl.BlockSpec(memory_space=pltpu.HBM)
    vmem = pl.BlockSpec(memory_space=pltpu.VMEM)
    outs = pl.pallas_call(
        functools.partial(results_kernel, share, held),
        out_shape=tuple(shapes + small_shapes),
        in_specs=[hbm] * 6 + [vmem],
        out_specs=tuple([hbm] * 6 + [vmem] * len(small_shapes)),
        scratch_shapes=[pltpu.VMEM(a.shape, BF16) for a in arrays]
        + [pltpu.VMEM(a.shape if kind == F32 else (16, LANES), kind) for a, kind in zip(arrays, kinds)]
        + [dma(6), dma(6)],
        compiler_params=pltpu.CompilerParams(vmem_limit_bytes=60 << 20),
    )(*arrays, small)
    if cut:
        return outs[:6], [part.reshape(-1) for part in outs[6:]]
    position = lax.axis_index("fsdp")
    lines = lax.dynamic_slice_in_dim(small[:5], position * share, share, axis=1)
    rest = small[5:].reshape(-1)
    return outs, [lines[i] for i in range(5)] + [lax.dynamic_slice_in_dim(rest, position * held, held)]


def per_device(
    fsdp_count,
    tokens,
    segment_ids,
    random_blocks,
    ln1_gain,
    ln1_bias,
    w_qkv,
    w_out,
    ln2_gain,
    ln2_bias,
    w_in,
    b_in,
    w_down,
    b_down,
    cotangent,
):
    width = tokens.shape[2]
    share, held = ln1_gain.shape[0], b_in.shape[0]
    lines = fsdp_count * held // width
    position = lax.axis_index("fsdp")
    column = jnp.arange(width, dtype=jnp.int32)
    narrow = jnp.tile(jnp.stack([ln1_gain, ln1_bias, ln2_gain, ln2_bias, b_down]), (1, fsdp_count))
    narrow = jnp.where(column // share == position, narrow, jnp.zeros((), BF16))
    line = jnp.arange(lines, dtype=jnp.int32)[:, None]
    broad = jnp.tile(b_in[None], (1, width // held))
    broad = jnp.where((line * width + column) // held == position, broad, jnp.zeros((), BF16))
    vec = jnp.concatenate([narrow, broad, jnp.zeros((-(5 + lines) % 16, width), BF16)], axis=0)
    tok_count = segment_ids.shape[1]
    seg_rows = -(-tok_count // (8 * LANES)) * 8
    seg = jnp.pad(segment_ids[0], (0, seg_rows * LANES - tok_count)).reshape(seg_rows, LANES)
    mask = block_mask(random_blocks)
    by_heads, lse, att_rows, out_weight, down_weight, in_weight, vec, normed_one, own_qkv, query_docs, key_feats = (
        forward_attention(fsdp_count, tokens[0], w_qkv, vec, seg, mask, w_out, w_down, w_in)
    )
    result, grad_att, grad_hidden, small, grad_out, grad_in, down_part = middle(
        fsdp_count, att_rows, tokens[0], cotangent[0], vec, out_weight, in_weight, down_weight
    )
    grad_tokens, small, total_qkv, total_out, total_in, total_down = backward_attention(
        fsdp_count,
        grad_att,
        (by_heads, mask, query_docs, key_feats, lse, normed_one, own_qkv, vec),
        tokens[0],
        grad_hidden,
        small,
        (grad_out, grad_in),
        down_part,
    )
    arrays, parts = write_results(
        share, held, (total_in, total_down, total_qkv, total_out, result, grad_tokens), small
    )
    return (
        arrays[4][None],
        arrays[5][None],
        parts[0],
        parts[1],
        arrays[2],
        arrays[3],
        parts[2],
        parts[3],
        arrays[0],
        parts[5],
        arrays[1],
        parts[4],
    )


def solution(mesh):
    return jax.shard_map(
        functools.partial(per_device, mesh.shape["fsdp"]),
        mesh=mesh,
        in_specs=(
            P("fsdp", "seq", None),
            P("fsdp", "seq"),
            P("seq", None, None),
            P("fsdp"),
            P("fsdp"),
            P("fsdp", None),
            P("fsdp", None),
            P("fsdp"),
            P("fsdp"),
            P("fsdp", None),
            P("fsdp"),
            P("fsdp", None),
            P("fsdp"),
            P("fsdp", "seq", None),
        ),
        out_specs=(
            P("fsdp", "seq", None),
            P("fsdp", "seq", None),
            P("fsdp"),
            P("fsdp"),
            P("fsdp", None),
            P("fsdp", None),
            P("fsdp"),
            P("fsdp"),
            P("fsdp", None),
            P("fsdp"),
            P("fsdp", None),
            P("fsdp"),
        ),
        check_vma=False,
    )
```

```python
import functools
import math

import jax
import jax.numpy as jnp
from jax import lax
from jax.experimental import pallas as pl
from jax.experimental.pallas import tpu as pltpu
from jax.sharding import PartitionSpec as P

DH = 64
BLK = 64
LANES = 128
NEG = -1e30
F32 = jnp.float32
BF16 = jnp.bfloat16


def dot_nn(a, b):
    return jnp.dot(a, b, preferred_element_type=F32)


def dot_nt(a, b):
    return lax.dot_general(a, b, (((1,), (1,)), ((), ())), preferred_element_type=F32)


def dot_tn(a, b):
    return lax.dot_general(a, b, (((0,), (0,)), ((), ())), preferred_element_type=F32)


DOCS = 6


def block_mask(random_blocks):
    heads, inner, _ = random_blocks.shape
    blocks = inner + 2
    ids = jnp.arange(blocks, dtype=jnp.int32)
    near = jnp.abs(ids[:, None] - ids[None, :]) <= 1
    edge = (ids == 0) | (ids == blocks - 1)
    fixed = near | edge[:, None] | edge[None, :]
    picked = jnp.any(random_blocks[:, :, :, None] == ids, axis=2)
    used = fixed[None] | jnp.pad(picked, ((0, 0), (1, 1), (0, 0)))
    row = jnp.pad(jnp.where(used, 0.0, NEG), ((0, 0), (0, 0), (0, DH - blocks)))
    return jnp.concatenate([row, row], axis=-1)


def token_features(start, docs, blocks):
    shape = (docs.shape[0], LANES)
    lane = lax.rem(lax.broadcasted_iota(jnp.int32, shape, 1), DH)
    block = lax.div(lax.broadcasted_iota(jnp.int32, shape, 0) + start, BLK)
    own = docs + blocks == lane
    other = jnp.where(own | (lane >= blocks + DOCS), 0.0, 1.0)
    key_part = jnp.where(lane < blocks, jnp.where(block == lane, 1.0, 0.0), other)
    return jnp.where(own, NEG, 0.0).astype(BF16), key_part.astype(BF16)


def query_tile(q_tile, doc_tile, mask_ref, head, first_block, lanes):
    scale = jnp.asarray(1.0 / math.sqrt(DH), BF16)
    count = q_tile.shape[0] // BLK
    mask = jnp.concatenate(
        [jnp.broadcast_to(mask_ref[head, pl.ds(first_block + i, 1), :], (BLK, LANES)) for i in range(count)], axis=0
    )
    return jnp.where(lanes, q_tile * scale, doc_tile + mask.astype(BF16))


def own_lanes(odd, shape):
    return lax.div(lax.broadcasted_iota(jnp.int32, shape, 1), DH) == odd


MESH = pl.DeviceIdType.MESH


class Place:
    def __init__(self, fsdp_count):
        self.depth = fsdp_count // 2
        self.s = lax.axis_index("seq")
        self.f = lax.axis_index("fsdp")
        self.z = lax.div(self.f, 2)
        self.c = lax.rem(self.f, 2)
        self.s1 = self.s + 1 - 2 * lax.rem(self.s, 2)
        self.s2 = self.s + 2 - 4 * lax.div(self.s, 2)
        self.s3 = 3 - self.s
        self.beside = (self.s, self.f + 1 - 2 * self.c)

    def across(self, index):
        return ((self.s1, self.s2, self.s3)[index], self.f)

    def far(self, step):
        return lax.rem(self.z + step, self.depth)

    def back(self, step):
        return lax.rem(self.z + self.depth - step, self.depth)

    def along(self, z):
        return (self.s, 2 * z + self.c)

    def meet(self):
        barrier = pltpu.get_barrier_semaphore()
        peers = [self.beside] + [self.across(i) for i in range(3)]
        for peer in peers:
            pl.semaphore_signal(barrier, inc=1, device_id=peer, device_id_type=MESH)
        self.each(1, self.depth, lambda step: pl.semaphore_signal(
            barrier, inc=1, device_id=self.along(self.far(step)), device_id_type=MESH
        ))
        pl.semaphore_wait(barrier, len(peers) + self.depth - 1)

    def each(self, start, stop, body):
        if stop - start <= 8:
            for step in range(start, stop):
                body(step)
        else:
            lax.fori_loop(start, stop, lambda step, carry: (body(step), carry)[1], 0)


def send(src, dst, sems, index, device):
    sent, got = sems
    return pltpu.make_async_remote_copy(
        src_ref=src,
        dst_ref=dst,
        send_sem=sent.at[index],
        recv_sem=got.at[index],
        device_id=device,
        device_id_type=MESH,
    )


def aligned(start, size):
    return pl.ds(pl.multiple_of(start, size), size)


class Gather:
    def __init__(self, place, src, dst, split, sems):
        self.place, self.src, self.dst, self.split = place, src, dst, split
        self.rows, self.cols = src.shape
        self.local, self.zs, self.xs, self.rs, self.cs = sems

    def block(self, z, core, quarter=None, half=None):
        rows = aligned((2 * z + core) * self.rows, self.rows)
        if quarter is None:
            return self.dst.at[rows]
        wide = self.cols // 4
        if half is None:
            return self.dst.at[rows, aligned(quarter * wide, wide)]
        return self.dst.at[rows, aligned(quarter * wide + half * (wide // 2), wide // 2)]

    def source(self, step, side):
        return self.place.z - step if side == 0 else self.place.z + step

    def has(self, step, side):
        z = self.source(step, side)
        return z >= 0 if side == 0 else z < self.place.depth

    def sends(self, step, side):
        p = self.place
        onward = p.z + 1 < p.depth if side == 0 else p.z > 0
        return jnp.logical_and(self.has(step - 1, side), onward)

    def slot(self, step, side):
        return 2 * step + side

    def own_copy(self):
        return pltpu.make_async_copy(self.src, self.block(self.place.z, self.place.c), self.local)

    def own_core(self):
        p = self.place
        return send(self.src, self.block(p.z, p.c), self.cs, 0, p.beside)

    def own_arrival(self):
        p = self.place
        there = self.block(p.z, 1 - p.c)
        return send(there, there, self.cs, 0, p.beside)

    def core_copy(self, step, side):
        p = self.place
        there = self.block(self.source(step, side), p.c)
        return send(there, there, self.cs, self.slot(step, side), p.beside)

    def core_arrival(self, step, side):
        p = self.place
        there = self.block(self.source(step, side), 1 - p.c)
        return send(there, there, self.cs, self.slot(step, side), p.beside)

    def z_copy(self, step, side):
        p = self.place
        z = self.source(step - 1, side)
        there = self.block(z, p.c, p.s) if self.split else self.block(z, p.c)
        src = there
        if isinstance(step, int) and step == 1:
            wide = self.cols // 4
            src = self.src.at[:, aligned(p.s * wide, wide)] if self.split else self.src
        return send(src, there, self.zs, self.slot(step, side), p.along(p.z + 1 - 2 * side))

    def z_arrival(self, step, side):
        p = self.place
        z = self.source(step, side)
        there = self.block(z, p.c, p.s) if self.split else self.block(z, p.c)
        return send(there, there, self.zs, self.slot(step, side), p.along(p.z - 1 + 2 * side))

    def x_copy(self, step, side, way):
        p = self.place
        there = self.block(self.source(step, side), p.c, p.s)
        return send(there, there, self.xs[way], self.slot(step, side), p.across(way))

    def x_arrival(self, step, side, way):
        p = self.place
        there = self.block(self.source(step, side), p.c, (p.s1, p.s2)[way])
        return send(there, there, self.xs[way], self.slot(step, side), p.across(way))

    def relay_copy(self, step, side, way):
        p = self.place
        there = self.block(self.source(step, side), p.c, (p.s2, p.s1)[way], 1 - way)
        return send(there, there, self.rs[way], self.slot(step, side), p.across(way))

    def relay_arrival(self, step, side, way):
        p = self.place
        there = self.block(self.source(step, side), p.c, p.s3, 1 - way)
        return send(there, there, self.rs[way], self.slot(step, side), p.across(way))

    def both(self, step, body, test=None):
        for side in (0, 1):
            pl.when((test or self.has)(step, side))(functools.partial(body, step, side))

    def begin(self):
        self.both(1, lambda step, side: self.z_copy(step, side).start(), self.sends)
        self.own_copy().start()
        self.own_core().start()

    def swap(self, step):
        def body(step, side):
            self.z_arrival(step, side).wait_recv()
            pl.when(self.sends(step + 1, side))(lambda: self.z_copy(step + 1, side).start())
            if self.split:
                for way in (0, 1):
                    self.x_copy(step, side, way).start()
            else:
                self.core_copy(step, side).start()

        self.both(step, body)

    def relay(self, step):
        def body(step, side):
            for way in (0, 1):
                self.x_arrival(step, side, way).wait_recv()
            for way in (0, 1):
                self.relay_copy(step, side, way).start()

        if self.split:
            self.both(step, body)

    def share(self, step):
        def body(step, side):
            for way in (0, 1):
                self.relay_arrival(step, side, way).wait_recv()
            self.core_copy(step, side).start()

        if self.split:
            self.both(step, body)

    def finish(self):
        self.own_copy().wait()
        self.own_core().wait_send()
        self.own_arrival().wait_recv()

        def close(step, side):
            if self.split:
                for way in (0, 1):
                    self.x_copy(step, side, way).wait_send()
                    self.relay_copy(step, side, way).wait_send()
            self.core_copy(step, side).wait_send()
            self.core_arrival(step, side).wait_recv()

        self.place.each(1, self.place.depth, lambda step: self.both(step, close))
        self.place.each(
            1,
            self.place.depth,
            lambda step: self.both(step, lambda step, side: self.z_copy(step, side).wait_send(), self.sends),
        )

    @staticmethod
    def scratch(depth, split):
        held = 2 * depth if split else 1
        return [dma()] + [dma(2 * depth)] * 2 + [dma(held)] * 8 + [dma(2 * depth)] * 2

    @staticmethod
    def take(refs):
        pairs = [(refs[i], refs[i + 1]) for i in range(1, 13, 2)]
        return (refs[0], pairs[0], pairs[1:3], pairs[3:5], pairs[5])


GATHER_SEMS = 13


def gather_steps(place, gathers, late, count, unit):
    depth = place.depth

    def swap(step):
        for one in gathers:
            one.swap(step)

    def relay(step):
        for one in gathers:
            one.relay(step)

    def share(step):
        for one in gathers:
            one.share(step)

    def late_swap(step):
        for one in late:
            one.swap(step)

    for one in late:
        one.begin()
    if depth <= 8:
        rounds = []
        for step in range(2, depth + 2):
            now = []
            if step <= depth:
                now.append(functools.partial(late_swap, step - 2)) if step > 2 else None
                now.append(functools.partial(share, step - 3)) if step > 3 else None
                now.append(functools.partial(swap, step)) if step < depth else None
                now.append(functools.partial(relay, step - 1))
            rounds.append(now)
        rounds[-1] = [functools.partial(share, step) for step in range(max(1, depth - 2), depth)]
        rounds[-1].append(functools.partial(late_swap, depth - 1))
        in_turn(count, unit, rounds[:count])
        for now in rounds[count:]:
            for one in now:
                one()
    else:
        in_turn(count, unit, [])
        swap(2)
        relay(1)

        def body(step, carry):
            late_swap(step - 2)
            share(step - 2)
            swap(step)
            relay(step - 1)
            return carry

        lax.fori_loop(3, depth, body, 0)
        late_swap(depth - 2)
        share(depth - 2)
        relay(depth - 1)
        share(depth - 1)
        late_swap(depth - 1)


def dma(*shape):
    return pltpu.SemaphoreType.DMA(shape) if shape else pltpu.SemaphoreType.DMA


def qkv_columns(heads_ref, pair):
    third = heads_ref.shape[1] // 3
    return tuple(aligned(i * third + pair * LANES, LANES) for i in range(3))


def attend_unit(pair, odd, tile, heads_ref, mask_ref, qd_ref, kf_ref, keys_sc, values_t, out_ref, lse_ref):
    length = heads_ref.shape[0]
    cols = aligned(pair * LANES, LANES)
    q_cols, k_cols, v_cols = qkv_columns(heads_ref, pair)
    mine = own_lanes(odd, (length, LANES))
    keys_sc[...] = jnp.where(mine, heads_ref[:, k_cols], kf_ref[...])

    @pl.when(odd == 0)
    def _():
        values_t[...] = heads_ref[:, v_cols].T
        out_ref[:, cols] = jnp.zeros((length, LANES), BF16)

    def one_tile(index, carry):
        rows = aligned(index * tile, tile)
        lanes = own_lanes(odd, (tile, LANES))
        queries = query_tile(
            heads_ref[rows, q_cols], qd_ref[rows, :], mask_ref, 2 * pair + odd, index * (tile // BLK), lanes
        )
        scores = dot_nt(keys_sc[...], queries)
        top = jnp.max(scores, axis=0, keepdims=True)
        prob = jnp.exp(scores - top)
        total = jnp.sum(prob, axis=0, keepdims=True)
        mixed = dot_nn(values_t[...], prob.astype(BF16)) / total
        lse_ref[pair, pl.ds(odd, 1), rows] = top + jnp.log(total)
        out_ref[rows, cols] = jnp.where(lanes, mixed.T.astype(BF16), out_ref[rows, cols])
        return carry

    lax.fori_loop(0, length // tile, one_tile, 0, unroll=2)


def in_turn(count, unit, actions):
    def body(index, carry):
        unit(index)
        for which, todo in enumerate(actions):
            if todo:

                @pl.when(index == which)
                def _(todo=todo):
                    for one in todo:
                        one()

        return carry

    lax.fori_loop(0, count, body, 0)


def forward_kernel(
    fsdp_count,
    x_ref,
    wq_ref,
    vec_ref,
    ids_ref,
    mask_ref,
    out_w_ref,
    down_w_ref,
    in_w_ref,
    heads_all,
    lse_ref,
    att_all,
    out_w_all,
    down_w_all,
    in_w_all,
    vec_sum,
    n1_all,
    wq_all,
    qd_ref,
    kf_ref,
    x_sc,
    n1_sc,
    wq_own,
    wq_sc,
    vec_sc,
    seg_ref,
    seg_sc,
    heads_sc,
    att_sc,
    keys_sc,
    values_t,
    *sems,
):
    place = Place(fsdp_count)
    rows, width = x_ref.shape
    own_width = wq_sc.shape[1]
    seats = (place.s1, place.s2, place.s3)

    def taken(i):
        return Gather.take(sems[i * GATHER_SEMS : (i + 1) * GATHER_SEMS])

    x_own, seg_own, keep_sems, pick_sems, x_sent, x_got, r_sent, r_got, g_sent, g_got, a_sent, a_got, a_own = sems[6 * GATHER_SEMS :]
    lone = pl.ds(0, in_w_ref.shape[1] // 2)
    shared = pl.ds(in_w_ref.shape[1] // 2, in_w_ref.shape[1] // 2)
    gathers = [
        Gather(place, src, dst, split, taken(i))
        for i, (src, dst, split) in enumerate(
            (
                (out_w_ref, out_w_all, True),
                (in_w_ref.at[:, shared], in_w_all.at[:, shared], True),
                (down_w_ref, down_w_all, True),
                (in_w_ref.at[:, lone], in_w_all.at[:, lone], False),
            )
        )
    ]
    late = [gathers.pop()]
    third = own_width // 3
    picks = [
        pltpu.make_async_copy(
            wq_ref.at[:, aligned((4 * i + place.s) * third, third)], wq_own.at[:, pl.ds(i * third, third)], pick_sems.at[i]
        )
        for i in range(3)
    ]
    for pick in picks:
        pick.start()
    seg_ref[...] = jnp.zeros_like(seg_ref)
    for part in range(ids_ref.shape[1] // LANES):
        seg_ref[part : part + 1, :] = ids_ref[:, part * LANES : (part + 1) * LANES]
    weight = Gather(place, wq_own, wq_sc, False, taken(4))
    vector = Gather(place, vec_ref, vec_sc, False, taken(5))
    half = rows // 2

    def x_rows(seat):
        return x_sc.at[aligned(seat * rows, rows)]

    def x_half(seat, part):
        return x_sc.at[aligned(seat * rows + part * half, half)]

    def x_copy(way):
        return send(x_ref, x_rows(place.s), (x_sent, x_got), way, place.across(way))

    def x_arrival(way):
        there = x_rows(seats[way])
        return send(there, there, (x_sent, x_got), way, place.across(way))

    def x_relay(way):
        there = x_half((place.s2, place.s1)[way], 1 - way)
        return send(there, there, (r_sent, r_got), way, place.across(way))

    def x_relayed(way):
        there = x_half(place.s3, 1 - way)
        return send(there, there, (r_sent, r_got), way, place.across(way))

    def seg_copy(way):
        return send(seg_ref, seg_sc.at[place.s], (g_sent, g_got), way, place.across(way))

    def seg_arrival(way):
        there = seg_sc.at[seats[way]]
        return send(there, there, (g_sent, g_got), way, place.across(way))

    place.meet()
    vector.begin()
    for pick in picks:
        pick.wait()
    weight.begin()
    for way in range(2):
        x_copy(way).start()
    for way in range(3):
        seg_copy(way).start()
    own_x = pltpu.make_async_copy(x_ref, x_rows(place.s), x_own)
    own_x.start()
    own_seg = pltpu.make_async_copy(seg_ref, seg_sc.at[place.s], seg_own)
    own_seg.start()
    def start_rest():
        for one in gathers:
            one.begin()

    if place.depth <= 8:
        for step in range(1, place.depth):
            vector.swap(step)
            weight.swap(step)
            if step == max(1, place.depth - 2):
                start_rest()
    else:
        place.each(1, place.depth, vector.swap)
        place.each(1, place.depth, weight.swap)
        start_rest()
    vector.finish()
    vec_rows = vec_ref.shape[0]
    total = vec_sc[pl.ds(0, vec_rows), :].astype(F32)
    if fsdp_count <= 8:
        for f in range(1, fsdp_count):
            total = total + vec_sc[pl.ds(f * vec_rows, vec_rows), :].astype(F32)
    else:
        total = lax.fori_loop(
            1, fsdp_count, lambda f, sofar: sofar + vec_sc[aligned(f * vec_rows, vec_rows), :].astype(F32), total
        )
    vec_sum[...] = total

    def normalise(seat):
        def body(part):
            token_rows = x_sc[aligned(seat * rows + part * 32, 32), :].astype(F32)
            center = token_rows - jnp.mean(token_rows, axis=-1, keepdims=True)
            variance = jnp.mean(center * center, axis=-1, keepdims=True)
            normed = center * lax.rsqrt(variance + 1e-05) * vec_sum[0:1, :] + vec_sum[1:2, :]
            n1_sc[aligned(seat * rows + part * 32, 32), :] = normed.astype(BF16)

        lax.fori_loop(0, rows // 32, lambda part, carry: (body(part), carry)[1], 0)

    def project(seat):
        here = aligned(seat * rows, rows)

        def body(part):
            cols = aligned(part * 256, 256)
            heads_sc[here, cols] = dot_nn(n1_sc[here, :], wq_sc[:, cols]).astype(BF16)

        lax.fori_loop(0, own_width // 256, lambda part, carry: (body(part), carry)[1], 0)

    own_x.wait()
    normalise(place.s)
    for way in range(2):
        x_arrival(way).wait_recv()
    for way in range(2):
        x_relay(way).start()
    for way in range(2):
        normalise(seats[way])
    weight.finish()
    project(place.s)
    for way in range(2):
        project(seats[way])
    for one in gathers:
        one.swap(1)
    for way in range(2):
        x_relayed(way).wait_recv()
    normalise(place.s3)
    project(place.s3)
    own_seg.wait()
    for way in range(3):
        seg_arrival(way).wait_recv()
    blocks = mask_ref.shape[1]
    for seat in range(4):
        columns = seg_sc[seat].T
        for part in range(rows // LANES):
            here = pl.ds(seat * rows + part * LANES, LANES)
            qd_ref[here, :], kf_ref[here, :] = token_features(
                seat * rows + part * LANES, columns[:, part : part + 1], blocks
            )
    keeps = [
        pltpu.make_async_copy(src, dst, keep_sems.at[i])
        for i, (src, dst) in enumerate(((heads_sc, heads_all), (n1_sc, n1_all), (wq_sc, wq_all)))
    ]
    for keep in keeps:
        keep.start()

    pairs = att_sc.shape[1] // LANES

    def att_copy(pair, way):
        cols = aligned((place.s * pairs + pair) * LANES, LANES)
        return send(
            att_sc.at[aligned(seats[way] * rows, rows), aligned(pair * LANES, LANES)],
            att_all.at[:, cols],
            (a_sent, a_got),
            pair * 3 + way,
            place.across(way),
        )

    def att_own(pair):
        cols = aligned((place.s * pairs + pair) * LANES, LANES)
        return pltpu.make_async_copy(
            att_sc.at[aligned(place.s * rows, rows), aligned(pair * LANES, LANES)],
            att_all.at[:, cols],
            a_own.at[pair],
        )

    def att_arrival(pair, way):
        there = att_all.at[:, aligned((seats[way] * pairs + pair) * LANES, LANES)]
        return send(there, there, (a_sent, a_got), pair * 3 + way, place.across(way))

    def unit(index):
        pair, odd = lax.div(index, 2), lax.rem(index, 2)
        attend_unit(pair, odd, 256, heads_sc, mask_ref, qd_ref, kf_ref, keys_sc, values_t, att_sc, lse_ref)

        @pl.when(odd == 1)
        def _():
            for way in range(3):
                att_copy(pair, way).start()
            att_own(pair).start()

    gather_steps(place, gathers, late, 2 * pairs, unit)
    for keep in keeps:
        keep.wait()
    for way in range(3):
        seg_copy(way).wait_send()
        if way < 2:
            x_copy(way).wait_send()
            x_relay(way).wait_send()
        for pair in range(pairs):
            att_copy(pair, way).wait_send()
            att_arrival(pair, way).wait_recv()
    for pair in range(pairs):
        att_own(pair).wait()
    for one in gathers + late:
        one.finish()


def forward_attention(fsdp_count, x, w_qkv, vec, seg, mask, w_out, w_down, w_in):
    rows, width = x.shape
    length = 4 * rows
    heads = mask.shape[0]
    pairs = heads // 2
    depth = fsdp_count // 2
    own_width = w_qkv.shape[1] // 4
    full = fsdp_count * w_qkv.shape[0]
    seg_rows = -(-seg.shape[1] // (8 * LANES)) * 8
    anywhere = pl.BlockSpec(memory_space=pltpu.HBM)
    vmem = pl.BlockSpec(memory_space=pltpu.VMEM)
    shape = jax.ShapeDtypeStruct

    def whole(shard):
        return shape((fsdp_count * shard.shape[0], shard.shape[1]), shard.dtype)

    return pl.pallas_call(
        functools.partial(forward_kernel, fsdp_count),
        out_shape=(
            shape((length, own_width), BF16),
            shape((pairs, 2, length), F32),
            shape((rows, heads * DH * 4), BF16),
            whole(w_out),
            whole(w_down),
            whole(w_in),
            shape(vec.shape, F32),
            shape((length, width), BF16),
            shape((full, own_width), BF16),
            shape((length, LANES), BF16),
            shape((length, LANES), BF16),
        ),
        in_specs=[anywhere] * 3 + [vmem] * 2 + [anywhere] * 3,
        out_specs=(anywhere, vmem, anywhere, anywhere, anywhere, anywhere, vmem, anywhere, anywhere, vmem, vmem),
        scratch_shapes=[
            pltpu.VMEM((length, width), BF16),
            pltpu.VMEM((length, width), BF16),
            pltpu.VMEM((w_qkv.shape[0], own_width), BF16),
            pltpu.VMEM((full, own_width), BF16),
            pltpu.VMEM((fsdp_count * vec.shape[0], vec.shape[1]), BF16),
            pltpu.VMEM((seg_rows, LANES), jnp.int32),
            pltpu.VMEM((4, seg_rows, LANES), jnp.int32),
            pltpu.VMEM((length, own_width), BF16),
            pltpu.VMEM((length, heads * DH), BF16),
            pltpu.VMEM((length, LANES), BF16),
            pltpu.VMEM((LANES, length), BF16),
        ]
        + Gather.scratch(depth, True) * 3
        + Gather.scratch(depth, False) * 3
        + [dma(), dma(), dma(3), dma(3), dma(2), dma(2), dma(2), dma(2), dma(3), dma(3)]
        + [dma(3 * pairs), dma(3 * pairs), dma(pairs)],
        compiler_params=pltpu.CompilerParams(
            collective_id=2, has_side_effects=True, vmem_limit_bytes=60 << 20
        ),
    )(x, w_qkv, vec, seg, mask, w_out, w_down, w_in)


def by_rows(count, cols, body):
    chunk = 16
    while count % (2 * chunk) == 0 and 2 * chunk * cols <= 16384:
        chunk *= 2
    lax.fori_loop(0, count // chunk, lambda i, carry: (body(aligned(i * chunk, chunk)), carry)[1], 0)


class Reduce:
    def __init__(self, place, grad, out, quartered, bufs, sems, direct=False, thirds=False, late=False, far_first=False):
        self.far_first = far_first
        self.place, self.grad, self.out, self.quartered, self.direct = place, grad, out, quartered, direct
        self.thirds, self.late = thirds, late
        self.rows, self.cols = out.shape
        self.wide = self.cols // 4
        self.acc, self.own, self.relay_in, self.quarter_in, self.z_in, self.total = bufs
        self.own_sem, self.put_sem, self.cs, self.rs, self.qs, self.zs, self.fs, self.gs = sems

    @staticmethod
    def scratch(depth, rows, cols, quartered, direct=False, far_first=False):
        held = cols // 4 if quartered else cols
        near = 1 if far_first else depth
        side = (1, 1, 16, LANES) if quartered else None
        return [
            pltpu.VMEM((depth, rows, held), BF16),
            pltpu.VMEM((16, LANES) if direct else (rows, held), BF16),
            pltpu.VMEM(side or (2, near, rows, cols // 8), BF16),
            pltpu.VMEM(side or (2, near, rows, cols // 4), BF16),
            pltpu.VMEM((depth, rows, cols if far_first else cols // 4), BF16),
            pltpu.VMEM((rows, cols // 4), BF16),
            dma(),
            dma(3),
        ] + [dma(depth)] * 12 + [dma(9)] * 2 + [dma(2)] * 2

    @staticmethod
    def take(place, grad, out, quartered, refs, direct=False, thirds=False, far_first=False):
        s = refs[8:]
        pairs = [(s[i], s[i + 1]) for i in range(0, 16, 2)]
        sems = (refs[6], refs[7], pairs[0], pairs[1:3], pairs[3:5], pairs[5], pairs[6], pairs[7])
        return Reduce(place, grad, out, quartered, refs[:6], sems, direct, thirds, False, far_first)

    def quarter(self, seat):
        return aligned(seat * self.wide, self.wide)

    def mine(self):
        if self.far_first:
            return pl.ds(0, self.cols)
        return pl.ds(0, self.wide) if self.quartered else self.quarter(self.place.s)

    def piece(self, seat, half):
        return aligned(seat * self.wide + half * (self.wide // 2), self.wide // 2)

    def own_copy(self, step):
        p = self.place
        rows = aligned((2 * p.far(step) + p.c) * self.rows, self.rows)
        return pltpu.make_async_copy(self.grad.at[rows], self.own, self.own_sem)

    def core_copy(self, step):
        p = self.place
        rows = aligned((2 * p.far(step) + 1 - p.c) * self.rows, self.rows)
        return send(self.grad.at[rows], self.acc.at[step], self.cs, step, p.beside)

    def relay_copy(self, step, way):
        p = self.place
        src = self.acc.at[step, :, self.piece(p.s3, way)]
        return send(src, self.relay_in.at[way, step], self.rs[way], step, p.across(way))

    def quarter_copy(self, step, way):
        p = self.place
        src = self.acc.at[step, :, self.quarter((p.s1, p.s2)[way])]
        return send(src, self.quarter_in.at[way, step], self.qs[way], step, p.across(way))

    def z_copy(self, step):
        p = self.place
        src = self.acc.at[step, :, self.mine()]
        return send(src, self.z_in.at[step], self.zs, step, p.along(p.far(step)))

    def columns(self, seat, part):
        if not self.thirds:
            return self.quarter(seat), pl.ds(0, self.wide)
        third = self.wide // 3
        return aligned((4 * part + seat) * third, third), pl.ds(part * third, third)

    @property
    def parts(self):
        return 3 if self.thirds else 1

    def put_copy(self, part):
        there, here = self.columns(self.place.s, part)
        return pltpu.make_async_copy(self.total.at[:, here], self.out.at[:, there], self.put_sem.at[part])

    def total_copy(self, way, part):
        p = self.place
        there, here = self.columns(p.s, part)
        return send(self.total.at[:, here], self.out.at[:, there], self.fs, 3 * way + part, p.across(way))

    def total_arrival(self, way, part):
        p = self.place
        there = self.out.at[:, self.columns((p.s1, p.s2, p.s3)[way], part)[0]]
        return send(there, there, self.fs, 3 * way + part, p.across(way))

    def totals(self):
        return [(way, part) for way in range(3 if self.thirds else 2) for part in range(self.parts)]

    def back_copy(self, way):
        p = self.place
        there = self.out.at[:, self.piece((p.s2, p.s1)[way], 1 - way)]
        return send(there, there, self.gs, way, p.across(way))

    def back_arrival(self, way):
        p = self.place
        there = self.out.at[:, self.piece(p.s3, 1 - way)]
        return send(there, there, self.gs, way, p.across(way))

    def begin(self):
        depth = self.place.depth
        self.place.each(1, depth, lambda step: self.core_copy(step).start())
        self.core_copy(0).start()
        self.own_copy(1).start()

    def fold(self, step, following):
        p, acc, own = self.place, self.acc, self.own
        self.core_copy(step).wait_recv()
        if not self.direct:
            self.own_copy(step).wait()
        base = (2 * p.far(step) + p.c) * self.rows

        def body(index, carry):
            rows = aligned(index * 16, 16)
            added = self.grad[aligned(base + index * 16, 16), :] if self.direct else own[rows, :]
            acc[step, rows, :] = acc[step, rows, :] + added
            return carry

        lax.fori_loop(0, self.rows // 16, body, 0)
        if following is not None:
            self.own_copy(following).start()
        if not (self.quartered or self.far_first):
            for way in (0, 1):
                self.relay_copy(step, way).start()
        elif not (isinstance(step, int) and step == 0):
            self.z_copy(step).start()

    def swap(self, step):
        if self.quartered:
            return
        p, acc = self.place, self.acc
        for way in (0, 1):
            self.relay_copy(step, way).wait_recv()
            cols = self.piece((p.s2, p.s1)[way], way)
            came = self.relay_in.at[way, step]

            def body(rows):
                acc[step, rows, cols] = acc[step, rows, cols] + came[rows, :]

            by_rows(self.rows, self.wide // 2, body)
        for way in (0, 1):
            self.quarter_copy(step, way).start()

    def close(self, step, own):
        if self.quartered:
            return
        p, acc, came = self.place, self.acc, self.quarter_in
        for way in (0, 1):
            self.quarter_copy(step, way).wait_recv()
        cols = self.quarter(p.s)

        def body(rows):
            acc[step, rows, cols] = (
                acc[step, rows, cols].astype(F32)
                + came[0, step, rows, :].astype(F32)
                + came[1, step, rows, :].astype(F32)
            ).astype(BF16)

        by_rows(self.rows, self.wide, body)
        if not self.far_first:
            pl.when(jnp.logical_not(own))(lambda: self.z_copy(step).start())

    def far_sum(self):
        p, acc, came = self.place, self.acc, self.z_in
        p.each(1, p.depth, lambda step: self.z_copy(step).wait_recv())

        def body(rows):
            start = acc[0, rows, :].astype(F32)
            if p.depth <= 8:
                for step in range(1, p.depth):
                    start = start + came[step, rows, :].astype(F32)
            else:
                start = lax.fori_loop(1, p.depth, lambda step, sofar: sofar + came[step, rows, :].astype(F32), start)
            acc[0, rows, :] = start.astype(BF16)

        by_rows(self.rows, self.cols, body)
        for way in (0, 1):
            self.relay_copy(0, way).start()

    def near_sum(self):
        self.close(0, True)
        total, acc, cols = self.total, self.acc, self.quarter(self.place.s)

        def body(rows):
            total[rows, :] = acc[0, rows, cols]

        by_rows(self.rows, self.wide, body)
        self.give()

    def collect(self):
        p, acc, came, total = self.place, self.acc, self.z_in, self.total
        p.each(1, p.depth, lambda step: self.z_copy(step).wait_recv())
        cols = self.mine()

        def body(rows):
            start = acc[0, rows, cols].astype(F32)
            if p.depth <= 8:
                for step in range(1, p.depth):
                    start = start + came[step, rows, :].astype(F32)
            else:
                start = lax.fori_loop(1, p.depth, lambda step, sofar: sofar + came[step, rows, :].astype(F32), start)
            total[rows, :] = start.astype(BF16)

        by_rows(self.rows, self.wide, body)
        if not self.direct:
            self.give()

    def give(self):
        for way, part in self.totals():
            self.total_copy(way, part).start()
        for part in range(self.parts):
            self.put_copy(part).start()

    def spread(self):
        for way, part in self.totals():
            self.total_arrival(way, part).wait_recv()
        if not self.thirds:
            for way in (0, 1):
                self.back_copy(way).start()

    def sent(self):
        def done(step):
            self.core_copy(step).wait_send()
            if not (self.quartered or self.far_first):
                for way in (0, 1):
                    self.relay_copy(step, way).wait_send()
                    self.quarter_copy(step, way).wait_send()

        self.place.each(0, self.place.depth, done)
        if self.far_first:
            for way in (0, 1):
                self.relay_copy(0, way).wait_send()
                self.quarter_copy(0, way).wait_send()

    def finish(self):
        for part in range(self.parts):
            self.put_copy(part).wait()
        if not self.late:
            self.sent()
            self.place.each(1, self.place.depth, lambda step: self.z_copy(step).wait_send())
        for way, part in self.totals():
            self.total_copy(way, part).wait_send()
        if not self.thirds:
            for way in (0, 1):
                self.back_arrival(way).wait_recv()
                self.back_copy(way).wait_send()


REDUCE_REFS = 24


def backward_unit(
    pair, odd, half, tile, heads_ref, mask_ref, qd_ref, kf_ref, go_ref, lse_ref, out_ref, keys_sc, values_sc, keys_t, p_sc, s_sc, k_acc, v_acc
):
    length = heads_ref.shape[0]
    span = p_sc.shape[1]
    scale = jnp.asarray(1.0 / math.sqrt(DH), BF16)
    q_cols, k_cols, v_cols = qkv_columns(heads_ref, pair)
    cols = aligned(pair * LANES, LANES)
    mine = own_lanes(odd, (length, LANES))

    @pl.when(half == 0)
    def _():
        keys_sc[...] = jnp.where(mine, heads_ref[:, k_cols], kf_ref[...])
        values_sc[...] = jnp.where(mine, heads_ref[:, v_cols], jnp.zeros((), BF16))
        keys_t[...] = heads_ref[:, k_cols].T
        k_acc[...] = jnp.zeros_like(k_acc)
        v_acc[...] = jnp.zeros_like(v_acc)

    def one_tile(index, carry):
        here = aligned(index * tile, tile)
        rows = aligned(half * span + index * tile, tile)
        lanes = own_lanes(odd, (tile, LANES))
        queries = query_tile(
            heads_ref[rows, q_cols],
            qd_ref[rows, :],
            mask_ref,
            2 * pair + odd,
            half * (span // BLK) + index * (tile // BLK),
            lanes,
        )
        prob = jnp.exp(dot_nt(keys_sc[...], queries) - lse_ref[pair, pl.ds(odd, 1), rows])
        grad_prob = dot_nt(values_sc[...], go_ref[rows, cols])
        delta = jnp.sum(prob * grad_prob, axis=0, keepdims=True)
        p_sc[:, here] = prob.astype(BF16)
        s_sc[:, here] = (prob * (grad_prob - delta)).astype(BF16)
        return carry

    lax.fori_loop(0, span // tile, one_tile, 0, unroll=True)
    part = aligned(half * span, span)
    v_acc[...] += dot_nn(p_sc[...], go_ref[part, cols])
    k_acc[...] += dot_nn(s_sc[...], heads_ref[part, q_cols] * scale)
    grad_q = (dot_nn(keys_t[...], s_sc[...]) * (1.0 / math.sqrt(DH))).T.astype(BF16)
    out_ref[part, q_cols] = jnp.where(own_lanes(odd, (span, LANES)), grad_q, out_ref[part, q_cols])

    @pl.when(half == 1)
    def _():
        out_ref[:, k_cols] = jnp.where(mine, k_acc[...].astype(BF16), out_ref[:, k_cols])
        out_ref[:, v_cols] = jnp.where(mine, v_acc[...].astype(BF16), out_ref[:, v_cols])


def backward_kernel(
    fsdp_count,
    go_hbm,
    heads_hbm,
    mask_ref,
    qd_hbm,
    kf_hbm,
    lse_ref,
    n1_ref,
    wq_hbm,
    x_hbm,
    hid_hbm,
    vec_ref,
    small_ref,
    out_g_ref,
    in_g_ref,
    down_part,
    tokens_out,
    small_out,
    qkv_total,
    out_total,
    in_total,
    down_total,
    go_sc,
    heads_ref,
    qd_ref,
    kf_ref,
    wq_ref,
    x_ref,
    hid_ref,
    load_sems,
    grads_sc,
    keys_sc,
    values_sc,
    keys_t,
    p_sc,
    s_sc,
    k_acc,
    v_acc,
    n1_sc,
    qkv_g,
    part_sc,
    part_in,
    half_in,
    small_sc,
    small_in,
    *rest,
):
    place = Place(fsdp_count)
    rows = x_ref.shape[0]
    cut_at = in_g_ref.shape[1] * 3 // 4
    shared = pl.ds(0, cut_at)
    apart = pl.ds(cut_at, in_g_ref.shape[1] - cut_at)
    reduces = [
        Reduce.take(place, grad, out, False, rest[i * REDUCE_REFS : (i + 1) * REDUCE_REFS])
        for i, (grad, out) in enumerate(
            ((out_g_ref, out_total), (in_g_ref.at[:, shared], in_total.at[:, shared]))
        )
    ]
    lone = Reduce.take(
        place,
        in_g_ref.at[:, apart],
        in_total.at[:, apart],
        False,
        rest[3 * REDUCE_REFS : 4 * REDUCE_REFS],
        far_first=True,
    )
    first = Reduce.take(place, qkv_g, qkv_total, True, rest[2 * REDUCE_REFS : 3 * REDUCE_REFS], thirds=True)
    put_sem, f_pair, g_pair = (
        rest[4 * REDUCE_REFS],
        rest[4 * REDUCE_REFS + 1 : 4 * REDUCE_REFS + 3],
        rest[4 * REDUCE_REFS + 3 : 4 * REDUCE_REFS + 5],
    )
    down = Reduce(
        place,
        None,
        down_total,
        True,
        (None, None, None, None, None, down_part),
        (None, put_sem, None, None, None, None, f_pair, g_pair),
        late=True,
    )
    n_own, h_sent, h_got, p_sent, p_got, c_sent, c_got, z_sent, z_got, x_sent, x_got = rest[
        4 * REDUCE_REFS + 5 :
    ]
    seats = (place.s1, place.s2, place.s3)
    width = go_sc.shape[1]
    pairs = width // LANES
    half = rows // 2

    loads = [
        pltpu.make_async_copy(src, dst, load_sems.at[i])
        for i, (src, dst) in enumerate(
            (
                (heads_hbm, heads_ref),
                (qd_hbm, qd_ref),
                (kf_hbm, kf_ref),
                (go_hbm, go_sc),
                (wq_hbm, wq_ref),
                (x_hbm, x_ref),
                (hid_hbm, hid_ref),
            )
        )
    ]
    for load in loads:
        load.start()
    later_loads = loads[4:]
    place.meet()
    def first_copies(step):
        for one in reduces + [lone]:
            one.core_copy(step).start()

    place.each(1, place.depth, first_copies)
    first_copies(0)
    for one in reduces + [lone]:
        one.own_copy(1).start()
    down.give()
    n1_copy = pltpu.make_async_copy(n1_ref, n1_sc, n_own)
    n1_copy.start()

    def unit(index):
        backward_unit(
            lax.div(index, 4), lax.rem(lax.div(index, 2), 2), lax.rem(index, 2), 256, heads_ref, mask_ref, qd_ref, kf_ref,
            go_sc, lse_ref, grads_sc, keys_sc, values_sc, keys_t, p_sc, s_sc, k_acc, v_acc,
        )

    def half_copy(way):
        src = part_sc.at[aligned(place.s3 * rows + way * half, half)]
        return send(src, half_in.at[way], (h_sent, h_got), way, place.across(way))

    def part_copy(way, late):
        side = 1 - way if late else way
        src = part_sc.at[aligned(seats[way] * rows + side * half, half)]
        dst = part_in.at[way, pl.ds(side * half, half)]
        return send(src, dst, (p_sent, p_got), 2 * way + late, place.across(way))

    def partial_dn1():
        later_loads[0].wait()
        for seat in (place.s3, place.s1, place.s2, place.s):
            here = aligned(seat * rows, rows)
            part_sc[here, :] = dot_nt(grads_sc[here, :], wq_ref[...]).astype(BF16)
            for way in (0, 1):
                if seat is place.s3:
                    half_copy(way).start()
                elif seat is seats[way]:
                    part_copy(way, 0).start()

    def weight_grad():
        n1_copy.wait()

        def body(index):
            cols = aligned(index * 256, 256)
            qkv_g[cols, :] = dot_tn(n1_sc[:, cols], grads_sc[...]).astype(BF16)

        lax.fori_loop(0, qkv_g.shape[0] // 256, lambda index, carry: (body(index), carry)[1], 0)
        first.begin()

    def swap_dn1():
        for way in (0, 1):
            half_copy(way).wait_recv()
            base = (place.s2, place.s1)[way] * rows + way * half

            def body(index):
                here = aligned(base + index * 32, 32)
                came = half_in[way, aligned(index * 32, 32), :]
                part_sc[here, :] = (part_sc[here, :].astype(F32) + came.astype(F32)).astype(BF16)

            lax.fori_loop(0, half // 32, lambda index, carry: (body(index), carry)[1], 0)
        for way in (0, 1):
            part_copy(way, 1).start()

    def fold_first():
        depth = place.depth
        place.each(1, depth, lambda step: first.fold(step, lax.rem(step + 1, depth)))
        first.fold(0, None)

    def core_small():
        return send(small_sc.at[0], small_sc.at[1], (c_sent, c_got), 0, place.beside)

    def z_small(step):
        return send(small_sc.at[2], small_in.at[step], (z_sent, z_got), step, place.along(place.far(step)))

    def x_small(way):
        return send(small_sc.at[3], small_sc.at[4 + way], (x_sent, x_got), way, place.across(way))

    def close_dn1():
        for way in (0, 1):
            for late in (0, 1):
                part_copy(way, late).wait_recv()
        for load in later_loads[1:]:
            load.wait()
        gain = vec_ref[0:1, :]

        def body(index, sums):
            here = aligned(index * 32, 32)
            mine = aligned(place.s * rows + index * 32, 32)
            dn1 = (
                part_sc[mine, :].astype(F32)
                + part_in[0, here, :].astype(F32)
                + part_in[1, here, :].astype(F32)
            )
            token_rows = x_ref[here, :].astype(F32)
            center = token_rows - jnp.mean(token_rows, axis=-1, keepdims=True)
            inv = lax.rsqrt(jnp.mean(center * center, axis=-1, keepdims=True) + 1e-05)
            hat = center * inv
            scaled = dn1 * gain
            grad = hid_ref[here, :] + inv * (
                scaled
                - jnp.mean(scaled, axis=-1, keepdims=True)
                - hat * jnp.mean(scaled * hat, axis=-1, keepdims=True)
            )
            tokens_out[here, :] = grad.astype(BF16)
            return (
                sums[0] + jnp.sum(dn1 * hat, axis=0, keepdims=True),
                sums[1] + jnp.sum(dn1, axis=0, keepdims=True),
            )

        none = jnp.zeros((1, x_ref.shape[1]), F32)
        gain_sum, bias_sum = lax.fori_loop(0, rows // 32, body, (none, none))
        small_sc[0] = small_ref[...]
        small_sc[0, 0:1, :] = gain_sum
        small_sc[0, 1:2, :] = bias_sum
        core_small().start()

    def small_z():
        core_small().wait_recv()
        small_sc[2] = small_sc[0] + small_sc[1]
        place.each(1, place.depth, lambda step: z_small(step).start())

    def small_x():
        place.each(1, place.depth, lambda step: z_small(step).wait_recv())
        small_in[0] = small_sc[2]
        if place.depth <= 8:
            total = small_in[place.back(0)]
            for z in range(1, place.depth):
                total = total + small_in[place.back(z)]
        else:
            total = lax.fori_loop(
                1, place.depth, lambda z, sofar: sofar + small_in[place.back(z)], small_in[place.back(0)]
            )
        small_sc[3] = total
        for way in range(3):
            x_small(way).start()

    def small_end():
        for way in range(3):
            x_small(way).wait_recv()
        small_out[...] = (small_sc[3] + small_sc[4]) + (small_sc[5] + small_sc[6])

    depth = place.depth
    loose = depth > 8

    def run(count, body):
        lax.fori_loop(1, count, lambda step, carry: (body(step), carry)[1], 0)

    def fold(index):
        for one in reduces + [lone]:
            if not loose:
                step = (index + 1) % depth
                one.fold(step, (step + 1) % depth if step else None)
            elif index == 0:
                run(depth, lambda step: one.fold(step, lax.rem(step + 1, depth)))
                one.fold(0, None)

    def swap(index):
        for one in reduces:
            if not loose:
                one.swap((index + 1) % depth)
            elif index == 0:
                run(depth, one.swap)
                one.swap(0)

    def close(index):
        for one in reduces:
            if not loose:
                one.close((index + 1) % depth, (index + 1) % depth == 0)
            elif index == 0:
                run(depth, lambda step: one.close(step, False))
                one.close(0, True)

    rounds = 1 if loose else depth
    fold(0)
    if rounds > 1:
        fold(1)
    for load in loads[:4]:
        load.wait()
    steps = []
    for index in range(rounds + 2):
        if 2 <= index < rounds:
            steps.append(functools.partial(fold, index))
        if index < rounds:
            steps.append(functools.partial(swap, index))
        if 0 <= index - 1 < rounds:
            steps.append(functools.partial(close, index - 1))
    steps.insert(len(steps) // 2, down.spread)
    count = 4 * pairs
    grads_sc[...] = jnp.zeros_like(grads_sc)
    in_turn(count, unit, [steps[i * len(steps) // count : (i + 1) * len(steps) // count] for i in range(count)])
    partial_dn1()
    weight_grad()
    lone.far_sum()
    swap_dn1()
    lone.swap(0)
    for one in reduces:
        one.collect()
    fold_first()
    lone.near_sum()
    close_dn1()
    small_z()
    for one in reduces + [lone]:
        one.spread()
    first.collect()
    small_x()
    first.spread()
    small_end()
    core_small().wait_send()
    place.each(1, place.depth, lambda step: z_small(step).wait_send())
    for way in range(3):
        x_small(way).wait_send()
        if way < 2:
            half_copy(way).wait_send()
            for late in (0, 1):
                part_copy(way, late).wait_send()
    for one in [first, down, lone] + reduces:
        one.finish()


def backward_attention(fsdp_count, grad_heads, saved, x, hid, small, grads, down_part):
    heads, mask, qd, kf, lse, n1, wq, vec = saved
    rows, width = x.shape
    length, own_width = grad_heads.shape
    depth = fsdp_count // 2
    span = length // 2
    anywhere = pl.BlockSpec(memory_space=pltpu.HBM)
    vmem = pl.BlockSpec(memory_space=pltpu.VMEM)
    share = wq.shape[0] // fsdp_count
    kept = [(grad.shape[0] // fsdp_count, grad.shape[1]) for grad in grads]
    kept_qkv = (share, 4 * wq.shape[1])
    down_kept = (down_part.shape[0], 4 * down_part.shape[1])
    shape = jax.ShapeDtypeStruct

    reduce_scratch = []
    cut_at = kept[1][1] * 3 // 4
    for one in (kept[0], (kept[1][0], cut_at)):
        reduce_scratch += Reduce.scratch(depth, *one, False)
    reduce_scratch += Reduce.scratch(depth, *kept_qkv, True)
    reduce_scratch += Reduce.scratch(depth, kept[1][0], kept[1][1] - cut_at, False, far_first=True)
    return pl.pallas_call(
        functools.partial(backward_kernel, fsdp_count),
        out_shape=(shape(x.shape, BF16), shape(small.shape, F32), shape(kept_qkv, BF16))
        + tuple(shape(one, BF16) for one in kept)
        + (shape(down_kept, BF16),),
        in_specs=[anywhere] * 2 + [vmem] + [anywhere] * 2 + [vmem] + [anywhere] * 4 + [vmem] * 2 + [anywhere] * 2 + [vmem],
        out_specs=(vmem, vmem, anywhere, anywhere, anywhere, anywhere),
        scratch_shapes=[
            pltpu.VMEM((length, own_width), BF16),
            pltpu.VMEM(heads.shape, BF16),
            pltpu.VMEM(qd.shape, BF16),
            pltpu.VMEM(kf.shape, BF16),
            pltpu.VMEM(wq.shape, BF16),
            pltpu.VMEM(x.shape, BF16),
            pltpu.VMEM(hid.shape, F32),
            dma(7),
            pltpu.VMEM((length, 3 * own_width), BF16),
            pltpu.VMEM((length, LANES), BF16),
            pltpu.VMEM((length, LANES), BF16),
            pltpu.VMEM((LANES, length), BF16),
            pltpu.VMEM((length, span), BF16),
            pltpu.VMEM((length, span), BF16),
            pltpu.VMEM((length, LANES), F32),
            pltpu.VMEM((length, LANES), F32),
            pltpu.VMEM((length, width), BF16),
            pltpu.VMEM(wq.shape, BF16),
            pltpu.VMEM((length, width), BF16),
            pltpu.VMEM((2, rows, width), BF16),
            pltpu.VMEM((2, rows // 2, width), BF16),
            pltpu.VMEM((7,) + small.shape, F32),
            pltpu.VMEM((depth,) + small.shape, F32),
        ]
        + reduce_scratch
        + [dma(3), dma(9), dma(9), dma(2), dma(2)]
        + [dma(), dma(2), dma(2), dma(4), dma(4)]
        + [dma(1), dma(1), dma(depth), dma(depth), dma(3), dma(3)],
        compiler_params=pltpu.CompilerParams(
            collective_id=3, has_side_effects=True, vmem_limit_bytes=60 << 20
        ),
    )(grad_heads, heads, mask, qd, kf, lse, n1, wq, x, hid, vec, small, *grads, down_part)


def middle_kernel(
    fsdp_count,
    att_hbm,
    x_hbm,
    cot_hbm,
    vec_ref,
    out_w_hbm,
    in_w_ref,
    down_w_ref,
    result_ref,
    go_all,
    hid_ref,
    small_ref,
    out_g_ref,
    in_g_ref,
    down_part,
    att_ref,
    x_ref,
    cot_ref,
    out_w_ref,
    fetch_sems,
    datt_ref,
    go_sems,
    go_sent,
    go_got,
    hidden_sc,
    n2_sc,
    n2_t,
    out_acc,
    dn2_acc,
    in_buf,
    down_buf,
    grad_buf,
    act_sc,
    slope_sc,
    down_g,
    in_sems,
    down_sems,
    grad_sems,
    *rest,
):
    place = Place(fsdp_count)
    depth = place.depth
    down_like = rest[0]
    total = Reduce.take(place, down_g, down_like, False, rest[1:], True)
    rows, width = x_ref.shape
    span = down_buf.shape[1]
    hidden_units = down_g.shape[0]
    chunks = hidden_units // span
    paired = total.rows == span
    lines = rows // 32

    def order(index):
        if not paired:
            return index
        z = place.far(lax.rem(lax.div(index, 2) + 1, depth))
        return 2 * z + jnp.where(lax.rem(index, 2) == 0, 1 - place.c, place.c)

    def in_load(index):
        slot = lax.rem(index, 4)
        return pltpu.make_async_copy(
            in_w_ref.at[:, aligned(order(index) * span, span)], in_buf.at[slot], in_sems.at[slot]
        )

    def down_load(index):
        slot = lax.rem(index, 4)
        return pltpu.make_async_copy(
            down_w_ref.at[aligned(order(index) * span, span)], down_buf.at[slot], down_sems.at[slot]
        )

    def grad_store(index):
        slot = lax.rem(index, 2)
        return pltpu.make_async_copy(
            grad_buf.at[slot], in_g_ref.at[:, aligned(order(index) * span, span)], grad_sems.at[slot]
        )

    def over_rows(body, start=0):
        return lax.fori_loop(0, lines, lambda index, carry: body(aligned(index * 32, 32), carry), start)

    for index in (0, 1):
        in_load(index).start()
        down_load(index).start()
    loads = [
        pltpu.make_async_copy(src, dst, fetch_sems.at[i])
        for i, (src, dst) in enumerate(((att_hbm, att_ref), (out_w_hbm, out_w_ref), (x_hbm, x_ref), (cot_hbm, cot_ref)))
    ]
    for load in loads:
        load.start()
    place.meet()
    for load in loads:
        load.wait()
    hidden_sc[...] = x_ref[...].astype(F32) + dot_nn(att_ref[...], out_w_ref[...])

    def normalise(here, carry):
        token_rows = hidden_sc[here, :]
        center = token_rows - jnp.mean(token_rows, axis=-1, keepdims=True)
        variance = jnp.mean(center * center, axis=-1, keepdims=True)
        normed = center * lax.rsqrt(variance + 1e-05) * vec_ref[2:3, :] + vec_ref[3:4, :]
        n2_sc[here, :] = normed.astype(BF16)
        out_acc[here, :] = token_rows + vec_ref[4:5, :]
        return carry

    over_rows(normalise)
    n2_t[...] = n2_sc[...].T
    dn2_acc[...] = jnp.zeros_like(dn2_acc)
    small_ref[...] = jnp.zeros_like(small_ref)

    def place_of(which):
        per = width // span
        return pl.ds(5 + lax.div(which, per), 1), aligned(lax.rem(which, per) * span, span)

    def activate(index):
        slot, side = lax.rem(index, 4), lax.rem(index, 2)
        which = order(index)
        in_load(index).wait()
        down_load(index).wait()

        def ahead():
            in_load(index + 2).start()
            down_load(index + 2).start()

        pl.when(index + 2 < chunks)(ahead)
        line, cols = place_of(which)
        pre = dot_nn(n2_sc[...], in_buf[slot]) + vec_ref[line, cols]
        inner = jnp.tanh(0.7978845608028654 * (pre + 0.044715 * pre * pre * pre))
        act = (0.5 * pre * (1.0 + inner)).astype(BF16)
        act_sc[side] = act
        down_g[aligned(which * span, span), :] = dot_tn(act, cot_ref[...]).astype(BF16)
        slope_sc[side] = 0.5 * (1.0 + inner) + (0.5 * 0.7978845608028654) * pre * (1.0 - inner * inner) * (
            1.0 + (3.0 * 0.044715) * pre * pre
        )

    def chunk(index):
        slot, side = lax.rem(index, 4), lax.rem(index, 2)
        which = order(index)
        line, cols = place_of(which)
        grad = dot_nt(cot_ref[...], down_buf[slot]) * slope_sc[side]
        low = grad.astype(BF16)
        small_ref[line, cols] = jnp.sum(low.astype(F32), axis=0, keepdims=True)
        out_acc[...] += dot_nn(act_sc[side], down_buf[slot])
        dn2_acc[...] += dot_nt(low, in_buf[slot])
        pl.when(index >= 2)(lambda: grad_store(index - 2).wait())
        grad_buf[side] = dot_nn(n2_t[...], low).astype(BF16)
        grad_store(index).start()

    def swap_before(t):
        pl.when(t >= 1)(lambda: total.swap(lax.rem(t, depth)))

    def close_before(t):
        pl.when(t >= 2)(lambda: total.close(lax.rem(t + depth - 1, depth), False))

    if paired:

        def step(t, carry):
            dest = lax.rem(t + 1, depth)

            def early(side, carry):
                activate(2 * t + side)
                pl.when(side == 0)(lambda: total.core_copy(dest).start())
                return carry

            lax.fori_loop(0, 2, early, 0)
            swap_before(t)
            chunk(2 * t)
            total.fold(dest, None)
            chunk(2 * t + 1)
            close_before(t)
            return carry

        lax.fori_loop(0, depth, step, 0)
    else:
        lax.fori_loop(0, chunks, lambda index, carry: (activate(index), chunk(index), carry)[2], 0)
        place.each(0, depth, lambda step: total.core_copy(step).start())

        def step(t, carry):
            swap_before(t)
            total.fold(lax.rem(t + 1, depth), None)
            close_before(t)
            return carry

        lax.fori_loop(0, depth, step, 0)

    def finish(here, sums):
        token_rows = hidden_sc[here, :]
        center = token_rows - jnp.mean(token_rows, axis=-1, keepdims=True)
        inv = lax.rsqrt(jnp.mean(center * center, axis=-1, keepdims=True) + 1e-05)
        hat = center * inv
        dn2 = dn2_acc[here, :]
        cot = cot_ref[here, :].astype(F32)
        scaled = dn2 * vec_ref[2:3, :]
        grad = cot + inv * (
            scaled
            - jnp.mean(scaled, axis=-1, keepdims=True)
            - hat * jnp.mean(scaled * hat, axis=-1, keepdims=True)
        )
        hid_ref[here, :] = grad
        n2_sc[here, :] = grad.astype(BF16)
        result_ref[here, :] = out_acc[here, :].astype(BF16)
        return (
            sums[0] + jnp.sum(dn2 * hat, axis=0, keepdims=True),
            sums[1] + jnp.sum(dn2, axis=0, keepdims=True),
            sums[2] + jnp.sum(cot, axis=0, keepdims=True),
        )

    total.swap(0)
    none = jnp.zeros((1, width), F32)
    gain_sum, bias_sum, cot_sum = over_rows(finish, (none, none, none))
    small_ref[2:3, :] = gain_sum
    small_ref[3:4, :] = bias_sum
    small_ref[4:5, :] = cot_sum
    if depth > 1:
        total.close(depth - 1, False)
    datt_ref[...] = dot_nt(n2_sc[...], out_w_ref[...]).astype(BF16)
    seats = (place.s1, place.s2, place.s3)
    part = width // 4

    def go_copy(way):
        src = datt_ref.at[:, aligned(seats[way] * part, part)]
        return send(src, go_all.at[aligned(place.s * rows, rows)], (go_sent, go_got), way, place.across(way))

    def go_arrival(way):
        there = go_all.at[aligned(seats[way] * rows, rows)]
        return send(there, there, (go_sent, go_got), way, place.across(way))

    own_go = pltpu.make_async_copy(
        datt_ref.at[:, aligned(place.s * part, part)], go_all.at[aligned(place.s * rows, rows)], go_sems
    )
    for way in range(3):
        go_copy(way).start()
    own_go.start()
    out_g_ref[...] = dot_tn(att_ref[...], n2_sc[...]).astype(BF16)
    total.close(0, True)
    total.collect()
    down_part[...] = total.total[...]
    for index in (chunks - 2, chunks - 1):
        grad_store(index).wait()
    own_go.wait()
    for way in range(3):
        go_arrival(way).wait_recv()
        go_copy(way).wait_send()
    total.sent()
    place.each(1, depth, lambda step: total.z_copy(step).wait_send())


def middle(fsdp_count, att, x, cot, vec, w_out, w_in, w_down):
    rows, width = x.shape
    hidden_units = w_in.shape[1]
    span = 512
    depth = fsdp_count // 2
    anywhere = pl.BlockSpec(memory_space=pltpu.HBM)
    vmem = pl.BlockSpec(memory_space=pltpu.VMEM)
    shape = jax.ShapeDtypeStruct
    kept = (hidden_units // fsdp_count, width)
    return pl.pallas_call(
        functools.partial(middle_kernel, fsdp_count),
        out_shape=(
            shape((rows, width), BF16),
            shape((4 * rows, width // 4), BF16),
            shape((rows, width), F32),
            shape(vec.shape, F32),
            shape(w_out.shape, BF16),
            shape(w_in.shape, BF16),
            shape((kept[0], width // 4), BF16),
        ),
        in_specs=[anywhere] * 3 + [vmem] + [anywhere] * 3,
        out_specs=(vmem, anywhere, vmem, vmem, vmem, anywhere, vmem),
        scratch_shapes=[
            pltpu.VMEM((rows, width), BF16),
            pltpu.VMEM((rows, width), BF16),
            pltpu.VMEM((rows, width), BF16),
            pltpu.VMEM(w_out.shape, BF16),
            dma(4),
            pltpu.VMEM((rows, width), BF16),
            dma(),
            dma(3),
            dma(3),
            pltpu.VMEM((rows, width), F32),
            pltpu.VMEM((rows, width), BF16),
            pltpu.VMEM((width, rows), BF16),
            pltpu.VMEM((rows, width), F32),
            pltpu.VMEM((rows, width), F32),
            pltpu.VMEM((4, width, span), BF16),
            pltpu.VMEM((4, span, width), BF16),
            pltpu.VMEM((2, width, span), BF16),
            pltpu.VMEM((2, rows, span), BF16),
            pltpu.VMEM((2, rows, span), F32),
            pltpu.VMEM((hidden_units, width), BF16),
            dma(4),
            dma(4),
            dma(2),
            pltpu.VMEM(kept, BF16),
        ]
        + Reduce.scratch(depth, *kept, False, True),
        compiler_params=pltpu.CompilerParams(
            collective_id=5, has_side_effects=True, vmem_limit_bytes=60 << 20
        ),
    )(att, x, cot, vec, w_out, w_in, w_down)


def results_kernel(share, held, *refs):
    sources, small, refs = refs[:6], refs[6], refs[7:]
    cut = len(refs) > 20
    count = 12 if cut else 6
    outs, refs = refs[:count], refs[count:]
    taken, given, in_sems, out_sems = refs[:6], refs[6:12], refs[12], refs[13]
    loads = [pltpu.make_async_copy(src, dst, in_sems.at[i]) for i, (src, dst) in enumerate(zip(sources, taken))]
    for load in loads:
        load.start()
    stores = []
    for i, load in enumerate(loads):
        load.wait()
        src, dst = taken[i], given[i]
        chunk = 32 if src.shape[0] % 32 == 0 else 16

        def body(index, carry):
            rows = aligned(index * chunk, chunk)
            dst[rows, :] = src[rows, :].astype(dst.dtype)
            return carry

        if dst.dtype == src.dtype:
            store = pltpu.make_async_copy(src, outs[i], out_sems.at[i])
        else:
            lax.fori_loop(0, src.shape[0] // chunk, body, 0)
            store = pltpu.make_async_copy(dst, outs[i], out_sems.at[i])
        store.start()
        stores.append(store)
    if cut:
        position = lax.axis_index("fsdp")
        cols = aligned(position * share, share)
        for line in range(5):
            outs[6 + line][...] = small[line : line + 1, cols]
        per = small.shape[1] // held
        outs[11][...] = small[pl.ds(5 + lax.div(position, per), 1), aligned(lax.rem(position, per) * held, held)]
    for store in stores:
        store.wait()


def write_results(share, held, arrays, small):
    shape = jax.ShapeDtypeStruct
    kinds = (F32, F32, F32, F32, BF16, BF16)
    shapes = [shape(a.shape, kind) for a, kind in zip(arrays, kinds)]
    cut = share % LANES == 0 and held % LANES == 0
    small_shapes = [shape((1, share), F32)] * 5 + [shape((1, held), F32)] if cut else []
    hbm = pl.BlockSpec(memory_space=pltpu.HBM)
    vmem = pl.BlockSpec(memory_space=pltpu.VMEM)
    outs = pl.pallas_call(
        functools.partial(results_kernel, share, held),
        out_shape=tuple(shapes + small_shapes),
        in_specs=[hbm] * 6 + [vmem],
        out_specs=tuple([hbm] * 6 + [vmem] * len(small_shapes)),
        scratch_shapes=[pltpu.VMEM(a.shape, BF16) for a in arrays]
        + [pltpu.VMEM(a.shape if kind == F32 else (16, LANES), kind) for a, kind in zip(arrays, kinds)]
        + [dma(6), dma(6)],
        compiler_params=pltpu.CompilerParams(vmem_limit_bytes=60 << 20),
    )(*arrays, small)
    if cut:
        return outs[:6], [part.reshape(-1) for part in outs[6:]]
    position = lax.axis_index("fsdp")
    lines = lax.dynamic_slice_in_dim(small[:5], position * share, share, axis=1)
    rest = small[5:].reshape(-1)
    return outs, [lines[i] for i in range(5)] + [lax.dynamic_slice_in_dim(rest, position * held, held)]


def per_device(
    fsdp_count,
    tokens,
    segment_ids,
    random_blocks,
    ln1_gain,
    ln1_bias,
    w_qkv,
    w_out,
    ln2_gain,
    ln2_bias,
    w_in,
    b_in,
    w_down,
    b_down,
    cotangent,
):
    width = tokens.shape[2]
    share, held = ln1_gain.shape[0], b_in.shape[0]
    lines = fsdp_count * held // width
    position = lax.axis_index("fsdp")
    column = jnp.arange(width, dtype=jnp.int32)
    narrow = jnp.tile(jnp.stack([ln1_gain, ln1_bias, ln2_gain, ln2_bias, b_down]), (1, fsdp_count))
    narrow = jnp.where(column // share == position, narrow, jnp.zeros((), BF16))
    line = jnp.arange(lines, dtype=jnp.int32)[:, None]
    broad = jnp.tile(b_in[None], (1, width // held))
    broad = jnp.where((line * width + column) // held == position, broad, jnp.zeros((), BF16))
    vec = jnp.concatenate([narrow, broad, jnp.zeros((-(5 + lines) % 16, width), BF16)], axis=0)
    mask = block_mask(random_blocks)
    by_heads, lse, att_rows, out_weight, down_weight, in_weight, vec, normed_one, own_qkv, query_docs, key_feats = (
        forward_attention(fsdp_count, tokens[0], w_qkv, vec, segment_ids, mask, w_out, w_down, w_in)
    )
    result, grad_att, grad_hidden, small, grad_out, grad_in, down_part = middle(
        fsdp_count, att_rows, tokens[0], cotangent[0], vec, out_weight, in_weight, down_weight
    )
    grad_tokens, small, total_qkv, total_out, total_in, total_down = backward_attention(
        fsdp_count,
        grad_att,
        (by_heads, mask, query_docs, key_feats, lse, normed_one, own_qkv, vec),
        tokens[0],
        grad_hidden,
        small,
        (grad_out, grad_in),
        down_part,
    )
    arrays, parts = write_results(
        share, held, (total_in, total_down, total_qkv, total_out, result, grad_tokens), small
    )
    return (
        arrays[4][None],
        arrays[5][None],
        parts[0],
        parts[1],
        arrays[2],
        arrays[3],
        parts[2],
        parts[3],
        arrays[0],
        parts[5],
        arrays[1],
        parts[4],
    )


def solution(mesh):
    return jax.shard_map(
        functools.partial(per_device, mesh.shape["fsdp"]),
        mesh=mesh,
        in_specs=(
            P("fsdp", "seq", None),
            P("fsdp", "seq"),
            P("seq", None, None),
            P("fsdp"),
            P("fsdp"),
            P("fsdp", None),
            P("fsdp", None),
            P("fsdp"),
            P("fsdp"),
            P("fsdp", None),
            P("fsdp"),
            P("fsdp", None),
            P("fsdp"),
            P("fsdp", "seq", None),
        ),
        out_specs=(
            P("fsdp", "seq", None),
            P("fsdp", "seq", None),
            P("fsdp"),
            P("fsdp"),
            P("fsdp", None),
            P("fsdp", None),
            P("fsdp"),
            P("fsdp"),
            P("fsdp", None),
            P("fsdp"),
            P("fsdp", None),
            P("fsdp"),
        ),
        check_vma=False,
    )
```

```python
import functools
import math

import jax
import jax.numpy as jnp
from jax import lax
from jax.experimental import pallas as pl
from jax.experimental.pallas import tpu as pltpu
from jax.sharding import PartitionSpec as P

DH = 64
BLK = 64
LANES = 128
NEG = -1e30
F32 = jnp.float32
BF16 = jnp.bfloat16


def dot_nn(a, b):
    return jnp.dot(a, b, preferred_element_type=F32)


def dot_nt(a, b):
    return lax.dot_general(a, b, (((1,), (1,)), ((), ())), preferred_element_type=F32)


def dot_tn(a, b):
    return lax.dot_general(a, b, (((0,), (0,)), ((), ())), preferred_element_type=F32)


DOCS = 6


def block_mask(random_blocks):
    heads, inner, _ = random_blocks.shape
    blocks = inner + 2
    ids = jnp.arange(blocks, dtype=jnp.int32)
    near = jnp.abs(ids[:, None] - ids[None, :]) <= 1
    edge = (ids == 0) | (ids == blocks - 1)
    fixed = near | edge[:, None] | edge[None, :]
    picked = jnp.any(random_blocks[:, :, :, None] == ids, axis=2)
    used = fixed[None] | jnp.pad(picked, ((0, 0), (1, 1), (0, 0)))
    row = jnp.pad(jnp.where(used, 0.0, NEG), ((0, 0), (0, 0), (0, DH - blocks)))
    return jnp.concatenate([row, row], axis=-1)


def token_features(start, docs, blocks):
    shape = (docs.shape[0], LANES)
    lane = lax.rem(lax.broadcasted_iota(jnp.int32, shape, 1), DH)
    block = lax.div(lax.broadcasted_iota(jnp.int32, shape, 0) + start, BLK)
    own = docs + blocks == lane
    other = jnp.where(own | (lane >= blocks + DOCS), 0.0, 1.0)
    key_part = jnp.where(lane < blocks, jnp.where(block == lane, 1.0, 0.0), other)
    return jnp.where(own, NEG, 0.0).astype(BF16), key_part.astype(BF16)


def query_tile(q_tile, doc_tile, mask_ref, head, first_block, lanes):
    scale = jnp.asarray(1.0 / math.sqrt(DH), BF16)
    count = q_tile.shape[0] // BLK
    mask = jnp.concatenate(
        [jnp.broadcast_to(mask_ref[head, pl.ds(first_block + i, 1), :], (BLK, LANES)) for i in range(count)], axis=0
    )
    return jnp.where(lanes, q_tile * scale, doc_tile + mask.astype(BF16))


def own_lanes(odd, shape):
    return lax.div(lax.broadcasted_iota(jnp.int32, shape, 1), DH) == odd


MESH = pl.DeviceIdType.MESH


class Place:
    def __init__(self, fsdp_count):
        self.depth = fsdp_count // 2
        self.s = lax.axis_index("seq")
        self.f = lax.axis_index("fsdp")
        self.z = lax.div(self.f, 2)
        self.c = lax.rem(self.f, 2)
        self.s1 = self.s + 1 - 2 * lax.rem(self.s, 2)
        self.s2 = self.s + 2 - 4 * lax.div(self.s, 2)
        self.s3 = 3 - self.s
        self.beside = (self.s, self.f + 1 - 2 * self.c)

    def across(self, index):
        return ((self.s1, self.s2, self.s3)[index], self.f)

    def far(self, step):
        return lax.rem(self.z + step, self.depth)

    def back(self, step):
        return lax.rem(self.z + self.depth - step, self.depth)

    def along(self, z):
        return (self.s, 2 * z + self.c)

    def meet(self):
        barrier = pltpu.get_barrier_semaphore()
        peers = [self.beside] + [self.across(i) for i in range(3)]
        for peer in peers:
            pl.semaphore_signal(barrier, inc=1, device_id=peer, device_id_type=MESH)
        self.each(1, self.depth, lambda step: pl.semaphore_signal(
            barrier, inc=1, device_id=self.along(self.far(step)), device_id_type=MESH
        ))
        pl.semaphore_wait(barrier, len(peers) + self.depth - 1)

    def each(self, start, stop, body):
        if stop - start <= 8:
            for step in range(start, stop):
                body(step)
        else:
            lax.fori_loop(start, stop, lambda step, carry: (body(step), carry)[1], 0)


def send(src, dst, sems, index, device):
    sent, got = sems
    return pltpu.make_async_remote_copy(
        src_ref=src,
        dst_ref=dst,
        send_sem=sent.at[index],
        recv_sem=got.at[index],
        device_id=device,
        device_id_type=MESH,
    )


def aligned(start, size):
    return pl.ds(pl.multiple_of(start, size), size)


class Gather:
    def __init__(self, place, src, dst, split, sems):
        self.place, self.src, self.dst, self.split = place, src, dst, split
        self.rows, self.cols = src.shape
        self.local, self.zs, self.xs, self.rs, self.cs = sems

    def block(self, z, core, quarter=None, half=None):
        rows = aligned((2 * z + core) * self.rows, self.rows)
        if quarter is None:
            return self.dst.at[rows]
        wide = self.cols // 4
        if half is None:
            return self.dst.at[rows, aligned(quarter * wide, wide)]
        return self.dst.at[rows, aligned(quarter * wide + half * (wide // 2), wide // 2)]

    def source(self, step, side):
        return self.place.z - step if side == 0 else self.place.z + step

    def has(self, step, side):
        z = self.source(step, side)
        return z >= 0 if side == 0 else z < self.place.depth

    def sends(self, step, side):
        p = self.place
        onward = p.z + 1 < p.depth if side == 0 else p.z > 0
        return jnp.logical_and(self.has(step - 1, side), onward)

    def slot(self, step, side):
        return 2 * step + side

    def own_copy(self):
        return pltpu.make_async_copy(self.src, self.block(self.place.z, self.place.c), self.local)

    def own_core(self):
        p = self.place
        return send(self.src, self.block(p.z, p.c), self.cs, 0, p.beside)

    def own_arrival(self):
        p = self.place
        there = self.block(p.z, 1 - p.c)
        return send(there, there, self.cs, 0, p.beside)

    def core_copy(self, step, side):
        p = self.place
        there = self.block(self.source(step, side), p.c)
        return send(there, there, self.cs, self.slot(step, side), p.beside)

    def core_arrival(self, step, side):
        p = self.place
        there = self.block(self.source(step, side), 1 - p.c)
        return send(there, there, self.cs, self.slot(step, side), p.beside)

    def z_copy(self, step, side):
        p = self.place
        z = self.source(step - 1, side)
        there = self.block(z, p.c, p.s) if self.split else self.block(z, p.c)
        src = there
        if isinstance(step, int) and step == 1:
            wide = self.cols // 4
            src = self.src.at[:, aligned(p.s * wide, wide)] if self.split else self.src
        return send(src, there, self.zs, self.slot(step, side), p.along(p.z + 1 - 2 * side))

    def z_arrival(self, step, side):
        p = self.place
        z = self.source(step, side)
        there = self.block(z, p.c, p.s) if self.split else self.block(z, p.c)
        return send(there, there, self.zs, self.slot(step, side), p.along(p.z - 1 + 2 * side))

    def x_copy(self, step, side, way):
        p = self.place
        there = self.block(self.source(step, side), p.c, p.s)
        return send(there, there, self.xs[way], self.slot(step, side), p.across(way))

    def x_arrival(self, step, side, way):
        p = self.place
        there = self.block(self.source(step, side), p.c, (p.s1, p.s2)[way])
        return send(there, there, self.xs[way], self.slot(step, side), p.across(way))

    def relay_copy(self, step, side, way):
        p = self.place
        there = self.block(self.source(step, side), p.c, (p.s2, p.s1)[way], 1 - way)
        return send(there, there, self.rs[way], self.slot(step, side), p.across(way))

    def relay_arrival(self, step, side, way):
        p = self.place
        there = self.block(self.source(step, side), p.c, p.s3, 1 - way)
        return send(there, there, self.rs[way], self.slot(step, side), p.across(way))

    def both(self, step, body, test=None):
        for side in (0, 1):
            pl.when((test or self.has)(step, side))(functools.partial(body, step, side))

    def begin(self):
        self.both(1, lambda step, side: self.z_copy(step, side).start(), self.sends)
        self.own_copy().start()
        self.own_core().start()

    def swap(self, step):
        def body(step, side):
            self.z_arrival(step, side).wait_recv()
            pl.when(self.sends(step + 1, side))(lambda: self.z_copy(step + 1, side).start())
            if self.split:
                for way in (0, 1):
                    self.x_copy(step, side, way).start()
            else:
                self.core_copy(step, side).start()

        self.both(step, body)

    def relay(self, step):
        def body(step, side):
            for way in (0, 1):
                self.x_arrival(step, side, way).wait_recv()
            for way in (0, 1):
                self.relay_copy(step, side, way).start()

        if self.split:
            self.both(step, body)

    def share(self, step):
        def body(step, side):
            for way in (0, 1):
                self.relay_arrival(step, side, way).wait_recv()
            self.core_copy(step, side).start()

        if self.split:
            self.both(step, body)

    def finish(self):
        self.own_copy().wait()
        self.own_core().wait_send()
        self.own_arrival().wait_recv()

        def close(step, side):
            if self.split:
                for way in (0, 1):
                    self.x_copy(step, side, way).wait_send()
                    self.relay_copy(step, side, way).wait_send()
            self.core_copy(step, side).wait_send()
            self.core_arrival(step, side).wait_recv()

        self.place.each(1, self.place.depth, lambda step: self.both(step, close))
        self.place.each(
            1,
            self.place.depth,
            lambda step: self.both(step, lambda step, side: self.z_copy(step, side).wait_send(), self.sends),
        )

    @staticmethod
    def scratch(depth, split):
        held = 2 * depth if split else 1
        return [dma()] + [dma(2 * depth)] * 2 + [dma(held)] * 8 + [dma(2 * depth)] * 2

    @staticmethod
    def take(refs):
        pairs = [(refs[i], refs[i + 1]) for i in range(1, 13, 2)]
        return (refs[0], pairs[0], pairs[1:3], pairs[3:5], pairs[5])


GATHER_SEMS = 13


def gather_steps(place, gathers, late, count, unit):
    depth = place.depth

    def swap(step):
        for one in gathers:
            one.swap(step)

    def relay(step):
        for one in gathers:
            one.relay(step)

    def share(step):
        for one in gathers:
            one.share(step)

    def late_swap(step):
        for one in late:
            one.swap(step)

    for one in late:
        one.begin()
    if depth <= 8:
        rounds = []
        for step in range(2, depth + 2):
            now = []
            if step <= depth:
                now.append(functools.partial(late_swap, step - 2)) if step > 2 else None
                now.append(functools.partial(share, step - 3)) if step > 3 else None
                now.append(functools.partial(swap, step)) if step < depth else None
                now.append(functools.partial(relay, step - 1))
            rounds.append(now)
        rounds[-1] = [functools.partial(share, step) for step in range(max(1, depth - 2), depth)]
        rounds[-1].append(functools.partial(late_swap, depth - 1))
        in_turn(count, unit, rounds[:count])
        for now in rounds[count:]:
            for one in now:
                one()
    else:
        in_turn(count, unit, [])
        swap(2)
        relay(1)

        def body(step, carry):
            late_swap(step - 2)
            share(step - 2)
            swap(step)
            relay(step - 1)
            return carry

        lax.fori_loop(3, depth, body, 0)
        late_swap(depth - 2)
        share(depth - 2)
        relay(depth - 1)
        share(depth - 1)
        late_swap(depth - 1)


def dma(*shape):
    return pltpu.SemaphoreType.DMA(shape) if shape else pltpu.SemaphoreType.DMA


def qkv_columns(heads_ref, pair):
    third = heads_ref.shape[1] // 3
    return tuple(aligned(i * third + pair * LANES, LANES) for i in range(3))


def attend_unit(pair, odd, tile, heads_ref, mask_ref, qd_ref, kf_ref, keys_sc, values_t, out_ref, lse_ref):
    length = heads_ref.shape[0]
    cols = aligned(pair * LANES, LANES)
    q_cols, k_cols, v_cols = qkv_columns(heads_ref, pair)
    mine = own_lanes(odd, (length, LANES))
    keys_sc[...] = jnp.where(mine, heads_ref[:, k_cols], kf_ref[...])

    @pl.when(odd == 0)
    def _():
        values_t[...] = heads_ref[:, v_cols].T
        out_ref[:, cols] = jnp.zeros((length, LANES), BF16)

    def one_tile(index, carry):
        rows = aligned(index * tile, tile)
        lanes = own_lanes(odd, (tile, LANES))
        queries = query_tile(
            heads_ref[rows, q_cols], qd_ref[rows, :], mask_ref, 2 * pair + odd, index * (tile // BLK), lanes
        )
        scores = dot_nt(keys_sc[...], queries)
        top = jnp.max(scores, axis=0, keepdims=True)
        prob = jnp.exp(scores - top)
        total = jnp.sum(prob, axis=0, keepdims=True)
        mixed = dot_nn(values_t[...], prob.astype(BF16)) / total
        lse_ref[pair, pl.ds(odd, 1), rows] = top + jnp.log(total)
        out_ref[rows, cols] = jnp.where(lanes, mixed.T.astype(BF16), out_ref[rows, cols])
        return carry

    lax.fori_loop(0, length // tile, one_tile, 0, unroll=2)


def in_turn(count, unit, actions):
    def body(index, carry):
        unit(index)
        for which, todo in enumerate(actions):
            if todo:

                @pl.when(index == which)
                def _(todo=todo):
                    for one in todo:
                        one()

        return carry

    lax.fori_loop(0, count, body, 0)


def forward_kernel(
    fsdp_count,
    x_ref,
    wq_ref,
    vec_ref,
    ids_ref,
    mask_ref,
    out_w_ref,
    down_w_ref,
    in_w_ref,
    heads_all,
    lse_ref,
    att_all,
    out_w_all,
    down_w_all,
    in_w_all,
    vec_sum,
    n1_all,
    wq_all,
    qd_ref,
    kf_ref,
    x_sc,
    n1_sc,
    wq_own,
    wq_sc,
    vec_sc,
    seg_ref,
    seg_sc,
    heads_sc,
    att_sc,
    keys_sc,
    values_t,
    *sems,
):
    place = Place(fsdp_count)
    rows, width = x_ref.shape
    own_width = wq_sc.shape[1]
    seats = (place.s1, place.s2, place.s3)

    def taken(i):
        return Gather.take(sems[i * GATHER_SEMS : (i + 1) * GATHER_SEMS])

    x_own, seg_own, keep_sems, pick_sems, x_sent, x_got, r_sent, r_got, g_sent, g_got, a_sent, a_got, a_own = sems[6 * GATHER_SEMS :]
    lone = pl.ds(0, in_w_ref.shape[1] // 2)
    shared = pl.ds(in_w_ref.shape[1] // 2, in_w_ref.shape[1] // 2)
    gathers = [
        Gather(place, src, dst, split, taken(i))
        for i, (src, dst, split) in enumerate(
            (
                (out_w_ref, out_w_all, True),
                (in_w_ref.at[:, shared], in_w_all.at[:, shared], True),
                (down_w_ref, down_w_all, True),
                (in_w_ref.at[:, lone], in_w_all.at[:, lone], False),
            )
        )
    ]
    late = [gathers.pop()]
    third = own_width // 3
    picks = [
        pltpu.make_async_copy(
            wq_ref.at[:, aligned((4 * i + place.s) * third, third)], wq_own.at[:, pl.ds(i * third, third)], pick_sems.at[i]
        )
        for i in range(3)
    ]
    for pick in picks:
        pick.start()
    seg_ref[...] = jnp.zeros_like(seg_ref)
    for part in range(ids_ref.shape[1] // LANES):
        seg_ref[part : part + 1, :] = ids_ref[:, part * LANES : (part + 1) * LANES]
    weight = Gather(place, wq_own, wq_sc, False, taken(4))
    vector = Gather(place, vec_ref, vec_sc, False, taken(5))
    half = rows // 2

    def x_rows(seat):
        return x_sc.at[aligned(seat * rows, rows)]

    def x_half(seat, part):
        return x_sc.at[aligned(seat * rows + part * half, half)]

    def x_copy(way):
        return send(x_ref, x_rows(place.s), (x_sent, x_got), way, place.across(way))

    def x_arrival(way):
        there = x_rows(seats[way])
        return send(there, there, (x_sent, x_got), way, place.across(way))

    def x_relay(way):
        there = x_half((place.s2, place.s1)[way], 1 - way)
        return send(there, there, (r_sent, r_got), way, place.across(way))

    def x_relayed(way):
        there = x_half(place.s3, 1 - way)
        return send(there, there, (r_sent, r_got), way, place.across(way))

    def seg_copy(way):
        return send(seg_ref, seg_sc.at[place.s], (g_sent, g_got), way, place.across(way))

    def seg_arrival(way):
        there = seg_sc.at[seats[way]]
        return send(there, there, (g_sent, g_got), way, place.across(way))

    place.meet()
    vector.begin()
    for pick in picks:
        pick.wait()
    weight.begin()
    for way in range(2):
        x_copy(way).start()
    for way in range(3):
        seg_copy(way).start()
    own_x = pltpu.make_async_copy(x_ref, x_rows(place.s), x_own)
    own_x.start()
    own_seg = pltpu.make_async_copy(seg_ref, seg_sc.at[place.s], seg_own)
    own_seg.start()
    def start_rest():
        for one in gathers:
            one.begin()

    if place.depth <= 8:
        for step in range(1, place.depth):
            vector.swap(step)
            weight.swap(step)
            if step == max(1, place.depth - 2):
                start_rest()
    else:
        place.each(1, place.depth, vector.swap)
        place.each(1, place.depth, weight.swap)
        start_rest()
    vector.finish()
    vec_rows = vec_ref.shape[0]
    total = vec_sc[pl.ds(0, vec_rows), :].astype(F32)
    if fsdp_count <= 8:
        for f in range(1, fsdp_count):
            total = total + vec_sc[pl.ds(f * vec_rows, vec_rows), :].astype(F32)
    else:
        total = lax.fori_loop(
            1, fsdp_count, lambda f, sofar: sofar + vec_sc[aligned(f * vec_rows, vec_rows), :].astype(F32), total
        )
    vec_sum[...] = total

    def normalise(seat):
        def body(part):
            token_rows = x_sc[aligned(seat * rows + part * 32, 32), :].astype(F32)
            center = token_rows - jnp.mean(token_rows, axis=-1, keepdims=True)
            variance = jnp.mean(center * center, axis=-1, keepdims=True)
            normed = center * lax.rsqrt(variance + 1e-05) * vec_sum[0:1, :] + vec_sum[1:2, :]
            n1_sc[aligned(seat * rows + part * 32, 32), :] = normed.astype(BF16)

        lax.fori_loop(0, rows // 32, lambda part, carry: (body(part), carry)[1], 0)

    def project(seat):
        here = aligned(seat * rows, rows)

        def body(part):
            cols = aligned(part * 256, 256)
            heads_sc[here, cols] = dot_nn(n1_sc[here, :], wq_sc[:, cols]).astype(BF16)

        lax.fori_loop(0, own_width // 256, lambda part, carry: (body(part), carry)[1], 0)

    own_x.wait()
    normalise(place.s)
    for way in range(2):
        x_arrival(way).wait_recv()
    for way in range(2):
        x_relay(way).start()
    for way in range(2):
        normalise(seats[way])
    weight.finish()
    project(place.s)
    for way in range(2):
        project(seats[way])
    for one in gathers:
        one.swap(1)
    for way in range(2):
        x_relayed(way).wait_recv()
    normalise(place.s3)
    project(place.s3)
    own_seg.wait()
    for way in range(3):
        seg_arrival(way).wait_recv()
    blocks = mask_ref.shape[1]
    for seat in range(4):
        columns = seg_sc[seat].T
        for part in range(rows // LANES):
            here = pl.ds(seat * rows + part * LANES, LANES)
            qd_ref[here, :], kf_ref[here, :] = token_features(
                seat * rows + part * LANES, columns[:, part : part + 1], blocks
            )
    keeps = [
        pltpu.make_async_copy(src, dst, keep_sems.at[i])
        for i, (src, dst) in enumerate(((heads_sc, heads_all), (n1_sc, n1_all), (wq_sc, wq_all)))
    ]
    for keep in keeps:
        keep.start()

    pairs = att_sc.shape[1] // LANES

    def att_copy(pair, way):
        cols = aligned((place.s * pairs + pair) * LANES, LANES)
        return send(
            att_sc.at[aligned(seats[way] * rows, rows), aligned(pair * LANES, LANES)],
            att_all.at[:, cols],
            (a_sent, a_got),
            pair * 3 + way,
            place.across(way),
        )

    def att_own(pair):
        cols = aligned((place.s * pairs + pair) * LANES, LANES)
        return pltpu.make_async_copy(
            att_sc.at[aligned(place.s * rows, rows), aligned(pair * LANES, LANES)],
            att_all.at[:, cols],
            a_own.at[pair],
        )

    def att_arrival(pair, way):
        there = att_all.at[:, aligned((seats[way] * pairs + pair) * LANES, LANES)]
        return send(there, there, (a_sent, a_got), pair * 3 + way, place.across(way))

    def unit(index):
        pair, odd = lax.div(index, 2), lax.rem(index, 2)
        attend_unit(pair, odd, 256, heads_sc, mask_ref, qd_ref, kf_ref, keys_sc, values_t, att_sc, lse_ref)

        @pl.when(odd == 1)
        def _():
            for way in range(3):
                att_copy(pair, way).start()
            att_own(pair).start()

    gather_steps(place, gathers, late, 2 * pairs, unit)
    for keep in keeps:
        keep.wait()
    for way in range(3):
        seg_copy(way).wait_send()
        if way < 2:
            x_copy(way).wait_send()
            x_relay(way).wait_send()
        for pair in range(pairs):
            att_copy(pair, way).wait_send()
            att_arrival(pair, way).wait_recv()
    for pair in range(pairs):
        att_own(pair).wait()
    for one in gathers + late:
        one.finish()


def forward_attention(fsdp_count, x, w_qkv, vec, seg, mask, w_out, w_down, w_in):
    rows, width = x.shape
    length = 4 * rows
    heads = mask.shape[0]
    pairs = heads // 2
    depth = fsdp_count // 2
    own_width = w_qkv.shape[1] // 4
    full = fsdp_count * w_qkv.shape[0]
    seg_rows = -(-seg.shape[1] // (8 * LANES)) * 8
    anywhere = pl.BlockSpec(memory_space=pltpu.HBM)
    vmem = pl.BlockSpec(memory_space=pltpu.VMEM)
    shape = jax.ShapeDtypeStruct

    def whole(shard):
        return shape((fsdp_count * shard.shape[0], shard.shape[1]), shard.dtype)

    return pl.pallas_call(
        functools.partial(forward_kernel, fsdp_count),
        out_shape=(
            shape((length, own_width), BF16),
            shape((pairs, 2, length), F32),
            shape((rows, heads * DH * 4), BF16),
            whole(w_out),
            whole(w_down),
            whole(w_in),
            shape(vec.shape, F32),
            shape((length, width), BF16),
            shape((full, own_width), BF16),
            shape((length, LANES), BF16),
            shape((length, LANES), BF16),
        ),
        in_specs=[anywhere] * 3 + [vmem] * 2 + [anywhere] * 3,
        out_specs=(anywhere, vmem, anywhere, anywhere, anywhere, anywhere, vmem, anywhere, anywhere, vmem, vmem),
        scratch_shapes=[
            pltpu.VMEM((length, width), BF16),
            pltpu.VMEM((length, width), BF16),
            pltpu.VMEM((w_qkv.shape[0], own_width), BF16),
            pltpu.VMEM((full, own_width), BF16),
            pltpu.VMEM((fsdp_count * vec.shape[0], vec.shape[1]), BF16),
            pltpu.VMEM((seg_rows, LANES), jnp.int32),
            pltpu.VMEM((4, seg_rows, LANES), jnp.int32),
            pltpu.VMEM((length, own_width), BF16),
            pltpu.VMEM((length, heads * DH), BF16),
            pltpu.VMEM((length, LANES), BF16),
            pltpu.VMEM((LANES, length), BF16),
        ]
        + Gather.scratch(depth, True) * 3
        + Gather.scratch(depth, False) * 3
        + [dma(), dma(), dma(3), dma(3), dma(2), dma(2), dma(2), dma(2), dma(3), dma(3)]
        + [dma(3 * pairs), dma(3 * pairs), dma(pairs)],
        compiler_params=pltpu.CompilerParams(
            collective_id=2, has_side_effects=True, vmem_limit_bytes=60 << 20
        ),
    )(x, w_qkv, vec, seg, mask, w_out, w_down, w_in)


def by_rows(count, cols, body):
    chunk = 16
    while count % (2 * chunk) == 0 and 2 * chunk * cols <= 16384:
        chunk *= 2
    lax.fori_loop(0, count // chunk, lambda i, carry: (body(aligned(i * chunk, chunk)), carry)[1], 0)


class Reduce:
    def __init__(self, place, grad, out, quartered, bufs, sems, direct=False, thirds=False, late=False, far_first=False):
        self.far_first = far_first
        self.place, self.grad, self.out, self.quartered, self.direct = place, grad, out, quartered, direct
        self.thirds, self.late = thirds, late
        self.rows, self.cols = out.shape
        self.wide = self.cols // 4
        self.acc, self.own, self.relay_in, self.quarter_in, self.z_in, self.total = bufs
        self.own_sem, self.put_sem, self.cs, self.rs, self.qs, self.zs, self.fs, self.gs = sems

    @staticmethod
    def scratch(depth, rows, cols, quartered, direct=False, far_first=False):
        held = cols // 4 if quartered else cols
        near = 1 if far_first else depth
        side = (1, 1, 16, LANES) if quartered else None
        return [
            pltpu.VMEM((depth, rows, held), BF16),
            pltpu.VMEM((16, LANES) if direct else (rows, held), BF16),
            pltpu.VMEM(side or (2, near, rows, cols // 8), BF16),
            pltpu.VMEM(side or (2, near, rows, cols // 4), BF16),
            pltpu.VMEM((depth, rows, cols if far_first else cols // 4), BF16),
            pltpu.VMEM((rows, cols // 4), BF16),
            dma(),
            dma(3),
        ] + [dma(depth)] * 12 + [dma(9)] * 2 + [dma(2)] * 2

    @staticmethod
    def take(place, grad, out, quartered, refs, direct=False, thirds=False, far_first=False):
        s = refs[8:]
        pairs = [(s[i], s[i + 1]) for i in range(0, 16, 2)]
        sems = (refs[6], refs[7], pairs[0], pairs[1:3], pairs[3:5], pairs[5], pairs[6], pairs[7])
        return Reduce(place, grad, out, quartered, refs[:6], sems, direct, thirds, False, far_first)

    def quarter(self, seat):
        return aligned(seat * self.wide, self.wide)

    def mine(self):
        if self.far_first:
            return pl.ds(0, self.cols)
        return pl.ds(0, self.wide) if self.quartered else self.quarter(self.place.s)

    def piece(self, seat, half):
        return aligned(seat * self.wide + half * (self.wide // 2), self.wide // 2)

    def own_copy(self, step):
        p = self.place
        rows = aligned((2 * p.far(step) + p.c) * self.rows, self.rows)
        return pltpu.make_async_copy(self.grad.at[rows], self.own, self.own_sem)

    def core_copy(self, step):
        p = self.place
        rows = aligned((2 * p.far(step) + 1 - p.c) * self.rows, self.rows)
        return send(self.grad.at[rows], self.acc.at[step], self.cs, step, p.beside)

    def relay_copy(self, step, way):
        p = self.place
        src = self.acc.at[step, :, self.piece(p.s3, way)]
        return send(src, self.relay_in.at[way, step], self.rs[way], step, p.across(way))

    def quarter_copy(self, step, way):
        p = self.place
        src = self.acc.at[step, :, self.quarter((p.s1, p.s2)[way])]
        return send(src, self.quarter_in.at[way, step], self.qs[way], step, p.across(way))

    def z_copy(self, step):
        p = self.place
        src = self.acc.at[step, :, self.mine()]
        return send(src, self.z_in.at[step], self.zs, step, p.along(p.far(step)))

    def columns(self, seat, part):
        if not self.thirds:
            return self.quarter(seat), pl.ds(0, self.wide)
        third = self.wide // 3
        return aligned((4 * part + seat) * third, third), pl.ds(part * third, third)

    @property
    def parts(self):
        return 3 if self.thirds else 1

    def put_copy(self, part):
        there, here = self.columns(self.place.s, part)
        return pltpu.make_async_copy(self.total.at[:, here], self.out.at[:, there], self.put_sem.at[part])

    def total_copy(self, way, part):
        p = self.place
        there, here = self.columns(p.s, part)
        return send(self.total.at[:, here], self.out.at[:, there], self.fs, 3 * way + part, p.across(way))

    def total_arrival(self, way, part):
        p = self.place
        there = self.out.at[:, self.columns((p.s1, p.s2, p.s3)[way], part)[0]]
        return send(there, there, self.fs, 3 * way + part, p.across(way))

    def totals(self):
        return [(way, part) for way in range(3 if self.thirds else 2) for part in range(self.parts)]

    def back_copy(self, way):
        p = self.place
        there = self.out.at[:, self.piece((p.s2, p.s1)[way], 1 - way)]
        return send(there, there, self.gs, way, p.across(way))

    def back_arrival(self, way):
        p = self.place
        there = self.out.at[:, self.piece(p.s3, 1 - way)]
        return send(there, there, self.gs, way, p.across(way))

    def begin(self):
        depth = self.place.depth
        self.place.each(1, depth, lambda step: self.core_copy(step).start())
        self.core_copy(0).start()
        self.own_copy(1).start()

    def fold(self, step, following):
        p, acc, own = self.place, self.acc, self.own
        self.core_copy(step).wait_recv()
        if not self.direct:
            self.own_copy(step).wait()
        base = (2 * p.far(step) + p.c) * self.rows

        def body(index, carry):
            rows = aligned(index * 16, 16)
            added = self.grad[aligned(base + index * 16, 16), :] if self.direct else own[rows, :]
            acc[step, rows, :] = acc[step, rows, :] + added
            return carry

        lax.fori_loop(0, self.rows // 16, body, 0)
        if following is not None:
            self.own_copy(following).start()
        if not (self.quartered or self.far_first):
            for way in (0, 1):
                self.relay_copy(step, way).start()
        elif not (isinstance(step, int) and step == 0):
            self.z_copy(step).start()

    def swap(self, step):
        if self.quartered:
            return
        p, acc = self.place, self.acc
        for way in (0, 1):
            self.relay_copy(step, way).wait_recv()
            cols = self.piece((p.s2, p.s1)[way], way)
            came = self.relay_in.at[way, step]

            def body(rows):
                acc[step, rows, cols] = acc[step, rows, cols] + came[rows, :]

            by_rows(self.rows, self.wide // 2, body)
        for way in (0, 1):
            self.quarter_copy(step, way).start()

    def close(self, step, own):
        if self.quartered:
            return
        p, acc, came = self.place, self.acc, self.quarter_in
        for way in (0, 1):
            self.quarter_copy(step, way).wait_recv()
        cols = self.quarter(p.s)

        def body(rows):
            acc[step, rows, cols] = (
                acc[step, rows, cols].astype(F32)
                + came[0, step, rows, :].astype(F32)
                + came[1, step, rows, :].astype(F32)
            ).astype(BF16)

        by_rows(self.rows, self.wide, body)
        if not self.far_first:
            pl.when(jnp.logical_not(own))(lambda: self.z_copy(step).start())

    def far_sum(self):
        p, acc, came = self.place, self.acc, self.z_in
        p.each(1, p.depth, lambda step: self.z_copy(step).wait_recv())

        def body(rows):
            start = acc[0, rows, :].astype(F32)
            if p.depth <= 8:
                for step in range(1, p.depth):
                    start = start + came[step, rows, :].astype(F32)
            else:
                start = lax.fori_loop(1, p.depth, lambda step, sofar: sofar + came[step, rows, :].astype(F32), start)
            acc[0, rows, :] = start.astype(BF16)

        by_rows(self.rows, self.cols, body)
        for way in (0, 1):
            self.relay_copy(0, way).start()

    def near_sum(self):
        self.close(0, True)
        total, acc, cols = self.total, self.acc, self.quarter(self.place.s)

        def body(rows):
            total[rows, :] = acc[0, rows, cols]

        by_rows(self.rows, self.wide, body)
        self.give()

    def collect(self):
        p, acc, came, total = self.place, self.acc, self.z_in, self.total
        p.each(1, p.depth, lambda step: self.z_copy(step).wait_recv())
        cols = self.mine()

        def body(rows):
            start = acc[0, rows, cols].astype(F32)
            if p.depth <= 8:
                for step in range(1, p.depth):
                    start = start + came[step, rows, :].astype(F32)
            else:
                start = lax.fori_loop(1, p.depth, lambda step, sofar: sofar + came[step, rows, :].astype(F32), start)
            total[rows, :] = start.astype(BF16)

        by_rows(self.rows, self.wide, body)
        if not self.direct:
            self.give()

    def give(self):
        for way, part in self.totals():
            self.total_copy(way, part).start()
        for part in range(self.parts):
            self.put_copy(part).start()

    def spread(self):
        for way, part in self.totals():
            self.total_arrival(way, part).wait_recv()
        if not self.thirds:
            for way in (0, 1):
                self.back_copy(way).start()

    def sent(self):
        def done(step):
            self.core_copy(step).wait_send()
            if not (self.quartered or self.far_first):
                for way in (0, 1):
                    self.relay_copy(step, way).wait_send()
                    self.quarter_copy(step, way).wait_send()

        self.place.each(0, self.place.depth, done)
        if self.far_first:
            for way in (0, 1):
                self.relay_copy(0, way).wait_send()
                self.quarter_copy(0, way).wait_send()

    def finish(self):
        for part in range(self.parts):
            self.put_copy(part).wait()
        if not self.late:
            self.sent()
            self.place.each(1, self.place.depth, lambda step: self.z_copy(step).wait_send())
        for way, part in self.totals():
            self.total_copy(way, part).wait_send()
        if not self.thirds:
            for way in (0, 1):
                self.back_arrival(way).wait_recv()
                self.back_copy(way).wait_send()


REDUCE_REFS = 24


def backward_unit(
    pair, odd, half, tile, heads_ref, mask_ref, qd_ref, kf_ref, go_ref, lse_ref, out_ref, keys_sc, values_sc, keys_t, p_sc, s_sc, k_acc, v_acc
):
    length = heads_ref.shape[0]
    span = p_sc.shape[1]
    scale = jnp.asarray(1.0 / math.sqrt(DH), BF16)
    q_cols, k_cols, v_cols = qkv_columns(heads_ref, pair)
    cols = aligned(pair * LANES, LANES)
    mine = own_lanes(odd, (length, LANES))

    @pl.when(half == 0)
    def _():
        keys_sc[...] = jnp.where(mine, heads_ref[:, k_cols], kf_ref[...])
        values_sc[...] = jnp.where(mine, heads_ref[:, v_cols], jnp.zeros((), BF16))
        keys_t[...] = heads_ref[:, k_cols].T
        k_acc[...] = jnp.zeros_like(k_acc)
        v_acc[...] = jnp.zeros_like(v_acc)

    def one_tile(index, carry):
        here = aligned(index * tile, tile)
        rows = aligned(half * span + index * tile, tile)
        lanes = own_lanes(odd, (tile, LANES))
        queries = query_tile(
            heads_ref[rows, q_cols],
            qd_ref[rows, :],
            mask_ref,
            2 * pair + odd,
            half * (span // BLK) + index * (tile // BLK),
            lanes,
        )
        prob = jnp.exp(dot_nt(keys_sc[...], queries) - lse_ref[pair, pl.ds(odd, 1), rows])
        grad_prob = dot_nt(values_sc[...], go_ref[rows, cols])
        delta = jnp.sum(prob * grad_prob, axis=0, keepdims=True)
        p_sc[:, here] = prob.astype(BF16)
        s_sc[:, here] = (prob * (grad_prob - delta)).astype(BF16)
        return carry

    lax.fori_loop(0, span // tile, one_tile, 0, unroll=True)
    part = aligned(half * span, span)
    v_acc[...] += dot_nn(p_sc[...], go_ref[part, cols])
    k_acc[...] += dot_nn(s_sc[...], heads_ref[part, q_cols] * scale)
    grad_q = (dot_nn(keys_t[...], s_sc[...]) * (1.0 / math.sqrt(DH))).T.astype(BF16)
    out_ref[part, q_cols] = jnp.where(own_lanes(odd, (span, LANES)), grad_q, out_ref[part, q_cols])

    @pl.when(half == 1)
    def _():
        out_ref[:, k_cols] = jnp.where(mine, k_acc[...].astype(BF16), out_ref[:, k_cols])
        out_ref[:, v_cols] = jnp.where(mine, v_acc[...].astype(BF16), out_ref[:, v_cols])


def backward_kernel(
    fsdp_count,
    go_hbm,
    heads_hbm,
    mask_ref,
    qd_hbm,
    kf_hbm,
    lse_ref,
    n1_ref,
    wq_hbm,
    x_hbm,
    hid_hbm,
    vec_ref,
    small_ref,
    out_g_ref,
    in_g_ref,
    down_part,
    tokens_out,
    small_out,
    qkv_total,
    out_total,
    in_total,
    down_total,
    go_sc,
    heads_ref,
    qd_ref,
    kf_ref,
    wq_ref,
    x_ref,
    hid_ref,
    load_sems,
    grads_sc,
    keys_sc,
    values_sc,
    keys_t,
    p_sc,
    s_sc,
    k_acc,
    v_acc,
    n1_sc,
    qkv_g,
    part_sc,
    part_in,
    half_in,
    small_sc,
    small_in,
    *rest,
):
    place = Place(fsdp_count)
    rows = x_ref.shape[0]
    cut_at = in_g_ref.shape[1] * 3 // 4
    shared = pl.ds(0, cut_at)
    apart = pl.ds(cut_at, in_g_ref.shape[1] - cut_at)
    reduces = [
        Reduce.take(place, grad, out, False, rest[i * REDUCE_REFS : (i + 1) * REDUCE_REFS])
        for i, (grad, out) in enumerate(
            ((out_g_ref, out_total), (in_g_ref.at[:, shared], in_total.at[:, shared]))
        )
    ]
    lone = Reduce.take(
        place,
        in_g_ref.at[:, apart],
        in_total.at[:, apart],
        False,
        rest[3 * REDUCE_REFS : 4 * REDUCE_REFS],
        far_first=True,
    )
    first = Reduce.take(place, qkv_g, qkv_total, True, rest[2 * REDUCE_REFS : 3 * REDUCE_REFS], thirds=True)
    put_sem, f_pair, g_pair = (
        rest[4 * REDUCE_REFS],
        rest[4 * REDUCE_REFS + 1 : 4 * REDUCE_REFS + 3],
        rest[4 * REDUCE_REFS + 3 : 4 * REDUCE_REFS + 5],
    )
    down = Reduce(
        place,
        None,
        down_total,
        True,
        (None, None, None, None, None, down_part),
        (None, put_sem, None, None, None, None, f_pair, g_pair),
        late=True,
    )
    n_own, h_sent, h_got, p_sent, p_got, c_sent, c_got, z_sent, z_got, x_sent, x_got = rest[
        4 * REDUCE_REFS + 5 :
    ]
    seats = (place.s1, place.s2, place.s3)
    width = go_sc.shape[1]
    pairs = width // LANES
    half = rows // 2

    loads = [
        pltpu.make_async_copy(src, dst, load_sems.at[i])
        for i, (src, dst) in enumerate(
            (
                (heads_hbm, heads_ref),
                (qd_hbm, qd_ref),
                (kf_hbm, kf_ref),
                (go_hbm, go_sc),
                (wq_hbm, wq_ref),
                (x_hbm, x_ref),
                (hid_hbm, hid_ref),
            )
        )
    ]
    for load in loads:
        load.start()
    later_loads = loads[4:]
    place.meet()
    def first_copies(step):
        for one in reduces + [lone]:
            one.core_copy(step).start()

    place.each(1, place.depth, first_copies)
    first_copies(0)
    for one in reduces + [lone]:
        one.own_copy(1).start()
    down.give()
    n1_copy = pltpu.make_async_copy(n1_ref, n1_sc, n_own)
    n1_copy.start()

    def unit(index):
        backward_unit(
            lax.div(index, 4), lax.rem(lax.div(index, 2), 2), lax.rem(index, 2), 256, heads_ref, mask_ref, qd_ref, kf_ref,
            go_sc, lse_ref, grads_sc, keys_sc, values_sc, keys_t, p_sc, s_sc, k_acc, v_acc,
        )

    def half_copy(way):
        src = part_sc.at[aligned(place.s3 * rows + way * half, half)]
        return send(src, half_in.at[way], (h_sent, h_got), way, place.across(way))

    def part_copy(way, late):
        side = 1 - way if late else way
        src = part_sc.at[aligned(seats[way] * rows + side * half, half)]
        dst = part_in.at[way, pl.ds(side * half, half)]
        return send(src, dst, (p_sent, p_got), 2 * way + late, place.across(way))

    def partial_dn1():
        later_loads[0].wait()
        for seat in (place.s3, place.s1, place.s2, place.s):
            here = aligned(seat * rows, rows)
            part_sc[here, :] = dot_nt(grads_sc[here, :], wq_ref[...]).astype(BF16)
            for way in (0, 1):
                if seat is place.s3:
                    half_copy(way).start()
                elif seat is seats[way]:
                    part_copy(way, 0).start()

    def weight_grad():
        n1_copy.wait()

        def body(index):
            cols = aligned(index * 256, 256)
            qkv_g[cols, :] = dot_tn(n1_sc[:, cols], grads_sc[...]).astype(BF16)

        lax.fori_loop(0, qkv_g.shape[0] // 256, lambda index, carry: (body(index), carry)[1], 0)
        first.begin()

    def swap_dn1():
        for way in (0, 1):
            half_copy(way).wait_recv()
            base = (place.s2, place.s1)[way] * rows + way * half

            def body(index):
                here = aligned(base + index * 32, 32)
                came = half_in[way, aligned(index * 32, 32), :]
                part_sc[here, :] = (part_sc[here, :].astype(F32) + came.astype(F32)).astype(BF16)

            lax.fori_loop(0, half // 32, lambda index, carry: (body(index), carry)[1], 0)
        for way in (0, 1):
            part_copy(way, 1).start()

    def fold_first():
        depth = place.depth
        place.each(1, depth, lambda step: first.fold(step, lax.rem(step + 1, depth)))
        first.fold(0, None)

    def core_small():
        return send(small_sc.at[0], small_sc.at[1], (c_sent, c_got), 0, place.beside)

    def z_small(step):
        return send(small_sc.at[2], small_in.at[step], (z_sent, z_got), step, place.along(place.far(step)))

    def x_small(way):
        return send(small_sc.at[3], small_sc.at[4 + way], (x_sent, x_got), way, place.across(way))

    def close_dn1():
        for way in (0, 1):
            for late in (0, 1):
                part_copy(way, late).wait_recv()
        for load in later_loads[1:]:
            load.wait()
        gain = vec_ref[0:1, :]

        def body(index, sums):
            here = aligned(index * 32, 32)
            mine = aligned(place.s * rows + index * 32, 32)
            dn1 = (
                part_sc[mine, :].astype(F32)
                + part_in[0, here, :].astype(F32)
                + part_in[1, here, :].astype(F32)
            )
            token_rows = x_ref[here, :].astype(F32)
            center = token_rows - jnp.mean(token_rows, axis=-1, keepdims=True)
            inv = lax.rsqrt(jnp.mean(center * center, axis=-1, keepdims=True) + 1e-05)
            hat = center * inv
            scaled = dn1 * gain
            grad = hid_ref[here, :] + inv * (
                scaled
                - jnp.mean(scaled, axis=-1, keepdims=True)
                - hat * jnp.mean(scaled * hat, axis=-1, keepdims=True)
            )
            tokens_out[here, :] = grad.astype(BF16)
            return (
                sums[0] + jnp.sum(dn1 * hat, axis=0, keepdims=True),
                sums[1] + jnp.sum(dn1, axis=0, keepdims=True),
            )

        none = jnp.zeros((1, x_ref.shape[1]), F32)
        gain_sum, bias_sum = lax.fori_loop(0, rows // 32, body, (none, none))
        small_sc[0] = small_ref[...]
        small_sc[0, 0:1, :] = gain_sum
        small_sc[0, 1:2, :] = bias_sum
        core_small().start()

    def small_z():
        core_small().wait_recv()
        small_sc[2] = small_sc[0] + small_sc[1]
        place.each(1, place.depth, lambda step: z_small(step).start())

    def small_x():
        place.each(1, place.depth, lambda step: z_small(step).wait_recv())
        small_in[0] = small_sc[2]
        if place.depth <= 8:
            total = small_in[place.back(0)]
            for z in range(1, place.depth):
                total = total + small_in[place.back(z)]
        else:
            total = lax.fori_loop(
                1, place.depth, lambda z, sofar: sofar + small_in[place.back(z)], small_in[place.back(0)]
            )
        small_sc[3] = total
        for way in range(3):
            x_small(way).start()

    def small_end():
        for way in range(3):
            x_small(way).wait_recv()
        small_out[...] = (small_sc[3] + small_sc[4]) + (small_sc[5] + small_sc[6])

    depth = place.depth
    loose = depth > 8

    def run(count, body):
        lax.fori_loop(1, count, lambda step, carry: (body(step), carry)[1], 0)

    def fold(index):
        for one in reduces + [lone]:
            if not loose:
                step = (index + 1) % depth
                one.fold(step, (step + 1) % depth if step else None)
            elif index == 0:
                run(depth, lambda step: one.fold(step, lax.rem(step + 1, depth)))
                one.fold(0, None)

    def swap(index):
        for one in reduces:
            if not loose:
                one.swap((index + 1) % depth)
            elif index == 0:
                run(depth, one.swap)
                one.swap(0)

    def close(index):
        for one in reduces:
            if not loose:
                one.close((index + 1) % depth, (index + 1) % depth == 0)
            elif index == 0:
                run(depth, lambda step: one.close(step, False))
                one.close(0, True)

    rounds = 1 if loose else depth
    fold(0)
    if rounds > 1:
        fold(1)
    for load in loads[:4]:
        load.wait()
    steps = []
    for index in range(rounds + 2):
        if 2 <= index < rounds:
            steps.append(functools.partial(fold, index))
        if index < rounds:
            steps.append(functools.partial(swap, index))
        if 0 <= index - 1 < rounds:
            steps.append(functools.partial(close, index - 1))
    steps.insert(len(steps) // 2, down.spread)
    count = 4 * pairs
    grads_sc[...] = jnp.zeros_like(grads_sc)
    in_turn(count, unit, [steps[i * len(steps) // count : (i + 1) * len(steps) // count] for i in range(count)])
    partial_dn1()
    weight_grad()
    swap_dn1()
    fold_first()
    lone.far_sum()
    for one in reduces:
        one.collect()
    lone.swap(0)
    first.collect()
    close_dn1()
    lone.near_sum()
    small_z()
    for one in reduces + [lone]:
        one.spread()
    small_x()
    first.spread()
    small_end()
    core_small().wait_send()
    place.each(1, place.depth, lambda step: z_small(step).wait_send())
    for way in range(3):
        x_small(way).wait_send()
        if way < 2:
            half_copy(way).wait_send()
            for late in (0, 1):
                part_copy(way, late).wait_send()
    for one in [first, down, lone] + reduces:
        one.finish()


def backward_attention(fsdp_count, grad_heads, saved, x, hid, small, grads, down_part):
    heads, mask, qd, kf, lse, n1, wq, vec = saved
    rows, width = x.shape
    length, own_width = grad_heads.shape
    depth = fsdp_count // 2
    span = length // 2
    anywhere = pl.BlockSpec(memory_space=pltpu.HBM)
    vmem = pl.BlockSpec(memory_space=pltpu.VMEM)
    share = wq.shape[0] // fsdp_count
    kept = [(grad.shape[0] // fsdp_count, grad.shape[1]) for grad in grads]
    kept_qkv = (share, 4 * wq.shape[1])
    down_kept = (down_part.shape[0], 4 * down_part.shape[1])
    shape = jax.ShapeDtypeStruct

    reduce_scratch = []
    cut_at = kept[1][1] * 3 // 4
    for one in (kept[0], (kept[1][0], cut_at)):
        reduce_scratch += Reduce.scratch(depth, *one, False)
    reduce_scratch += Reduce.scratch(depth, *kept_qkv, True)
    reduce_scratch += Reduce.scratch(depth, kept[1][0], kept[1][1] - cut_at, False, far_first=True)
    return pl.pallas_call(
        functools.partial(backward_kernel, fsdp_count),
        out_shape=(shape(x.shape, BF16), shape(small.shape, F32), shape(kept_qkv, BF16))
        + tuple(shape(one, BF16) for one in kept)
        + (shape(down_kept, BF16),),
        in_specs=[anywhere] * 2 + [vmem] + [anywhere] * 2 + [vmem] + [anywhere] * 4 + [vmem] * 2 + [anywhere] * 2 + [vmem],
        out_specs=(vmem, vmem, anywhere, anywhere, anywhere, anywhere),
        scratch_shapes=[
            pltpu.VMEM((length, own_width), BF16),
            pltpu.VMEM(heads.shape, BF16),
            pltpu.VMEM(qd.shape, BF16),
            pltpu.VMEM(kf.shape, BF16),
            pltpu.VMEM(wq.shape, BF16),
            pltpu.VMEM(x.shape, BF16),
            pltpu.VMEM(hid.shape, F32),
            dma(7),
            pltpu.VMEM((length, 3 * own_width), BF16),
            pltpu.VMEM((length, LANES), BF16),
            pltpu.VMEM((length, LANES), BF16),
            pltpu.VMEM((LANES, length), BF16),
            pltpu.VMEM((length, span), BF16),
            pltpu.VMEM((length, span), BF16),
            pltpu.VMEM((length, LANES), F32),
            pltpu.VMEM((length, LANES), F32),
            pltpu.VMEM((length, width), BF16),
            pltpu.VMEM(wq.shape, BF16),
            pltpu.VMEM((length, width), BF16),
            pltpu.VMEM((2, rows, width), BF16),
            pltpu.VMEM((2, rows // 2, width), BF16),
            pltpu.VMEM((7,) + small.shape, F32),
            pltpu.VMEM((depth,) + small.shape, F32),
        ]
        + reduce_scratch
        + [dma(3), dma(9), dma(9), dma(2), dma(2)]
        + [dma(), dma(2), dma(2), dma(4), dma(4)]
        + [dma(1), dma(1), dma(depth), dma(depth), dma(3), dma(3)],
        compiler_params=pltpu.CompilerParams(
            collective_id=3, has_side_effects=True, vmem_limit_bytes=60 << 20
        ),
    )(grad_heads, heads, mask, qd, kf, lse, n1, wq, x, hid, vec, small, *grads, down_part)


def middle_kernel(
    fsdp_count,
    att_hbm,
    x_hbm,
    cot_hbm,
    vec_ref,
    out_w_hbm,
    in_w_ref,
    down_w_ref,
    result_hbm,
    go_all,
    hid_hbm,
    small_ref,
    out_g_hbm,
    in_g_ref,
    down_part,
    result_ref,
    hid_ref,
    out_g_ref,
    put_sems,
    att_ref,
    x_ref,
    cot_ref,
    out_w_ref,
    fetch_sems,
    datt_ref,
    go_sems,
    go_sent,
    go_got,
    hidden_sc,
    n2_sc,
    n2_t,
    out_acc,
    dn2_acc,
    in_buf,
    down_buf,
    grad_buf,
    act_sc,
    slope_sc,
    down_g,
    in_sems,
    down_sems,
    grad_sems,
    *rest,
):
    place = Place(fsdp_count)
    depth = place.depth
    down_like = rest[0]
    total = Reduce.take(place, down_g, down_like, False, rest[1:], True)
    rows, width = x_ref.shape
    span = down_buf.shape[1]
    hidden_units = down_g.shape[0]
    chunks = hidden_units // span
    paired = total.rows == span
    lines = rows // 32

    def order(index):
        if not paired:
            return index
        z = place.far(lax.rem(lax.div(index, 2) + 1, depth))
        return 2 * z + jnp.where(lax.rem(index, 2) == 0, 1 - place.c, place.c)

    def in_load(index):
        slot = lax.rem(index, 4)
        return pltpu.make_async_copy(
            in_w_ref.at[:, aligned(order(index) * span, span)], in_buf.at[slot], in_sems.at[slot]
        )

    def down_load(index):
        slot = lax.rem(index, 4)
        return pltpu.make_async_copy(
            down_w_ref.at[aligned(order(index) * span, span)], down_buf.at[slot], down_sems.at[slot]
        )

    def grad_store(index):
        slot = lax.rem(index, 2)
        return pltpu.make_async_copy(
            grad_buf.at[slot], in_g_ref.at[:, aligned(order(index) * span, span)], grad_sems.at[slot]
        )

    def over_rows(body, start=0):
        return lax.fori_loop(0, lines, lambda index, carry: body(aligned(index * 32, 32), carry), start)

    for index in (0, 1):
        in_load(index).start()
        down_load(index).start()
    loads = [
        pltpu.make_async_copy(src, dst, fetch_sems.at[i])
        for i, (src, dst) in enumerate(((att_hbm, att_ref), (out_w_hbm, out_w_ref), (x_hbm, x_ref), (cot_hbm, cot_ref)))
    ]
    for load in loads:
        load.start()
    place.meet()
    for load in loads:
        load.wait()
    hidden_sc[...] = x_ref[...].astype(F32) + dot_nn(att_ref[...], out_w_ref[...])

    def normalise(here, carry):
        token_rows = hidden_sc[here, :]
        center = token_rows - jnp.mean(token_rows, axis=-1, keepdims=True)
        variance = jnp.mean(center * center, axis=-1, keepdims=True)
        normed = center * lax.rsqrt(variance + 1e-05) * vec_ref[2:3, :] + vec_ref[3:4, :]
        n2_sc[here, :] = normed.astype(BF16)
        out_acc[here, :] = token_rows + vec_ref[4:5, :]
        return carry

    over_rows(normalise)
    n2_t[...] = n2_sc[...].T
    dn2_acc[...] = jnp.zeros_like(dn2_acc)
    small_ref[...] = jnp.zeros_like(small_ref)

    def place_of(which):
        per = width // span
        return pl.ds(5 + lax.div(which, per), 1), aligned(lax.rem(which, per) * span, span)

    def activate(index):
        slot, side = lax.rem(index, 4), lax.rem(index, 2)
        which = order(index)
        in_load(index).wait()
        down_load(index).wait()

        def ahead():
            in_load(index + 2).start()
            down_load(index + 2).start()

        pl.when(index + 2 < chunks)(ahead)
        line, cols = place_of(which)
        pre = dot_nn(n2_sc[...], in_buf[slot]) + vec_ref[line, cols]
        inner = jnp.tanh(0.7978845608028654 * (pre + 0.044715 * pre * pre * pre))
        act = (0.5 * pre * (1.0 + inner)).astype(BF16)
        act_sc[side] = act
        down_g[aligned(which * span, span), :] = dot_tn(act, cot_ref[...]).astype(BF16)
        slope_sc[side] = 0.5 * (1.0 + inner) + (0.5 * 0.7978845608028654) * pre * (1.0 - inner * inner) * (
            1.0 + (3.0 * 0.044715) * pre * pre
        )

    def chunk(index):
        slot, side = lax.rem(index, 4), lax.rem(index, 2)
        which = order(index)
        line, cols = place_of(which)
        grad = dot_nt(cot_ref[...], down_buf[slot]) * slope_sc[side]
        low = grad.astype(BF16)
        small_ref[line, cols] = jnp.sum(low.astype(F32), axis=0, keepdims=True)
        out_acc[...] += dot_nn(act_sc[side], down_buf[slot])
        dn2_acc[...] += dot_nt(low, in_buf[slot])
        pl.when(index >= 2)(lambda: grad_store(index - 2).wait())
        grad_buf[side] = dot_nn(n2_t[...], low).astype(BF16)
        grad_store(index).start()

    def swap_before(t):
        pl.when(t >= 1)(lambda: total.swap(lax.rem(t, depth)))

    def close_before(t):
        pl.when(t >= 2)(lambda: total.close(lax.rem(t + depth - 1, depth), False))

    if paired:

        def step(t, carry):
            dest = lax.rem(t + 1, depth)

            def early(side, carry):
                activate(2 * t + side)
                pl.when(side == 0)(lambda: total.core_copy(dest).start())
                return carry

            lax.fori_loop(0, 2, early, 0)
            swap_before(t)
            chunk(2 * t)
            total.fold(dest, None)
            chunk(2 * t + 1)
            close_before(t)
            return carry

        lax.fori_loop(0, depth, step, 0)
    else:
        lax.fori_loop(0, chunks, lambda index, carry: (activate(index), chunk(index), carry)[2], 0)
        place.each(0, depth, lambda step: total.core_copy(step).start())

        def step(t, carry):
            swap_before(t)
            total.fold(lax.rem(t + 1, depth), None)
            close_before(t)
            return carry

        lax.fori_loop(0, depth, step, 0)

    def finish(here, sums):
        token_rows = hidden_sc[here, :]
        center = token_rows - jnp.mean(token_rows, axis=-1, keepdims=True)
        inv = lax.rsqrt(jnp.mean(center * center, axis=-1, keepdims=True) + 1e-05)
        hat = center * inv
        dn2 = dn2_acc[here, :]
        cot = cot_ref[here, :].astype(F32)
        scaled = dn2 * vec_ref[2:3, :]
        grad = cot + inv * (
            scaled
            - jnp.mean(scaled, axis=-1, keepdims=True)
            - hat * jnp.mean(scaled * hat, axis=-1, keepdims=True)
        )
        hid_ref[here, :] = grad
        n2_sc[here, :] = grad.astype(BF16)
        result_ref[here, :] = out_acc[here, :].astype(BF16)
        return (
            sums[0] + jnp.sum(dn2 * hat, axis=0, keepdims=True),
            sums[1] + jnp.sum(dn2, axis=0, keepdims=True),
            sums[2] + jnp.sum(cot, axis=0, keepdims=True),
        )

    total.swap(0)
    none = jnp.zeros((1, width), F32)
    gain_sum, bias_sum, cot_sum = over_rows(finish, (none, none, none))
    small_ref[2:3, :] = gain_sum
    small_ref[3:4, :] = bias_sum
    small_ref[4:5, :] = cot_sum
    puts = [
        pltpu.make_async_copy(src, dst, put_sems.at[i])
        for i, (src, dst) in enumerate(((result_ref, result_hbm), (hid_ref, hid_hbm), (out_g_ref, out_g_hbm)))
    ]
    puts[0].start()
    puts[1].start()
    if depth > 1:
        total.close(depth - 1, False)
    datt_ref[...] = dot_nt(n2_sc[...], out_w_ref[...]).astype(BF16)
    seats = (place.s1, place.s2, place.s3)
    part = width // 4

    def go_copy(way):
        src = datt_ref.at[:, aligned(seats[way] * part, part)]
        return send(src, go_all.at[aligned(place.s * rows, rows)], (go_sent, go_got), way, place.across(way))

    def go_arrival(way):
        there = go_all.at[aligned(seats[way] * rows, rows)]
        return send(there, there, (go_sent, go_got), way, place.across(way))

    own_go = pltpu.make_async_copy(
        datt_ref.at[:, aligned(place.s * part, part)], go_all.at[aligned(place.s * rows, rows)], go_sems
    )
    for way in range(3):
        go_copy(way).start()
    own_go.start()
    out_g_ref[...] = dot_tn(att_ref[...], n2_sc[...]).astype(BF16)
    puts[2].start()
    total.close(0, True)
    total.collect()
    down_part[...] = total.total[...]
    for index in (chunks - 2, chunks - 1):
        grad_store(index).wait()
    for put in puts:
        put.wait()
    own_go.wait()
    for way in range(3):
        go_arrival(way).wait_recv()
        go_copy(way).wait_send()
    total.sent()
    place.each(1, depth, lambda step: total.z_copy(step).wait_send())


def middle(fsdp_count, att, x, cot, vec, w_out, w_in, w_down):
    rows, width = x.shape
    hidden_units = w_in.shape[1]
    span = 512
    depth = fsdp_count // 2
    anywhere = pl.BlockSpec(memory_space=pltpu.HBM)
    vmem = pl.BlockSpec(memory_space=pltpu.VMEM)
    shape = jax.ShapeDtypeStruct
    kept = (hidden_units // fsdp_count, width)
    return pl.pallas_call(
        functools.partial(middle_kernel, fsdp_count),
        out_shape=(
            shape((rows, width), BF16),
            shape((4 * rows, width // 4), BF16),
            shape((rows, width), F32),
            shape(vec.shape, F32),
            shape(w_out.shape, BF16),
            shape(w_in.shape, BF16),
            shape((kept[0], width // 4), BF16),
        ),
        in_specs=[anywhere] * 3 + [vmem] + [anywhere] * 3,
        out_specs=(anywhere, anywhere, anywhere, vmem, anywhere, anywhere, vmem),
        scratch_shapes=[
            pltpu.VMEM((rows, width), BF16),
            pltpu.VMEM((rows, width), F32),
            pltpu.VMEM(w_out.shape, BF16),
            dma(3),
            pltpu.VMEM((rows, width), BF16),
            pltpu.VMEM((rows, width), BF16),
            pltpu.VMEM((rows, width), BF16),
            pltpu.VMEM(w_out.shape, BF16),
            dma(4),
            pltpu.VMEM((rows, width), BF16),
            dma(),
            dma(3),
            dma(3),
            pltpu.VMEM((rows, width), F32),
            pltpu.VMEM((rows, width), BF16),
            pltpu.VMEM((width, rows), BF16),
            pltpu.VMEM((rows, width), F32),
            pltpu.VMEM((rows, width), F32),
            pltpu.VMEM((4, width, span), BF16),
            pltpu.VMEM((4, span, width), BF16),
            pltpu.VMEM((2, width, span), BF16),
            pltpu.VMEM((2, rows, span), BF16),
            pltpu.VMEM((2, rows, span), F32),
            pltpu.VMEM((hidden_units, width), BF16),
            dma(4),
            dma(4),
            dma(2),
            pltpu.VMEM(kept, BF16),
        ]
        + Reduce.scratch(depth, *kept, False, True),
        compiler_params=pltpu.CompilerParams(
            collective_id=5, has_side_effects=True, vmem_limit_bytes=60 << 20
        ),
    )(att, x, cot, vec, w_out, w_in, w_down)


def results_kernel(share, held, *refs):
    sources, small, refs = refs[:6], refs[6], refs[7:]
    cut = len(refs) > 20
    count = 12 if cut else 6
    outs, refs = refs[:count], refs[count:]
    taken, given, in_sems, out_sems = refs[:6], refs[6:10], refs[10], refs[11]
    given = given + taken[4:]
    pieces = []
    for i in range(6):
        rows = sources[i].shape[0]
        parts = 4 if rows % 64 == 0 else 1
        for part in range(parts):
            pieces.append((i, part, pl.ds(part * (rows // parts), rows // parts), rows // parts))
    loads = [
        pltpu.make_async_copy(sources[i].at[here], taken[i].at[here], in_sems.at[i, part]) for i, part, here, _ in pieces
    ]
    for load in loads:
        load.start()
    stores = []
    for load, (i, part, here, rows) in zip(loads, pieces):
        load.wait()
        src, dst, base = taken[i], given[i], part * rows

        def body(index, carry):
            line = aligned(base + index * 16, 16)
            dst[line, :] = src[line, :].astype(F32)
            return carry

        if i < 4:
            lax.fori_loop(0, rows // 16, body, 0)
        store = pltpu.make_async_copy(dst.at[here], outs[i].at[here], out_sems.at[i, part])
        store.start()
        stores.append(store)
    if cut:
        position = lax.axis_index("fsdp")
        cols = aligned(position * share, share)
        for line in range(5):
            outs[6 + line][...] = small[line : line + 1, cols]
        per = small.shape[1] // held
        outs[11][...] = small[pl.ds(5 + lax.div(position, per), 1), aligned(lax.rem(position, per) * held, held)]
    for store in stores:
        store.wait()


def write_results(share, held, arrays, small):
    shape = jax.ShapeDtypeStruct
    kinds = (F32, F32, F32, F32, BF16, BF16)
    shapes = [shape(a.shape, kind) for a, kind in zip(arrays, kinds)]
    cut = share % LANES == 0 and held % LANES == 0
    small_shapes = [shape((1, share), F32)] * 5 + [shape((1, held), F32)] if cut else []
    hbm = pl.BlockSpec(memory_space=pltpu.HBM)
    vmem = pl.BlockSpec(memory_space=pltpu.VMEM)
    outs = pl.pallas_call(
        functools.partial(results_kernel, share, held),
        out_shape=tuple(shapes + small_shapes),
        in_specs=[hbm] * 6 + [vmem],
        out_specs=tuple([hbm] * 6 + [vmem] * len(small_shapes)),
        scratch_shapes=[pltpu.VMEM(a.shape, BF16) for a in arrays]
        + [pltpu.VMEM(a.shape, F32) for a in arrays[:4]]
        + [dma(6, 4), dma(6, 4)],
        compiler_params=pltpu.CompilerParams(vmem_limit_bytes=60 << 20),
    )(*arrays, small)
    if cut:
        return outs[:6], [part.reshape(-1) for part in outs[6:]]
    position = lax.axis_index("fsdp")
    lines = lax.dynamic_slice_in_dim(small[:5], position * share, share, axis=1)
    rest = small[5:].reshape(-1)
    return outs, [lines[i] for i in range(5)] + [lax.dynamic_slice_in_dim(rest, position * held, held)]


def per_device(
    fsdp_count,
    tokens,
    segment_ids,
    random_blocks,
    ln1_gain,
    ln1_bias,
    w_qkv,
    w_out,
    ln2_gain,
    ln2_bias,
    w_in,
    b_in,
    w_down,
    b_down,
    cotangent,
):
    width = tokens.shape[2]
    share, held = ln1_gain.shape[0], b_in.shape[0]
    lines = fsdp_count * held // width
    position = lax.axis_index("fsdp")
    column = jnp.arange(width, dtype=jnp.int32)
    narrow = jnp.tile(jnp.stack([ln1_gain, ln1_bias, ln2_gain, ln2_bias, b_down]), (1, fsdp_count))
    narrow = jnp.where(column // share == position, narrow, jnp.zeros((), BF16))
    line = jnp.arange(lines, dtype=jnp.int32)[:, None]
    broad = jnp.tile(b_in[None], (1, width // held))
    broad = jnp.where((line * width + column) // held == position, broad, jnp.zeros((), BF16))
    vec = jnp.concatenate([narrow, broad, jnp.zeros((-(5 + lines) % 16, width), BF16)], axis=0)
    mask = block_mask(random_blocks)
    by_heads, lse, att_rows, out_weight, down_weight, in_weight, vec, normed_one, own_qkv, query_docs, key_feats = (
        forward_attention(fsdp_count, tokens[0], w_qkv, vec, segment_ids, mask, w_out, w_down, w_in)
    )
    result, grad_att, grad_hidden, small, grad_out, grad_in, down_part = middle(
        fsdp_count, att_rows, tokens[0], cotangent[0], vec, out_weight, in_weight, down_weight
    )
    grad_tokens, small, total_qkv, total_out, total_in, total_down = backward_attention(
        fsdp_count,
        grad_att,
        (by_heads, mask, query_docs, key_feats, lse, normed_one, own_qkv, vec),
        tokens[0],
        grad_hidden,
        small,
        (grad_out, grad_in),
        down_part,
    )
    arrays, parts = write_results(
        share, held, (total_in, total_down, total_qkv, total_out, result, grad_tokens), small
    )
    return (
        arrays[4][None],
        arrays[5][None],
        parts[0],
        parts[1],
        arrays[2],
        arrays[3],
        parts[2],
        parts[3],
        arrays[0],
        parts[5],
        arrays[1],
        parts[4],
    )


def solution(mesh):
    return jax.shard_map(
        functools.partial(per_device, mesh.shape["fsdp"]),
        mesh=mesh,
        in_specs=(
            P("fsdp", "seq", None),
            P("fsdp", "seq"),
            P("seq", None, None),
            P("fsdp"),
            P("fsdp"),
            P("fsdp", None),
            P("fsdp", None),
            P("fsdp"),
            P("fsdp"),
            P("fsdp", None),
            P("fsdp"),
            P("fsdp", None),
            P("fsdp"),
            P("fsdp", "seq", None),
        ),
        out_specs=(
            P("fsdp", "seq", None),
            P("fsdp", "seq", None),
            P("fsdp"),
            P("fsdp"),
            P("fsdp", None),
            P("fsdp", None),
            P("fsdp"),
            P("fsdp"),
            P("fsdp", None),
            P("fsdp"),
            P("fsdp", None),
            P("fsdp"),
        ),
        check_vma=False,
    )
```

```python
import functools
import math

import jax
import jax.numpy as jnp
from jax import lax
from jax.experimental import pallas as pl
from jax.experimental.pallas import tpu as pltpu
from jax.sharding import PartitionSpec as P

DH = 64
BLK = 64
LANES = 128
NEG = -1e30
F32 = jnp.float32
BF16 = jnp.bfloat16


def dot_nn(a, b):
    return jnp.dot(a, b, preferred_element_type=F32)


def dot_nt(a, b):
    return lax.dot_general(a, b, (((1,), (1,)), ((), ())), preferred_element_type=F32)


def dot_tn(a, b):
    return lax.dot_general(a, b, (((0,), (0,)), ((), ())), preferred_element_type=F32)


DOCS = 6


def block_mask(random_blocks):
    heads, inner, _ = random_blocks.shape
    blocks = inner + 2
    ids = jnp.arange(blocks, dtype=jnp.int32)
    near = jnp.abs(ids[:, None] - ids[None, :]) <= 1
    edge = (ids == 0) | (ids == blocks - 1)
    fixed = near | edge[:, None] | edge[None, :]
    picked = jnp.any(random_blocks[:, :, :, None] == ids, axis=2)
    used = fixed[None] | jnp.pad(picked, ((0, 0), (1, 1), (0, 0)))
    row = jnp.pad(jnp.where(used, 0.0, NEG), ((0, 0), (0, 0), (0, DH - blocks)))
    return jnp.concatenate([row, row], axis=-1)


def token_features(start, docs, blocks):
    shape = (docs.shape[0], LANES)
    lane = lax.rem(lax.broadcasted_iota(jnp.int32, shape, 1), DH)
    block = lax.div(lax.broadcasted_iota(jnp.int32, shape, 0) + start, BLK)
    own = docs + blocks == lane
    other = jnp.where(own | (lane >= blocks + DOCS), 0.0, 1.0)
    key_part = jnp.where(lane < blocks, jnp.where(block == lane, 1.0, 0.0), other)
    return jnp.where(own, NEG, 0.0).astype(BF16), key_part.astype(BF16)


def query_tile(q_tile, doc_tile, mask_ref, head, first_block, lanes):
    scale = jnp.asarray(1.0 / math.sqrt(DH), BF16)
    count = q_tile.shape[0] // BLK
    mask = jnp.concatenate(
        [jnp.broadcast_to(mask_ref[head, pl.ds(first_block + i, 1), :], (BLK, LANES)) for i in range(count)], axis=0
    )
    return jnp.where(lanes, q_tile * scale, doc_tile + mask.astype(BF16))


def own_lanes(odd, shape):
    return lax.div(lax.broadcasted_iota(jnp.int32, shape, 1), DH) == odd


MESH = pl.DeviceIdType.MESH


class Place:
    def __init__(self, fsdp_count):
        self.depth = fsdp_count // 2
        self.s = lax.axis_index("seq")
        self.f = lax.axis_index("fsdp")
        self.z = lax.div(self.f, 2)
        self.c = lax.rem(self.f, 2)
        self.s1 = self.s + 1 - 2 * lax.rem(self.s, 2)
        self.s2 = self.s + 2 - 4 * lax.div(self.s, 2)
        self.s3 = 3 - self.s
        self.beside = (self.s, self.f + 1 - 2 * self.c)

    def across(self, index):
        return ((self.s1, self.s2, self.s3)[index], self.f)

    def far(self, step):
        return lax.rem(self.z + step, self.depth)

    def back(self, step):
        return lax.rem(self.z + self.depth - step, self.depth)

    def along(self, z):
        return (self.s, 2 * z + self.c)

    def meet(self):
        barrier = pltpu.get_barrier_semaphore()
        peers = [self.beside] + [self.across(i) for i in range(3)]
        for peer in peers:
            pl.semaphore_signal(barrier, inc=1, device_id=peer, device_id_type=MESH)
        self.each(1, self.depth, lambda step: pl.semaphore_signal(
            barrier, inc=1, device_id=self.along(self.far(step)), device_id_type=MESH
        ))
        pl.semaphore_wait(barrier, len(peers) + self.depth - 1)

    def each(self, start, stop, body):
        if stop - start <= 8:
            for step in range(start, stop):
                body(step)
        else:
            lax.fori_loop(start, stop, lambda step, carry: (body(step), carry)[1], 0)


def send(src, dst, sems, index, device):
    sent, got = sems
    return pltpu.make_async_remote_copy(
        src_ref=src,
        dst_ref=dst,
        send_sem=sent.at[index],
        recv_sem=got.at[index],
        device_id=device,
        device_id_type=MESH,
    )


def aligned(start, size):
    return pl.ds(pl.multiple_of(start, size), size)


class Gather:
    def __init__(self, place, src, dst, split, sems):
        self.place, self.src, self.dst, self.split = place, src, dst, split
        self.rows, self.cols = src.shape
        self.local, self.zs, self.xs, self.rs, self.cs = sems

    def block(self, z, core, quarter=None, half=None):
        rows = aligned((2 * z + core) * self.rows, self.rows)
        if quarter is None:
            return self.dst.at[rows]
        wide = self.cols // 4
        if half is None:
            return self.dst.at[rows, aligned(quarter * wide, wide)]
        return self.dst.at[rows, aligned(quarter * wide + half * (wide // 2), wide // 2)]

    def source(self, step, side):
        return self.place.z - step if side == 0 else self.place.z + step

    def has(self, step, side):
        z = self.source(step, side)
        return z >= 0 if side == 0 else z < self.place.depth

    def sends(self, step, side):
        p = self.place
        onward = p.z + 1 < p.depth if side == 0 else p.z > 0
        return jnp.logical_and(self.has(step - 1, side), onward)

    def slot(self, step, side):
        return 2 * step + side

    def own_copy(self):
        return pltpu.make_async_copy(self.src, self.block(self.place.z, self.place.c), self.local)

    def own_core(self):
        p = self.place
        return send(self.src, self.block(p.z, p.c), self.cs, 0, p.beside)

    def own_arrival(self):
        p = self.place
        there = self.block(p.z, 1 - p.c)
        return send(there, there, self.cs, 0, p.beside)

    def core_copy(self, step, side):
        p = self.place
        there = self.block(self.source(step, side), p.c)
        return send(there, there, self.cs, self.slot(step, side), p.beside)

    def core_arrival(self, step, side):
        p = self.place
        there = self.block(self.source(step, side), 1 - p.c)
        return send(there, there, self.cs, self.slot(step, side), p.beside)

    def z_copy(self, step, side):
        p = self.place
        z = self.source(step - 1, side)
        there = self.block(z, p.c, p.s) if self.split else self.block(z, p.c)
        src = there
        if isinstance(step, int) and step == 1:
            wide = self.cols // 4
            src = self.src.at[:, aligned(p.s * wide, wide)] if self.split else self.src
        return send(src, there, self.zs, self.slot(step, side), p.along(p.z + 1 - 2 * side))

    def z_arrival(self, step, side):
        p = self.place
        z = self.source(step, side)
        there = self.block(z, p.c, p.s) if self.split else self.block(z, p.c)
        return send(there, there, self.zs, self.slot(step, side), p.along(p.z - 1 + 2 * side))

    def x_copy(self, step, side, way):
        p = self.place
        there = self.block(self.source(step, side), p.c, p.s)
        return send(there, there, self.xs[way], self.slot(step, side), p.across(way))

    def x_arrival(self, step, side, way):
        p = self.place
        there = self.block(self.source(step, side), p.c, (p.s1, p.s2)[way])
        return send(there, there, self.xs[way], self.slot(step, side), p.across(way))

    def relay_copy(self, step, side, way):
        p = self.place
        there = self.block(self.source(step, side), p.c, (p.s2, p.s1)[way], 1 - way)
        return send(there, there, self.rs[way], self.slot(step, side), p.across(way))

    def relay_arrival(self, step, side, way):
        p = self.place
        there = self.block(self.source(step, side), p.c, p.s3, 1 - way)
        return send(there, there, self.rs[way], self.slot(step, side), p.across(way))

    def both(self, step, body, test=None):
        for side in (0, 1):
            pl.when((test or self.has)(step, side))(functools.partial(body, step, side))

    def begin(self):
        self.both(1, lambda step, side: self.z_copy(step, side).start(), self.sends)
        self.own_copy().start()
        self.own_core().start()

    def swap(self, step):
        def body(step, side):
            self.z_arrival(step, side).wait_recv()
            pl.when(self.sends(step + 1, side))(lambda: self.z_copy(step + 1, side).start())
            if self.split:
                for way in (0, 1):
                    self.x_copy(step, side, way).start()
            else:
                self.core_copy(step, side).start()

        self.both(step, body)

    def relay(self, step):
        def body(step, side):
            for way in (0, 1):
                self.x_arrival(step, side, way).wait_recv()
            for way in (0, 1):
                self.relay_copy(step, side, way).start()

        if self.split:
            self.both(step, body)

    def share(self, step):
        def body(step, side):
            for way in (0, 1):
                self.relay_arrival(step, side, way).wait_recv()
            self.core_copy(step, side).start()

        if self.split:
            self.both(step, body)

    def finish(self):
        self.own_copy().wait()
        self.own_core().wait_send()
        self.own_arrival().wait_recv()

        def close(step, side):
            if self.split:
                for way in (0, 1):
                    self.x_copy(step, side, way).wait_send()
                    self.relay_copy(step, side, way).wait_send()
            self.core_copy(step, side).wait_send()
            self.core_arrival(step, side).wait_recv()

        self.place.each(1, self.place.depth, lambda step: self.both(step, close))
        self.place.each(
            1,
            self.place.depth,
            lambda step: self.both(step, lambda step, side: self.z_copy(step, side).wait_send(), self.sends),
        )

    @staticmethod
    def scratch(depth, split):
        held = 2 * depth if split else 1
        return [dma()] + [dma(2 * depth)] * 2 + [dma(held)] * 8 + [dma(2 * depth)] * 2

    @staticmethod
    def take(refs):
        pairs = [(refs[i], refs[i + 1]) for i in range(1, 13, 2)]
        return (refs[0], pairs[0], pairs[1:3], pairs[3:5], pairs[5])


GATHER_SEMS = 13


def gather_steps(place, gathers, late, count, unit):
    depth = place.depth

    def swap(step):
        for one in gathers:
            one.swap(step)

    def relay(step):
        for one in gathers:
            one.relay(step)

    def share(step):
        for one in gathers:
            one.share(step)

    def late_swap(step):
        for one in late:
            one.swap(step)

    for one in late:
        one.begin()
    if depth <= 8:
        rounds = []
        for step in range(2, depth + 2):
            now = []
            if step <= depth:
                now.append(functools.partial(late_swap, step - 2)) if step > 2 else None
                now.append(functools.partial(share, step - 3)) if step > 3 else None
                now.append(functools.partial(swap, step)) if step < depth else None
                now.append(functools.partial(relay, step - 1))
            rounds.append(now)
        rounds[-1] = [functools.partial(share, step) for step in range(max(1, depth - 2), depth)]
        rounds[-1].append(functools.partial(late_swap, depth - 1))
        in_turn(count, unit, rounds[:count])
        for now in rounds[count:]:
            for one in now:
                one()
    else:
        in_turn(count, unit, [])
        swap(2)
        relay(1)

        def body(step, carry):
            late_swap(step - 2)
            share(step - 2)
            swap(step)
            relay(step - 1)
            return carry

        lax.fori_loop(3, depth, body, 0)
        late_swap(depth - 2)
        share(depth - 2)
        relay(depth - 1)
        share(depth - 1)
        late_swap(depth - 1)


def dma(*shape):
    return pltpu.SemaphoreType.DMA(shape) if shape else pltpu.SemaphoreType.DMA


def qkv_columns(heads_ref, pair):
    third = heads_ref.shape[1] // 3
    return tuple(aligned(i * third + pair * LANES, LANES) for i in range(3))


def attend_unit(pair, odd, tile, heads_ref, mask_ref, qd_ref, kf_ref, keys_sc, values_t, out_ref, lse_ref):
    length = heads_ref.shape[0]
    cols = aligned(pair * LANES, LANES)
    q_cols, k_cols, v_cols = qkv_columns(heads_ref, pair)
    mine = own_lanes(odd, (length, LANES))
    keys_sc[...] = jnp.where(mine, heads_ref[:, k_cols], kf_ref[...])

    @pl.when(odd == 0)
    def _():
        values_t[...] = heads_ref[:, v_cols].T
        out_ref[:, cols] = jnp.zeros((length, LANES), BF16)

    def one_tile(index, carry):
        rows = aligned(index * tile, tile)
        lanes = own_lanes(odd, (tile, LANES))
        queries = query_tile(
            heads_ref[rows, q_cols], qd_ref[rows, :], mask_ref, 2 * pair + odd, index * (tile // BLK), lanes
        )
        scores = dot_nt(keys_sc[...], queries)
        top = jnp.max(scores, axis=0, keepdims=True)
        prob = jnp.exp(scores - top)
        total = jnp.sum(prob, axis=0, keepdims=True)
        mixed = dot_nn(values_t[...], prob.astype(BF16)) / total
        lse_ref[pair, pl.ds(odd, 1), rows] = top + jnp.log(total)
        out_ref[rows, cols] = jnp.where(lanes, mixed.T.astype(BF16), out_ref[rows, cols])
        return carry

    lax.fori_loop(0, length // tile, one_tile, 0, unroll=2)


def in_turn(count, unit, actions):
    def body(index, carry):
        unit(index)
        for which, todo in enumerate(actions):
            if todo:

                @pl.when(index == which)
                def _(todo=todo):
                    for one in todo:
                        one()

        return carry

    lax.fori_loop(0, count, body, 0)


def forward_kernel(
    fsdp_count,
    x_ref,
    wq_ref,
    vec_ref,
    ids_ref,
    mask_ref,
    out_w_ref,
    down_w_ref,
    in_w_ref,
    heads_all,
    lse_ref,
    att_all,
    out_w_all,
    down_w_all,
    in_w_all,
    vec_sum,
    n1_all,
    wq_all,
    qd_ref,
    kf_ref,
    x_sc,
    n1_sc,
    wq_own,
    wq_sc,
    vec_sc,
    seg_ref,
    seg_sc,
    heads_sc,
    att_sc,
    keys_sc,
    values_t,
    *sems,
):
    place = Place(fsdp_count)
    rows, width = x_ref.shape
    own_width = wq_sc.shape[1]
    seats = (place.s1, place.s2, place.s3)

    def taken(i):
        return Gather.take(sems[i * GATHER_SEMS : (i + 1) * GATHER_SEMS])

    x_own, seg_own, keep_sems, pick_sems, x_sent, x_got, r_sent, r_got, g_sent, g_got, a_sent, a_got, a_own = sems[6 * GATHER_SEMS :]
    lone = pl.ds(0, in_w_ref.shape[1] // 2)
    shared = pl.ds(in_w_ref.shape[1] // 2, in_w_ref.shape[1] // 2)
    gathers = [
        Gather(place, src, dst, split, taken(i))
        for i, (src, dst, split) in enumerate(
            (
                (out_w_ref, out_w_all, True),
                (in_w_ref.at[:, shared], in_w_all.at[:, shared], True),
                (down_w_ref, down_w_all, True),
                (in_w_ref.at[:, lone], in_w_all.at[:, lone], False),
            )
        )
    ]
    late = [gathers.pop()]
    third = own_width // 3
    picks = [
        pltpu.make_async_copy(
            wq_ref.at[:, aligned((4 * i + place.s) * third, third)], wq_own.at[:, pl.ds(i * third, third)], pick_sems.at[i]
        )
        for i in range(3)
    ]
    for pick in picks:
        pick.start()
    seg_ref[...] = jnp.zeros_like(seg_ref)
    for part in range(ids_ref.shape[1] // LANES):
        seg_ref[part : part + 1, :] = ids_ref[:, part * LANES : (part + 1) * LANES]
    weight = Gather(place, wq_own, wq_sc, False, taken(4))
    vector = Gather(place, vec_ref, vec_sc, False, taken(5))
    half = rows // 2

    def x_rows(seat):
        return x_sc.at[aligned(seat * rows, rows)]

    def x_half(seat, part):
        return x_sc.at[aligned(seat * rows + part * half, half)]

    def x_copy(way):
        return send(x_ref, x_rows(place.s), (x_sent, x_got), way, place.across(way))

    def x_arrival(way):
        there = x_rows(seats[way])
        return send(there, there, (x_sent, x_got), way, place.across(way))

    def x_relay(way):
        there = x_half((place.s2, place.s1)[way], 1 - way)
        return send(there, there, (r_sent, r_got), way, place.across(way))

    def x_relayed(way):
        there = x_half(place.s3, 1 - way)
        return send(there, there, (r_sent, r_got), way, place.across(way))

    def seg_copy(way):
        return send(seg_ref, seg_sc.at[place.s], (g_sent, g_got), way, place.across(way))

    def seg_arrival(way):
        there = seg_sc.at[seats[way]]
        return send(there, there, (g_sent, g_got), way, place.across(way))

    place.meet()
    vector.begin()
    for pick in picks:
        pick.wait()
    weight.begin()
    for way in range(2):
        x_copy(way).start()
    for way in range(3):
        seg_copy(way).start()
    own_x = pltpu.make_async_copy(x_ref, x_rows(place.s), x_own)
    own_x.start()
    own_seg = pltpu.make_async_copy(seg_ref, seg_sc.at[place.s], seg_own)
    own_seg.start()
    def start_rest():
        for one in gathers:
            one.begin()

    if place.depth <= 8:
        for step in range(1, place.depth):
            vector.swap(step)
            weight.swap(step)
            if step == max(1, place.depth - 2):
                start_rest()
    else:
        place.each(1, place.depth, vector.swap)
        place.each(1, place.depth, weight.swap)
        start_rest()
    vector.finish()
    vec_rows = vec_ref.shape[0]
    total = vec_sc[pl.ds(0, vec_rows), :].astype(F32)
    if fsdp_count <= 8:
        for f in range(1, fsdp_count):
            total = total + vec_sc[pl.ds(f * vec_rows, vec_rows), :].astype(F32)
    else:
        total = lax.fori_loop(
            1, fsdp_count, lambda f, sofar: sofar + vec_sc[aligned(f * vec_rows, vec_rows), :].astype(F32), total
        )
    vec_sum[...] = total

    def normalise(seat):
        def body(part):
            token_rows = x_sc[aligned(seat * rows + part * 32, 32), :].astype(F32)
            center = token_rows - jnp.mean(token_rows, axis=-1, keepdims=True)
            variance = jnp.mean(center * center, axis=-1, keepdims=True)
            normed = center * lax.rsqrt(variance + 1e-05) * vec_sum[0:1, :] + vec_sum[1:2, :]
            n1_sc[aligned(seat * rows + part * 32, 32), :] = normed.astype(BF16)

        lax.fori_loop(0, rows // 32, lambda part, carry: (body(part), carry)[1], 0)

    def project(seat):
        here = aligned(seat * rows, rows)

        def body(part):
            cols = aligned(part * 256, 256)
            heads_sc[here, cols] = dot_nn(n1_sc[here, :], wq_sc[:, cols]).astype(BF16)

        lax.fori_loop(0, own_width // 256, lambda part, carry: (body(part), carry)[1], 0)

    own_x.wait()
    normalise(place.s)
    for way in range(2):
        x_arrival(way).wait_recv()
    for way in range(2):
        x_relay(way).start()
    for way in range(2):
        normalise(seats[way])
    weight.finish()
    project(place.s)
    for way in range(2):
        project(seats[way])
    for one in gathers:
        one.swap(1)
    for way in range(2):
        x_relayed(way).wait_recv()
    normalise(place.s3)
    project(place.s3)
    own_seg.wait()
    for way in range(3):
        seg_arrival(way).wait_recv()
    blocks = mask_ref.shape[1]
    for seat in range(4):
        columns = seg_sc[seat].T
        for part in range(rows // LANES):
            here = pl.ds(seat * rows + part * LANES, LANES)
            qd_ref[here, :], kf_ref[here, :] = token_features(
                seat * rows + part * LANES, columns[:, part : part + 1], blocks
            )
    keeps = [
        pltpu.make_async_copy(src, dst, keep_sems.at[i])
        for i, (src, dst) in enumerate(((heads_sc, heads_all), (n1_sc, n1_all), (wq_sc, wq_all)))
    ]
    for keep in keeps:
        keep.start()

    pairs = att_sc.shape[1] // LANES

    def att_copy(pair, way):
        cols = aligned((place.s * pairs + pair) * LANES, LANES)
        return send(
            att_sc.at[aligned(seats[way] * rows, rows), aligned(pair * LANES, LANES)],
            att_all.at[:, cols],
            (a_sent, a_got),
            pair * 3 + way,
            place.across(way),
        )

    def att_own(pair):
        cols = aligned((place.s * pairs + pair) * LANES, LANES)
        return pltpu.make_async_copy(
            att_sc.at[aligned(place.s * rows, rows), aligned(pair * LANES, LANES)],
            att_all.at[:, cols],
            a_own.at[pair],
        )

    def att_arrival(pair, way):
        there = att_all.at[:, aligned((seats[way] * pairs + pair) * LANES, LANES)]
        return send(there, there, (a_sent, a_got), pair * 3 + way, place.across(way))

    def unit(index):
        pair, odd = lax.div(index, 2), lax.rem(index, 2)
        attend_unit(pair, odd, 256, heads_sc, mask_ref, qd_ref, kf_ref, keys_sc, values_t, att_sc, lse_ref)

        @pl.when(odd == 1)
        def _():
            for way in range(3):
                att_copy(pair, way).start()
            att_own(pair).start()

    gather_steps(place, gathers, late, 2 * pairs, unit)
    for keep in keeps:
        keep.wait()
    for way in range(3):
        seg_copy(way).wait_send()
        if way < 2:
            x_copy(way).wait_send()
            x_relay(way).wait_send()
        for pair in range(pairs):
            att_copy(pair, way).wait_send()
            att_arrival(pair, way).wait_recv()
    for pair in range(pairs):
        att_own(pair).wait()
    for one in gathers + late:
        one.finish()


def forward_attention(fsdp_count, x, w_qkv, vec, seg, mask, w_out, w_down, w_in):
    rows, width = x.shape
    length = 4 * rows
    heads = mask.shape[0]
    pairs = heads // 2
    depth = fsdp_count // 2
    own_width = w_qkv.shape[1] // 4
    full = fsdp_count * w_qkv.shape[0]
    seg_rows = -(-seg.shape[1] // (8 * LANES)) * 8
    anywhere = pl.BlockSpec(memory_space=pltpu.HBM)
    vmem = pl.BlockSpec(memory_space=pltpu.VMEM)
    shape = jax.ShapeDtypeStruct

    def whole(shard):
        return shape((fsdp_count * shard.shape[0], shard.shape[1]), shard.dtype)

    return pl.pallas_call(
        functools.partial(forward_kernel, fsdp_count),
        out_shape=(
            shape((length, own_width), BF16),
            shape((pairs, 2, length), F32),
            shape((rows, heads * DH * 4), BF16),
            whole(w_out),
            whole(w_down),
            whole(w_in),
            shape(vec.shape, F32),
            shape((length, width), BF16),
            shape((full, own_width), BF16),
            shape((length, LANES), BF16),
            shape((length, LANES), BF16),
        ),
        in_specs=[anywhere] * 3 + [vmem] * 2 + [anywhere] * 3,
        out_specs=(anywhere, vmem, anywhere, anywhere, anywhere, anywhere, vmem, anywhere, anywhere, vmem, vmem),
        scratch_shapes=[
            pltpu.VMEM((length, width), BF16),
            pltpu.VMEM((length, width), BF16),
            pltpu.VMEM((w_qkv.shape[0], own_width), BF16),
            pltpu.VMEM((full, own_width), BF16),
            pltpu.VMEM((fsdp_count * vec.shape[0], vec.shape[1]), BF16),
            pltpu.VMEM((seg_rows, LANES), jnp.int32),
            pltpu.VMEM((4, seg_rows, LANES), jnp.int32),
            pltpu.VMEM((length, own_width), BF16),
            pltpu.VMEM((length, heads * DH), BF16),
            pltpu.VMEM((length, LANES), BF16),
            pltpu.VMEM((LANES, length), BF16),
        ]
        + Gather.scratch(depth, True) * 3
        + Gather.scratch(depth, False) * 3
        + [dma(), dma(), dma(3), dma(3), dma(2), dma(2), dma(2), dma(2), dma(3), dma(3)]
        + [dma(3 * pairs), dma(3 * pairs), dma(pairs)],
        compiler_params=pltpu.CompilerParams(
            collective_id=2, has_side_effects=True, vmem_limit_bytes=60 << 20
        ),
    )(x, w_qkv, vec, seg, mask, w_out, w_down, w_in)


def by_rows(count, cols, body):
    chunk = 16
    while count % (2 * chunk) == 0 and 2 * chunk * cols <= 16384:
        chunk *= 2
    lax.fori_loop(0, count // chunk, lambda i, carry: (body(aligned(i * chunk, chunk)), carry)[1], 0)


class Reduce:
    def __init__(self, place, grad, out, quartered, bufs, sems, direct=False, thirds=False, late=False, far_first=False):
        self.far_first = far_first
        self.place, self.grad, self.out, self.quartered, self.direct = place, grad, out, quartered, direct
        self.thirds, self.late = thirds, late
        self.rows, self.cols = out.shape
        self.wide = self.cols // 4
        self.acc, self.own, self.relay_in, self.quarter_in, self.z_in, self.total = bufs
        self.own_sem, self.put_sem, self.cs, self.rs, self.qs, self.zs, self.fs, self.gs = sems

    @staticmethod
    def scratch(depth, rows, cols, quartered, direct=False, far_first=False):
        held = cols // 4 if quartered else cols
        near = 1 if far_first else depth
        side = (1, 1, 16, LANES) if quartered else None
        return [
            pltpu.VMEM((depth, rows, held), BF16),
            pltpu.VMEM((16, LANES) if direct else (rows, held), BF16),
            pltpu.VMEM(side or (2, near, rows, cols // 8), BF16),
            pltpu.VMEM(side or (2, near, rows, cols // 4), BF16),
            pltpu.VMEM((depth, rows, cols if far_first else cols // 4), BF16),
            pltpu.VMEM((rows, cols // 4), BF16),
            dma(),
            dma(3),
        ] + [dma(depth)] * 12 + [dma(6)] * 4

    @staticmethod
    def take(place, grad, out, quartered, refs, direct=False, thirds=False, far_first=False):
        s = refs[8:]
        pairs = [(s[i], s[i + 1]) for i in range(0, 16, 2)]
        sems = (refs[6], refs[7], pairs[0], pairs[1:3], pairs[3:5], pairs[5], pairs[6], pairs[7])
        return Reduce(place, grad, out, quartered, refs[:6], sems, direct, thirds, False, far_first)

    def quarter(self, seat):
        return aligned(seat * self.wide, self.wide)

    def mine(self):
        if self.far_first:
            return pl.ds(0, self.cols)
        return pl.ds(0, self.wide) if self.quartered else self.quarter(self.place.s)

    def piece(self, seat, half):
        return aligned(seat * self.wide + half * (self.wide // 2), self.wide // 2)

    def own_copy(self, step):
        p = self.place
        rows = aligned((2 * p.far(step) + p.c) * self.rows, self.rows)
        return pltpu.make_async_copy(self.grad.at[rows], self.own, self.own_sem)

    def core_copy(self, step):
        p = self.place
        rows = aligned((2 * p.far(step) + 1 - p.c) * self.rows, self.rows)
        return send(self.grad.at[rows], self.acc.at[step], self.cs, step, p.beside)

    def relay_copy(self, step, way):
        p = self.place
        src = self.acc.at[step, :, self.piece(p.s3, way)]
        return send(src, self.relay_in.at[way, step], self.rs[way], step, p.across(way))

    def quarter_copy(self, step, way):
        p = self.place
        src = self.acc.at[step, :, self.quarter((p.s1, p.s2)[way])]
        return send(src, self.quarter_in.at[way, step], self.qs[way], step, p.across(way))

    def z_copy(self, step):
        p = self.place
        src = self.acc.at[step, :, self.mine()]
        return send(src, self.z_in.at[step], self.zs, step, p.along(p.far(step)))

    def columns(self, seat, part):
        if not self.thirds:
            return self.quarter(seat), pl.ds(0, self.wide)
        third = self.wide // 3
        return aligned((4 * part + seat) * third, third), pl.ds(part * third, third)

    @property
    def parts(self):
        return 3 if self.thirds else 1

    def put_copy(self, part):
        there, here = self.columns(self.place.s, part)
        return pltpu.make_async_copy(self.total.at[:, here], self.out.at[:, there], self.put_sem.at[part])

    def total_copy(self, way, part):
        p = self.place
        there, here = self.columns(p.s, part)
        return send(self.total.at[:, here], self.out.at[:, there], self.fs, 3 * way + part, p.across(way))

    def total_arrival(self, way, part):
        p = self.place
        there = self.out.at[:, self.columns((p.s1, p.s2, p.s3)[way], part)[0]]
        return send(there, there, self.fs, 3 * way + part, p.across(way))

    def totals(self):
        return [(way, part) for way in range(2) for part in range(self.parts)]

    def split_piece(self, seat, part, half):
        if not self.thirds:
            return self.piece(seat, half)
        width = self.wide // 6
        return aligned(((4 * part + seat) * 2 + half) * width, width)

    def back_copy(self, way, part):
        p = self.place
        there = self.out.at[:, self.split_piece((p.s2, p.s1)[way], part, 1 - way)]
        return send(there, there, self.gs, 3 * way + part, p.across(way))

    def back_arrival(self, way, part):
        p = self.place
        there = self.out.at[:, self.split_piece(p.s3, part, 1 - way)]
        return send(there, there, self.gs, 3 * way + part, p.across(way))

    def begin(self):
        depth = self.place.depth
        self.place.each(1, depth, lambda step: self.core_copy(step).start())
        self.core_copy(0).start()
        self.own_copy(1).start()

    def fold(self, step, following):
        p, acc, own = self.place, self.acc, self.own
        self.core_copy(step).wait_recv()
        if not self.direct:
            self.own_copy(step).wait()
        base = (2 * p.far(step) + p.c) * self.rows

        def body(index, carry):
            rows = aligned(index * 16, 16)
            added = self.grad[aligned(base + index * 16, 16), :] if self.direct else own[rows, :]
            acc[step, rows, :] = acc[step, rows, :] + added
            return carry

        lax.fori_loop(0, self.rows // 16, body, 0)
        if following is not None:
            self.own_copy(following).start()
        if not (self.quartered or self.far_first):
            for way in (0, 1):
                self.relay_copy(step, way).start()
        elif not (isinstance(step, int) and step == 0):
            self.z_copy(step).start()

    def swap(self, step):
        if self.quartered:
            return
        p, acc = self.place, self.acc
        for way in (0, 1):
            self.relay_copy(step, way).wait_recv()
            cols = self.piece((p.s2, p.s1)[way], way)
            came = self.relay_in.at[way, step]

            def body(rows):
                acc[step, rows, cols] = acc[step, rows, cols] + came[rows, :]

            by_rows(self.rows, self.wide // 2, body)
        for way in (0, 1):
            self.quarter_copy(step, way).start()

    def close(self, step, own):
        if self.quartered:
            return
        p, acc, came = self.place, self.acc, self.quarter_in
        for way in (0, 1):
            self.quarter_copy(step, way).wait_recv()
        cols = self.quarter(p.s)

        def body(rows):
            acc[step, rows, cols] = (
                acc[step, rows, cols].astype(F32)
                + came[0, step, rows, :].astype(F32)
                + came[1, step, rows, :].astype(F32)
            ).astype(BF16)

        by_rows(self.rows, self.wide, body)
        if not self.far_first:
            pl.when(jnp.logical_not(own))(lambda: self.z_copy(step).start())

    def far_sum(self):
        p, acc, came = self.place, self.acc, self.z_in
        p.each(1, p.depth, lambda step: self.z_copy(step).wait_recv())

        def body(rows):
            start = acc[0, rows, :].astype(F32)
            if p.depth <= 8:
                for step in range(1, p.depth):
                    start = start + came[step, rows, :].astype(F32)
            else:
                start = lax.fori_loop(1, p.depth, lambda step, sofar: sofar + came[step, rows, :].astype(F32), start)
            acc[0, rows, :] = start.astype(BF16)

        by_rows(self.rows, self.cols, body)
        for way in (0, 1):
            self.relay_copy(0, way).start()

    def near_sum(self):
        self.close(0, True)
        total, acc, cols = self.total, self.acc, self.quarter(self.place.s)

        def body(rows):
            total[rows, :] = acc[0, rows, cols]

        by_rows(self.rows, self.wide, body)
        self.give()

    def collect(self):
        p, acc, came, total = self.place, self.acc, self.z_in, self.total
        p.each(1, p.depth, lambda step: self.z_copy(step).wait_recv())
        cols = self.mine()

        def body(rows):
            start = acc[0, rows, cols].astype(F32)
            if p.depth <= 8:
                for step in range(1, p.depth):
                    start = start + came[step, rows, :].astype(F32)
            else:
                start = lax.fori_loop(1, p.depth, lambda step, sofar: sofar + came[step, rows, :].astype(F32), start)
            total[rows, :] = start.astype(BF16)

        by_rows(self.rows, self.wide, body)
        if not self.direct:
            self.give()

    def give(self):
        for way, part in self.totals():
            self.total_copy(way, part).start()
        for part in range(self.parts):
            self.put_copy(part).start()

    def spread(self):
        for way, part in self.totals():
            self.total_arrival(way, part).wait_recv()
        for way, part in self.totals():
            self.back_copy(way, part).start()

    def sent(self):
        def done(step):
            self.core_copy(step).wait_send()
            if not (self.quartered or self.far_first):
                for way in (0, 1):
                    self.relay_copy(step, way).wait_send()
                    self.quarter_copy(step, way).wait_send()

        self.place.each(0, self.place.depth, done)
        if self.far_first:
            for way in (0, 1):
                self.relay_copy(0, way).wait_send()
                self.quarter_copy(0, way).wait_send()

    def finish(self):
        for part in range(self.parts):
            self.put_copy(part).wait()
        if not self.late:
            self.sent()
            self.place.each(1, self.place.depth, lambda step: self.z_copy(step).wait_send())
        for way, part in self.totals():
            self.total_copy(way, part).wait_send()
        for way, part in self.totals():
            self.back_arrival(way, part).wait_recv()
            self.back_copy(way, part).wait_send()


REDUCE_REFS = 24


def backward_unit(
    pair, odd, half, tile, heads_ref, mask_ref, qd_ref, kf_ref, go_ref, lse_ref, out_ref, keys_sc, values_sc, keys_t, p_sc, s_sc, k_acc, v_acc
):
    length = heads_ref.shape[0]
    span = p_sc.shape[1]
    scale = jnp.asarray(1.0 / math.sqrt(DH), BF16)
    q_cols, k_cols, v_cols = qkv_columns(heads_ref, pair)
    cols = aligned(pair * LANES, LANES)
    mine = own_lanes(odd, (length, LANES))

    @pl.when(half == 0)
    def _():
        keys_sc[...] = jnp.where(mine, heads_ref[:, k_cols], kf_ref[...])
        values_sc[...] = jnp.where(mine, heads_ref[:, v_cols], jnp.zeros((), BF16))
        keys_t[...] = heads_ref[:, k_cols].T
        k_acc[...] = jnp.zeros_like(k_acc)
        v_acc[...] = jnp.zeros_like(v_acc)

    def one_tile(index, carry):
        here = aligned(index * tile, tile)
        rows = aligned(half * span + index * tile, tile)
        lanes = own_lanes(odd, (tile, LANES))
        queries = query_tile(
            heads_ref[rows, q_cols],
            qd_ref[rows, :],
            mask_ref,
            2 * pair + odd,
            half * (span // BLK) + index * (tile // BLK),
            lanes,
        )
        prob = jnp.exp(dot_nt(keys_sc[...], queries) - lse_ref[pair, pl.ds(odd, 1), rows])
        grad_prob = dot_nt(values_sc[...], go_ref[rows, cols])
        delta = jnp.sum(prob * grad_prob, axis=0, keepdims=True)
        p_sc[:, here] = prob.astype(BF16)
        s_sc[:, here] = (prob * (grad_prob - delta)).astype(BF16)
        return carry

    lax.fori_loop(0, span // tile, one_tile, 0, unroll=True)
    part = aligned(half * span, span)
    v_acc[...] += dot_nn(p_sc[...], go_ref[part, cols])
    k_acc[...] += dot_nn(s_sc[...], heads_ref[part, q_cols] * scale)
    grad_q = (dot_nn(keys_t[...], s_sc[...]) * (1.0 / math.sqrt(DH))).T.astype(BF16)
    out_ref[part, q_cols] = jnp.where(own_lanes(odd, (span, LANES)), grad_q, out_ref[part, q_cols])

    @pl.when(half == 1)
    def _():
        out_ref[:, k_cols] = jnp.where(mine, k_acc[...].astype(BF16), out_ref[:, k_cols])
        out_ref[:, v_cols] = jnp.where(mine, v_acc[...].astype(BF16), out_ref[:, v_cols])


def backward_kernel(
    fsdp_count,
    go_hbm,
    heads_hbm,
    mask_ref,
    qd_hbm,
    kf_hbm,
    lse_ref,
    n1_ref,
    wq_hbm,
    x_hbm,
    hid_hbm,
    vec_ref,
    small_ref,
    out_g_ref,
    in_g_ref,
    down_part,
    tokens_out,
    small_out,
    qkv_total,
    out_total,
    in_total,
    down_total,
    go_sc,
    heads_ref,
    qd_ref,
    kf_ref,
    wq_ref,
    x_ref,
    hid_ref,
    load_sems,
    grads_sc,
    keys_sc,
    values_sc,
    keys_t,
    p_sc,
    s_sc,
    k_acc,
    v_acc,
    n1_sc,
    qkv_g,
    part_sc,
    part_in,
    half_in,
    small_sc,
    small_in,
    *rest,
):
    place = Place(fsdp_count)
    rows = x_ref.shape[0]
    cut_at = in_g_ref.shape[1] * 3 // 4
    shared = pl.ds(0, cut_at)
    apart = pl.ds(cut_at, in_g_ref.shape[1] - cut_at)
    reduces = [
        Reduce.take(place, grad, out, False, rest[i * REDUCE_REFS : (i + 1) * REDUCE_REFS])
        for i, (grad, out) in enumerate(
            ((out_g_ref, out_total), (in_g_ref.at[:, shared], in_total.at[:, shared]))
        )
    ]
    lone = Reduce.take(
        place,
        in_g_ref.at[:, apart],
        in_total.at[:, apart],
        False,
        rest[3 * REDUCE_REFS : 4 * REDUCE_REFS],
        far_first=True,
    )
    first = Reduce.take(place, qkv_g, qkv_total, True, rest[2 * REDUCE_REFS : 3 * REDUCE_REFS], thirds=True)
    put_sem, f_pair, g_pair = (
        rest[4 * REDUCE_REFS],
        rest[4 * REDUCE_REFS + 1 : 4 * REDUCE_REFS + 3],
        rest[4 * REDUCE_REFS + 3 : 4 * REDUCE_REFS + 5],
    )
    down = Reduce(
        place,
        None,
        down_total,
        True,
        (None, None, None, None, None, down_part),
        (None, put_sem, None, None, None, None, f_pair, g_pair),
        late=True,
    )
    n_own, h_sent, h_got, p_sent, p_got, c_sent, c_got, z_sent, z_got, x_sent, x_got = rest[
        4 * REDUCE_REFS + 5 :
    ]
    seats = (place.s1, place.s2, place.s3)
    width = go_sc.shape[1]
    pairs = width // LANES
    half = rows // 2

    loads = [
        pltpu.make_async_copy(src, dst, load_sems.at[i])
        for i, (src, dst) in enumerate(
            (
                (heads_hbm, heads_ref),
                (qd_hbm, qd_ref),
                (kf_hbm, kf_ref),
                (go_hbm, go_sc),
                (wq_hbm, wq_ref),
                (x_hbm, x_ref),
                (hid_hbm, hid_ref),
            )
        )
    ]
    for load in loads:
        load.start()
    later_loads = loads[4:]
    place.meet()
    def first_copies(step):
        for one in reduces + [lone]:
            one.core_copy(step).start()

    place.each(1, place.depth, first_copies)
    first_copies(0)
    for one in reduces + [lone]:
        one.own_copy(1).start()
    down.give()
    n1_copy = pltpu.make_async_copy(n1_ref, n1_sc, n_own)
    n1_copy.start()

    def unit(index):
        backward_unit(
            lax.div(index, 4), lax.rem(lax.div(index, 2), 2), lax.rem(index, 2), 256, heads_ref, mask_ref, qd_ref, kf_ref,
            go_sc, lse_ref, grads_sc, keys_sc, values_sc, keys_t, p_sc, s_sc, k_acc, v_acc,
        )

    def half_copy(way):
        src = part_sc.at[aligned(place.s3 * rows + way * half, half)]
        return send(src, half_in.at[way], (h_sent, h_got), way, place.across(way))

    def part_copy(way, late):
        side = 1 - way if late else way
        src = part_sc.at[aligned(seats[way] * rows + side * half, half)]
        dst = part_in.at[way, pl.ds(side * half, half)]
        return send(src, dst, (p_sent, p_got), 2 * way + late, place.across(way))

    def partial_dn1():
        later_loads[0].wait()
        for seat in (place.s3, place.s1, place.s2, place.s):
            here = aligned(seat * rows, rows)
            part_sc[here, :] = dot_nt(grads_sc[here, :], wq_ref[...]).astype(BF16)
            for way in (0, 1):
                if seat is place.s3:
                    half_copy(way).start()
                elif seat is seats[way]:
                    part_copy(way, 0).start()

    def weight_grad():
        n1_copy.wait()

        def body(index):
            cols = aligned(index * 256, 256)
            qkv_g[cols, :] = dot_tn(n1_sc[:, cols], grads_sc[...]).astype(BF16)

        lax.fori_loop(0, qkv_g.shape[0] // 256, lambda index, carry: (body(index), carry)[1], 0)
        first.begin()

    def swap_dn1():
        for way in (0, 1):
            half_copy(way).wait_recv()
            base = (place.s2, place.s1)[way] * rows + way * half

            def body(index):
                here = aligned(base + index * 32, 32)
                came = half_in[way, aligned(index * 32, 32), :]
                part_sc[here, :] = (part_sc[here, :].astype(F32) + came.astype(F32)).astype(BF16)

            lax.fori_loop(0, half // 32, lambda index, carry: (body(index), carry)[1], 0)
        for way in (0, 1):
            part_copy(way, 1).start()

    def fold_first():
        depth = place.depth
        place.each(1, depth, lambda step: first.fold(step, lax.rem(step + 1, depth)))
        first.fold(0, None)

    def core_small():
        return send(small_sc.at[0], small_sc.at[1], (c_sent, c_got), 0, place.beside)

    def z_small(step):
        return send(small_sc.at[2], small_in.at[step], (z_sent, z_got), step, place.along(place.far(step)))

    def x_small(way):
        return send(small_sc.at[3], small_sc.at[4 + way], (x_sent, x_got), way, place.across(way))

    def close_dn1():
        for way in (0, 1):
            for late in (0, 1):
                part_copy(way, late).wait_recv()
        for load in later_loads[1:]:
            load.wait()
        gain = vec_ref[0:1, :]

        def body(index, sums):
            here = aligned(index * 32, 32)
            mine = aligned(place.s * rows + index * 32, 32)
            dn1 = (
                part_sc[mine, :].astype(F32)
                + part_in[0, here, :].astype(F32)
                + part_in[1, here, :].astype(F32)
            )
            token_rows = x_ref[here, :].astype(F32)
            center = token_rows - jnp.mean(token_rows, axis=-1, keepdims=True)
            inv = lax.rsqrt(jnp.mean(center * center, axis=-1, keepdims=True) + 1e-05)
            hat = center * inv
            scaled = dn1 * gain
            grad = hid_ref[here, :] + inv * (
                scaled
                - jnp.mean(scaled, axis=-1, keepdims=True)
                - hat * jnp.mean(scaled * hat, axis=-1, keepdims=True)
            )
            tokens_out[here, :] = grad.astype(BF16)
            return (
                sums[0] + jnp.sum(dn1 * hat, axis=0, keepdims=True),
                sums[1] + jnp.sum(dn1, axis=0, keepdims=True),
            )

        none = jnp.zeros((1, x_ref.shape[1]), F32)
        gain_sum, bias_sum = lax.fori_loop(0, rows // 32, body, (none, none))
        small_sc[0] = small_ref[...]
        small_sc[0, 0:1, :] = gain_sum
        small_sc[0, 1:2, :] = bias_sum
        core_small().start()

    def small_z():
        core_small().wait_recv()
        small_sc[2] = small_sc[0] + small_sc[1]
        place.each(1, place.depth, lambda step: z_small(step).start())

    def small_x():
        place.each(1, place.depth, lambda step: z_small(step).wait_recv())
        small_in[0] = small_sc[2]
        if place.depth <= 8:
            total = small_in[place.back(0)]
            for z in range(1, place.depth):
                total = total + small_in[place.back(z)]
        else:
            total = lax.fori_loop(
                1, place.depth, lambda z, sofar: sofar + small_in[place.back(z)], small_in[place.back(0)]
            )
        small_sc[3] = total
        for way in range(3):
            x_small(way).start()

    def small_end():
        for way in range(3):
            x_small(way).wait_recv()
        small_out[...] = (small_sc[3] + small_sc[4]) + (small_sc[5] + small_sc[6])

    depth = place.depth
    loose = depth > 8

    def run(count, body):
        lax.fori_loop(1, count, lambda step, carry: (body(step), carry)[1], 0)

    def fold(index):
        for one in reduces + [lone]:
            if not loose:
                step = (index + 1) % depth
                one.fold(step, (step + 1) % depth if step else None)
            elif index == 0:
                run(depth, lambda step: one.fold(step, lax.rem(step + 1, depth)))
                one.fold(0, None)

    def swap(index):
        for one in reduces:
            if not loose:
                one.swap((index + 1) % depth)
            elif index == 0:
                run(depth, one.swap)
                one.swap(0)

    def close(index):
        for one in reduces:
            if not loose:
                one.close((index + 1) % depth, (index + 1) % depth == 0)
            elif index == 0:
                run(depth, lambda step: one.close(step, False))
                one.close(0, True)

    rounds = 1 if loose else depth
    fold(0)
    if rounds > 1:
        fold(1)
    for load in loads[:4]:
        load.wait()
    steps = []
    for index in range(rounds + 2):
        if 2 <= index < rounds:
            steps.append(functools.partial(fold, index))
        if index < rounds:
            steps.append(functools.partial(swap, index))
        if 0 <= index - 1 < rounds:
            steps.append(functools.partial(close, index - 1))
    steps.insert(len(steps) // 2, down.spread)
    count = 4 * pairs
    grads_sc[...] = jnp.zeros_like(grads_sc)
    in_turn(count, unit, [steps[i * len(steps) // count : (i + 1) * len(steps) // count] for i in range(count)])
    partial_dn1()
    weight_grad()
    swap_dn1()
    fold_first()
    lone.far_sum()
    for one in reduces:
        one.collect()
    lone.swap(0)
    first.collect()
    close_dn1()
    lone.near_sum()
    small_z()
    for one in reduces + [lone]:
        one.spread()
    small_x()
    first.spread()
    small_end()
    core_small().wait_send()
    place.each(1, place.depth, lambda step: z_small(step).wait_send())
    for way in range(3):
        x_small(way).wait_send()
        if way < 2:
            half_copy(way).wait_send()
            for late in (0, 1):
                part_copy(way, late).wait_send()
    for one in [first, down, lone] + reduces:
        one.finish()


def backward_attention(fsdp_count, grad_heads, saved, x, hid, small, grads, down_part):
    heads, mask, qd, kf, lse, n1, wq, vec = saved
    rows, width = x.shape
    length, own_width = grad_heads.shape
    depth = fsdp_count // 2
    span = length // 2
    anywhere = pl.BlockSpec(memory_space=pltpu.HBM)
    vmem = pl.BlockSpec(memory_space=pltpu.VMEM)
    share = wq.shape[0] // fsdp_count
    kept = [(grad.shape[0] // fsdp_count, grad.shape[1]) for grad in grads]
    kept_qkv = (share, 4 * wq.shape[1])
    down_kept = (down_part.shape[0], 4 * down_part.shape[1])
    shape = jax.ShapeDtypeStruct

    reduce_scratch = []
    cut_at = kept[1][1] * 3 // 4
    for one in (kept[0], (kept[1][0], cut_at)):
        reduce_scratch += Reduce.scratch(depth, *one, False)
    reduce_scratch += Reduce.scratch(depth, *kept_qkv, True)
    reduce_scratch += Reduce.scratch(depth, kept[1][0], kept[1][1] - cut_at, False, far_first=True)
    return pl.pallas_call(
        functools.partial(backward_kernel, fsdp_count),
        out_shape=(shape(x.shape, BF16), shape(small.shape, F32), shape(kept_qkv, BF16))
        + tuple(shape(one, BF16) for one in kept)
        + (shape(down_kept, BF16),),
        in_specs=[anywhere] * 2 + [vmem] + [anywhere] * 2 + [vmem] + [anywhere] * 4 + [vmem] * 2 + [anywhere] * 2 + [vmem],
        out_specs=(vmem, vmem, anywhere, anywhere, anywhere, anywhere),
        scratch_shapes=[
            pltpu.VMEM((length, own_width), BF16),
            pltpu.VMEM(heads.shape, BF16),
            pltpu.VMEM(qd.shape, BF16),
            pltpu.VMEM(kf.shape, BF16),
            pltpu.VMEM(wq.shape, BF16),
            pltpu.VMEM(x.shape, BF16),
            pltpu.VMEM(hid.shape, F32),
            dma(7),
            pltpu.VMEM((length, 3 * own_width), BF16),
            pltpu.VMEM((length, LANES), BF16),
            pltpu.VMEM((length, LANES), BF16),
            pltpu.VMEM((LANES, length), BF16),
            pltpu.VMEM((length, span), BF16),
            pltpu.VMEM((length, span), BF16),
            pltpu.VMEM((length, LANES), F32),
            pltpu.VMEM((length, LANES), F32),
            pltpu.VMEM((length, width), BF16),
            pltpu.VMEM(wq.shape, BF16),
            pltpu.VMEM((length, width), BF16),
            pltpu.VMEM((2, rows, width), BF16),
            pltpu.VMEM((2, rows // 2, width), BF16),
            pltpu.VMEM((7,) + small.shape, F32),
            pltpu.VMEM((depth,) + small.shape, F32),
        ]
        + reduce_scratch
        + [dma(3), dma(6), dma(6), dma(6), dma(6)]
        + [dma(), dma(2), dma(2), dma(4), dma(4)]
        + [dma(1), dma(1), dma(depth), dma(depth), dma(3), dma(3)],
        compiler_params=pltpu.CompilerParams(
            collective_id=3, has_side_effects=True, vmem_limit_bytes=60 << 20
        ),
    )(grad_heads, heads, mask, qd, kf, lse, n1, wq, x, hid, vec, small, *grads, down_part)


def middle_kernel(
    fsdp_count,
    att_hbm,
    x_hbm,
    cot_hbm,
    vec_ref,
    out_w_hbm,
    in_w_ref,
    down_w_ref,
    result_hbm,
    go_all,
    hid_hbm,
    small_ref,
    out_g_hbm,
    in_g_ref,
    down_part,
    result_ref,
    hid_ref,
    out_g_ref,
    put_sems,
    att_ref,
    x_ref,
    cot_ref,
    out_w_ref,
    fetch_sems,
    datt_ref,
    go_sems,
    go_sent,
    go_got,
    hidden_sc,
    n2_sc,
    n2_t,
    out_acc,
    dn2_acc,
    in_buf,
    down_buf,
    grad_buf,
    act_sc,
    slope_sc,
    down_g,
    in_sems,
    down_sems,
    grad_sems,
    *rest,
):
    place = Place(fsdp_count)
    depth = place.depth
    down_like = rest[0]
    total = Reduce.take(place, down_g, down_like, False, rest[1:], True)
    rows, width = x_ref.shape
    span = down_buf.shape[1]
    hidden_units = down_g.shape[0]
    chunks = hidden_units // span
    paired = total.rows == span
    lines = rows // 32

    def order(index):
        if not paired:
            return index
        z = place.far(lax.rem(lax.div(index, 2) + 1, depth))
        return 2 * z + jnp.where(lax.rem(index, 2) == 0, 1 - place.c, place.c)

    def in_load(index):
        slot = lax.rem(index, 4)
        return pltpu.make_async_copy(
            in_w_ref.at[:, aligned(order(index) * span, span)], in_buf.at[slot], in_sems.at[slot]
        )

    def down_load(index):
        slot = lax.rem(index, 4)
        return pltpu.make_async_copy(
            down_w_ref.at[aligned(order(index) * span, span)], down_buf.at[slot], down_sems.at[slot]
        )

    def grad_store(index):
        slot = lax.rem(index, 2)
        return pltpu.make_async_copy(
            grad_buf.at[slot], in_g_ref.at[:, aligned(order(index) * span, span)], grad_sems.at[slot]
        )

    def over_rows(body, start=0):
        return lax.fori_loop(0, lines, lambda index, carry: body(aligned(index * 32, 32), carry), start)

    for index in (0, 1):
        in_load(index).start()
        down_load(index).start()
    loads = [
        pltpu.make_async_copy(src, dst, fetch_sems.at[i])
        for i, (src, dst) in enumerate(((att_hbm, att_ref), (out_w_hbm, out_w_ref), (x_hbm, x_ref), (cot_hbm, cot_ref)))
    ]
    for load in loads:
        load.start()
    place.meet()
    for load in loads:
        load.wait()
    hidden_sc[...] = x_ref[...].astype(F32) + dot_nn(att_ref[...], out_w_ref[...])

    def normalise(here, carry):
        token_rows = hidden_sc[here, :]
        center = token_rows - jnp.mean(token_rows, axis=-1, keepdims=True)
        variance = jnp.mean(center * center, axis=-1, keepdims=True)
        normed = center * lax.rsqrt(variance + 1e-05) * vec_ref[2:3, :] + vec_ref[3:4, :]
        n2_sc[here, :] = normed.astype(BF16)
        out_acc[here, :] = token_rows + vec_ref[4:5, :]
        return carry

    over_rows(normalise)
    n2_t[...] = n2_sc[...].T
    dn2_acc[...] = jnp.zeros_like(dn2_acc)
    small_ref[...] = jnp.zeros_like(small_ref)

    def place_of(which):
        per = width // span
        return pl.ds(5 + lax.div(which, per), 1), aligned(lax.rem(which, per) * span, span)

    def activate(index):
        slot, side = lax.rem(index, 4), lax.rem(index, 2)
        which = order(index)
        in_load(index).wait()
        down_load(index).wait()

        def ahead():
            in_load(index + 2).start()
            down_load(index + 2).start()

        pl.when(index + 2 < chunks)(ahead)
        line, cols = place_of(which)
        pre = dot_nn(n2_sc[...], in_buf[slot]) + vec_ref[line, cols]
        inner = jnp.tanh(0.7978845608028654 * (pre + 0.044715 * pre * pre * pre))
        act = (0.5 * pre * (1.0 + inner)).astype(BF16)
        act_sc[side] = act
        down_g[aligned(which * span, span), :] = dot_tn(act, cot_ref[...]).astype(BF16)
        slope_sc[side] = 0.5 * (1.0 + inner) + (0.5 * 0.7978845608028654) * pre * (1.0 - inner * inner) * (
            1.0 + (3.0 * 0.044715) * pre * pre
        )

    def chunk(index):
        slot, side = lax.rem(index, 4), lax.rem(index, 2)
        which = order(index)
        line, cols = place_of(which)
        grad = dot_nt(cot_ref[...], down_buf[slot]) * slope_sc[side]
        low = grad.astype(BF16)
        small_ref[line, cols] = jnp.sum(low.astype(F32), axis=0, keepdims=True)
        out_acc[...] += dot_nn(act_sc[side], down_buf[slot])
        dn2_acc[...] += dot_nt(low, in_buf[slot])
        pl.when(index >= 2)(lambda: grad_store(index - 2).wait())
        grad_buf[side] = dot_nn(n2_t[...], low).astype(BF16)
        grad_store(index).start()

    def swap_before(t):
        pl.when(t >= 1)(lambda: total.swap(lax.rem(t, depth)))

    def close_before(t):
        pl.when(t >= 2)(lambda: total.close(lax.rem(t + depth - 1, depth), False))

    if paired:

        def step(t, carry):
            dest = lax.rem(t + 1, depth)

            def early(side, carry):
                activate(2 * t + side)
                pl.when(side == 0)(lambda: total.core_copy(dest).start())
                return carry

            lax.fori_loop(0, 2, early, 0)
            swap_before(t)
            chunk(2 * t)
            total.fold(dest, None)
            chunk(2 * t + 1)
            close_before(t)
            return carry

        lax.fori_loop(0, depth, step, 0)
    else:
        lax.fori_loop(0, chunks, lambda index, carry: (activate(index), chunk(index), carry)[2], 0)
        place.each(0, depth, lambda step: total.core_copy(step).start())

        def step(t, carry):
            swap_before(t)
            total.fold(lax.rem(t + 1, depth), None)
            close_before(t)
            return carry

        lax.fori_loop(0, depth, step, 0)

    def finish(here, sums):
        token_rows = hidden_sc[here, :]
        center = token_rows - jnp.mean(token_rows, axis=-1, keepdims=True)
        inv = lax.rsqrt(jnp.mean(center * center, axis=-1, keepdims=True) + 1e-05)
        hat = center * inv
        dn2 = dn2_acc[here, :]
        cot = cot_ref[here, :].astype(F32)
        scaled = dn2 * vec_ref[2:3, :]
        grad = cot + inv * (
            scaled
            - jnp.mean(scaled, axis=-1, keepdims=True)
            - hat * jnp.mean(scaled * hat, axis=-1, keepdims=True)
        )
        hid_ref[here, :] = grad
        n2_sc[here, :] = grad.astype(BF16)
        result_ref[here, :] = out_acc[here, :].astype(BF16)
        return (
            sums[0] + jnp.sum(dn2 * hat, axis=0, keepdims=True),
            sums[1] + jnp.sum(dn2, axis=0, keepdims=True),
            sums[2] + jnp.sum(cot, axis=0, keepdims=True),
        )

    seats = (place.s1, place.s2, place.s3)
    part = width // 4
    half = rows // 2

    def go_copy(way, side):
        src = datt_ref.at[pl.ds(side * half, half), aligned(seats[way] * part, part)]
        dst = go_all.at[aligned(place.s * rows + side * half, half)]
        return send(src, dst, (go_sent, go_got), 2 * way + side, place.across(way))

    def go_arrival(way, side):
        there = go_all.at[aligned(seats[way] * rows + side * half, half)]
        return send(there, there, (go_sent, go_got), 2 * way + side, place.across(way))

    total.swap(0)
    none = jnp.zeros((1, width), F32)
    sums = (none, none, none)
    for side in (0, 1):
        sums = lax.fori_loop(
            0, lines // 2, lambda index, carry: finish(aligned(side * half + index * 32, 32), carry), sums
        )
        rows_here = pl.ds(side * half, half)
        datt_ref[rows_here, :] = dot_nt(n2_sc[rows_here, :], out_w_ref[...]).astype(BF16)
        for way in range(3):
            go_copy(way, side).start()
    gain_sum, bias_sum, cot_sum = sums
    small_ref[2:3, :] = gain_sum
    small_ref[3:4, :] = bias_sum
    small_ref[4:5, :] = cot_sum
    puts = [
        pltpu.make_async_copy(src, dst, put_sems.at[i])
        for i, (src, dst) in enumerate(((result_ref, result_hbm), (hid_ref, hid_hbm), (out_g_ref, out_g_hbm)))
    ]
    puts[0].start()
    puts[1].start()
    own_go = pltpu.make_async_copy(
        datt_ref.at[:, aligned(place.s * part, part)], go_all.at[aligned(place.s * rows, rows)], go_sems
    )
    own_go.start()
    if depth > 1:
        total.close(depth - 1, False)
    out_g_ref[...] = dot_tn(att_ref[...], n2_sc[...]).astype(BF16)
    puts[2].start()
    total.close(0, True)
    total.collect()
    down_part[...] = total.total[...]
    for index in (chunks - 2, chunks - 1):
        grad_store(index).wait()
    for put in puts:
        put.wait()
    own_go.wait()
    for way in range(3):
        for side in (0, 1):
            go_arrival(way, side).wait_recv()
            go_copy(way, side).wait_send()
    total.sent()
    place.each(1, depth, lambda step: total.z_copy(step).wait_send())


def middle(fsdp_count, att, x, cot, vec, w_out, w_in, w_down):
    rows, width = x.shape
    hidden_units = w_in.shape[1]
    span = 512
    depth = fsdp_count // 2
    anywhere = pl.BlockSpec(memory_space=pltpu.HBM)
    vmem = pl.BlockSpec(memory_space=pltpu.VMEM)
    shape = jax.ShapeDtypeStruct
    kept = (hidden_units // fsdp_count, width)
    return pl.pallas_call(
        functools.partial(middle_kernel, fsdp_count),
        out_shape=(
            shape((rows, width), BF16),
            shape((4 * rows, width // 4), BF16),
            shape((rows, width), F32),
            shape(vec.shape, F32),
            shape(w_out.shape, BF16),
            shape(w_in.shape, BF16),
            shape((kept[0], width // 4), BF16),
        ),
        in_specs=[anywhere] * 3 + [vmem] + [anywhere] * 3,
        out_specs=(anywhere, anywhere, anywhere, vmem, anywhere, anywhere, vmem),
        scratch_shapes=[
            pltpu.VMEM((rows, width), BF16),
            pltpu.VMEM((rows, width), F32),
            pltpu.VMEM(w_out.shape, BF16),
            dma(3),
            pltpu.VMEM((rows, width), BF16),
            pltpu.VMEM((rows, width), BF16),
            pltpu.VMEM((rows, width), BF16),
            pltpu.VMEM(w_out.shape, BF16),
            dma(4),
            pltpu.VMEM((rows, width), BF16),
            dma(),
            dma(6),
            dma(6),
            pltpu.VMEM((rows, width), F32),
            pltpu.VMEM((rows, width), BF16),
            pltpu.VMEM((width, rows), BF16),
            pltpu.VMEM((rows, width), F32),
            pltpu.VMEM((rows, width), F32),
            pltpu.VMEM((4, width, span), BF16),
            pltpu.VMEM((4, span, width), BF16),
            pltpu.VMEM((2, width, span), BF16),
            pltpu.VMEM((2, rows, span), BF16),
            pltpu.VMEM((2, rows, span), F32),
            pltpu.VMEM((hidden_units, width), BF16),
            dma(4),
            dma(4),
            dma(2),
            pltpu.VMEM(kept, BF16),
        ]
        + Reduce.scratch(depth, *kept, False, True),
        compiler_params=pltpu.CompilerParams(
            collective_id=5, has_side_effects=True, vmem_limit_bytes=60 << 20
        ),
    )(att, x, cot, vec, w_out, w_in, w_down)


def results_kernel(share, held, *refs):
    sources, small, refs = refs[:6], refs[6], refs[7:]
    cut = len(refs) > 20
    count = 12 if cut else 6
    outs, refs = refs[:count], refs[count:]
    taken, given, in_sems, out_sems = refs[:6], refs[6:10], refs[10], refs[11]
    given = given + taken[4:]
    pieces = []
    for i in range(6):
        rows = sources[i].shape[0]
        parts = 4 if rows % 64 == 0 else 1
        for part in range(parts):
            pieces.append((i, part, pl.ds(part * (rows // parts), rows // parts), rows // parts))
    loads = [
        pltpu.make_async_copy(sources[i].at[here], taken[i].at[here], in_sems.at[i, part]) for i, part, here, _ in pieces
    ]
    for load in loads:
        load.start()
    stores = []
    for load, (i, part, here, rows) in zip(loads, pieces):
        load.wait()
        src, dst, base = taken[i], given[i], part * rows

        def body(index, carry):
            line = aligned(base + index * 16, 16)
            dst[line, :] = src[line, :].astype(F32)
            return carry

        if i < 4:
            lax.fori_loop(0, rows // 16, body, 0)
        store = pltpu.make_async_copy(dst.at[here], outs[i].at[here], out_sems.at[i, part])
        store.start()
        stores.append(store)
    if cut:
        position = lax.axis_index("fsdp")
        cols = aligned(position * share, share)
        for line in range(5):
            outs[6 + line][...] = small[line : line + 1, cols]
        per = small.shape[1] // held
        outs[11][...] = small[pl.ds(5 + lax.div(position, per), 1), aligned(lax.rem(position, per) * held, held)]
    for store in stores:
        store.wait()


def write_results(share, held, arrays, small):
    shape = jax.ShapeDtypeStruct
    kinds = (F32, F32, F32, F32, BF16, BF16)
    shapes = [shape(a.shape, kind) for a, kind in zip(arrays, kinds)]
    cut = share % LANES == 0 and held % LANES == 0
    small_shapes = [shape((1, share), F32)] * 5 + [shape((1, held), F32)] if cut else []
    hbm = pl.BlockSpec(memory_space=pltpu.HBM)
    vmem = pl.BlockSpec(memory_space=pltpu.VMEM)
    outs = pl.pallas_call(
        functools.partial(results_kernel, share, held),
        out_shape=tuple(shapes + small_shapes),
        in_specs=[hbm] * 6 + [vmem],
        out_specs=tuple([hbm] * 6 + [vmem] * len(small_shapes)),
        scratch_shapes=[pltpu.VMEM(a.shape, BF16) for a in arrays]
        + [pltpu.VMEM(a.shape, F32) for a in arrays[:4]]
        + [dma(6, 4), dma(6, 4)],
        compiler_params=pltpu.CompilerParams(vmem_limit_bytes=60 << 20),
    )(*arrays, small)
    if cut:
        return outs[:6], [part.reshape(-1) for part in outs[6:]]
    position = lax.axis_index("fsdp")
    lines = lax.dynamic_slice_in_dim(small[:5], position * share, share, axis=1)
    rest = small[5:].reshape(-1)
    return outs, [lines[i] for i in range(5)] + [lax.dynamic_slice_in_dim(rest, position * held, held)]


def per_device(
    fsdp_count,
    tokens,
    segment_ids,
    random_blocks,
    ln1_gain,
    ln1_bias,
    w_qkv,
    w_out,
    ln2_gain,
    ln2_bias,
    w_in,
    b_in,
    w_down,
    b_down,
    cotangent,
):
    width = tokens.shape[2]
    share, held = ln1_gain.shape[0], b_in.shape[0]
    lines = fsdp_count * held // width
    position = lax.axis_index("fsdp")
    column = jnp.arange(width, dtype=jnp.int32)
    narrow = jnp.tile(jnp.stack([ln1_gain, ln1_bias, ln2_gain, ln2_bias, b_down]), (1, fsdp_count))
    narrow = jnp.where(column // share == position, narrow, jnp.zeros((), BF16))
    line = jnp.arange(lines, dtype=jnp.int32)[:, None]
    broad = jnp.tile(b_in[None], (1, width // held))
    broad = jnp.where((line * width + column) // held == position, broad, jnp.zeros((), BF16))
    vec = jnp.concatenate([narrow, broad, jnp.zeros((-(5 + lines) % 16, width), BF16)], axis=0)
    mask = block_mask(random_blocks)
    by_heads, lse, att_rows, out_weight, down_weight, in_weight, vec, normed_one, own_qkv, query_docs, key_feats = (
        forward_attention(fsdp_count, tokens[0], w_qkv, vec, segment_ids, mask, w_out, w_down, w_in)
    )
    result, grad_att, grad_hidden, small, grad_out, grad_in, down_part = middle(
        fsdp_count, att_rows, tokens[0], cotangent[0], vec, out_weight, in_weight, down_weight
    )
    grad_tokens, small, total_qkv, total_out, total_in, total_down = backward_attention(
        fsdp_count,
        grad_att,
        (by_heads, mask, query_docs, key_feats, lse, normed_one, own_qkv, vec),
        tokens[0],
        grad_hidden,
        small,
        (grad_out, grad_in),
        down_part,
    )
    arrays, parts = write_results(
        share, held, (total_in, total_down, total_qkv, total_out, result, grad_tokens), small
    )
    return (
        arrays[4][None],
        arrays[5][None],
        parts[0],
        parts[1],
        arrays[2],
        arrays[3],
        parts[2],
        parts[3],
        arrays[0],
        parts[5],
        arrays[1],
        parts[4],
    )


def solution(mesh):
    return jax.shard_map(
        functools.partial(per_device, mesh.shape["fsdp"]),
        mesh=mesh,
        in_specs=(
            P("fsdp", "seq", None),
            P("fsdp", "seq"),
            P("seq", None, None),
            P("fsdp"),
            P("fsdp"),
            P("fsdp", None),
            P("fsdp", None),
            P("fsdp"),
            P("fsdp"),
            P("fsdp", None),
            P("fsdp"),
            P("fsdp", None),
            P("fsdp"),
            P("fsdp", "seq", None),
        ),
        out_specs=(
            P("fsdp", "seq", None),
            P("fsdp", "seq", None),
            P("fsdp"),
            P("fsdp"),
            P("fsdp", None),
            P("fsdp", None),
            P("fsdp"),
            P("fsdp"),
            P("fsdp", None),
            P("fsdp"),
            P("fsdp", None),
            P("fsdp"),
        ),
        check_vma=False,
    )
```

```python
import functools
import math

import jax
import jax.numpy as jnp
from jax import lax
from jax.experimental import pallas as pl
from jax.experimental.pallas import tpu as pltpu
from jax.sharding import PartitionSpec as P

DH = 64
BLK = 64
LANES = 128
NEG = -1e30
F32 = jnp.float32
BF16 = jnp.bfloat16


def dot_nn(a, b):
    return jnp.dot(a, b, preferred_element_type=F32)


def dot_nt(a, b):
    return lax.dot_general(a, b, (((1,), (1,)), ((), ())), preferred_element_type=F32)


def dot_tn(a, b):
    return lax.dot_general(a, b, (((0,), (0,)), ((), ())), preferred_element_type=F32)


DOCS = 6


def write_block_mask(picks_ref, mask_ref):
    heads, inner, count = picks_ref.shape
    last = inner + 1
    shape = (inner, LANES)
    lane = lax.rem(lax.broadcasted_iota(jnp.int32, shape, 1), DH)
    block = lax.broadcasted_iota(jnp.int32, shape, 0) + 1
    fixed = (jnp.abs(lane - block) <= 1) | (lane == 0) | (lane >= last)
    for head in range(heads):
        picks = picks_ref[head]
        used = fixed
        for slot in range(count):
            used = used | (picks[:, slot : slot + 1] == lane)
        mask_ref[head, 0:1, :] = jnp.zeros((1, LANES), F32)
        mask_ref[head, 1:last, :] = jnp.where(used, 0.0, NEG)
        mask_ref[head, last : last + 1, :] = jnp.zeros((1, LANES), F32)


def token_features(start, docs, blocks):
    shape = (docs.shape[0], LANES)
    lane = lax.rem(lax.broadcasted_iota(jnp.int32, shape, 1), DH)
    block = lax.div(lax.broadcasted_iota(jnp.int32, shape, 0) + start, BLK)
    own = docs + blocks == lane
    other = jnp.where(own | (lane >= blocks + DOCS), 0.0, 1.0)
    key_part = jnp.where(lane < blocks, jnp.where(block == lane, 1.0, 0.0), other)
    return jnp.where(own, NEG, 0.0).astype(BF16), key_part.astype(BF16)


def query_tile(q_tile, doc_tile, mask_ref, head, first_block, lanes):
    scale = jnp.asarray(1.0 / math.sqrt(DH), BF16)
    count = q_tile.shape[0] // BLK
    mask = jnp.concatenate(
        [jnp.broadcast_to(mask_ref[head, pl.ds(first_block + i, 1), :], (BLK, LANES)) for i in range(count)], axis=0
    )
    return jnp.where(lanes, q_tile * scale, doc_tile + mask.astype(BF16))


def own_lanes(odd, shape):
    return lax.div(lax.broadcasted_iota(jnp.int32, shape, 1), DH) == odd


MESH = pl.DeviceIdType.MESH


class Place:
    def __init__(self, fsdp_count):
        self.depth = fsdp_count // 2
        self.s = lax.axis_index("seq")
        self.f = lax.axis_index("fsdp")
        self.z = lax.div(self.f, 2)
        self.c = lax.rem(self.f, 2)
        self.s1 = self.s + 1 - 2 * lax.rem(self.s, 2)
        self.s2 = self.s + 2 - 4 * lax.div(self.s, 2)
        self.s3 = 3 - self.s
        self.beside = (self.s, self.f + 1 - 2 * self.c)

    def across(self, index):
        return ((self.s1, self.s2, self.s3)[index], self.f)

    def far(self, step):
        return lax.rem(self.z + step, self.depth)

    def back(self, step):
        return lax.rem(self.z + self.depth - step, self.depth)

    def along(self, z):
        return (self.s, 2 * z + self.c)

    def meet(self):
        barrier = pltpu.get_barrier_semaphore()
        peers = [self.beside] + [self.across(i) for i in range(3)]
        for peer in peers:
            pl.semaphore_signal(barrier, inc=1, device_id=peer, device_id_type=MESH)
        self.each(1, self.depth, lambda step: pl.semaphore_signal(
            barrier, inc=1, device_id=self.along(self.far(step)), device_id_type=MESH
        ))
        pl.semaphore_wait(barrier, len(peers) + self.depth - 1)

    def each(self, start, stop, body):
        if stop - start <= 8:
            for step in range(start, stop):
                body(step)
        else:
            lax.fori_loop(start, stop, lambda step, carry: (body(step), carry)[1], 0)


def send(src, dst, sems, index, device):
    sent, got = sems
    return pltpu.make_async_remote_copy(
        src_ref=src,
        dst_ref=dst,
        send_sem=sent.at[index],
        recv_sem=got.at[index],
        device_id=device,
        device_id_type=MESH,
    )


def aligned(start, size):
    return pl.ds(pl.multiple_of(start, size), size)


class Gather:
    def __init__(self, place, src, dst, split, sems):
        self.place, self.src, self.dst, self.split = place, src, dst, split
        self.rows, self.cols = src.shape
        self.local, self.zs, self.xs, self.rs, self.cs = sems

    def block(self, z, core, quarter=None, half=None):
        rows = aligned((2 * z + core) * self.rows, self.rows)
        if quarter is None:
            return self.dst.at[rows]
        wide = self.cols // 4
        if half is None:
            return self.dst.at[rows, aligned(quarter * wide, wide)]
        return self.dst.at[rows, aligned(quarter * wide + half * (wide // 2), wide // 2)]

    def source(self, step, side):
        return self.place.z - step if side == 0 else self.place.z + step

    def has(self, step, side):
        z = self.source(step, side)
        return z >= 0 if side == 0 else z < self.place.depth

    def sends(self, step, side):
        p = self.place
        onward = p.z + 1 < p.depth if side == 0 else p.z > 0
        return jnp.logical_and(self.has(step - 1, side), onward)

    def slot(self, step, side):
        return 2 * step + side

    def own_copy(self):
        return pltpu.make_async_copy(self.src, self.block(self.place.z, self.place.c), self.local)

    def own_core(self):
        p = self.place
        return send(self.src, self.block(p.z, p.c), self.cs, 0, p.beside)

    def own_arrival(self):
        p = self.place
        there = self.block(p.z, 1 - p.c)
        return send(there, there, self.cs, 0, p.beside)

    def core_copy(self, step, side):
        p = self.place
        there = self.block(self.source(step, side), p.c)
        return send(there, there, self.cs, self.slot(step, side), p.beside)

    def core_arrival(self, step, side):
        p = self.place
        there = self.block(self.source(step, side), 1 - p.c)
        return send(there, there, self.cs, self.slot(step, side), p.beside)

    def z_copy(self, step, side):
        p = self.place
        z = self.source(step - 1, side)
        there = self.block(z, p.c, p.s) if self.split else self.block(z, p.c)
        src = there
        if isinstance(step, int) and step == 1:
            wide = self.cols // 4
            src = self.src.at[:, aligned(p.s * wide, wide)] if self.split else self.src
        return send(src, there, self.zs, self.slot(step, side), p.along(p.z + 1 - 2 * side))

    def z_arrival(self, step, side):
        p = self.place
        z = self.source(step, side)
        there = self.block(z, p.c, p.s) if self.split else self.block(z, p.c)
        return send(there, there, self.zs, self.slot(step, side), p.along(p.z - 1 + 2 * side))

    def x_copy(self, step, side, way):
        p = self.place
        there = self.block(self.source(step, side), p.c, p.s)
        return send(there, there, self.xs[way], self.slot(step, side), p.across(way))

    def x_arrival(self, step, side, way):
        p = self.place
        there = self.block(self.source(step, side), p.c, (p.s1, p.s2)[way])
        return send(there, there, self.xs[way], self.slot(step, side), p.across(way))

    def relay_copy(self, step, side, way):
        p = self.place
        there = self.block(self.source(step, side), p.c, (p.s2, p.s1)[way], 1 - way)
        return send(there, there, self.rs[way], self.slot(step, side), p.across(way))

    def relay_arrival(self, step, side, way):
        p = self.place
        there = self.block(self.source(step, side), p.c, p.s3, 1 - way)
        return send(there, there, self.rs[way], self.slot(step, side), p.across(way))

    def both(self, step, body, test=None):
        for side in (0, 1):
            pl.when((test or self.has)(step, side))(functools.partial(body, step, side))

    def begin(self):
        self.both(1, lambda step, side: self.z_copy(step, side).start(), self.sends)
        self.own_copy().start()
        self.own_core().start()

    def swap(self, step):
        def body(step, side):
            self.z_arrival(step, side).wait_recv()
            pl.when(self.sends(step + 1, side))(lambda: self.z_copy(step + 1, side).start())
            if self.split:
                for way in (0, 1):
                    self.x_copy(step, side, way).start()
            else:
                self.core_copy(step, side).start()

        self.both(step, body)

    def relay(self, step):
        def body(step, side):
            for way in (0, 1):
                self.x_arrival(step, side, way).wait_recv()
            for way in (0, 1):
                self.relay_copy(step, side, way).start()

        if self.split:
            self.both(step, body)

    def share(self, step):
        def body(step, side):
            for way in (0, 1):
                self.relay_arrival(step, side, way).wait_recv()
            self.core_copy(step, side).start()

        if self.split:
            self.both(step, body)

    def finish(self):
        self.own_copy().wait()
        self.own_core().wait_send()
        self.own_arrival().wait_recv()

        def close(step, side):
            if self.split:
                for way in (0, 1):
                    self.x_copy(step, side, way).wait_send()
                    self.relay_copy(step, side, way).wait_send()
            self.core_copy(step, side).wait_send()
            self.core_arrival(step, side).wait_recv()

        self.place.each(1, self.place.depth, lambda step: self.both(step, close))
        self.place.each(
            1,
            self.place.depth,
            lambda step: self.both(step, lambda step, side: self.z_copy(step, side).wait_send(), self.sends),
        )

    @staticmethod
    def scratch(depth, split):
        held = 2 * depth if split else 1
        return [dma()] + [dma(2 * depth)] * 2 + [dma(held)] * 8 + [dma(2 * depth)] * 2

    @staticmethod
    def take(refs):
        pairs = [(refs[i], refs[i + 1]) for i in range(1, 13, 2)]
        return (refs[0], pairs[0], pairs[1:3], pairs[3:5], pairs[5])


GATHER_SEMS = 13


def gather_steps(place, gathers, late, count, unit):
    depth = place.depth

    def swap(step):
        for one in gathers:
            one.swap(step)

    def relay(step):
        for one in gathers:
            one.relay(step)

    def share(step):
        for one in gathers:
            one.share(step)

    def late_swap(step):
        for one in late:
            one.swap(step)

    for one in late:
        one.begin()
    if depth <= 8:
        rounds = []
        for step in range(2, depth + 2):
            now = []
            if step <= depth:
                now.append(functools.partial(late_swap, step - 2)) if step > 2 else None
                now.append(functools.partial(share, step - 3)) if step > 3 else None
                now.append(functools.partial(swap, step)) if step < depth else None
                now.append(functools.partial(relay, step - 1))
            rounds.append(now)
        rounds[-1] = [functools.partial(share, step) for step in range(max(1, depth - 2), depth)]
        rounds[-1].append(functools.partial(late_swap, depth - 1))
        in_turn(count, unit, rounds[:count])
        for now in rounds[count:]:
            for one in now:
                one()
    else:
        in_turn(count, unit, [])
        swap(2)
        relay(1)

        def body(step, carry):
            late_swap(step - 2)
            share(step - 2)
            swap(step)
            relay(step - 1)
            return carry

        lax.fori_loop(3, depth, body, 0)
        late_swap(depth - 2)
        share(depth - 2)
        relay(depth - 1)
        share(depth - 1)
        late_swap(depth - 1)


def dma(*shape):
    return pltpu.SemaphoreType.DMA(shape) if shape else pltpu.SemaphoreType.DMA


def qkv_columns(heads_ref, pair):
    third = heads_ref.shape[1] // 3
    return tuple(aligned(i * third + pair * LANES, LANES) for i in range(3))


def attend_unit(pair, odd, tile, heads_ref, mask_ref, qd_ref, kf_ref, keys_sc, values_t, out_ref, lse_ref):
    length = heads_ref.shape[0]
    cols = aligned(pair * LANES, LANES)
    q_cols, k_cols, v_cols = qkv_columns(heads_ref, pair)
    mine = own_lanes(odd, (length, LANES))
    keys_sc[...] = jnp.where(mine, heads_ref[:, k_cols], kf_ref[...])

    @pl.when(odd == 0)
    def _():
        values_t[...] = heads_ref[:, v_cols].T
        out_ref[:, cols] = jnp.zeros((length, LANES), BF16)

    def one_tile(index, carry):
        rows = aligned(index * tile, tile)
        lanes = own_lanes(odd, (tile, LANES))
        queries = query_tile(
            heads_ref[rows, q_cols], qd_ref[rows, :], mask_ref, 2 * pair + odd, index * (tile // BLK), lanes
        )
        scores = dot_nt(keys_sc[...], queries)
        top = jnp.max(scores, axis=0, keepdims=True)
        prob = jnp.exp(scores - top)
        total = jnp.sum(prob, axis=0, keepdims=True)
        mixed = dot_nn(values_t[...], prob.astype(BF16)) / total
        lse_ref[pair, pl.ds(odd, 1), rows] = top + jnp.log(total)
        out_ref[rows, cols] = jnp.where(lanes, mixed.T.astype(BF16), out_ref[rows, cols])
        return carry

    lax.fori_loop(0, length // tile, one_tile, 0, unroll=2)


def in_turn(count, unit, actions):
    def body(index, carry):
        unit(index)
        for which, todo in enumerate(actions):
            if todo:

                @pl.when(index == which)
                def _(todo=todo):
                    for one in todo:
                        one()

        return carry

    lax.fori_loop(0, count, body, 0)


def forward_kernel(
    fsdp_count,
    x_ref,
    wq_ref,
    vec_ref,
    ids_ref,
    picks_ref,
    out_w_ref,
    down_w_ref,
    in_w_ref,
    heads_all,
    lse_ref,
    att_all,
    out_w_all,
    down_w_all,
    in_w_all,
    vec_sum,
    n1_all,
    wq_all,
    qd_ref,
    kf_ref,
    mask_ref,
    x_sc,
    n1_sc,
    wq_own,
    wq_sc,
    vec_sc,
    seg_ref,
    seg_sc,
    heads_sc,
    att_sc,
    keys_sc,
    values_t,
    *sems,
):
    place = Place(fsdp_count)
    rows, width = x_ref.shape
    own_width = wq_sc.shape[1]
    seats = (place.s1, place.s2, place.s3)

    def taken(i):
        return Gather.take(sems[i * GATHER_SEMS : (i + 1) * GATHER_SEMS])

    x_own, seg_own, keep_sems, pick_sems, x_sent, x_got, r_sent, r_got, g_sent, g_got, a_sent, a_got, a_own = sems[6 * GATHER_SEMS :]
    lone = pl.ds(0, in_w_ref.shape[1] // 2)
    shared = pl.ds(in_w_ref.shape[1] // 2, in_w_ref.shape[1] // 2)
    gathers = [
        Gather(place, src, dst, split, taken(i))
        for i, (src, dst, split) in enumerate(
            (
                (out_w_ref, out_w_all, True),
                (in_w_ref.at[:, shared], in_w_all.at[:, shared], True),
                (down_w_ref, down_w_all, True),
                (in_w_ref.at[:, lone], in_w_all.at[:, lone], False),
            )
        )
    ]
    late = [gathers.pop()]
    third = own_width // 3
    picks = [
        pltpu.make_async_copy(
            wq_ref.at[:, aligned((4 * i + place.s) * third, third)], wq_own.at[:, pl.ds(i * third, third)], pick_sems.at[i]
        )
        for i in range(3)
    ]
    for pick in picks:
        pick.start()
    write_block_mask(picks_ref, mask_ref)
    seg_ref[...] = jnp.zeros_like(seg_ref)
    for part in range(ids_ref.shape[1] // LANES):
        seg_ref[part : part + 1, :] = ids_ref[:, part * LANES : (part + 1) * LANES]
    weight = Gather(place, wq_own, wq_sc, False, taken(4))
    vector = Gather(place, vec_ref, vec_sc, False, taken(5))
    half = rows // 2

    def x_rows(seat):
        return x_sc.at[aligned(seat * rows, rows)]

    def x_half(seat, part):
        return x_sc.at[aligned(seat * rows + part * half, half)]

    def x_copy(way):
        return send(x_ref, x_rows(place.s), (x_sent, x_got), way, place.across(way))

    def x_arrival(way):
        there = x_rows(seats[way])
        return send(there, there, (x_sent, x_got), way, place.across(way))

    def x_relay(way):
        there = x_half((place.s2, place.s1)[way], 1 - way)
        return send(there, there, (r_sent, r_got), way, place.across(way))

    def x_relayed(way):
        there = x_half(place.s3, 1 - way)
        return send(there, there, (r_sent, r_got), way, place.across(way))

    def seg_copy(way):
        return send(seg_ref, seg_sc.at[place.s], (g_sent, g_got), way, place.across(way))

    def seg_arrival(way):
        there = seg_sc.at[seats[way]]
        return send(there, there, (g_sent, g_got), way, place.across(way))

    place.meet()
    vector.begin()
    for pick in picks:
        pick.wait()
    weight.begin()
    for way in range(2):
        x_copy(way).start()
    for way in range(3):
        seg_copy(way).start()
    own_x = pltpu.make_async_copy(x_ref, x_rows(place.s), x_own)
    own_x.start()
    own_seg = pltpu.make_async_copy(seg_ref, seg_sc.at[place.s], seg_own)
    own_seg.start()
    def start_rest():
        for one in gathers:
            one.begin()

    if place.depth <= 8:
        for step in range(1, place.depth):
            vector.swap(step)
            weight.swap(step)
            if step == max(1, place.depth - 2):
                start_rest()
    else:
        place.each(1, place.depth, vector.swap)
        place.each(1, place.depth, weight.swap)
        start_rest()
    vector.finish()
    vec_rows = vec_ref.shape[0]
    total = vec_sc[pl.ds(0, vec_rows), :].astype(F32)
    if fsdp_count <= 8:
        for f in range(1, fsdp_count):
            total = total + vec_sc[pl.ds(f * vec_rows, vec_rows), :].astype(F32)
    else:
        total = lax.fori_loop(
            1, fsdp_count, lambda f, sofar: sofar + vec_sc[aligned(f * vec_rows, vec_rows), :].astype(F32), total
        )
    vec_sum[...] = total

    def normalise(seat):
        def body(part):
            token_rows = x_sc[aligned(seat * rows + part * 32, 32), :].astype(F32)
            center = token_rows - jnp.mean(token_rows, axis=-1, keepdims=True)
            variance = jnp.mean(center * center, axis=-1, keepdims=True)
            normed = center * lax.rsqrt(variance + 1e-05) * vec_sum[0:1, :] + vec_sum[1:2, :]
            n1_sc[aligned(seat * rows + part * 32, 32), :] = normed.astype(BF16)

        lax.fori_loop(0, rows // 32, lambda part, carry: (body(part), carry)[1], 0)

    def project(seat):
        here = aligned(seat * rows, rows)

        def body(part):
            cols = aligned(part * 256, 256)
            heads_sc[here, cols] = dot_nn(n1_sc[here, :], wq_sc[:, cols]).astype(BF16)

        lax.fori_loop(0, own_width // 256, lambda part, carry: (body(part), carry)[1], 0)

    own_x.wait()
    normalise(place.s)
    for way in range(2):
        x_arrival(way).wait_recv()
    for way in range(2):
        x_relay(way).start()
    for way in range(2):
        normalise(seats[way])
    weight.finish()
    project(place.s)
    for way in range(2):
        project(seats[way])
    for one in gathers:
        one.swap(1)
    for way in range(2):
        x_relayed(way).wait_recv()
    normalise(place.s3)
    project(place.s3)
    own_seg.wait()
    for way in range(3):
        seg_arrival(way).wait_recv()
    blocks = mask_ref.shape[1]
    for seat in range(4):
        columns = seg_sc[seat].T
        for part in range(rows // LANES):
            here = pl.ds(seat * rows + part * LANES, LANES)
            qd_ref[here, :], kf_ref[here, :] = token_features(
                seat * rows + part * LANES, columns[:, part : part + 1], blocks
            )
    keeps = [
        pltpu.make_async_copy(src, dst, keep_sems.at[i])
        for i, (src, dst) in enumerate(((heads_sc, heads_all), (n1_sc, n1_all), (wq_sc, wq_all)))
    ]
    for keep in keeps:
        keep.start()

    pairs = att_sc.shape[1] // LANES

    def att_copy(pair, way):
        cols = aligned((place.s * pairs + pair) * LANES, LANES)
        return send(
            att_sc.at[aligned(seats[way] * rows, rows), aligned(pair * LANES, LANES)],
            att_all.at[:, cols],
            (a_sent, a_got),
            pair * 3 + way,
            place.across(way),
        )

    def att_own(pair):
        cols = aligned((place.s * pairs + pair) * LANES, LANES)
        return pltpu.make_async_copy(
            att_sc.at[aligned(place.s * rows, rows), aligned(pair * LANES, LANES)],
            att_all.at[:, cols],
            a_own.at[pair],
        )

    def att_arrival(pair, way):
        there = att_all.at[:, aligned((seats[way] * pairs + pair) * LANES, LANES)]
        return send(there, there, (a_sent, a_got), pair * 3 + way, place.across(way))

    def unit(index):
        pair, odd = lax.div(index, 2), lax.rem(index, 2)
        attend_unit(pair, odd, 256, heads_sc, mask_ref, qd_ref, kf_ref, keys_sc, values_t, att_sc, lse_ref)

        @pl.when(odd == 1)
        def _():
            for way in range(3):
                att_copy(pair, way).start()
            att_own(pair).start()

    gather_steps(place, gathers, late, 2 * pairs, unit)
    for keep in keeps:
        keep.wait()
    for way in range(3):
        seg_copy(way).wait_send()
        if way < 2:
            x_copy(way).wait_send()
            x_relay(way).wait_send()
        for pair in range(pairs):
            att_copy(pair, way).wait_send()
            att_arrival(pair, way).wait_recv()
    for pair in range(pairs):
        att_own(pair).wait()
    for one in gathers + late:
        one.finish()


def forward_attention(fsdp_count, x, w_qkv, vec, seg, picks, w_out, w_down, w_in):
    rows, width = x.shape
    length = 4 * rows
    heads = picks.shape[0]
    pairs = heads // 2
    depth = fsdp_count // 2
    own_width = w_qkv.shape[1] // 4
    full = fsdp_count * w_qkv.shape[0]
    seg_rows = -(-seg.shape[1] // (8 * LANES)) * 8
    anywhere = pl.BlockSpec(memory_space=pltpu.HBM)
    vmem = pl.BlockSpec(memory_space=pltpu.VMEM)
    shape = jax.ShapeDtypeStruct

    def whole(shard):
        return shape((fsdp_count * shard.shape[0], shard.shape[1]), shard.dtype)

    return pl.pallas_call(
        functools.partial(forward_kernel, fsdp_count),
        out_shape=(
            shape((length, own_width), BF16),
            shape((pairs, 2, length), F32),
            shape((rows, heads * DH * 4), BF16),
            whole(w_out),
            whole(w_down),
            whole(w_in),
            shape(vec.shape, F32),
            shape((length, width), BF16),
            shape((full, own_width), BF16),
            shape((length, LANES), BF16),
            shape((length, LANES), BF16),
            shape((heads, picks.shape[1] + 2, LANES), F32),
        ),
        in_specs=[anywhere] * 3 + [vmem] * 2 + [anywhere] * 3,
        out_specs=(anywhere, vmem, anywhere, anywhere, anywhere, anywhere, vmem, anywhere, anywhere, vmem, vmem, vmem),
        scratch_shapes=[
            pltpu.VMEM((length, width), BF16),
            pltpu.VMEM((length, width), BF16),
            pltpu.VMEM((w_qkv.shape[0], own_width), BF16),
            pltpu.VMEM((full, own_width), BF16),
            pltpu.VMEM((fsdp_count * vec.shape[0], vec.shape[1]), BF16),
            pltpu.VMEM((seg_rows, LANES), jnp.int32),
            pltpu.VMEM((4, seg_rows, LANES), jnp.int32),
            pltpu.VMEM((length, own_width), BF16),
            pltpu.VMEM((length, heads * DH), BF16),
            pltpu.VMEM((length, LANES), BF16),
            pltpu.VMEM((LANES, length), BF16),
        ]
        + Gather.scratch(depth, True) * 3
        + Gather.scratch(depth, False) * 3
        + [dma(), dma(), dma(3), dma(3), dma(2), dma(2), dma(2), dma(2), dma(3), dma(3)]
        + [dma(3 * pairs), dma(3 * pairs), dma(pairs)],
        compiler_params=pltpu.CompilerParams(
            collective_id=2, has_side_effects=True, vmem_limit_bytes=60 << 20
        ),
    )(x, w_qkv, vec, seg, picks, w_out, w_down, w_in)


def by_rows(count, cols, body):
    chunk = 16
    while count % (2 * chunk) == 0 and 2 * chunk * cols <= 16384:
        chunk *= 2
    lax.fori_loop(0, count // chunk, lambda i, carry: (body(aligned(i * chunk, chunk)), carry)[1], 0)


class Reduce:
    def __init__(self, place, grad, out, quartered, bufs, sems, direct=False, thirds=False, late=False, far_first=False):
        self.far_first = far_first
        self.place, self.grad, self.out, self.quartered, self.direct = place, grad, out, quartered, direct
        self.thirds, self.late = thirds, late
        self.rows, self.cols = out.shape
        self.wide = self.cols // 4
        self.acc, self.own, self.relay_in, self.quarter_in, self.z_in, self.total = bufs
        self.own_sem, self.put_sem, self.cs, self.rs, self.qs, self.zs, self.fs, self.gs = sems

    @staticmethod
    def scratch(depth, rows, cols, quartered, direct=False, far_first=False):
        held = cols // 4 if quartered else cols
        near = 1 if far_first else depth
        side = (1, 1, 16, LANES) if quartered else None
        return [
            pltpu.VMEM((depth, rows, held), BF16),
            pltpu.VMEM((16, LANES) if direct else (rows, held), BF16),
            pltpu.VMEM(side or (2, near, rows, cols // 8), BF16),
            pltpu.VMEM(side or (2, near, rows, cols // 4), BF16),
            pltpu.VMEM((depth, rows, cols if far_first else cols // 4), BF16),
            pltpu.VMEM((rows, cols // 4), BF16),
            dma(),
            dma(3),
        ] + [dma(depth)] * 12 + [dma(6)] * 4

    @staticmethod
    def take(place, grad, out, quartered, refs, direct=False, thirds=False, far_first=False):
        s = refs[8:]
        pairs = [(s[i], s[i + 1]) for i in range(0, 16, 2)]
        sems = (refs[6], refs[7], pairs[0], pairs[1:3], pairs[3:5], pairs[5], pairs[6], pairs[7])
        return Reduce(place, grad, out, quartered, refs[:6], sems, direct, thirds, False, far_first)

    def quarter(self, seat):
        return aligned(seat * self.wide, self.wide)

    def mine(self):
        if self.far_first:
            return pl.ds(0, self.cols)
        return pl.ds(0, self.wide) if self.quartered else self.quarter(self.place.s)

    def piece(self, seat, half):
        return aligned(seat * self.wide + half * (self.wide // 2), self.wide // 2)

    def own_copy(self, step):
        p = self.place
        rows = aligned((2 * p.far(step) + p.c) * self.rows, self.rows)
        return pltpu.make_async_copy(self.grad.at[rows], self.own, self.own_sem)

    def core_copy(self, step):
        p = self.place
        rows = aligned((2 * p.far(step) + 1 - p.c) * self.rows, self.rows)
        return send(self.grad.at[rows], self.acc.at[step], self.cs, step, p.beside)

    def relay_copy(self, step, way):
        p = self.place
        src = self.acc.at[step, :, self.piece(p.s3, way)]
        return send(src, self.relay_in.at[way, step], self.rs[way], step, p.across(way))

    def quarter_copy(self, step, way):
        p = self.place
        src = self.acc.at[step, :, self.quarter((p.s1, p.s2)[way])]
        return send(src, self.quarter_in.at[way, step], self.qs[way], step, p.across(way))

    def z_copy(self, step):
        p = self.place
        src = self.acc.at[step, :, self.mine()]
        return send(src, self.z_in.at[step], self.zs, step, p.along(p.far(step)))

    def columns(self, seat, part):
        if not self.thirds:
            return self.quarter(seat), pl.ds(0, self.wide)
        third = self.wide // 3
        return aligned((4 * part + seat) * third, third), pl.ds(part * third, third)

    @property
    def parts(self):
        return 3 if self.thirds else 1

    def put_copy(self, part):
        there, here = self.columns(self.place.s, part)
        return pltpu.make_async_copy(self.total.at[:, here], self.out.at[:, there], self.put_sem.at[part])

    def total_copy(self, way, part):
        p = self.place
        there, here = self.columns(p.s, part)
        return send(self.total.at[:, here], self.out.at[:, there], self.fs, 3 * way + part, p.across(way))

    def total_arrival(self, way, part):
        p = self.place
        there = self.out.at[:, self.columns((p.s1, p.s2, p.s3)[way], part)[0]]
        return send(there, there, self.fs, 3 * way + part, p.across(way))

    def totals(self):
        return [(way, part) for way in range(2) for part in range(self.parts)]

    def split_piece(self, seat, part, half):
        if not self.thirds:
            return self.piece(seat, half)
        width = self.wide // 6
        return aligned(((4 * part + seat) * 2 + half) * width, width)

    def back_copy(self, way, part):
        p = self.place
        there = self.out.at[:, self.split_piece((p.s2, p.s1)[way], part, 1 - way)]
        return send(there, there, self.gs, 3 * way + part, p.across(way))

    def back_arrival(self, way, part):
        p = self.place
        there = self.out.at[:, self.split_piece(p.s3, part, 1 - way)]
        return send(there, there, self.gs, 3 * way + part, p.across(way))

    def begin(self):
        depth = self.place.depth
        self.place.each(1, depth, lambda step: self.core_copy(step).start())
        self.core_copy(0).start()
        self.own_copy(1).start()

    def fold(self, step, following):
        p, acc, own = self.place, self.acc, self.own
        self.core_copy(step).wait_recv()
        if not self.direct:
            self.own_copy(step).wait()
        base = (2 * p.far(step) + p.c) * self.rows

        def body(index, carry):
            rows = aligned(index * 16, 16)
            added = self.grad[aligned(base + index * 16, 16), :] if self.direct else own[rows, :]
            acc[step, rows, :] = acc[step, rows, :] + added
            return carry

        lax.fori_loop(0, self.rows // 16, body, 0)
        if following is not None:
            self.own_copy(following).start()
        if not (self.quartered or self.far_first):
            for way in (0, 1):
                self.relay_copy(step, way).start()
        elif not (isinstance(step, int) and step == 0):
            self.z_copy(step).start()

    def swap(self, step):
        if self.quartered:
            return
        p, acc = self.place, self.acc
        for way in (0, 1):
            self.relay_copy(step, way).wait_recv()
            cols = self.piece((p.s2, p.s1)[way], way)
            came = self.relay_in.at[way, step]

            def body(rows):
                acc[step, rows, cols] = acc[step, rows, cols] + came[rows, :]

            by_rows(self.rows, self.wide // 2, body)
        for way in (0, 1):
            self.quarter_copy(step, way).start()

    def close(self, step, own):
        if self.quartered:
            return
        p, acc, came = self.place, self.acc, self.quarter_in
        for way in (0, 1):
            self.quarter_copy(step, way).wait_recv()
        cols = self.quarter(p.s)

        def body(rows):
            acc[step, rows, cols] = (
                acc[step, rows, cols].astype(F32)
                + came[0, step, rows, :].astype(F32)
                + came[1, step, rows, :].astype(F32)
            ).astype(BF16)

        by_rows(self.rows, self.wide, body)
        if not self.far_first:
            pl.when(jnp.logical_not(own))(lambda: self.z_copy(step).start())

    def far_sum(self):
        p, acc, came = self.place, self.acc, self.z_in
        p.each(1, p.depth, lambda step: self.z_copy(step).wait_recv())

        def body(rows):
            start = acc[0, rows, :].astype(F32)
            if p.depth <= 8:
                for step in range(1, p.depth):
                    start = start + came[step, rows, :].astype(F32)
            else:
                start = lax.fori_loop(1, p.depth, lambda step, sofar: sofar + came[step, rows, :].astype(F32), start)
            acc[0, rows, :] = start.astype(BF16)

        by_rows(self.rows, self.cols, body)
        for way in (0, 1):
            self.relay_copy(0, way).start()

    def near_sum(self):
        self.close(0, True)
        total, acc, cols = self.total, self.acc, self.quarter(self.place.s)

        def body(rows):
            total[rows, :] = acc[0, rows, cols]

        by_rows(self.rows, self.wide, body)
        self.give()

    def collect(self):
        p, acc, came, total = self.place, self.acc, self.z_in, self.total
        p.each(1, p.depth, lambda step: self.z_copy(step).wait_recv())
        cols = self.mine()

        def body(rows):
            start = acc[0, rows, cols].astype(F32)
            if p.depth <= 8:
                for step in range(1, p.depth):
                    start = start + came[step, rows, :].astype(F32)
            else:
                start = lax.fori_loop(1, p.depth, lambda step, sofar: sofar + came[step, rows, :].astype(F32), start)
            total[rows, :] = start.astype(BF16)

        by_rows(self.rows, self.wide, body)
        if not self.direct:
            self.give()

    def give(self):
        for way, part in self.totals():
            self.total_copy(way, part).start()
        for part in range(self.parts):
            self.put_copy(part).start()

    def spread(self):
        for way, part in self.totals():
            self.total_arrival(way, part).wait_recv()
        for way, part in self.totals():
            self.back_copy(way, part).start()

    def sent(self):
        def done(step):
            self.core_copy(step).wait_send()
            if not (self.quartered or self.far_first):
                for way in (0, 1):
                    self.relay_copy(step, way).wait_send()
                    self.quarter_copy(step, way).wait_send()

        self.place.each(0, self.place.depth, done)
        if self.far_first:
            for way in (0, 1):
                self.relay_copy(0, way).wait_send()
                self.quarter_copy(0, way).wait_send()

    def finish(self):
        for part in range(self.parts):
            self.put_copy(part).wait()
        if not self.late:
            self.sent()
            self.place.each(1, self.place.depth, lambda step: self.z_copy(step).wait_send())
        for way, part in self.totals():
            self.total_copy(way, part).wait_send()
        for way, part in self.totals():
            self.back_arrival(way, part).wait_recv()
            self.back_copy(way, part).wait_send()


REDUCE_REFS = 24


def backward_unit(
    pair, odd, half, tile, heads_ref, mask_ref, qd_ref, kf_ref, go_ref, lse_ref, out_ref, keys_sc, values_sc, keys_t, p_sc, s_sc, k_acc, v_acc
):
    length = heads_ref.shape[0]
    span = p_sc.shape[1]
    scale = jnp.asarray(1.0 / math.sqrt(DH), BF16)
    q_cols, k_cols, v_cols = qkv_columns(heads_ref, pair)
    cols = aligned(pair * LANES, LANES)
    mine = own_lanes(odd, (length, LANES))

    @pl.when(half == 0)
    def _():
        keys_sc[...] = jnp.where(mine, heads_ref[:, k_cols], kf_ref[...])
        values_sc[...] = jnp.where(mine, heads_ref[:, v_cols], jnp.zeros((), BF16))
        keys_t[...] = heads_ref[:, k_cols].T
        k_acc[...] = jnp.zeros_like(k_acc)
        v_acc[...] = jnp.zeros_like(v_acc)

    def one_tile(index, carry):
        here = aligned(index * tile, tile)
        rows = aligned(half * span + index * tile, tile)
        lanes = own_lanes(odd, (tile, LANES))
        queries = query_tile(
            heads_ref[rows, q_cols],
            qd_ref[rows, :],
            mask_ref,
            2 * pair + odd,
            half * (span // BLK) + index * (tile // BLK),
            lanes,
        )
        prob = jnp.exp(dot_nt(keys_sc[...], queries) - lse_ref[pair, pl.ds(odd, 1), rows])
        grad_prob = dot_nt(values_sc[...], go_ref[rows, cols])
        delta = jnp.sum(prob * grad_prob, axis=0, keepdims=True)
        p_sc[:, here] = prob.astype(BF16)
        s_sc[:, here] = (prob * (grad_prob - delta)).astype(BF16)
        return carry

    lax.fori_loop(0, span // tile, one_tile, 0, unroll=True)
    part = aligned(half * span, span)
    v_acc[...] += dot_nn(p_sc[...], go_ref[part, cols])
    k_acc[...] += dot_nn(s_sc[...], heads_ref[part, q_cols] * scale)
    grad_q = (dot_nn(keys_t[...], s_sc[...]) * (1.0 / math.sqrt(DH))).T.astype(BF16)
    out_ref[part, q_cols] = jnp.where(own_lanes(odd, (span, LANES)), grad_q, out_ref[part, q_cols])

    @pl.when(half == 1)
    def _():
        out_ref[:, k_cols] = jnp.where(mine, k_acc[...].astype(BF16), out_ref[:, k_cols])
        out_ref[:, v_cols] = jnp.where(mine, v_acc[...].astype(BF16), out_ref[:, v_cols])


def backward_kernel(
    fsdp_count,
    go_hbm,
    heads_hbm,
    mask_ref,
    qd_hbm,
    kf_hbm,
    lse_ref,
    n1_ref,
    wq_hbm,
    x_hbm,
    hid_hbm,
    vec_ref,
    small_ref,
    out_g_ref,
    in_g_ref,
    down_part,
    tokens_out,
    small_out,
    qkv_total,
    out_total,
    in_total,
    down_total,
    go_sc,
    heads_ref,
    qd_ref,
    kf_ref,
    wq_ref,
    x_ref,
    hid_ref,
    load_sems,
    grads_sc,
    keys_sc,
    values_sc,
    keys_t,
    p_sc,
    s_sc,
    k_acc,
    v_acc,
    n1_sc,
    qkv_g,
    part_sc,
    part_in,
    half_in,
    small_sc,
    small_in,
    *rest,
):
    place = Place(fsdp_count)
    rows = x_ref.shape[0]
    cut_at = in_g_ref.shape[1] * 3 // 4
    shared = pl.ds(0, cut_at)
    apart = pl.ds(cut_at, in_g_ref.shape[1] - cut_at)
    reduces = [
        Reduce.take(place, grad, out, False, rest[i * REDUCE_REFS : (i + 1) * REDUCE_REFS])
        for i, (grad, out) in enumerate(
            ((out_g_ref, out_total), (in_g_ref.at[:, shared], in_total.at[:, shared]))
        )
    ]
    lone = Reduce.take(
        place,
        in_g_ref.at[:, apart],
        in_total.at[:, apart],
        False,
        rest[3 * REDUCE_REFS : 4 * REDUCE_REFS],
        far_first=True,
    )
    first = Reduce.take(place, qkv_g, qkv_total, True, rest[2 * REDUCE_REFS : 3 * REDUCE_REFS], thirds=True)
    put_sem, f_pair, g_pair = (
        rest[4 * REDUCE_REFS],
        rest[4 * REDUCE_REFS + 1 : 4 * REDUCE_REFS + 3],
        rest[4 * REDUCE_REFS + 3 : 4 * REDUCE_REFS + 5],
    )
    down = Reduce(
        place,
        None,
        down_total,
        True,
        (None, None, None, None, None, down_part),
        (None, put_sem, None, None, None, None, f_pair, g_pair),
        late=True,
    )
    n_own, h_sent, h_got, p_sent, p_got, c_sent, c_got, z_sent, z_got, x_sent, x_got = rest[
        4 * REDUCE_REFS + 5 :
    ]
    seats = (place.s1, place.s2, place.s3)
    width = go_sc.shape[1]
    pairs = width // LANES
    half = rows // 2

    loads = [
        pltpu.make_async_copy(src, dst, load_sems.at[i])
        for i, (src, dst) in enumerate(
            (
                (heads_hbm, heads_ref),
                (qd_hbm, qd_ref),
                (kf_hbm, kf_ref),
                (go_hbm, go_sc),
                (wq_hbm, wq_ref),
                (x_hbm, x_ref),
                (hid_hbm, hid_ref),
            )
        )
    ]
    for load in loads:
        load.start()
    later_loads = loads[4:]
    place.meet()
    def first_copies(step):
        for one in reduces + [lone]:
            one.core_copy(step).start()

    place.each(1, place.depth, first_copies)
    first_copies(0)
    for one in reduces + [lone]:
        one.own_copy(1).start()
    down.give()
    n1_copy = pltpu.make_async_copy(n1_ref, n1_sc, n_own)
    n1_copy.start()

    def unit(index):
        backward_unit(
            lax.div(index, 4), lax.rem(lax.div(index, 2), 2), lax.rem(index, 2), 256, heads_ref, mask_ref, qd_ref, kf_ref,
            go_sc, lse_ref, grads_sc, keys_sc, values_sc, keys_t, p_sc, s_sc, k_acc, v_acc,
        )

    def half_copy(way):
        src = part_sc.at[aligned(place.s3 * rows + way * half, half)]
        return send(src, half_in.at[way], (h_sent, h_got), way, place.across(way))

    def part_copy(way, late):
        side = 1 - way if late else way
        src = part_sc.at[aligned(seats[way] * rows + side * half, half)]
        dst = part_in.at[way, pl.ds(side * half, half)]
        return send(src, dst, (p_sent, p_got), 2 * way + late, place.across(way))

    def partial_dn1():
        later_loads[0].wait()
        for seat in (place.s3, place.s1, place.s2, place.s):
            here = aligned(seat * rows, rows)
            part_sc[here, :] = dot_nt(grads_sc[here, :], wq_ref[...]).astype(BF16)
            for way in (0, 1):
                if seat is place.s3:
                    half_copy(way).start()
                elif seat is seats[way]:
                    part_copy(way, 0).start()

    def weight_grad():
        n1_copy.wait()

        def body(index):
            cols = aligned(index * 256, 256)
            qkv_g[cols, :] = dot_tn(n1_sc[:, cols], grads_sc[...]).astype(BF16)

        lax.fori_loop(0, qkv_g.shape[0] // 256, lambda index, carry: (body(index), carry)[1], 0)
        first.begin()

    def swap_dn1():
        for way in (0, 1):
            half_copy(way).wait_recv()
            base = (place.s2, place.s1)[way] * rows + way * half

            def body(index):
                here = aligned(base + index * 32, 32)
                came = half_in[way, aligned(index * 32, 32), :]
                part_sc[here, :] = (part_sc[here, :].astype(F32) + came.astype(F32)).astype(BF16)

            lax.fori_loop(0, half // 32, lambda index, carry: (body(index), carry)[1], 0)
        for way in (0, 1):
            part_copy(way, 1).start()

    def fold_first():
        depth = place.depth
        place.each(1, depth, lambda step: first.fold(step, lax.rem(step + 1, depth)))
        first.fold(0, None)

    def core_small():
        return send(small_sc.at[0], small_sc.at[1], (c_sent, c_got), 0, place.beside)

    def z_small(step):
        return send(small_sc.at[2], small_in.at[step], (z_sent, z_got), step, place.along(place.far(step)))

    def x_small(way):
        return send(small_sc.at[3], small_sc.at[4 + way], (x_sent, x_got), way, place.across(way))

    def close_dn1():
        for way in (0, 1):
            for late in (0, 1):
                part_copy(way, late).wait_recv()
        for load in later_loads[1:]:
            load.wait()
        gain = vec_ref[0:1, :]

        def body(index, sums):
            here = aligned(index * 32, 32)
            mine = aligned(place.s * rows + index * 32, 32)
            dn1 = (
                part_sc[mine, :].astype(F32)
                + part_in[0, here, :].astype(F32)
                + part_in[1, here, :].astype(F32)
            )
            token_rows = x_ref[here, :].astype(F32)
            center = token_rows - jnp.mean(token_rows, axis=-1, keepdims=True)
            inv = lax.rsqrt(jnp.mean(center * center, axis=-1, keepdims=True) + 1e-05)
            hat = center * inv
            scaled = dn1 * gain
            grad = hid_ref[here, :] + inv * (
                scaled
                - jnp.mean(scaled, axis=-1, keepdims=True)
                - hat * jnp.mean(scaled * hat, axis=-1, keepdims=True)
            )
            tokens_out[here, :] = grad.astype(BF16)
            return (
                sums[0] + jnp.sum(dn1 * hat, axis=0, keepdims=True),
                sums[1] + jnp.sum(dn1, axis=0, keepdims=True),
            )

        none = jnp.zeros((1, x_ref.shape[1]), F32)
        gain_sum, bias_sum = lax.fori_loop(0, rows // 32, body, (none, none))
        small_sc[0] = small_ref[...]
        small_sc[0, 0:1, :] = gain_sum
        small_sc[0, 1:2, :] = bias_sum
        core_small().start()

    def small_z():
        core_small().wait_recv()
        small_sc[2] = small_sc[0] + small_sc[1]
        place.each(1, place.depth, lambda step: z_small(step).start())

    def small_x():
        place.each(1, place.depth, lambda step: z_small(step).wait_recv())
        small_in[0] = small_sc[2]
        if place.depth <= 8:
            total = small_in[place.back(0)]
            for z in range(1, place.depth):
                total = total + small_in[place.back(z)]
        else:
            total = lax.fori_loop(
                1, place.depth, lambda z, sofar: sofar + small_in[place.back(z)], small_in[place.back(0)]
            )
        small_sc[3] = total
        for way in range(3):
            x_small(way).start()

    def small_end():
        for way in range(3):
            x_small(way).wait_recv()
        small_out[...] = (small_sc[3] + small_sc[4]) + (small_sc[5] + small_sc[6])

    depth = place.depth
    loose = depth > 8

    def run(count, body):
        lax.fori_loop(1, count, lambda step, carry: (body(step), carry)[1], 0)

    def fold(index):
        for one in reduces + [lone]:
            if not loose:
                step = (index + 1) % depth
                one.fold(step, (step + 1) % depth if step else None)
            elif index == 0:
                run(depth, lambda step: one.fold(step, lax.rem(step + 1, depth)))
                one.fold(0, None)

    def swap(index):
        for one in reduces:
            if not loose:
                one.swap((index + 1) % depth)
            elif index == 0:
                run(depth, one.swap)
                one.swap(0)

    def close(index):
        for one in reduces:
            if not loose:
                one.close((index + 1) % depth, (index + 1) % depth == 0)
            elif index == 0:
                run(depth, lambda step: one.close(step, False))
                one.close(0, True)

    rounds = 1 if loose else depth
    fold(0)
    if rounds > 1:
        fold(1)
    for load in loads[:4]:
        load.wait()
    steps = []
    for index in range(rounds + 2):
        if 2 <= index < rounds:
            steps.append(functools.partial(fold, index))
        if index < rounds:
            steps.append(functools.partial(swap, index))
        if 0 <= index - 1 < rounds:
            steps.append(functools.partial(close, index - 1))
    steps.insert(len(steps) // 2, down.spread)
    count = 4 * pairs
    grads_sc[...] = jnp.zeros_like(grads_sc)
    in_turn(count, unit, [steps[i * len(steps) // count : (i + 1) * len(steps) // count] for i in range(count)])
    partial_dn1()
    weight_grad()
    swap_dn1()
    fold_first()
    lone.far_sum()
    for one in reduces:
        one.collect()
    lone.swap(0)
    first.collect()
    close_dn1()
    lone.near_sum()
    small_z()
    for one in reduces + [lone]:
        one.spread()
    small_x()
    first.spread()
    small_end()
    core_small().wait_send()
    place.each(1, place.depth, lambda step: z_small(step).wait_send())
    for way in range(3):
        x_small(way).wait_send()
        if way < 2:
            half_copy(way).wait_send()
            for late in (0, 1):
                part_copy(way, late).wait_send()
    for one in [first, down, lone] + reduces:
        one.finish()


def backward_attention(fsdp_count, grad_heads, saved, x, hid, small, grads, down_part):
    heads, mask, qd, kf, lse, n1, wq, vec = saved
    rows, width = x.shape
    length, own_width = grad_heads.shape
    depth = fsdp_count // 2
    span = length // 2
    anywhere = pl.BlockSpec(memory_space=pltpu.HBM)
    vmem = pl.BlockSpec(memory_space=pltpu.VMEM)
    share = wq.shape[0] // fsdp_count
    kept = [(grad.shape[0] // fsdp_count, grad.shape[1]) for grad in grads]
    kept_qkv = (share, 4 * wq.shape[1])
    down_kept = (down_part.shape[0], 4 * down_part.shape[1])
    shape = jax.ShapeDtypeStruct

    reduce_scratch = []
    cut_at = kept[1][1] * 3 // 4
    for one in (kept[0], (kept[1][0], cut_at)):
        reduce_scratch += Reduce.scratch(depth, *one, False)
    reduce_scratch += Reduce.scratch(depth, *kept_qkv, True)
    reduce_scratch += Reduce.scratch(depth, kept[1][0], kept[1][1] - cut_at, False, far_first=True)
    return pl.pallas_call(
        functools.partial(backward_kernel, fsdp_count),
        out_shape=(shape(x.shape, BF16), shape(small.shape, F32), shape(kept_qkv, BF16))
        + tuple(shape(one, BF16) for one in kept)
        + (shape(down_kept, BF16),),
        in_specs=[anywhere] * 2 + [vmem] + [anywhere] * 2 + [vmem] + [anywhere] * 4 + [vmem] * 2 + [anywhere] * 2 + [vmem],
        out_specs=(vmem, vmem, anywhere, anywhere, anywhere, anywhere),
        scratch_shapes=[
            pltpu.VMEM((length, own_width), BF16),
            pltpu.VMEM(heads.shape, BF16),
            pltpu.VMEM(qd.shape, BF16),
            pltpu.VMEM(kf.shape, BF16),
            pltpu.VMEM(wq.shape, BF16),
            pltpu.VMEM(x.shape, BF16),
            pltpu.VMEM(hid.shape, F32),
            dma(7),
            pltpu.VMEM((length, 3 * own_width), BF16),
            pltpu.VMEM((length, LANES), BF16),
            pltpu.VMEM((length, LANES), BF16),
            pltpu.VMEM((LANES, length), BF16),
            pltpu.VMEM((length, span), BF16),
            pltpu.VMEM((length, span), BF16),
            pltpu.VMEM((length, LANES), F32),
            pltpu.VMEM((length, LANES), F32),
            pltpu.VMEM((length, width), BF16),
            pltpu.VMEM(wq.shape, BF16),
            pltpu.VMEM((length, width), BF16),
            pltpu.VMEM((2, rows, width), BF16),
            pltpu.VMEM((2, rows // 2, width), BF16),
            pltpu.VMEM((7,) + small.shape, F32),
            pltpu.VMEM((depth,) + small.shape, F32),
        ]
        + reduce_scratch
        + [dma(3), dma(6), dma(6), dma(6), dma(6)]
        + [dma(), dma(2), dma(2), dma(4), dma(4)]
        + [dma(1), dma(1), dma(depth), dma(depth), dma(3), dma(3)],
        compiler_params=pltpu.CompilerParams(
            collective_id=3, has_side_effects=True, vmem_limit_bytes=60 << 20
        ),
    )(grad_heads, heads, mask, qd, kf, lse, n1, wq, x, hid, vec, small, *grads, down_part)


def middle_kernel(
    fsdp_count,
    att_hbm,
    x_hbm,
    cot_hbm,
    vec_ref,
    out_w_hbm,
    in_w_ref,
    down_w_ref,
    result_hbm,
    go_all,
    hid_hbm,
    small_ref,
    out_g_hbm,
    in_g_ref,
    down_part,
    result_ref,
    hid_ref,
    out_g_ref,
    put_sems,
    att_ref,
    x_ref,
    cot_ref,
    out_w_ref,
    fetch_sems,
    datt_ref,
    go_sems,
    go_sent,
    go_got,
    hidden_sc,
    n2_sc,
    n2_t,
    out_acc,
    dn2_acc,
    in_buf,
    down_buf,
    grad_buf,
    act_sc,
    slope_sc,
    down_g,
    in_sems,
    down_sems,
    grad_sems,
    *rest,
):
    place = Place(fsdp_count)
    depth = place.depth
    down_like = rest[0]
    total = Reduce.take(place, down_g, down_like, False, rest[1:], True)
    rows, width = x_ref.shape
    span = down_buf.shape[1]
    hidden_units = down_g.shape[0]
    chunks = hidden_units // span
    paired = total.rows == span
    lines = rows // 32

    def order(index):
        if not paired:
            return index
        z = place.far(lax.rem(lax.div(index, 2) + 1, depth))
        return 2 * z + jnp.where(lax.rem(index, 2) == 0, 1 - place.c, place.c)

    def in_load(index):
        slot = lax.rem(index, 4)
        return pltpu.make_async_copy(
            in_w_ref.at[:, aligned(order(index) * span, span)], in_buf.at[slot], in_sems.at[slot]
        )

    def down_load(index):
        slot = lax.rem(index, 4)
        return pltpu.make_async_copy(
            down_w_ref.at[aligned(order(index) * span, span)], down_buf.at[slot], down_sems.at[slot]
        )

    def grad_store(index):
        slot = lax.rem(index, 2)
        return pltpu.make_async_copy(
            grad_buf.at[slot], in_g_ref.at[:, aligned(order(index) * span, span)], grad_sems.at[slot]
        )

    def over_rows(body, start=0):
        return lax.fori_loop(0, lines, lambda index, carry: body(aligned(index * 32, 32), carry), start)

    for index in (0, 1):
        in_load(index).start()
        down_load(index).start()
    loads = [
        pltpu.make_async_copy(src, dst, fetch_sems.at[i])
        for i, (src, dst) in enumerate(((att_hbm, att_ref), (out_w_hbm, out_w_ref), (x_hbm, x_ref), (cot_hbm, cot_ref)))
    ]
    for load in loads:
        load.start()
    place.meet()
    for load in loads:
        load.wait()
    hidden_sc[...] = x_ref[...].astype(F32) + dot_nn(att_ref[...], out_w_ref[...])

    def normalise(here, carry):
        token_rows = hidden_sc[here, :]
        center = token_rows - jnp.mean(token_rows, axis=-1, keepdims=True)
        variance = jnp.mean(center * center, axis=-1, keepdims=True)
        normed = center * lax.rsqrt(variance + 1e-05) * vec_ref[2:3, :] + vec_ref[3:4, :]
        n2_sc[here, :] = normed.astype(BF16)
        out_acc[here, :] = token_rows + vec_ref[4:5, :]
        return carry

    over_rows(normalise)
    n2_t[...] = n2_sc[...].T
    dn2_acc[...] = jnp.zeros_like(dn2_acc)
    small_ref[...] = jnp.zeros_like(small_ref)

    def place_of(which):
        per = width // span
        return pl.ds(5 + lax.div(which, per), 1), aligned(lax.rem(which, per) * span, span)

    def activate(index):
        slot, side = lax.rem(index, 4), lax.rem(index, 2)
        which = order(index)
        in_load(index).wait()
        down_load(index).wait()

        def ahead():
            in_load(index + 2).start()
            down_load(index + 2).start()

        pl.when(index + 2 < chunks)(ahead)
        line, cols = place_of(which)
        pre = dot_nn(n2_sc[...], in_buf[slot]) + vec_ref[line, cols]
        inner = jnp.tanh(0.7978845608028654 * (pre + 0.044715 * pre * pre * pre))
        act = (0.5 * pre * (1.0 + inner)).astype(BF16)
        act_sc[side] = act
        down_g[aligned(which * span, span), :] = dot_tn(act, cot_ref[...]).astype(BF16)
        slope_sc[side] = 0.5 * (1.0 + inner) + (0.5 * 0.7978845608028654) * pre * (1.0 - inner * inner) * (
            1.0 + (3.0 * 0.044715) * pre * pre
        )

    def chunk(index):
        slot, side = lax.rem(index, 4), lax.rem(index, 2)
        which = order(index)
        line, cols = place_of(which)
        grad = dot_nt(cot_ref[...], down_buf[slot]) * slope_sc[side]
        low = grad.astype(BF16)
        small_ref[line, cols] = jnp.sum(low.astype(F32), axis=0, keepdims=True)
        out_acc[...] += dot_nn(act_sc[side], down_buf[slot])
        dn2_acc[...] += dot_nt(low, in_buf[slot])
        pl.when(index >= 2)(lambda: grad_store(index - 2).wait())
        grad_buf[side] = dot_nn(n2_t[...], low).astype(BF16)
        grad_store(index).start()

    def swap_before(t):
        pl.when(t >= 1)(lambda: total.swap(lax.rem(t, depth)))

    def close_before(t):
        pl.when(t >= 2)(lambda: total.close(lax.rem(t + depth - 1, depth), False))

    if paired:

        def step(t, carry):
            dest = lax.rem(t + 1, depth)

            def early(side, carry):
                activate(2 * t + side)
                pl.when(side == 0)(lambda: total.core_copy(dest).start())
                return carry

            lax.fori_loop(0, 2, early, 0)
            swap_before(t)
            chunk(2 * t)
            total.fold(dest, None)
            chunk(2 * t + 1)
            close_before(t)
            return carry

        lax.fori_loop(0, depth, step, 0)
    else:
        lax.fori_loop(0, chunks, lambda index, carry: (activate(index), chunk(index), carry)[2], 0)
        place.each(0, depth, lambda step: total.core_copy(step).start())

        def step(t, carry):
            swap_before(t)
            total.fold(lax.rem(t + 1, depth), None)
            close_before(t)
            return carry

        lax.fori_loop(0, depth, step, 0)

    def finish(here, sums):
        token_rows = hidden_sc[here, :]
        center = token_rows - jnp.mean(token_rows, axis=-1, keepdims=True)
        inv = lax.rsqrt(jnp.mean(center * center, axis=-1, keepdims=True) + 1e-05)
        hat = center * inv
        dn2 = dn2_acc[here, :]
        cot = cot_ref[here, :].astype(F32)
        scaled = dn2 * vec_ref[2:3, :]
        grad = cot + inv * (
            scaled
            - jnp.mean(scaled, axis=-1, keepdims=True)
            - hat * jnp.mean(scaled * hat, axis=-1, keepdims=True)
        )
        hid_ref[here, :] = grad
        n2_sc[here, :] = grad.astype(BF16)
        result_ref[here, :] = out_acc[here, :].astype(BF16)
        return (
            sums[0] + jnp.sum(dn2 * hat, axis=0, keepdims=True),
            sums[1] + jnp.sum(dn2, axis=0, keepdims=True),
            sums[2] + jnp.sum(cot, axis=0, keepdims=True),
        )

    seats = (place.s1, place.s2, place.s3)
    part = width // 4
    half = rows // 2

    def go_copy(way, side):
        src = datt_ref.at[pl.ds(side * half, half), aligned(seats[way] * part, part)]
        dst = go_all.at[aligned(place.s * rows + side * half, half)]
        return send(src, dst, (go_sent, go_got), 2 * way + side, place.across(way))

    def go_arrival(way, side):
        there = go_all.at[aligned(seats[way] * rows + side * half, half)]
        return send(there, there, (go_sent, go_got), 2 * way + side, place.across(way))

    total.swap(0)
    none = jnp.zeros((1, width), F32)
    sums = (none, none, none)
    for side in (0, 1):
        sums = lax.fori_loop(
            0, lines // 2, lambda index, carry: finish(aligned(side * half + index * 32, 32), carry), sums
        )
        rows_here = pl.ds(side * half, half)
        datt_ref[rows_here, :] = dot_nt(n2_sc[rows_here, :], out_w_ref[...]).astype(BF16)
        for way in range(3):
            go_copy(way, side).start()
    gain_sum, bias_sum, cot_sum = sums
    small_ref[2:3, :] = gain_sum
    small_ref[3:4, :] = bias_sum
    small_ref[4:5, :] = cot_sum
    puts = [
        pltpu.make_async_copy(src, dst, put_sems.at[i])
        for i, (src, dst) in enumerate(((result_ref, result_hbm), (hid_ref, hid_hbm), (out_g_ref, out_g_hbm)))
    ]
    puts[0].start()
    puts[1].start()
    own_go = pltpu.make_async_copy(
        datt_ref.at[:, aligned(place.s * part, part)], go_all.at[aligned(place.s * rows, rows)], go_sems
    )
    own_go.start()
    if depth > 1:
        total.close(depth - 1, False)
    out_g_ref[...] = dot_tn(att_ref[...], n2_sc[...]).astype(BF16)
    puts[2].start()
    total.close(0, True)
    total.collect()
    down_part[...] = total.total[...]
    for index in (chunks - 2, chunks - 1):
        grad_store(index).wait()
    for put in puts:
        put.wait()
    own_go.wait()
    for way in range(3):
        for side in (0, 1):
            go_arrival(way, side).wait_recv()
            go_copy(way, side).wait_send()
    total.sent()
    place.each(1, depth, lambda step: total.z_copy(step).wait_send())


def middle(fsdp_count, att, x, cot, vec, w_out, w_in, w_down):
    rows, width = x.shape
    hidden_units = w_in.shape[1]
    span = 512
    depth = fsdp_count // 2
    anywhere = pl.BlockSpec(memory_space=pltpu.HBM)
    vmem = pl.BlockSpec(memory_space=pltpu.VMEM)
    shape = jax.ShapeDtypeStruct
    kept = (hidden_units // fsdp_count, width)
    return pl.pallas_call(
        functools.partial(middle_kernel, fsdp_count),
        out_shape=(
            shape((rows, width), BF16),
            shape((4 * rows, width // 4), BF16),
            shape((rows, width), F32),
            shape(vec.shape, F32),
            shape(w_out.shape, BF16),
            shape(w_in.shape, BF16),
            shape((kept[0], width // 4), BF16),
        ),
        in_specs=[anywhere] * 3 + [vmem] + [anywhere] * 3,
        out_specs=(anywhere, anywhere, anywhere, vmem, anywhere, anywhere, vmem),
        scratch_shapes=[
            pltpu.VMEM((rows, width), BF16),
            pltpu.VMEM((rows, width), F32),
            pltpu.VMEM(w_out.shape, BF16),
            dma(3),
            pltpu.VMEM((rows, width), BF16),
            pltpu.VMEM((rows, width), BF16),
            pltpu.VMEM((rows, width), BF16),
            pltpu.VMEM(w_out.shape, BF16),
            dma(4),
            pltpu.VMEM((rows, width), BF16),
            dma(),
            dma(6),
            dma(6),
            pltpu.VMEM((rows, width), F32),
            pltpu.VMEM((rows, width), BF16),
            pltpu.VMEM((width, rows), BF16),
            pltpu.VMEM((rows, width), F32),
            pltpu.VMEM((rows, width), F32),
            pltpu.VMEM((4, width, span), BF16),
            pltpu.VMEM((4, span, width), BF16),
            pltpu.VMEM((2, width, span), BF16),
            pltpu.VMEM((2, rows, span), BF16),
            pltpu.VMEM((2, rows, span), F32),
            pltpu.VMEM((hidden_units, width), BF16),
            dma(4),
            dma(4),
            dma(2),
            pltpu.VMEM(kept, BF16),
        ]
        + Reduce.scratch(depth, *kept, False, True),
        compiler_params=pltpu.CompilerParams(
            collective_id=5, has_side_effects=True, vmem_limit_bytes=60 << 20
        ),
    )(att, x, cot, vec, w_out, w_in, w_down)


def results_kernel(share, held, *refs):
    sources, small, refs = refs[:6], refs[6], refs[7:]
    cut = len(refs) > 20
    count = 12 if cut else 6
    outs, refs = refs[:count], refs[count:]
    taken, given, in_sems, out_sems = refs[:6], refs[6:10], refs[10], refs[11]
    given = given + taken[4:]
    pieces = []
    for i in range(6):
        rows = sources[i].shape[0]
        parts = 4 if rows % 64 == 0 else 1
        for part in range(parts):
            pieces.append((i, part, pl.ds(part * (rows // parts), rows // parts), rows // parts))
    loads = [
        pltpu.make_async_copy(sources[i].at[here], taken[i].at[here], in_sems.at[i, part]) for i, part, here, _ in pieces
    ]
    for load in loads:
        load.start()
    stores = []
    for load, (i, part, here, rows) in zip(loads, pieces):
        load.wait()
        src, dst, base = taken[i], given[i], part * rows

        def body(index, carry):
            line = aligned(base + index * 16, 16)
            dst[line, :] = src[line, :].astype(F32)
            return carry

        if i < 4:
            lax.fori_loop(0, rows // 16, body, 0)
        store = pltpu.make_async_copy(dst.at[here], outs[i].at[here], out_sems.at[i, part])
        store.start()
        stores.append(store)
    if cut:
        position = lax.axis_index("fsdp")
        cols = aligned(position * share, share)
        for line in range(5):
            outs[6 + line][...] = small[line : line + 1, cols]
        per = small.shape[1] // held
        outs[11][...] = small[pl.ds(5 + lax.div(position, per), 1), aligned(lax.rem(position, per) * held, held)]
    for store in stores:
        store.wait()


def write_results(share, held, arrays, small):
    shape = jax.ShapeDtypeStruct
    kinds = (F32, F32, F32, F32, BF16, BF16)
    shapes = [shape(a.shape, kind) for a, kind in zip(arrays, kinds)]
    cut = share % LANES == 0 and held % LANES == 0
    small_shapes = [shape((1, share), F32)] * 5 + [shape((1, held), F32)] if cut else []
    hbm = pl.BlockSpec(memory_space=pltpu.HBM)
    vmem = pl.BlockSpec(memory_space=pltpu.VMEM)
    outs = pl.pallas_call(
        functools.partial(results_kernel, share, held),
        out_shape=tuple(shapes + small_shapes),
        in_specs=[hbm] * 6 + [vmem],
        out_specs=tuple([hbm] * 6 + [vmem] * len(small_shapes)),
        scratch_shapes=[pltpu.VMEM(a.shape, BF16) for a in arrays]
        + [pltpu.VMEM(a.shape, F32) for a in arrays[:4]]
        + [dma(6, 4), dma(6, 4)],
        compiler_params=pltpu.CompilerParams(vmem_limit_bytes=60 << 20),
    )(*arrays, small)
    if cut:
        return outs[:6], [part.reshape(-1) for part in outs[6:]]
    position = lax.axis_index("fsdp")
    lines = lax.dynamic_slice_in_dim(small[:5], position * share, share, axis=1)
    rest = small[5:].reshape(-1)
    return outs, [lines[i] for i in range(5)] + [lax.dynamic_slice_in_dim(rest, position * held, held)]


def per_device(
    fsdp_count,
    tokens,
    segment_ids,
    random_blocks,
    ln1_gain,
    ln1_bias,
    w_qkv,
    w_out,
    ln2_gain,
    ln2_bias,
    w_in,
    b_in,
    w_down,
    b_down,
    cotangent,
):
    width = tokens.shape[2]
    share, held = ln1_gain.shape[0], b_in.shape[0]
    lines = fsdp_count * held // width
    position = lax.axis_index("fsdp")
    column = jnp.arange(width, dtype=jnp.int32)
    narrow = jnp.tile(jnp.stack([ln1_gain, ln1_bias, ln2_gain, ln2_bias, b_down]), (1, fsdp_count))
    narrow = jnp.where(column // share == position, narrow, jnp.zeros((), BF16))
    line = jnp.arange(lines, dtype=jnp.int32)[:, None]
    broad = jnp.tile(b_in[None], (1, width // held))
    broad = jnp.where((line * width + column) // held == position, broad, jnp.zeros((), BF16))
    vec = jnp.concatenate([narrow, broad, jnp.zeros((-(5 + lines) % 16, width), BF16)], axis=0)
    by_heads, lse, att_rows, out_weight, down_weight, in_weight, vec, normed_one, own_qkv, query_docs, key_feats, mask = (
        forward_attention(fsdp_count, tokens[0], w_qkv, vec, segment_ids, random_blocks, w_out, w_down, w_in)
    )
    result, grad_att, grad_hidden, small, grad_out, grad_in, down_part = middle(
        fsdp_count, att_rows, tokens[0], cotangent[0], vec, out_weight, in_weight, down_weight
    )
    grad_tokens, small, total_qkv, total_out, total_in, total_down = backward_attention(
        fsdp_count,
        grad_att,
        (by_heads, mask, query_docs, key_feats, lse, normed_one, own_qkv, vec),
        tokens[0],
        grad_hidden,
        small,
        (grad_out, grad_in),
        down_part,
    )
    arrays, parts = write_results(
        share, held, (total_in, total_down, total_qkv, total_out, result, grad_tokens), small
    )
    return (
        arrays[4][None],
        arrays[5][None],
        parts[0],
        parts[1],
        arrays[2],
        arrays[3],
        parts[2],
        parts[3],
        arrays[0],
        parts[5],
        arrays[1],
        parts[4],
    )


def solution(mesh):
    return jax.shard_map(
        functools.partial(per_device, mesh.shape["fsdp"]),
        mesh=mesh,
        in_specs=(
            P("fsdp", "seq", None),
            P("fsdp", "seq"),
            P("seq", None, None),
            P("fsdp"),
            P("fsdp"),
            P("fsdp", None),
            P("fsdp", None),
            P("fsdp"),
            P("fsdp"),
            P("fsdp", None),
            P("fsdp"),
            P("fsdp", None),
            P("fsdp"),
            P("fsdp", "seq", None),
        ),
        out_specs=(
            P("fsdp", "seq", None),
            P("fsdp", "seq", None),
            P("fsdp"),
            P("fsdp"),
            P("fsdp", None),
            P("fsdp", None),
            P("fsdp"),
            P("fsdp"),
            P("fsdp", None),
            P("fsdp"),
            P("fsdp", None),
            P("fsdp"),
        ),
        check_vma=False,
    )
```

```python
import functools
import math

import jax
import jax.numpy as jnp
from jax import lax
from jax.experimental import pallas as pl
from jax.experimental.pallas import tpu as pltpu
from jax.sharding import PartitionSpec as P

DH = 64
BLK = 64
LANES = 128
NEG = -1e30
F32 = jnp.float32
BF16 = jnp.bfloat16


def dot_nn(a, b):
    return jnp.dot(a, b, preferred_element_type=F32)


def dot_nt(a, b):
    return lax.dot_general(a, b, (((1,), (1,)), ((), ())), preferred_element_type=F32)


def dot_tn(a, b):
    return lax.dot_general(a, b, (((0,), (0,)), ((), ())), preferred_element_type=F32)


DOCS = 6


def write_block_mask(picks_ref, mask_ref):
    heads, inner, count = picks_ref.shape
    last = inner + 1
    shape = (inner, LANES)
    lane = lax.rem(lax.broadcasted_iota(jnp.int32, shape, 1), DH)
    block = lax.broadcasted_iota(jnp.int32, shape, 0) + 1
    fixed = (jnp.abs(lane - block) <= 1) | (lane == 0) | (lane >= last)
    for head in range(heads):
        picks = picks_ref[head]
        used = fixed
        for slot in range(count):
            used = used | (picks[:, slot : slot + 1] == lane)
        mask_ref[head, 0:1, :] = jnp.zeros((1, LANES), F32)
        mask_ref[head, 1:last, :] = jnp.where(used, 0.0, NEG)
        mask_ref[head, last : last + 1, :] = jnp.zeros((1, LANES), F32)


def token_features(start, docs, blocks):
    shape = (docs.shape[0], LANES)
    lane = lax.rem(lax.broadcasted_iota(jnp.int32, shape, 1), DH)
    block = lax.div(lax.broadcasted_iota(jnp.int32, shape, 0) + start, BLK)
    own = docs + blocks == lane
    other = jnp.where(own | (lane >= blocks + DOCS), 0.0, 1.0)
    key_part = jnp.where(lane < blocks, jnp.where(block == lane, 1.0, 0.0), other)
    return jnp.where(own, NEG, 0.0).astype(BF16), key_part.astype(BF16)


def query_tile(q_tile, doc_tile, mask_ref, head, first_block, lanes):
    scale = jnp.asarray(1.0 / math.sqrt(DH), BF16)
    count = q_tile.shape[0] // BLK
    mask = jnp.concatenate(
        [jnp.broadcast_to(mask_ref[head, pl.ds(first_block + i, 1), :], (BLK, LANES)) for i in range(count)], axis=0
    )
    return jnp.where(lanes, q_tile * scale, doc_tile + mask.astype(BF16))


def own_lanes(odd, shape):
    return lax.div(lax.broadcasted_iota(jnp.int32, shape, 1), DH) == odd


MESH = pl.DeviceIdType.MESH


class Place:
    def __init__(self, fsdp_count):
        self.depth = fsdp_count // 2
        self.s = lax.axis_index("seq")
        self.f = lax.axis_index("fsdp")
        self.z = lax.div(self.f, 2)
        self.c = lax.rem(self.f, 2)
        self.s1 = self.s + 1 - 2 * lax.rem(self.s, 2)
        self.s2 = self.s + 2 - 4 * lax.div(self.s, 2)
        self.s3 = 3 - self.s
        self.beside = (self.s, self.f + 1 - 2 * self.c)

    def across(self, index):
        return ((self.s1, self.s2, self.s3)[index], self.f)

    def far(self, step):
        return lax.rem(self.z + step, self.depth)

    def back(self, step):
        return lax.rem(self.z + self.depth - step, self.depth)

    def along(self, z):
        return (self.s, 2 * z + self.c)

    def meet(self):
        barrier = pltpu.get_barrier_semaphore()
        peers = [self.beside] + [self.across(i) for i in range(3)]
        for peer in peers:
            pl.semaphore_signal(barrier, inc=1, device_id=peer, device_id_type=MESH)
        self.each(1, self.depth, lambda step: pl.semaphore_signal(
            barrier, inc=1, device_id=self.along(self.far(step)), device_id_type=MESH
        ))
        pl.semaphore_wait(barrier, len(peers) + self.depth - 1)

    def each(self, start, stop, body):
        if stop - start <= 8:
            for step in range(start, stop):
                body(step)
        else:
            lax.fori_loop(start, stop, lambda step, carry: (body(step), carry)[1], 0)


def send(src, dst, sems, index, device):
    sent, got = sems
    return pltpu.make_async_remote_copy(
        src_ref=src,
        dst_ref=dst,
        send_sem=sent.at[index],
        recv_sem=got.at[index],
        device_id=device,
        device_id_type=MESH,
    )


def aligned(start, size):
    return pl.ds(pl.multiple_of(start, size), size)


class Gather:
    def __init__(self, place, src, dst, split, sems):
        self.place, self.src, self.dst, self.split = place, src, dst, split
        self.rows, self.cols = src.shape
        self.local, self.zs, self.xs, self.rs, self.cs = sems

    def block(self, z, core, quarter=None, half=None):
        rows = aligned((2 * z + core) * self.rows, self.rows)
        if quarter is None:
            return self.dst.at[rows]
        wide = self.cols // 4
        if half is None:
            return self.dst.at[rows, aligned(quarter * wide, wide)]
        return self.dst.at[rows, aligned(quarter * wide + half * (wide // 2), wide // 2)]

    def source(self, step, side):
        return self.place.z - step if side == 0 else self.place.z + step

    def has(self, step, side):
        z = self.source(step, side)
        return z >= 0 if side == 0 else z < self.place.depth

    def sends(self, step, side):
        p = self.place
        onward = p.z + 1 < p.depth if side == 0 else p.z > 0
        return jnp.logical_and(self.has(step - 1, side), onward)

    def slot(self, step, side):
        return 2 * step + side

    def own_copy(self):
        return pltpu.make_async_copy(self.src, self.block(self.place.z, self.place.c), self.local)

    def own_core(self):
        p = self.place
        return send(self.src, self.block(p.z, p.c), self.cs, 0, p.beside)

    def own_arrival(self):
        p = self.place
        there = self.block(p.z, 1 - p.c)
        return send(there, there, self.cs, 0, p.beside)

    def core_copy(self, step, side):
        p = self.place
        there = self.block(self.source(step, side), p.c)
        return send(there, there, self.cs, self.slot(step, side), p.beside)

    def core_arrival(self, step, side):
        p = self.place
        there = self.block(self.source(step, side), 1 - p.c)
        return send(there, there, self.cs, self.slot(step, side), p.beside)

    def z_copy(self, step, side):
        p = self.place
        z = self.source(step - 1, side)
        there = self.block(z, p.c, p.s) if self.split else self.block(z, p.c)
        src = there
        if isinstance(step, int) and step == 1:
            wide = self.cols // 4
            src = self.src.at[:, aligned(p.s * wide, wide)] if self.split else self.src
        return send(src, there, self.zs, self.slot(step, side), p.along(p.z + 1 - 2 * side))

    def z_arrival(self, step, side):
        p = self.place
        z = self.source(step, side)
        there = self.block(z, p.c, p.s) if self.split else self.block(z, p.c)
        return send(there, there, self.zs, self.slot(step, side), p.along(p.z - 1 + 2 * side))

    def x_copy(self, step, side, way):
        p = self.place
        there = self.block(self.source(step, side), p.c, p.s)
        return send(there, there, self.xs[way], self.slot(step, side), p.across(way))

    def x_arrival(self, step, side, way):
        p = self.place
        there = self.block(self.source(step, side), p.c, (p.s1, p.s2)[way])
        return send(there, there, self.xs[way], self.slot(step, side), p.across(way))

    def relay_copy(self, step, side, way):
        p = self.place
        there = self.block(self.source(step, side), p.c, (p.s2, p.s1)[way], 1 - way)
        return send(there, there, self.rs[way], self.slot(step, side), p.across(way))

    def relay_arrival(self, step, side, way):
        p = self.place
        there = self.block(self.source(step, side), p.c, p.s3, 1 - way)
        return send(there, there, self.rs[way], self.slot(step, side), p.across(way))

    def both(self, step, body, test=None):
        for side in (0, 1):
            pl.when((test or self.has)(step, side))(functools.partial(body, step, side))

    def begin(self):
        self.both(1, lambda step, side: self.z_copy(step, side).start(), self.sends)
        self.own_copy().start()
        self.own_core().start()

    def swap(self, step):
        def body(step, side):
            self.z_arrival(step, side).wait_recv()
            pl.when(self.sends(step + 1, side))(lambda: self.z_copy(step + 1, side).start())
            if self.split:
                for way in (0, 1):
                    self.x_copy(step, side, way).start()
            else:
                self.core_copy(step, side).start()

        self.both(step, body)

    def relay(self, step):
        def body(step, side):
            for way in (0, 1):
                self.x_arrival(step, side, way).wait_recv()
            for way in (0, 1):
                self.relay_copy(step, side, way).start()

        if self.split:
            self.both(step, body)

    def share(self, step):
        def body(step, side):
            for way in (0, 1):
                self.relay_arrival(step, side, way).wait_recv()
            self.core_copy(step, side).start()

        if self.split:
            self.both(step, body)

    def finish(self):
        self.own_copy().wait()
        self.own_core().wait_send()
        self.own_arrival().wait_recv()

        def close(step, side):
            if self.split:
                for way in (0, 1):
                    self.x_copy(step, side, way).wait_send()
                    self.relay_copy(step, side, way).wait_send()
            self.core_copy(step, side).wait_send()
            self.core_arrival(step, side).wait_recv()

        self.place.each(1, self.place.depth, lambda step: self.both(step, close))
        self.place.each(
            1,
            self.place.depth,
            lambda step: self.both(step, lambda step, side: self.z_copy(step, side).wait_send(), self.sends),
        )

    @staticmethod
    def scratch(depth, split):
        held = 2 * depth if split else 1
        return [dma()] + [dma(2 * depth)] * 2 + [dma(held)] * 8 + [dma(2 * depth)] * 2

    @staticmethod
    def take(refs):
        pairs = [(refs[i], refs[i + 1]) for i in range(1, 13, 2)]
        return (refs[0], pairs[0], pairs[1:3], pairs[3:5], pairs[5])


GATHER_SEMS = 13


def gather_steps(place, gathers, late, count, unit):
    depth = place.depth

    def swap(step):
        for one in gathers:
            one.swap(step)

    def relay(step):
        for one in gathers:
            one.relay(step)

    def share(step):
        for one in gathers:
            one.share(step)

    def late_swap(step):
        for one in late:
            one.swap(step)

    for one in late:
        one.begin()
    if depth <= 8:
        rounds = []
        for step in range(2, depth + 2):
            now = []
            if step <= depth:
                now.append(functools.partial(late_swap, step - 2)) if step > 2 else None
                now.append(functools.partial(share, step - 3)) if step > 3 else None
                now.append(functools.partial(swap, step)) if step < depth else None
                now.append(functools.partial(relay, step - 1))
            rounds.append(now)
        rounds[-1] = [functools.partial(share, step) for step in range(max(1, depth - 2), depth)]
        rounds[-1].append(functools.partial(late_swap, depth - 1))
        in_turn(count, unit, rounds[:count])
        for now in rounds[count:]:
            for one in now:
                one()
    else:
        in_turn(count, unit, [])
        swap(2)
        relay(1)

        def body(step, carry):
            late_swap(step - 2)
            share(step - 2)
            swap(step)
            relay(step - 1)
            return carry

        lax.fori_loop(3, depth, body, 0)
        late_swap(depth - 2)
        share(depth - 2)
        relay(depth - 1)
        share(depth - 1)
        late_swap(depth - 1)


def dma(*shape):
    return pltpu.SemaphoreType.DMA(shape) if shape else pltpu.SemaphoreType.DMA


def qkv_columns(heads_ref, pair):
    third = heads_ref.shape[1] // 3
    return tuple(aligned(i * third + pair * LANES, LANES) for i in range(3))


def attend_unit(pair, odd, tile, heads_ref, mask_ref, qd_ref, kf_ref, keys_sc, values_t, out_ref, lse_ref):
    length = heads_ref.shape[0]
    cols = aligned(pair * LANES, LANES)
    q_cols, k_cols, v_cols = qkv_columns(heads_ref, pair)
    mine = own_lanes(odd, (length, LANES))
    keys_sc[...] = jnp.where(mine, heads_ref[:, k_cols], kf_ref[...])

    @pl.when(odd == 0)
    def _():
        values_t[...] = heads_ref[:, v_cols].T
        out_ref[:, cols] = jnp.zeros((length, LANES), BF16)

    def one_tile(index, carry):
        rows = aligned(index * tile, tile)
        lanes = own_lanes(odd, (tile, LANES))
        queries = query_tile(
            heads_ref[rows, q_cols], qd_ref[rows, :], mask_ref, 2 * pair + odd, index * (tile // BLK), lanes
        )
        scores = dot_nt(keys_sc[...], queries)
        top = jnp.max(scores, axis=0, keepdims=True)
        prob = jnp.exp(scores - top)
        total = jnp.sum(prob, axis=0, keepdims=True)
        mixed = dot_nn(values_t[...], prob.astype(BF16)) / total
        lse_ref[pair, pl.ds(odd, 1), rows] = top + jnp.log(total)
        out_ref[rows, cols] = jnp.where(lanes, mixed.T.astype(BF16), out_ref[rows, cols])
        return carry

    lax.fori_loop(0, length // tile, one_tile, 0, unroll=2)


def in_turn(count, unit, actions):
    def body(index, carry):
        unit(index)
        for which, todo in enumerate(actions):
            if todo:

                @pl.when(index == which)
                def _(todo=todo):
                    for one in todo:
                        one()

        return carry

    lax.fori_loop(0, count, body, 0)


def forward_kernel(
    fsdp_count,
    x_ref,
    wq_ref,
    vec_ref,
    ids_ref,
    picks_ref,
    out_w_ref,
    down_w_ref,
    in_w_ref,
    heads_all,
    lse_ref,
    att_all,
    out_w_all,
    down_w_all,
    in_w_all,
    vec_sum,
    n1_all,
    wq_all,
    qd_ref,
    kf_ref,
    mask_ref,
    x_sc,
    n1_sc,
    wq_own,
    wq_sc,
    vec_sc,
    seg_ref,
    seg_sc,
    heads_sc,
    att_sc,
    keys_sc,
    values_t,
    *sems,
):
    place = Place(fsdp_count)
    rows, width = x_ref.shape
    own_width = wq_sc.shape[1]
    seats = (place.s1, place.s2, place.s3)

    def taken(i):
        return Gather.take(sems[i * GATHER_SEMS : (i + 1) * GATHER_SEMS])

    x_own, seg_own, keep_sems, pick_sems, x_sent, x_got, r_sent, r_got, g_sent, g_got, a_sent, a_got, a_own = sems[6 * GATHER_SEMS :]
    lone = pl.ds(0, in_w_ref.shape[1] // 2)
    shared = pl.ds(in_w_ref.shape[1] // 2, in_w_ref.shape[1] // 2)
    gathers = [
        Gather(place, src, dst, split, taken(i))
        for i, (src, dst, split) in enumerate(
            (
                (out_w_ref, out_w_all, True),
                (in_w_ref.at[:, shared], in_w_all.at[:, shared], True),
                (down_w_ref, down_w_all, True),
                (in_w_ref.at[:, lone], in_w_all.at[:, lone], False),
            )
        )
    ]
    late = [gathers.pop()]
    third = own_width // 3
    picks = [
        pltpu.make_async_copy(
            wq_ref.at[:, aligned((4 * i + place.s) * third, third)], wq_own.at[:, pl.ds(i * third, third)], pick_sems.at[i]
        )
        for i in range(3)
    ]
    for pick in picks:
        pick.start()
    write_block_mask(picks_ref, mask_ref)
    seg_ref[...] = jnp.zeros_like(seg_ref)
    for part in range(ids_ref.shape[1] // LANES):
        seg_ref[part : part + 1, :] = ids_ref[:, part * LANES : (part + 1) * LANES]
    weight = Gather(place, wq_own, wq_sc, False, taken(4))
    vector = Gather(place, vec_ref, vec_sc, False, taken(5))
    half = rows // 2

    def x_rows(seat):
        return x_sc.at[aligned(seat * rows, rows)]

    def x_half(seat, part):
        return x_sc.at[aligned(seat * rows + part * half, half)]

    def x_copy(way):
        return send(x_ref, x_rows(place.s), (x_sent, x_got), way, place.across(way))

    def x_arrival(way):
        there = x_rows(seats[way])
        return send(there, there, (x_sent, x_got), way, place.across(way))

    def x_relay(way):
        there = x_half((place.s2, place.s1)[way], 1 - way)
        return send(there, there, (r_sent, r_got), way, place.across(way))

    def x_relayed(way):
        there = x_half(place.s3, 1 - way)
        return send(there, there, (r_sent, r_got), way, place.across(way))

    def seg_copy(way):
        return send(seg_ref, seg_sc.at[place.s], (g_sent, g_got), way, place.across(way))

    def seg_arrival(way):
        there = seg_sc.at[seats[way]]
        return send(there, there, (g_sent, g_got), way, place.across(way))

    place.meet()
    vector.begin()
    for pick in picks:
        pick.wait()
    weight.begin()
    for way in range(2):
        x_copy(way).start()
    for way in range(3):
        seg_copy(way).start()
    own_x = pltpu.make_async_copy(x_ref, x_rows(place.s), x_own)
    own_x.start()
    own_seg = pltpu.make_async_copy(seg_ref, seg_sc.at[place.s], seg_own)
    own_seg.start()
    def start_rest():
        for one in gathers:
            one.begin()

    if place.depth <= 8:
        for step in range(1, place.depth):
            vector.swap(step)
            weight.swap(step)
            if step == max(1, place.depth - 2):
                start_rest()
    else:
        place.each(1, place.depth, vector.swap)
        place.each(1, place.depth, weight.swap)
        start_rest()
    vector.finish()
    vec_rows = vec_ref.shape[0]
    total = vec_sc[pl.ds(0, vec_rows), :].astype(F32)
    if fsdp_count <= 8:
        for f in range(1, fsdp_count):
            total = total + vec_sc[pl.ds(f * vec_rows, vec_rows), :].astype(F32)
    else:
        total = lax.fori_loop(
            1, fsdp_count, lambda f, sofar: sofar + vec_sc[aligned(f * vec_rows, vec_rows), :].astype(F32), total
        )
    vec_sum[...] = total

    def normalise(seat):
        def body(part):
            token_rows = x_sc[aligned(seat * rows + part * 32, 32), :].astype(F32)
            center = token_rows - jnp.mean(token_rows, axis=-1, keepdims=True)
            variance = jnp.mean(center * center, axis=-1, keepdims=True)
            normed = center * lax.rsqrt(variance + 1e-05) * vec_sum[0:1, :] + vec_sum[1:2, :]
            n1_sc[aligned(seat * rows + part * 32, 32), :] = normed.astype(BF16)

        lax.fori_loop(0, rows // 32, lambda part, carry: (body(part), carry)[1], 0)

    def project(seat):
        here = aligned(seat * rows, rows)

        def body(part):
            cols = aligned(part * 256, 256)
            heads_sc[here, cols] = dot_nn(n1_sc[here, :], wq_sc[:, cols]).astype(BF16)

        lax.fori_loop(0, own_width // 256, lambda part, carry: (body(part), carry)[1], 0)

    own_x.wait()
    normalise(place.s)
    for way in range(2):
        x_arrival(way).wait_recv()
    for way in range(2):
        x_relay(way).start()
    for way in range(2):
        normalise(seats[way])
    weight.finish()
    project(place.s)
    for way in range(2):
        project(seats[way])
    for one in gathers:
        one.swap(1)
    for way in range(2):
        x_relayed(way).wait_recv()
    normalise(place.s3)
    project(place.s3)
    own_seg.wait()
    for way in range(3):
        seg_arrival(way).wait_recv()
    blocks = mask_ref.shape[1]
    for seat in range(4):
        columns = seg_sc[seat].T
        for part in range(rows // LANES):
            here = pl.ds(seat * rows + part * LANES, LANES)
            qd_ref[here, :], kf_ref[here, :] = token_features(
                seat * rows + part * LANES, columns[:, part : part + 1], blocks
            )
    keeps = [
        pltpu.make_async_copy(src, dst, keep_sems.at[i])
        for i, (src, dst) in enumerate(((heads_sc, heads_all), (n1_sc, n1_all), (wq_sc, wq_all)))
    ]
    for keep in keeps:
        keep.start()

    pairs = att_sc.shape[1] // LANES

    def att_copy(pair, way):
        cols = aligned((place.s * pairs + pair) * LANES, LANES)
        return send(
            att_sc.at[aligned(seats[way] * rows, rows), aligned(pair * LANES, LANES)],
            att_all.at[:, cols],
            (a_sent, a_got),
            pair * 3 + way,
            place.across(way),
        )

    def att_own(pair):
        cols = aligned((place.s * pairs + pair) * LANES, LANES)
        return pltpu.make_async_copy(
            att_sc.at[aligned(place.s * rows, rows), aligned(pair * LANES, LANES)],
            att_all.at[:, cols],
            a_own.at[pair],
        )

    def att_arrival(pair, way):
        there = att_all.at[:, aligned((seats[way] * pairs + pair) * LANES, LANES)]
        return send(there, there, (a_sent, a_got), pair * 3 + way, place.across(way))

    def unit(index):
        pair, odd = lax.div(index, 2), lax.rem(index, 2)
        attend_unit(pair, odd, 256, heads_sc, mask_ref, qd_ref, kf_ref, keys_sc, values_t, att_sc, lse_ref)

        @pl.when(odd == 1)
        def _():
            for way in range(3):
                att_copy(pair, way).start()
            att_own(pair).start()

    gather_steps(place, gathers, late, 2 * pairs, unit)
    for keep in keeps:
        keep.wait()
    for way in range(3):
        seg_copy(way).wait_send()
        if way < 2:
            x_copy(way).wait_send()
            x_relay(way).wait_send()
        for pair in range(pairs):
            att_copy(pair, way).wait_send()
            att_arrival(pair, way).wait_recv()
    for pair in range(pairs):
        att_own(pair).wait()
    for one in gathers + late:
        one.finish()


def forward_attention(fsdp_count, x, w_qkv, vec, seg, picks, w_out, w_down, w_in):
    rows, width = x.shape
    length = 4 * rows
    heads = picks.shape[0]
    pairs = heads // 2
    depth = fsdp_count // 2
    own_width = w_qkv.shape[1] // 4
    full = fsdp_count * w_qkv.shape[0]
    seg_rows = -(-seg.shape[1] // (8 * LANES)) * 8
    anywhere = pl.BlockSpec(memory_space=pltpu.HBM)
    vmem = pl.BlockSpec(memory_space=pltpu.VMEM)
    shape = jax.ShapeDtypeStruct

    def whole(shard):
        return shape((fsdp_count * shard.shape[0], shard.shape[1]), shard.dtype)

    return pl.pallas_call(
        functools.partial(forward_kernel, fsdp_count),
        out_shape=(
            shape((length, own_width), BF16),
            shape((pairs, 2, length), F32),
            shape((rows, heads * DH * 4), BF16),
            whole(w_out),
            whole(w_down),
            whole(w_in),
            shape(vec.shape, F32),
            shape((length, width), BF16),
            shape((full, own_width), BF16),
            shape((length, LANES), BF16),
            shape((length, LANES), BF16),
            shape((heads, picks.shape[1] + 2, LANES), F32),
        ),
        in_specs=[anywhere] * 3 + [vmem] * 2 + [anywhere] * 3,
        out_specs=(anywhere, vmem, anywhere, anywhere, anywhere, anywhere, vmem, anywhere, anywhere, vmem, vmem, vmem),
        scratch_shapes=[
            pltpu.VMEM((length, width), BF16),
            pltpu.VMEM((length, width), BF16),
            pltpu.VMEM((w_qkv.shape[0], own_width), BF16),
            pltpu.VMEM((full, own_width), BF16),
            pltpu.VMEM((fsdp_count * vec.shape[0], vec.shape[1]), BF16),
            pltpu.VMEM((seg_rows, LANES), jnp.int32),
            pltpu.VMEM((4, seg_rows, LANES), jnp.int32),
            pltpu.VMEM((length, own_width), BF16),
            pltpu.VMEM((length, heads * DH), BF16),
            pltpu.VMEM((length, LANES), BF16),
            pltpu.VMEM((LANES, length), BF16),
        ]
        + Gather.scratch(depth, True) * 3
        + Gather.scratch(depth, False) * 3
        + [dma(), dma(), dma(3), dma(3), dma(2), dma(2), dma(2), dma(2), dma(3), dma(3)]
        + [dma(3 * pairs), dma(3 * pairs), dma(pairs)],
        compiler_params=pltpu.CompilerParams(
            collective_id=2, has_side_effects=True, vmem_limit_bytes=60 << 20
        ),
    )(x, w_qkv, vec, seg, picks, w_out, w_down, w_in)


def by_rows(count, cols, body):
    chunk = 16
    while count % (2 * chunk) == 0 and 2 * chunk * cols <= 16384:
        chunk *= 2
    lax.fori_loop(0, count // chunk, lambda i, carry: (body(aligned(i * chunk, chunk)), carry)[1], 0)


class Reduce:
    def __init__(self, place, grad, out, quartered, bufs, sems, direct=False, thirds=False, late=False, far_first=False):
        self.far_first = far_first
        self.place, self.grad, self.out, self.quartered, self.direct = place, grad, out, quartered, direct
        self.thirds, self.late = thirds, late
        self.rows, self.cols = out.shape
        self.wide = self.cols // 4
        self.acc, self.own, self.relay_in, self.quarter_in, self.z_in, self.total = bufs
        self.own_sem, self.put_sem, self.cs, self.rs, self.qs, self.zs, self.fs, self.gs = sems

    @staticmethod
    def scratch(depth, rows, cols, quartered, direct=False, far_first=False):
        held = cols // 4 if quartered else cols
        near = 1 if far_first else depth
        side = (1, 1, 16, LANES) if quartered else None
        return [
            pltpu.VMEM((depth, rows, held), BF16),
            pltpu.VMEM((16, LANES) if direct else (rows, held), BF16),
            pltpu.VMEM(side or (2, near, rows, cols // 8), BF16),
            pltpu.VMEM(side or (2, near, rows, cols // 4), BF16),
            pltpu.VMEM((depth, rows, cols if far_first else cols // 4), BF16),
            pltpu.VMEM((rows, cols // 4), BF16),
            dma(),
            dma(3),
        ] + [dma(depth)] * 12 + [dma(6)] * 4

    @staticmethod
    def take(place, grad, out, quartered, refs, direct=False, thirds=False, far_first=False):
        s = refs[8:]
        pairs = [(s[i], s[i + 1]) for i in range(0, 16, 2)]
        sems = (refs[6], refs[7], pairs[0], pairs[1:3], pairs[3:5], pairs[5], pairs[6], pairs[7])
        return Reduce(place, grad, out, quartered, refs[:6], sems, direct, thirds, False, far_first)

    def quarter(self, seat):
        return aligned(seat * self.wide, self.wide)

    def mine(self):
        if self.far_first:
            return pl.ds(0, self.cols)
        return pl.ds(0, self.wide) if self.quartered else self.quarter(self.place.s)

    def piece(self, seat, half):
        return aligned(seat * self.wide + half * (self.wide // 2), self.wide // 2)

    def own_copy(self, step):
        p = self.place
        rows = aligned((2 * p.far(step) + p.c) * self.rows, self.rows)
        return pltpu.make_async_copy(self.grad.at[rows], self.own, self.own_sem)

    def core_copy(self, step):
        p = self.place
        rows = aligned((2 * p.far(step) + 1 - p.c) * self.rows, self.rows)
        return send(self.grad.at[rows], self.acc.at[step], self.cs, step, p.beside)

    def relay_copy(self, step, way):
        p = self.place
        src = self.acc.at[step, :, self.piece(p.s3, way)]
        return send(src, self.relay_in.at[way, step], self.rs[way], step, p.across(way))

    def quarter_copy(self, step, way):
        p = self.place
        src = self.acc.at[step, :, self.quarter((p.s1, p.s2)[way])]
        return send(src, self.quarter_in.at[way, step], self.qs[way], step, p.across(way))

    def z_copy(self, step):
        p = self.place
        src = self.acc.at[step, :, self.mine()]
        return send(src, self.z_in.at[step], self.zs, step, p.along(p.far(step)))

    def columns(self, seat, part):
        if not self.thirds:
            return self.quarter(seat), pl.ds(0, self.wide)
        third = self.wide // 3
        return aligned((4 * part + seat) * third, third), pl.ds(part * third, third)

    @property
    def parts(self):
        return 3 if self.thirds else 1

    def put_copy(self, part):
        there, here = self.columns(self.place.s, part)
        return pltpu.make_async_copy(self.total.at[:, here], self.out.at[:, there], self.put_sem.at[part])

    def total_copy(self, way, part):
        p = self.place
        there, here = self.columns(p.s, part)
        return send(self.total.at[:, here], self.out.at[:, there], self.fs, 3 * way + part, p.across(way))

    def total_arrival(self, way, part):
        p = self.place
        there = self.out.at[:, self.columns((p.s1, p.s2, p.s3)[way], part)[0]]
        return send(there, there, self.fs, 3 * way + part, p.across(way))

    def totals(self):
        return [(way, part) for way in range(2) for part in range(self.parts)]

    def split_piece(self, seat, part, half):
        if not self.thirds:
            return self.piece(seat, half)
        width = self.wide // 6
        return aligned(((4 * part + seat) * 2 + half) * width, width)

    def back_copy(self, way, part):
        p = self.place
        there = self.out.at[:, self.split_piece((p.s2, p.s1)[way], part, 1 - way)]
        return send(there, there, self.gs, 3 * way + part, p.across(way))

    def back_arrival(self, way, part):
        p = self.place
        there = self.out.at[:, self.split_piece(p.s3, part, 1 - way)]
        return send(there, there, self.gs, 3 * way + part, p.across(way))

    def begin(self):
        depth = self.place.depth
        self.place.each(1, depth, lambda step: self.core_copy(step).start())
        self.core_copy(0).start()
        self.own_copy(1).start()

    def fold(self, step, following):
        p, acc, own = self.place, self.acc, self.own
        self.core_copy(step).wait_recv()
        if not self.direct:
            self.own_copy(step).wait()
        base = (2 * p.far(step) + p.c) * self.rows

        def body(index, carry):
            rows = aligned(index * 16, 16)
            added = self.grad[aligned(base + index * 16, 16), :] if self.direct else own[rows, :]
            acc[step, rows, :] = acc[step, rows, :] + added
            return carry

        lax.fori_loop(0, self.rows // 16, body, 0)
        if following is not None:
            self.own_copy(following).start()
        if not (self.quartered or self.far_first):
            for way in (0, 1):
                self.relay_copy(step, way).start()
        elif not (isinstance(step, int) and step == 0):
            self.z_copy(step).start()

    def swap(self, step):
        if self.quartered:
            return
        p, acc = self.place, self.acc
        for way in (0, 1):
            self.relay_copy(step, way).wait_recv()
            cols = self.piece((p.s2, p.s1)[way], way)
            came = self.relay_in.at[way, step]

            def body(rows):
                acc[step, rows, cols] = acc[step, rows, cols] + came[rows, :]

            by_rows(self.rows, self.wide // 2, body)
        for way in (0, 1):
            self.quarter_copy(step, way).start()

    def close(self, step, own):
        if self.quartered:
            return
        p, acc, came = self.place, self.acc, self.quarter_in
        for way in (0, 1):
            self.quarter_copy(step, way).wait_recv()
        cols = self.quarter(p.s)

        def body(rows):
            acc[step, rows, cols] = (
                acc[step, rows, cols].astype(F32)
                + came[0, step, rows, :].astype(F32)
                + came[1, step, rows, :].astype(F32)
            ).astype(BF16)

        by_rows(self.rows, self.wide, body)
        if not self.far_first:
            pl.when(jnp.logical_not(own))(lambda: self.z_copy(step).start())

    def far_sum(self):
        p, acc, came = self.place, self.acc, self.z_in
        p.each(1, p.depth, lambda step: self.z_copy(step).wait_recv())

        def body(rows):
            start = acc[0, rows, :].astype(F32)
            if p.depth <= 8:
                for step in range(1, p.depth):
                    start = start + came[step, rows, :].astype(F32)
            else:
                start = lax.fori_loop(1, p.depth, lambda step, sofar: sofar + came[step, rows, :].astype(F32), start)
            acc[0, rows, :] = start.astype(BF16)

        by_rows(self.rows, self.cols, body)
        for way in (0, 1):
            self.relay_copy(0, way).start()

    def near_sum(self):
        self.close(0, True)
        total, acc, cols = self.total, self.acc, self.quarter(self.place.s)

        def body(rows):
            total[rows, :] = acc[0, rows, cols]

        by_rows(self.rows, self.wide, body)
        self.give()

    def collect(self):
        p, acc, came, total = self.place, self.acc, self.z_in, self.total
        p.each(1, p.depth, lambda step: self.z_copy(step).wait_recv())
        cols = self.mine()

        def body(rows):
            start = acc[0, rows, cols].astype(F32)
            if p.depth <= 8:
                for step in range(1, p.depth):
                    start = start + came[step, rows, :].astype(F32)
            else:
                start = lax.fori_loop(1, p.depth, lambda step, sofar: sofar + came[step, rows, :].astype(F32), start)
            total[rows, :] = start.astype(BF16)

        by_rows(self.rows, self.wide, body)
        if not self.direct:
            self.give()

    def give(self):
        for way, part in self.totals():
            self.total_copy(way, part).start()
        for part in range(self.parts):
            self.put_copy(part).start()

    def spread(self):
        for way, part in self.totals():
            self.total_arrival(way, part).wait_recv()
        for way, part in self.totals():
            self.back_copy(way, part).start()

    def sent(self):
        def done(step):
            self.core_copy(step).wait_send()
            if not (self.quartered or self.far_first):
                for way in (0, 1):
                    self.relay_copy(step, way).wait_send()
                    self.quarter_copy(step, way).wait_send()

        self.place.each(0, self.place.depth, done)
        if self.far_first:
            for way in (0, 1):
                self.relay_copy(0, way).wait_send()
                self.quarter_copy(0, way).wait_send()

    def finish(self):
        for part in range(self.parts):
            self.put_copy(part).wait()
        if not self.late:
            self.sent()
            self.place.each(1, self.place.depth, lambda step: self.z_copy(step).wait_send())
        for way, part in self.totals():
            self.total_copy(way, part).wait_send()
        for way, part in self.totals():
            self.back_arrival(way, part).wait_recv()
            self.back_copy(way, part).wait_send()


REDUCE_REFS = 24


def backward_unit(
    pair, odd, half, tile, heads_ref, mask_ref, qd_ref, kf_ref, go_ref, lse_ref, out_ref, keys_sc, values_sc, keys_t, p_sc, s_sc, k_acc, v_acc
):
    length = heads_ref.shape[0]
    span = p_sc.shape[1]
    scale = jnp.asarray(1.0 / math.sqrt(DH), BF16)
    q_cols, k_cols, v_cols = qkv_columns(heads_ref, pair)
    cols = aligned(pair * LANES, LANES)
    mine = own_lanes(odd, (length, LANES))

    @pl.when(half == 0)
    def _():
        keys_sc[...] = jnp.where(mine, heads_ref[:, k_cols], kf_ref[...])
        values_sc[...] = jnp.where(mine, heads_ref[:, v_cols], jnp.zeros((), BF16))
        keys_t[...] = heads_ref[:, k_cols].T
        k_acc[...] = jnp.zeros_like(k_acc)
        v_acc[...] = jnp.zeros_like(v_acc)

    def one_tile(index, carry):
        here = aligned(index * tile, tile)
        rows = aligned(half * span + index * tile, tile)
        lanes = own_lanes(odd, (tile, LANES))
        queries = query_tile(
            heads_ref[rows, q_cols],
            qd_ref[rows, :],
            mask_ref,
            2 * pair + odd,
            half * (span // BLK) + index * (tile // BLK),
            lanes,
        )
        prob = jnp.exp(dot_nt(keys_sc[...], queries) - lse_ref[pair, pl.ds(odd, 1), rows])
        grad_prob = dot_nt(values_sc[...], go_ref[rows, cols])
        delta = jnp.sum(prob * grad_prob, axis=0, keepdims=True)
        p_sc[:, here] = prob.astype(BF16)
        s_sc[:, here] = (prob * (grad_prob - delta)).astype(BF16)
        return carry

    lax.fori_loop(0, span // tile, one_tile, 0, unroll=True)
    part = aligned(half * span, span)
    v_acc[...] += dot_nn(p_sc[...], go_ref[part, cols])
    k_acc[...] += dot_nn(s_sc[...], heads_ref[part, q_cols] * scale)
    grad_q = (dot_nn(keys_t[...], s_sc[...]) * (1.0 / math.sqrt(DH))).T.astype(BF16)
    out_ref[part, q_cols] = jnp.where(own_lanes(odd, (span, LANES)), grad_q, out_ref[part, q_cols])

    @pl.when(half == 1)
    def _():
        out_ref[:, k_cols] = jnp.where(mine, k_acc[...].astype(BF16), out_ref[:, k_cols])
        out_ref[:, v_cols] = jnp.where(mine, v_acc[...].astype(BF16), out_ref[:, v_cols])


def backward_kernel(
    fsdp_count,
    go_hbm,
    heads_hbm,
    mask_ref,
    qd_hbm,
    kf_hbm,
    lse_ref,
    n1_ref,
    wq_hbm,
    x_hbm,
    hid_hbm,
    vec_ref,
    small_ref,
    out_g_ref,
    in_g_ref,
    down_part,
    tokens_out,
    small_out,
    qkv_total,
    out_total,
    in_total,
    down_total,
    go_sc,
    heads_ref,
    qd_ref,
    kf_ref,
    wq_ref,
    x_ref,
    hid_ref,
    load_sems,
    grads_sc,
    keys_sc,
    values_sc,
    keys_t,
    p_sc,
    s_sc,
    k_acc,
    v_acc,
    n1_sc,
    qkv_g,
    part_sc,
    part_in,
    half_in,
    small_sc,
    small_in,
    *rest,
):
    place = Place(fsdp_count)
    rows = x_ref.shape[0]
    cut_at = in_g_ref.shape[1] * 3 // 4
    shared = pl.ds(0, cut_at)
    apart = pl.ds(cut_at, in_g_ref.shape[1] - cut_at)
    reduces = [
        Reduce.take(place, grad, out, False, rest[i * REDUCE_REFS : (i + 1) * REDUCE_REFS])
        for i, (grad, out) in enumerate(
            ((out_g_ref, out_total), (in_g_ref.at[:, shared], in_total.at[:, shared]))
        )
    ]
    lone = Reduce.take(
        place,
        in_g_ref.at[:, apart],
        in_total.at[:, apart],
        False,
        rest[3 * REDUCE_REFS : 4 * REDUCE_REFS],
        far_first=True,
    )
    first = Reduce.take(place, qkv_g, qkv_total, True, rest[2 * REDUCE_REFS : 3 * REDUCE_REFS], thirds=True)
    put_sem, f_pair, g_pair = (
        rest[4 * REDUCE_REFS],
        rest[4 * REDUCE_REFS + 1 : 4 * REDUCE_REFS + 3],
        rest[4 * REDUCE_REFS + 3 : 4 * REDUCE_REFS + 5],
    )
    down = Reduce(
        place,
        None,
        down_total,
        True,
        (None, None, None, None, None, down_part),
        (None, put_sem, None, None, None, None, f_pair, g_pair),
        late=True,
    )
    n_own, h_sent, h_got, p_sent, p_got, c_sent, c_got, z_sent, z_got, x_sent, x_got = rest[
        4 * REDUCE_REFS + 5 :
    ]
    seats = (place.s1, place.s2, place.s3)
    width = go_sc.shape[1]
    pairs = width // LANES
    half = rows // 2

    loads = [
        pltpu.make_async_copy(src, dst, load_sems.at[i])
        for i, (src, dst) in enumerate(
            (
                (heads_hbm, heads_ref),
                (qd_hbm, qd_ref),
                (kf_hbm, kf_ref),
                (go_hbm, go_sc),
                (wq_hbm, wq_ref),
                (x_hbm, x_ref),
                (hid_hbm, hid_ref),
            )
        )
    ]
    for load in loads:
        load.start()
    later_loads = loads[4:]
    place.meet()
    def first_copies(step):
        for one in reduces + [lone]:
            one.core_copy(step).start()

    place.each(1, place.depth, first_copies)
    first_copies(0)
    for one in reduces + [lone]:
        one.own_copy(1).start()
    down.give()
    n1_copy = pltpu.make_async_copy(n1_ref, n1_sc, n_own)
    n1_copy.start()

    def unit(index):
        backward_unit(
            lax.div(index, 4), lax.rem(lax.div(index, 2), 2), lax.rem(index, 2), 256, heads_ref, mask_ref, qd_ref, kf_ref,
            go_sc, lse_ref, grads_sc, keys_sc, values_sc, keys_t, p_sc, s_sc, k_acc, v_acc,
        )

    def half_copy(way):
        src = part_sc.at[aligned(place.s3 * rows + way * half, half)]
        return send(src, half_in.at[way], (h_sent, h_got), way, place.across(way))

    def part_copy(way, late):
        side = 1 - way if late else way
        src = part_sc.at[aligned(seats[way] * rows + side * half, half)]
        dst = part_in.at[way, pl.ds(side * half, half)]
        return send(src, dst, (p_sent, p_got), 2 * way + late, place.across(way))

    def partial_dn1():
        later_loads[0].wait()
        for seat in (place.s3, place.s1, place.s2, place.s):
            here = aligned(seat * rows, rows)
            part_sc[here, :] = dot_nt(grads_sc[here, :], wq_ref[...]).astype(BF16)
            for way in (0, 1):
                if seat is place.s3:
                    half_copy(way).start()
                elif seat is seats[way]:
                    part_copy(way, 0).start()

    def weight_grad():
        n1_copy.wait()

        def body(index):
            cols = aligned(index * 256, 256)
            qkv_g[cols, :] = dot_tn(n1_sc[:, cols], grads_sc[...]).astype(BF16)

        lax.fori_loop(0, qkv_g.shape[0] // 256, lambda index, carry: (body(index), carry)[1], 0)
        first.begin()

    def swap_dn1():
        for way in (0, 1):
            half_copy(way).wait_recv()
            base = (place.s2, place.s1)[way] * rows + way * half

            def body(index):
                here = aligned(base + index * 32, 32)
                came = half_in[way, aligned(index * 32, 32), :]
                part_sc[here, :] = (part_sc[here, :].astype(F32) + came.astype(F32)).astype(BF16)

            lax.fori_loop(0, half // 32, lambda index, carry: (body(index), carry)[1], 0)
        for way in (0, 1):
            part_copy(way, 1).start()

    def fold_first():
        depth = place.depth
        place.each(1, depth, lambda step: first.fold(step, lax.rem(step + 1, depth)))
        first.fold(0, None)

    def core_small():
        return send(small_sc.at[0], small_sc.at[1], (c_sent, c_got), 0, place.beside)

    def z_small(step):
        return send(small_sc.at[2], small_in.at[step], (z_sent, z_got), step, place.along(place.far(step)))

    def x_small(way):
        return send(small_sc.at[3], small_sc.at[4 + way], (x_sent, x_got), way, place.across(way))

    def close_dn1():
        for way in (0, 1):
            for late in (0, 1):
                part_copy(way, late).wait_recv()
        for load in later_loads[1:]:
            load.wait()
        gain = vec_ref[0:1, :]

        def body(index, sums):
            here = aligned(index * 32, 32)
            mine = aligned(place.s * rows + index * 32, 32)
            dn1 = (
                part_sc[mine, :].astype(F32)
                + part_in[0, here, :].astype(F32)
                + part_in[1, here, :].astype(F32)
            )
            token_rows = x_ref[here, :].astype(F32)
            center = token_rows - jnp.mean(token_rows, axis=-1, keepdims=True)
            inv = lax.rsqrt(jnp.mean(center * center, axis=-1, keepdims=True) + 1e-05)
            hat = center * inv
            scaled = dn1 * gain
            grad = hid_ref[here, :] + inv * (
                scaled
                - jnp.mean(scaled, axis=-1, keepdims=True)
                - hat * jnp.mean(scaled * hat, axis=-1, keepdims=True)
            )
            tokens_out[here, :] = grad.astype(BF16)
            return (
                sums[0] + jnp.sum(dn1 * hat, axis=0, keepdims=True),
                sums[1] + jnp.sum(dn1, axis=0, keepdims=True),
            )

        none = jnp.zeros((1, x_ref.shape[1]), F32)
        gain_sum, bias_sum = lax.fori_loop(0, rows // 32, body, (none, none))
        small_sc[0] = small_ref[...]
        small_sc[0, 0:1, :] = gain_sum
        small_sc[0, 1:2, :] = bias_sum
        core_small().start()

    def small_z():
        core_small().wait_recv()
        small_sc[2] = small_sc[0] + small_sc[1]
        place.each(1, place.depth, lambda step: z_small(step).start())

    def small_x():
        place.each(1, place.depth, lambda step: z_small(step).wait_recv())
        small_in[0] = small_sc[2]
        if place.depth <= 8:
            total = small_in[place.back(0)]
            for z in range(1, place.depth):
                total = total + small_in[place.back(z)]
        else:
            total = lax.fori_loop(
                1, place.depth, lambda z, sofar: sofar + small_in[place.back(z)], small_in[place.back(0)]
            )
        small_sc[3] = total
        for way in range(3):
            x_small(way).start()

    def small_end():
        for way in range(3):
            x_small(way).wait_recv()
        small_out[...] = (small_sc[3] + small_sc[4]) + (small_sc[5] + small_sc[6])

    depth = place.depth
    loose = depth > 8

    def run(count, body):
        lax.fori_loop(1, count, lambda step, carry: (body(step), carry)[1], 0)

    def fold(index):
        for one in reduces + [lone]:
            if not loose:
                step = (index + 1) % depth
                one.fold(step, (step + 1) % depth if step else None)
            elif index == 0:
                run(depth, lambda step: one.fold(step, lax.rem(step + 1, depth)))
                one.fold(0, None)

    def swap(index):
        for one in reduces:
            if not loose:
                one.swap((index + 1) % depth)
            elif index == 0:
                run(depth, one.swap)
                one.swap(0)

    def close(index):
        for one in reduces:
            if not loose:
                one.close((index + 1) % depth, (index + 1) % depth == 0)
            elif index == 0:
                run(depth, lambda step: one.close(step, False))
                one.close(0, True)

    rounds = 1 if loose else depth
    fold(0)
    if rounds > 1:
        fold(1)
    for load in loads[:4]:
        load.wait()
    steps = []
    for index in range(rounds + 2):
        if 2 <= index < rounds:
            steps.append(functools.partial(fold, index))
        if index < rounds:
            steps.append(functools.partial(swap, index))
        if 0 <= index - 1 < rounds:
            steps.append(functools.partial(close, index - 1))
    steps.insert(len(steps) // 2, down.spread)
    count = 4 * pairs
    grads_sc[...] = jnp.zeros_like(grads_sc)
    in_turn(count, unit, [steps[i * len(steps) // count : (i + 1) * len(steps) // count] for i in range(count)])
    partial_dn1()
    weight_grad()
    swap_dn1()
    fold_first()
    lone.far_sum()
    for one in reduces:
        one.collect()
    lone.swap(0)
    first.collect()
    close_dn1()
    lone.near_sum()
    small_z()
    for one in reduces + [lone]:
        one.spread()
    small_x()
    first.spread()
    small_end()
    core_small().wait_send()
    place.each(1, place.depth, lambda step: z_small(step).wait_send())
    for way in range(3):
        x_small(way).wait_send()
        if way < 2:
            half_copy(way).wait_send()
            for late in (0, 1):
                part_copy(way, late).wait_send()
    for one in [first, down, lone] + reduces:
        one.finish()


def backward_attention(fsdp_count, grad_heads, saved, x, hid, small, grads, down_part):
    heads, mask, qd, kf, lse, n1, wq, vec = saved
    rows, width = x.shape
    length, own_width = grad_heads.shape
    depth = fsdp_count // 2
    span = length // 2
    anywhere = pl.BlockSpec(memory_space=pltpu.HBM)
    vmem = pl.BlockSpec(memory_space=pltpu.VMEM)
    share = wq.shape[0] // fsdp_count
    kept = [(grad.shape[0] // fsdp_count, grad.shape[1]) for grad in grads]
    kept_qkv = (share, 4 * wq.shape[1])
    down_kept = (down_part.shape[0], 4 * down_part.shape[1])
    shape = jax.ShapeDtypeStruct

    reduce_scratch = []
    cut_at = kept[1][1] * 3 // 4
    for one in (kept[0], (kept[1][0], cut_at)):
        reduce_scratch += Reduce.scratch(depth, *one, False)
    reduce_scratch += Reduce.scratch(depth, *kept_qkv, True)
    reduce_scratch += Reduce.scratch(depth, kept[1][0], kept[1][1] - cut_at, False, far_first=True)
    return pl.pallas_call(
        functools.partial(backward_kernel, fsdp_count),
        out_shape=(shape(x.shape, BF16), shape(small.shape, F32), shape(kept_qkv, BF16))
        + tuple(shape(one, BF16) for one in kept)
        + (shape(down_kept, BF16),),
        in_specs=[anywhere] * 2 + [vmem] + [anywhere] * 2 + [vmem] + [anywhere] * 4 + [vmem] * 2 + [anywhere] * 2 + [vmem],
        out_specs=(vmem, vmem, anywhere, anywhere, anywhere, anywhere),
        scratch_shapes=[
            pltpu.VMEM((length, own_width), BF16),
            pltpu.VMEM(heads.shape, BF16),
            pltpu.VMEM(qd.shape, BF16),
            pltpu.VMEM(kf.shape, BF16),
            pltpu.VMEM(wq.shape, BF16),
            pltpu.VMEM(x.shape, BF16),
            pltpu.VMEM(hid.shape, F32),
            dma(7),
            pltpu.VMEM((length, 3 * own_width), BF16),
            pltpu.VMEM((length, LANES), BF16),
            pltpu.VMEM((length, LANES), BF16),
            pltpu.VMEM((LANES, length), BF16),
            pltpu.VMEM((length, span), BF16),
            pltpu.VMEM((length, span), BF16),
            pltpu.VMEM((length, LANES), F32),
            pltpu.VMEM((length, LANES), F32),
            pltpu.VMEM((length, width), BF16),
            pltpu.VMEM(wq.shape, BF16),
            pltpu.VMEM((length, width), BF16),
            pltpu.VMEM((2, rows, width), BF16),
            pltpu.VMEM((2, rows // 2, width), BF16),
            pltpu.VMEM((7,) + small.shape, F32),
            pltpu.VMEM((depth,) + small.shape, F32),
        ]
        + reduce_scratch
        + [dma(3), dma(6), dma(6), dma(6), dma(6)]
        + [dma(), dma(2), dma(2), dma(4), dma(4)]
        + [dma(1), dma(1), dma(depth), dma(depth), dma(3), dma(3)],
        compiler_params=pltpu.CompilerParams(
            collective_id=3, has_side_effects=True, vmem_limit_bytes=60 << 20
        ),
    )(grad_heads, heads, mask, qd, kf, lse, n1, wq, x, hid, vec, small, *grads, down_part)


def middle_kernel(
    fsdp_count,
    att_hbm,
    x_hbm,
    cot_hbm,
    vec_ref,
    out_w_hbm,
    in_w_ref,
    down_w_ref,
    result_hbm,
    go_all,
    hid_hbm,
    small_ref,
    out_g_hbm,
    in_g_ref,
    down_part,
    result_ref,
    hid_ref,
    out_g_ref,
    put_sems,
    att_ref,
    x_ref,
    cot_ref,
    out_w_ref,
    fetch_sems,
    datt_ref,
    go_sems,
    go_sent,
    go_got,
    hidden_sc,
    n2_sc,
    n2_t,
    out_acc,
    dn2_acc,
    in_buf,
    down_buf,
    grad_buf,
    act_sc,
    slope_sc,
    down_g,
    in_sems,
    down_sems,
    grad_sems,
    *rest,
):
    place = Place(fsdp_count)
    depth = place.depth
    down_like = rest[0]
    total = Reduce.take(place, down_g, down_like, False, rest[1:], True)
    rows, width = x_ref.shape
    span = down_buf.shape[1]
    hidden_units = down_g.shape[0]
    chunks = hidden_units // span
    paired = total.rows == span
    lines = rows // 32

    def order(index):
        if not paired:
            return index
        z = place.far(lax.rem(lax.div(index, 2) + 1, depth))
        return 2 * z + jnp.where(lax.rem(index, 2) == 0, 1 - place.c, place.c)

    def in_load(index):
        slot = lax.rem(index, 4)
        return pltpu.make_async_copy(
            in_w_ref.at[:, aligned(order(index) * span, span)], in_buf.at[slot], in_sems.at[slot]
        )

    def down_load(index):
        slot = lax.rem(index, 4)
        return pltpu.make_async_copy(
            down_w_ref.at[aligned(order(index) * span, span)], down_buf.at[slot], down_sems.at[slot]
        )

    def grad_store(index):
        slot = lax.rem(index, 2)
        return pltpu.make_async_copy(
            grad_buf.at[slot], in_g_ref.at[:, aligned(order(index) * span, span)], grad_sems.at[slot]
        )

    def over_rows(body, start=0):
        return lax.fori_loop(0, lines, lambda index, carry: body(aligned(index * 32, 32), carry), start)

    for index in (0, 1):
        in_load(index).start()
        down_load(index).start()
    loads = [
        pltpu.make_async_copy(src, dst, fetch_sems.at[i])
        for i, (src, dst) in enumerate(((att_hbm, att_ref), (out_w_hbm, out_w_ref), (x_hbm, x_ref), (cot_hbm, cot_ref)))
    ]
    for load in loads:
        load.start()
    place.meet()
    for load in loads:
        load.wait()
    hidden_sc[...] = x_ref[...].astype(F32) + dot_nn(att_ref[...], out_w_ref[...])

    def normalise(here, carry):
        token_rows = hidden_sc[here, :]
        center = token_rows - jnp.mean(token_rows, axis=-1, keepdims=True)
        variance = jnp.mean(center * center, axis=-1, keepdims=True)
        normed = center * lax.rsqrt(variance + 1e-05) * vec_ref[2:3, :] + vec_ref[3:4, :]
        n2_sc[here, :] = normed.astype(BF16)
        out_acc[here, :] = token_rows + vec_ref[4:5, :]
        return carry

    over_rows(normalise)
    n2_t[...] = n2_sc[...].T
    dn2_acc[...] = jnp.zeros_like(dn2_acc)
    small_ref[...] = jnp.zeros_like(small_ref)

    def place_of(which):
        per = width // span
        return pl.ds(5 + lax.div(which, per), 1), aligned(lax.rem(which, per) * span, span)

    def activate(index):
        slot, side = lax.rem(index, 4), lax.rem(index, 2)
        which = order(index)
        in_load(index).wait()
        down_load(index).wait()

        def ahead():
            in_load(index + 2).start()
            down_load(index + 2).start()

        pl.when(index + 2 < chunks)(ahead)
        line, cols = place_of(which)
        pre = dot_nn(n2_sc[...], in_buf[slot]) + vec_ref[line, cols]
        inner = jnp.tanh(0.7978845608028654 * (pre + 0.044715 * pre * pre * pre))
        act = (0.5 * pre * (1.0 + inner)).astype(BF16)
        act_sc[side] = act
        down_g[aligned(which * span, span), :] = dot_tn(act, cot_ref[...]).astype(BF16)
        slope_sc[side] = 0.5 * (1.0 + inner) + (0.5 * 0.7978845608028654) * pre * (1.0 - inner * inner) * (
            1.0 + (3.0 * 0.044715) * pre * pre
        )

    def chunk(index):
        slot, side = lax.rem(index, 4), lax.rem(index, 2)
        which = order(index)
        line, cols = place_of(which)
        grad = dot_nt(cot_ref[...], down_buf[slot]) * slope_sc[side]
        low = grad.astype(BF16)
        small_ref[line, cols] = jnp.sum(low.astype(F32), axis=0, keepdims=True)
        out_acc[...] += dot_nn(act_sc[side], down_buf[slot])
        dn2_acc[...] += dot_nt(low, in_buf[slot])
        pl.when(index >= 2)(lambda: grad_store(index - 2).wait())
        grad_buf[side] = dot_nn(n2_t[...], low).astype(BF16)
        grad_store(index).start()

    def swap_before(t):
        pl.when(t >= 1)(lambda: total.swap(lax.rem(t, depth)))

    def close_before(t):
        pl.when(t >= 2)(lambda: total.close(lax.rem(t + depth - 1, depth), False))

    if paired:

        def step(t, carry):
            dest = lax.rem(t + 1, depth)

            def early(side, carry):
                activate(2 * t + side)
                pl.when(side == 0)(lambda: total.core_copy(dest).start())
                return carry

            lax.fori_loop(0, 2, early, 0)
            total.fold(dest, None)
            swap_before(t)
            chunk(2 * t)
            chunk(2 * t + 1)
            close_before(t)
            return carry

        lax.fori_loop(0, depth, step, 0)
    else:
        lax.fori_loop(0, chunks, lambda index, carry: (activate(index), chunk(index), carry)[2], 0)
        place.each(0, depth, lambda step: total.core_copy(step).start())

        def step(t, carry):
            swap_before(t)
            total.fold(lax.rem(t + 1, depth), None)
            close_before(t)
            return carry

        lax.fori_loop(0, depth, step, 0)

    def finish(here, sums):
        token_rows = hidden_sc[here, :]
        center = token_rows - jnp.mean(token_rows, axis=-1, keepdims=True)
        inv = lax.rsqrt(jnp.mean(center * center, axis=-1, keepdims=True) + 1e-05)
        hat = center * inv
        dn2 = dn2_acc[here, :]
        cot = cot_ref[here, :].astype(F32)
        scaled = dn2 * vec_ref[2:3, :]
        grad = cot + inv * (
            scaled
            - jnp.mean(scaled, axis=-1, keepdims=True)
            - hat * jnp.mean(scaled * hat, axis=-1, keepdims=True)
        )
        hid_ref[here, :] = grad
        n2_sc[here, :] = grad.astype(BF16)
        result_ref[here, :] = out_acc[here, :].astype(BF16)
        return (
            sums[0] + jnp.sum(dn2 * hat, axis=0, keepdims=True),
            sums[1] + jnp.sum(dn2, axis=0, keepdims=True),
            sums[2] + jnp.sum(cot, axis=0, keepdims=True),
        )

    seats = (place.s1, place.s2, place.s3)
    part = width // 4
    half = rows // 2

    def go_copy(way, side):
        src = datt_ref.at[pl.ds(side * half, half), aligned(seats[way] * part, part)]
        dst = go_all.at[aligned(place.s * rows + side * half, half)]
        return send(src, dst, (go_sent, go_got), 2 * way + side, place.across(way))

    def go_arrival(way, side):
        there = go_all.at[aligned(seats[way] * rows + side * half, half)]
        return send(there, there, (go_sent, go_got), 2 * way + side, place.across(way))

    total.swap(0)
    none = jnp.zeros((1, width), F32)
    sums = (none, none, none)
    for side in (0, 1):
        sums = lax.fori_loop(
            0, lines // 2, lambda index, carry: finish(aligned(side * half + index * 32, 32), carry), sums
        )
        rows_here = pl.ds(side * half, half)
        datt_ref[rows_here, :] = dot_nt(n2_sc[rows_here, :], out_w_ref[...]).astype(BF16)
        for way in range(3):
            go_copy(way, side).start()
    gain_sum, bias_sum, cot_sum = sums
    small_ref[2:3, :] = gain_sum
    small_ref[3:4, :] = bias_sum
    small_ref[4:5, :] = cot_sum
    puts = [
        pltpu.make_async_copy(src, dst, put_sems.at[i])
        for i, (src, dst) in enumerate(((result_ref, result_hbm), (hid_ref, hid_hbm), (out_g_ref, out_g_hbm)))
    ]
    puts[0].start()
    puts[1].start()
    own_go = pltpu.make_async_copy(
        datt_ref.at[:, aligned(place.s * part, part)], go_all.at[aligned(place.s * rows, rows)], go_sems
    )
    own_go.start()
    if depth > 1:
        total.close(depth - 1, False)
    out_g_ref[...] = dot_tn(att_ref[...], n2_sc[...]).astype(BF16)
    puts[2].start()
    total.close(0, True)
    total.collect()
    down_part[...] = total.total[...]
    for index in (chunks - 2, chunks - 1):
        grad_store(index).wait()
    for put in puts:
        put.wait()
    own_go.wait()
    for way in range(3):
        for side in (0, 1):
            go_arrival(way, side).wait_recv()
            go_copy(way, side).wait_send()
    total.sent()
    place.each(1, depth, lambda step: total.z_copy(step).wait_send())


def middle(fsdp_count, att, x, cot, vec, w_out, w_in, w_down):
    rows, width = x.shape
    hidden_units = w_in.shape[1]
    span = 512
    depth = fsdp_count // 2
    anywhere = pl.BlockSpec(memory_space=pltpu.HBM)
    vmem = pl.BlockSpec(memory_space=pltpu.VMEM)
    shape = jax.ShapeDtypeStruct
    kept = (hidden_units // fsdp_count, width)
    return pl.pallas_call(
        functools.partial(middle_kernel, fsdp_count),
        out_shape=(
            shape((rows, width), BF16),
            shape((4 * rows, width // 4), BF16),
            shape((rows, width), F32),
            shape(vec.shape, F32),
            shape(w_out.shape, BF16),
            shape(w_in.shape, BF16),
            shape((kept[0], width // 4), BF16),
        ),
        in_specs=[anywhere] * 3 + [vmem] + [anywhere] * 3,
        out_specs=(anywhere, anywhere, anywhere, vmem, anywhere, anywhere, vmem),
        scratch_shapes=[
            pltpu.VMEM((rows, width), BF16),
            pltpu.VMEM((rows, width), F32),
            pltpu.VMEM(w_out.shape, BF16),
            dma(3),
            pltpu.VMEM((rows, width), BF16),
            pltpu.VMEM((rows, width), BF16),
            pltpu.VMEM((rows, width), BF16),
            pltpu.VMEM(w_out.shape, BF16),
            dma(4),
            pltpu.VMEM((rows, width), BF16),
            dma(),
            dma(6),
            dma(6),
            pltpu.VMEM((rows, width), F32),
            pltpu.VMEM((rows, width), BF16),
            pltpu.VMEM((width, rows), BF16),
            pltpu.VMEM((rows, width), F32),
            pltpu.VMEM((rows, width), F32),
            pltpu.VMEM((4, width, span), BF16),
            pltpu.VMEM((4, span, width), BF16),
            pltpu.VMEM((2, width, span), BF16),
            pltpu.VMEM((2, rows, span), BF16),
            pltpu.VMEM((2, rows, span), F32),
            pltpu.VMEM((hidden_units, width), BF16),
            dma(4),
            dma(4),
            dma(2),
            pltpu.VMEM(kept, BF16),
        ]
        + Reduce.scratch(depth, *kept, False, True),
        compiler_params=pltpu.CompilerParams(
            collective_id=5, has_side_effects=True, vmem_limit_bytes=60 << 20
        ),
    )(att, x, cot, vec, w_out, w_in, w_down)


def results_kernel(share, held, *refs):
    sources, small, refs = refs[:6], refs[6], refs[7:]
    cut = len(refs) > 20
    count = 12 if cut else 6
    outs, refs = refs[:count], refs[count:]
    taken, given, in_sems, out_sems = refs[:6], refs[6:10], refs[10], refs[11]
    given = given + taken[4:]
    pieces = []
    for i in range(6):
        rows = sources[i].shape[0]
        parts = 4 if rows % 64 == 0 else 1
        for part in range(parts):
            pieces.append((i, part, pl.ds(part * (rows // parts), rows // parts), rows // parts))
    loads = [
        pltpu.make_async_copy(sources[i].at[here], taken[i].at[here], in_sems.at[i, part]) for i, part, here, _ in pieces
    ]
    for load in loads:
        load.start()
    stores = []
    for load, (i, part, here, rows) in zip(loads, pieces):
        load.wait()
        src, dst, base = taken[i], given[i], part * rows

        def body(index, carry):
            line = aligned(base + index * 16, 16)
            dst[line, :] = src[line, :].astype(F32)
            return carry

        if i < 4:
            lax.fori_loop(0, rows // 16, body, 0)
        store = pltpu.make_async_copy(dst.at[here], outs[i].at[here], out_sems.at[i, part])
        store.start()
        stores.append(store)
    if cut:
        position = lax.axis_index("fsdp")
        cols = aligned(position * share, share)
        for line in range(5):
            outs[6 + line][...] = small[line : line + 1, cols]
        per = small.shape[1] // held
        outs[11][...] = small[pl.ds(5 + lax.div(position, per), 1), aligned(lax.rem(position, per) * held, held)]
    for store in stores:
        store.wait()


def write_results(share, held, arrays, small):
    shape = jax.ShapeDtypeStruct
    kinds = (F32, F32, F32, F32, BF16, BF16)
    shapes = [shape(a.shape, kind) for a, kind in zip(arrays, kinds)]
    cut = share % LANES == 0 and held % LANES == 0
    small_shapes = [shape((1, share), F32)] * 5 + [shape((1, held), F32)] if cut else []
    hbm = pl.BlockSpec(memory_space=pltpu.HBM)
    vmem = pl.BlockSpec(memory_space=pltpu.VMEM)
    outs = pl.pallas_call(
        functools.partial(results_kernel, share, held),
        out_shape=tuple(shapes + small_shapes),
        in_specs=[hbm] * 6 + [vmem],
        out_specs=tuple([hbm] * 6 + [vmem] * len(small_shapes)),
        scratch_shapes=[pltpu.VMEM(a.shape, BF16) for a in arrays]
        + [pltpu.VMEM(a.shape, F32) for a in arrays[:4]]
        + [dma(6, 4), dma(6, 4)],
        compiler_params=pltpu.CompilerParams(vmem_limit_bytes=60 << 20),
    )(*arrays, small)
    if cut:
        return outs[:6], [part.reshape(-1) for part in outs[6:]]
    position = lax.axis_index("fsdp")
    lines = lax.dynamic_slice_in_dim(small[:5], position * share, share, axis=1)
    rest = small[5:].reshape(-1)
    return outs, [lines[i] for i in range(5)] + [lax.dynamic_slice_in_dim(rest, position * held, held)]


def per_device(
    fsdp_count,
    tokens,
    segment_ids,
    random_blocks,
    ln1_gain,
    ln1_bias,
    w_qkv,
    w_out,
    ln2_gain,
    ln2_bias,
    w_in,
    b_in,
    w_down,
    b_down,
    cotangent,
):
    width = tokens.shape[2]
    share, held = ln1_gain.shape[0], b_in.shape[0]
    lines = fsdp_count * held // width
    position = lax.axis_index("fsdp")
    column = jnp.arange(width, dtype=jnp.int32)
    narrow = jnp.tile(jnp.stack([ln1_gain, ln1_bias, ln2_gain, ln2_bias, b_down]), (1, fsdp_count))
    narrow = jnp.where(column // share == position, narrow, jnp.zeros((), BF16))
    line = jnp.arange(lines, dtype=jnp.int32)[:, None]
    broad = jnp.tile(b_in[None], (1, width // held))
    broad = jnp.where((line * width + column) // held == position, broad, jnp.zeros((), BF16))
    vec = jnp.concatenate([narrow, broad, jnp.zeros((-(5 + lines) % 16, width), BF16)], axis=0)
    by_heads, lse, att_rows, out_weight, down_weight, in_weight, vec, normed_one, own_qkv, query_docs, key_feats, mask = (
        forward_attention(fsdp_count, tokens[0], w_qkv, vec, segment_ids, random_blocks, w_out, w_down, w_in)
    )
    result, grad_att, grad_hidden, small, grad_out, grad_in, down_part = middle(
        fsdp_count, att_rows, tokens[0], cotangent[0], vec, out_weight, in_weight, down_weight
    )
    grad_tokens, small, total_qkv, total_out, total_in, total_down = backward_attention(
        fsdp_count,
        grad_att,
        (by_heads, mask, query_docs, key_feats, lse, normed_one, own_qkv, vec),
        tokens[0],
        grad_hidden,
        small,
        (grad_out, grad_in),
        down_part,
    )
    arrays, parts = write_results(
        share, held, (total_in, total_down, total_qkv, total_out, result, grad_tokens), small
    )
    return (
        arrays[4][None],
        arrays[5][None],
        parts[0],
        parts[1],
        arrays[2],
        arrays[3],
        parts[2],
        parts[3],
        arrays[0],
        parts[5],
        arrays[1],
        parts[4],
    )


def solution(mesh):
    return jax.shard_map(
        functools.partial(per_device, mesh.shape["fsdp"]),
        mesh=mesh,
        in_specs=(
            P("fsdp", "seq", None),
            P("fsdp", "seq"),
            P("seq", None, None),
            P("fsdp"),
            P("fsdp"),
            P("fsdp", None),
            P("fsdp", None),
            P("fsdp"),
            P("fsdp"),
            P("fsdp", None),
            P("fsdp"),
            P("fsdp", None),
            P("fsdp"),
            P("fsdp", "seq", None),
        ),
        out_specs=(
            P("fsdp", "seq", None),
            P("fsdp", "seq", None),
            P("fsdp"),
            P("fsdp"),
            P("fsdp", None),
            P("fsdp", None),
            P("fsdp"),
            P("fsdp"),
            P("fsdp", None),
            P("fsdp"),
            P("fsdp", None),
            P("fsdp"),
        ),
        check_vma=False,
    )
```
